32 devices in a mesh: frames: 8 (over y, x, core), pos: 4 (over z).
Axes of the slice: x: 2, y: 2, z: 4, core: 2. Of those that a mesh axis runs over, the one named last changes fastest.
Arguments:
- frame_rows: bfloat16 [512, 16, 1024], P(('frames', 'pos')), may hold values from -6 to 6
- frame_mask: int32 [512], P(('frames', 'pos')), may hold values from 0 to 1, as said below
- gain_attention: float32 [1024], replicated, may hold values from 0.25 to 1.75
- gain_feed: float32 [1024], replicated, may hold values from 0.25 to 1.75
- qkv_master: float32 [1024, 3072], P(('frames', 'pos')), may hold values from -0.1875 to 0.1875
- out_master: float32 [1024, 1024], P(('frames', 'pos')), may hold values from -0.375 to 0.375
- gate_master: float32 [16, 1024, 2816], P('pos', 'frames'), may hold values from -0.1875 to 0.1875
- up_master: float32 [16, 1024, 2816], P('pos', 'frames'), may hold values from -0.1875 to 0.1875
- down_master: float32 [16, 2816, 1024], P('pos', 'frames'), may hold values from -0.109375 to 0.109375
- out_cotangent: bfloat16 [512, 16, 1024], P(('frames', 'pos')), may hold values from -6 to 6
Outputs:
- block_out: bfloat16 [512, 16, 1024], P(('frames', 'pos'))
- rows_grad: float32 [512, 16, 1024], P(('frames', 'pos'))
- gain_attention_grad: float32 [1024], P(('frames', 'pos'))
- gain_feed_grad: float32 [1024], P(('frames', 'pos'))
- qkv_grad: float32 [1024, 3072], P(('frames', 'pos'))
- out_proj_grad: float32 [1024, 1024], P(('frames', 'pos'))
- gate_grad: float32 [16, 1024, 2816], P('pos', 'frames')
- up_grad: float32 [16, 1024, 2816], P('pos', 'frames')
- down_grad: float32 [16, 2816, 1024], P('pos', 'frames')
The draws below stay inside these ranges and needn't reach their ends.
Inputs may be any that keep to these rules, and one draw needn't show every extreme that they name: `frame_mask`: in each aligned block of 16 frames the live frames come first and are at least half of the block; some block is all live.
All inputs are finite; a program needn't handle non-finite values.
Results may differ from the reference program's by a relative error of at most 0.013.
Values may be sent and summed in bfloat16 or wider, within the bound.
A program may use at most 384 MiB of HBM per device.

```python
import math
import jax
import jax.numpy as jnp
from jax import lax

D = 1024
H = 16
HD = 64
FF = 2816
P_SIZE = 16
FR_DEV = 16
FRAMES = 512


def draw_frame_mask(key, part):
    blocks = FRAMES // FR_DEV
    live = jax.random.randint(jax.random.fold_in(key, 11), (blocks,), FR_DEV // 2, FR_DEV + 1)
    chosen = jax.random.randint(jax.random.fold_in(key, 12), (), 0, blocks)
    live = jnp.where(jnp.arange(blocks) == chosen, FR_DEV, live)
    places = jnp.arange(FR_DEV)
    return (places[None, :] < live[:, None]).astype(jnp.int32).reshape(FRAMES)


def spiked(result, rng, source, target, shards_of, factor):
    def block_of(axis_at):
        return (jnp.arange(result.shape[axis_at]) // (result.shape[axis_at] // shards_of)).reshape((-1,) + (1,) * (result.ndim - 1 - axis_at))

    first = jax.random.permutation(rng, shards_of)[block_of(target)]
    second = (block_of(target) + shards_of // 2) % shards_of
    return jnp.where((block_of(source) == first) | (block_of(source) == second), factor * result, result)


def level_of(rng, dims, cuts, smallest, largest):
    loudness = 1.0
    for axis_at, blocks in cuts:
        steps = jax.random.uniform(jax.random.fold_in(jax.random.fold_in(rng, 6), axis_at), (blocks,), jnp.float32, smallest / len(cuts), largest / len(cuts))
        loudness = loudness * jnp.repeat(jnp.exp(steps), dims[axis_at] // blocks).reshape((-1,) + (1,) * (len(dims) - 1 - axis_at))
    return loudness


def normal_values(own_key, shape, width, bound, split=(), kind=jnp.bfloat16):
    values = jax.random.normal(own_key, shape, jnp.float32) * width
    if len(split) > 0:
        values = level_of(own_key, shape, split, -0.22, 0.18) * values
    return jnp.clip(values, min=-bound, max=bound).astype(kind)


def gaussian_with(key, shape, spread, bound, split, heavy, held_as=jnp.bfloat16):
    drawn = spread * jax.random.normal(key, shape, jnp.float32)
    if split:
        drawn = drawn * level_of(key, shape, split, -0.22, 0.18)
    return jnp.clip(spiked(drawn, jax.random.fold_in(key, 3), *heavy), -bound, bound).astype(held_as)


def setup_inputs(seed: int = 0) -> dict:
    seeds = jax.random.split(jax.random.key(seed), 11)
    return {
        "frame_rows": gaussian_with(seeds[0], (FRAMES, P_SIZE, D), 1.0, 6.0, ((0, 32),), (0, 2, 32, 2.75)),
        "frame_mask": draw_frame_mask(jax.random.fold_in(seeds[10], 71), 0),
        "gain_attention": jnp.clip(1.0 + 0.15 * jax.random.normal(seeds[2], (D,), jnp.float32), 0.25, 1.75),
        "gain_feed": jnp.clip(1.0 + 0.15 * jax.random.normal(seeds[3], (D,), jnp.float32), 0.25, 1.75),
        "qkv_master": normal_values(seeds[4], (D, 3 * D), D ** -0.5, 0.1875, ((0, 32),), jnp.float32),
        "out_master": normal_values(seeds[5], (D, D), (D // 4) ** -0.5, 0.375, ((0, 32),), jnp.float32),
        "gate_master": normal_values(seeds[6], (P_SIZE, D, FF), D ** -0.5, 0.1875, ((0, 4), (1, 8)), jnp.float32),
        "up_master": normal_values(seeds[7], (P_SIZE, D, FF), D ** -0.5, 0.1875, ((0, 4), (1, 8)), jnp.float32),
        "down_master": normal_values(seeds[8], (P_SIZE, FF, D), FF ** -0.5, 0.109375, ((0, 4), (1, 8)), jnp.float32),
        "out_cotangent": normal_values(seeds[9], (FRAMES, P_SIZE, D), 1.0, 6.0, ((0, 32),)),
    }


HIGHEST = lax.Precision.HIGHEST

@jax.custom_vjp
def low(v):
    return lax.optimization_barrier(v.astype(jnp.bfloat16)).astype(jnp.float32)

@jax.custom_vjp
def low_back(v):
    return v

def low_keep(v):
    return (low(v), None)

def low_pass(kept, grad):
    return (grad,)

def back_keep(v):
    return (v, None)

def back_low(kept, grad):
    return (low(grad),)
low.defvjp(low_keep, low_pass)
low_back.defvjp(back_keep, back_low)

def rms_norm(values, gain_vector):
    return values * lax.rsqrt(lax.optimization_barrier(jnp.mean(values * values, axis=-1, keepdims=True)) + 1e-05) * gain_vector

def attend(qkv_rows):
    frame_count = qkv_rows.shape[0]
    positions = qkv_rows.shape[1]
    split_rows = qkv_rows.reshape(frame_count, positions, 3, H, HD)
    queries = split_rows[:, :, 0]
    keys_all = split_rows[:, :, 1]
    values_all = split_rows[:, :, 2]
    scores = jnp.einsum('fqhe,fkhe->fhqk', queries, keys_all, precision=HIGHEST) * (1.0 / math.sqrt(HD))
    causal = jnp.arange(positions)[:, None] >= jnp.arange(positions)[None, :]
    scores = jnp.where(causal, scores, -1e+30)
    weights = jax.nn.softmax(scores, axis=-1)
    mixed = jnp.einsum('fhqk,fkhe->fqhe', weights, values_all, precision=HIGHEST)
    return mixed.reshape(frame_count, positions, H * HD)

def block_forward(rows_in, keep_block, gain_attention, gain_feed, qkv_w, out_w, gate_w, up_w, down_w):
    normed_one = low(rms_norm(rows_in, gain_attention))
    qkv_rows = low_back(jnp.einsum('fpd,de->fpe', normed_one, low(qkv_w), precision=HIGHEST))
    mixed = attend(qkv_rows)
    branch = low_back(jnp.einsum('fpd,de->fpe', low(mixed), low(out_w), precision=HIGHEST))
    middle = rows_in + branch
    normed_two = low_back(low(rms_norm(middle, gain_feed)))
    gate_rows = low_back(jnp.einsum('fpd,pdh->fph', normed_two, low(gate_w), precision=HIGHEST))
    up_rows = low_back(jnp.einsum('fpd,pdh->fph', normed_two, low(up_w), precision=HIGHEST))
    hidden = low(jax.nn.silu(gate_rows) * up_rows)
    feed_out = low(low_back(jnp.einsum('fph,phd->fpd', hidden, low(down_w), precision=HIGHEST)))
    return keep_block[:, None, None] * (middle + feed_out)

def reference(frame_rows, frame_mask, gain_attention, gain_feed, qkv_master, out_master, gate_master, up_master, down_master, out_cotangent):
    block_frames = math.gcd(FRAMES, 256)
    blocks = FRAMES // block_frames
    rows_all = frame_rows.astype(jnp.float32).reshape(blocks, block_frames, P_SIZE, D)
    keep_all = frame_mask.astype(jnp.float32).reshape(blocks, block_frames)
    grads_all = out_cotangent.astype(jnp.float32).reshape(blocks, block_frames, P_SIZE, D)
    params = (gain_attention, gain_feed, qkv_master, out_master, gate_master, up_master, down_master)

    def one_block(totals, inputs):
        rows_block, keep_block, cotangent = inputs

        def forward(rows_in, *weights):
            return block_forward(rows_in, keep_block, *weights)
        outputs, pullback = jax.vjp(forward, rows_block, *params)
        pulled = pullback(cotangent)
        totals = tuple((running + extra for running, extra in zip(totals, pulled[1:])))
        return (totals, (outputs.astype(jnp.bfloat16), pulled[0]))
    initial = tuple((jnp.zeros_like(item) for item in params))
    totals, (outputs, row_grads) = lax.scan(one_block, initial, (rows_all, keep_all, grads_all))
    return (outputs.reshape(FRAMES, P_SIZE, D), row_grads.reshape(FRAMES, P_SIZE, D), totals[0], totals[1], totals[2], totals[3], totals[4], totals[5], totals[6])
```

```python
import math

import jax
import jax.numpy as jnp
from jax import lax
from jax.sharding import PartitionSpec as P

H = 16
HD = 64
BF = jnp.bfloat16
F32 = jnp.float32


def rms_norm(values, gain_vector):
    return (
        values * lax.rsqrt(jnp.mean(values * values, axis=-1, keepdims=True) + 1e-05) * gain_vector
    )


def attend(qkv_rows):
    frame_count = qkv_rows.shape[0]
    positions = qkv_rows.shape[1]
    split_rows = qkv_rows.reshape(frame_count, positions, 3, H, HD)
    queries = split_rows[:, :, 0]
    keys_all = split_rows[:, :, 1]
    values_all = split_rows[:, :, 2]
    scores = jnp.einsum("fqhe,fkhe->fhqk", queries, keys_all, preferred_element_type=F32) * (
        1.0 / math.sqrt(HD)
    )
    causal = jnp.arange(positions)[:, None] >= jnp.arange(positions)[None, :]
    scores = jnp.where(causal, scores, -1e30)
    weights = jax.nn.softmax(scores, axis=-1)
    mixed = jnp.einsum("fhqk,fkhe->fqhe", weights, values_all, preferred_element_type=F32)
    return mixed.reshape(frame_count, positions, H * HD)


def local(
    frame_rows,
    frame_mask,
    gain_attention,
    gain_feed,
    qkv_master,
    out_master,
    gate_master,
    up_master,
    down_master,
    out_cotangent,
):
    nf = lax.axis_size("frames")
    nz = lax.axis_size("pos")
    lp, dslice, ff = gate_master.shape
    ffs = down_master.shape[1]
    fr, npos, d = frame_rows.shape

    keep_rows = frame_mask.astype(F32)[:, None, None]
    inputs = frame_rows.astype(F32)

    def turned(w):
        return w.astype(BF).reshape(lp, dslice, nf, ffs).transpose(2, 0, 3, 1)

    def untwist(w):
        return w.transpose(1, 2, 0, 3).reshape(lp, ffs, d)

    def to_pos(rows):
        moved = rows.transpose(1, 0, 2).reshape(nz, lp, fr, d)
        return lax.all_to_all(moved, "pos", split_axis=0, concat_axis=0, tiled=True)

    def gathered(rows):
        every = lax.all_gather(rows, "frames", axis=0, tiled=False)
        return every.transpose(2, 0, 1, 3, 4).reshape(lp, nf * nz * fr, d)

    def scattered(rows):
        moved = rows.reshape(lp, nf, nz, fr, d).transpose(1, 2, 0, 3, 4)
        summed = lax.psum_scatter(moved, "frames", scatter_dimension=0, tiled=False)
        back = lax.all_to_all(summed.astype(BF), "pos", split_axis=0, concat_axis=0, tiled=True)
        return back.reshape(npos, fr, d).transpose(1, 0, 2)

    both = jnp.concatenate((qkv_master.astype(BF), out_master.astype(BF)), axis=1)
    w_all = lax.all_gather(both, ("frames", "pos"), axis=0, tiled=True)
    w_qkv = w_all[:, : 3 * d]
    w_out = w_all[:, 3 * d :]
    pair = jnp.stack((turned(gate_master), turned(up_master)), axis=1)
    pair = lax.all_to_all(pair, "frames", split_axis=0, concat_axis=0, tiled=True)
    gate_t = untwist(pair[:, 0])
    up_t = untwist(pair[:, 1])
    down = down_master.astype(BF)
    upstream = keep_rows * out_cotangent.astype(F32)
    gy = gathered(to_pos(upstream.astype(BF)))

    normed_one, norm_one_pull = jax.vjp(rms_norm, inputs, gain_attention)
    normed_low = normed_one.astype(BF)
    qkv_rows = jnp.einsum("fpd,de->fpe", normed_low, w_qkv, preferred_element_type=F32)
    mixed, attend_pull = jax.vjp(attend, qkv_rows)
    mixed_low = mixed.astype(BF)
    branch = jnp.einsum("fpd,de->fpe", mixed_low, w_out, preferred_element_type=F32)
    middle = inputs + branch
    normed_two, norm_two_pull = jax.vjp(rms_norm, middle, gain_feed)
    b = gathered(to_pos(normed_two.astype(BF)))

    gate_rows = jnp.einsum("prd,phd->phr", b, gate_t, preferred_element_type=F32)
    up_rows = jnp.einsum("prd,phd->phr", b, up_t, preferred_element_type=F32)
    hidden_grad = jnp.einsum("prd,phd->phr", gy, down, preferred_element_type=F32)
    sigma = jax.nn.sigmoid(gate_rows)
    silu_gate = gate_rows * sigma
    hidden = (silu_gate * up_rows).astype(BF)
    gate_back = (hidden_grad * up_rows * sigma * (1.0 + gate_rows * (1.0 - sigma))).astype(BF)
    up_back = (hidden_grad * silu_gate).astype(BF)
    db = jnp.einsum("phr,phd->prd", gate_back, gate_t, preferred_element_type=F32) + jnp.einsum(
        "phr,phd->prd", up_back, up_t, preferred_element_type=F32
    )
    back_rows = scattered(db.astype(BF)).astype(F32)
    feed = jnp.einsum("phr,phd->prd", hidden, down, preferred_element_type=F32)
    returned = scattered(feed.astype(BF)).astype(F32)
    block_out = (keep_rows * (middle + returned)).astype(BF)
    gate_grad = jnp.einsum("phr,prd->phd", gate_back, b, preferred_element_type=F32).astype(BF)
    up_grad = jnp.einsum("phr,prd->phd", up_back, b, preferred_element_type=F32).astype(BF)
    down_grad = jnp.einsum("phr,prd->phd", hidden, gy, preferred_element_type=F32)

    grads = jnp.stack((gate_grad, up_grad), axis=0).reshape(2, lp, ffs, nf, dslice)
    grads = lax.all_to_all(
        grads.transpose(3, 0, 1, 2, 4), "frames", split_axis=0, concat_axis=0, tiled=True
    )
    grads = grads.transpose(1, 2, 4, 0, 3).reshape(2, lp, dslice, ff).astype(F32)

    pulled_two = norm_two_pull(back_rows)
    middle_grad = upstream + pulled_two[0]
    branch_grad = middle_grad.astype(BF)
    out_weight_grad = jnp.einsum("fpd,fpe->de", mixed_low, branch_grad, preferred_element_type=F32)
    mixed_grad = jnp.einsum("fpe,de->fpd", branch_grad, w_out, preferred_element_type=F32)
    qkv_back = attend_pull(mixed_grad)[0].astype(BF)
    qkv_weight_grad = jnp.einsum("fpd,fpe->de", normed_low, qkv_back, preferred_element_type=F32)
    normed_grad = jnp.einsum("fpe,de->fpd", qkv_back, w_qkv, preferred_element_type=F32)
    pulled_one = norm_one_pull(normed_grad)
    rows_grad = middle_grad + pulled_one[0]

    gains = jnp.stack((pulled_one[1], pulled_two[1]), axis=1)
    gains_hi = gains.astype(BF)
    gains_lo = (gains - gains_hi.astype(F32)).astype(BF)
    tail = jnp.concatenate((gains_hi, gains_lo, jnp.zeros((d, 124), BF)), axis=1)
    total = jnp.concatenate(
        (qkv_weight_grad.astype(BF), out_weight_grad.astype(BF), tail), axis=1
    )
    total = lax.psum_scatter(total, "frames", scatter_dimension=0, tiled=True)
    total = lax.psum_scatter(total, "pos", scatter_dimension=0, tiled=True).astype(F32)
    gain_grads = total[:, 4 * d : 4 * d + 2] + total[:, 4 * d + 2 : 4 * d + 4]
    return (
        block_out,
        rows_grad,
        gain_grads[:, 0],
        gain_grads[:, 1],
        total[:, : 3 * d],
        total[:, 3 * d : 4 * d],
        grads[0],
        grads[1],
        down_grad,
    )
def solution(mesh):
    in_specs = (
        P(("frames", "pos"), None, None),
        P(("frames", "pos")),
        P(),
        P(),
        P(("frames", "pos"), None),
        P(("frames", "pos"), None),
        P("pos", "frames", None),
        P("pos", "frames", None),
        P("pos", "frames", None),
        P(("frames", "pos"), None, None),
    )
    out_specs = (
        P(("frames", "pos"), None, None),
        P(("frames", "pos"), None, None),
        P(("frames", "pos")),
        P(("frames", "pos")),
        P(("frames", "pos"), None),
        P(("frames", "pos"), None),
        P("pos", "frames", None),
        P("pos", "frames", None),
        P("pos", "frames", None),
    )
    return jax.shard_map(local, mesh=mesh, in_specs=in_specs, out_specs=out_specs, check_vma=False)
```

```python
import functools
import math

import jax
import jax.numpy as jnp
from jax import lax
from jax.experimental import pallas as pl
from jax.experimental.pallas import tpu as pltpu
from jax.sharding import PartitionSpec as P

H = 16
HD = 64
BF = jnp.bfloat16
F32 = jnp.float32
MESH = pl.DeviceIdType.MESH
ANY = pl.BlockSpec(memory_space=pl.ANY)
VM = pl.BlockSpec(memory_space=pltpu.VMEM)


def place():
    return lax.axis_index("frames"), lax.axis_index("pos")


def flip(index, mask):
    bit = 1
    while bit <= mask:
        if mask & bit:
            index = index + bit * (1 - 2 * ((index // bit) % 2))
        bit *= 2
    return index


def greet(nf, nz, every_frame):
    f, z = place()
    hops = [1] + [2 * m for m in range(1, nf // 2)]
    if every_frame:
        hops = list(range(1, nf))
    others = [(flip(f, h), z) for h in hops] + [(f, flip(z, k)) for k in range(1, nz)]
    barrier = pltpu.get_barrier_semaphore()
    for other in others:
        pl.semaphore_signal(barrier, inc=1, device_id=other, device_id_type=MESH)
    pl.semaphore_wait(barrier, len(others))


def remote(src, dst, send, recv, to):
    copy = pltpu.make_async_remote_copy(
        src_ref=src, dst_ref=dst, send_sem=send, recv_sem=recv, device_id=to, device_id_type=MESH
    )
    copy.start()
    return copy


def relay_of(k):
    return 1 if k % 2 == 0 else 2


class Gather:
    def __init__(self, nf, nz, src_for, out, sems):
        self.nf, self.nz, self.nc = nf, nz, nf // 2
        self.f, self.z = place()
        self.src_for, self.out, self.sems = src_for, out, sems
        self.sent = []
        self.tree = self.nc == 4

    @staticmethod
    def sem_shape(nf, nz):
        return (2, 1 + 2 * (nf // 2), nz)

    def push(self, src, dst, hop, k, to):
        self.sent.append(remote(src, dst, self.sems.at[0, hop, k], self.sems.at[1, hop, k], to))

    def arrive(self, dst, hop, k):
        pltpu.make_async_remote_copy(
            src_ref=dst,
            dst_ref=dst,
            send_sem=self.sems.at[0, hop, k],
            recv_sem=self.sems.at[1, hop, k],
            device_id=(flip(self.f, 1), self.z),
            device_id_type=MESH,
        ).wait_recv()

    def begin(self):
        f, z = self.f, self.z
        for k in range(1, self.nz):
            self.push(self.src_for(flip(z, k)), self.out.at[f, z], 0, k, (f, flip(z, k)))
        self.own = pltpu.make_async_copy(self.src_for(z), self.out.at[f, z], self.sems.at[0, 0, 0])
        self.own.start()
        self.spread(self.src_for(z), 0)

    def spread(self, src, k):
        f, z = self.f, self.z
        block = self.out.at[f, flip(z, k)]
        for m in range(1, self.nc):
            if self.tree and m == 3:
                continue
            self.push(src, block, m, k, (flip(f, 2 * m), z))
        self.push(src, block, self.nc, k, (flip(f, 1), z))

    def along(self, k):
        block = self.out.at[self.f, flip(self.z, k)]
        self.arrive(block, 0, k)
        self.spread(block, k)

    def over(self, m, k):
        f, z = self.f, self.z
        block = self.out.at[flip(f, 2 * m), flip(z, k)]
        self.arrive(block, m, k)
        if self.tree and m == relay_of(k):
            self.push(block, block, 3, k, (flip(f, 2 * (3 - m)), z))
        self.push(block, block, self.nc + m, k, (flip(f, 1), z))

    def order(self, k):
        first = relay_of(k) if self.tree else 1
        return [first] + [m for m in range(1, self.nc) if m != first]

    def finish(self):
        f, z = self.f, self.z
        for k in range(self.nz):
            for m in range(self.nc):
                self.arrive(self.out.at[flip(f, 2 * m + 1), flip(z, k)], self.nc + m, k)
        self.own.wait()
        for copy in self.sent:
            copy.wait_send()


class Swap:
    def __init__(self, nf, src, out, sems):
        self.nf, self.src, self.out, self.sems = nf, src, out, sems
        self.f, self.z = place()
        self.sent = []

    @staticmethod
    def sem_shape(nf):
        return (2, nf)

    def start(self):
        f, z = self.f, self.z
        self.own = pltpu.make_async_copy(self.src.at[f], self.out.at[f], self.sems.at[0, 0])
        self.own.start()
        for m in range(self.nf - 1, 0, -1):
            self.sent.append(
                remote(
                    self.src.at[flip(f, m)],
                    self.out.at[f],
                    self.sems.at[0, m],
                    self.sems.at[1, m],
                    (flip(f, m), z),
                )
            )

    def finish(self):
        self.own.wait()
        for copy in self.sent:
            copy.wait()


class Scatter:
    def __init__(self, nf, nz, src, sib, tx, rx, ty, land, sems):
        self.nf, self.nz, self.nc = nf, nz, nf // 2
        self.f, self.z = place()
        self.src, self.sib, self.tx, self.rx, self.ty = src, sib, tx, rx, ty
        self.land, self.sems = land, sems
        self.sent = []

    @staticmethod
    def scratch(nf, nz, rows, columns):
        nc = nf // 2
        block = (rows, columns)
        return [
            pltpu.VMEM((nz, nc) + block, BF),
            pltpu.VMEM((nz, nc) + block, BF),
            pltpu.VMEM((nz, nc) + block, BF),
            pltpu.VMEM((nz,) + block, BF),
            pltpu.VMEM((nz,) + block, BF),
            pltpu.SemaphoreType.DMA((2, 1 + 2 * nc, nz)),
        ]

    def push(self, src, dst, hop, k, to):
        copy = remote(src, dst, self.sems.at[0, hop, k], self.sems.at[1, hop, k], to)
        self.sent.append(copy)

    def arrive(self, dst, hop, k):
        pltpu.make_async_remote_copy(
            src_ref=dst,
            dst_ref=dst,
            send_sem=self.sems.at[0, hop, k],
            recv_sem=self.sems.at[1, hop, k],
            device_id=(flip(self.f, 1), self.z),
            device_id_type=MESH,
        ).wait_recv()

    def pairs(self, k):
        f, z = self.f, self.z
        for m in list(range(self.nc - 1, 0, -1)) + [0]:
            self.push(
                self.src.at[flip(f, 2 * m + 1), flip(z, k)],
                self.sib.at[k, m],
                self.nc + m,
                k,
                (flip(f, 1), z),
            )

    def chips(self, k):
        f, z = self.f, self.z
        for m in list(range(self.nc - 1, 0, -1)):
            self.arrive(self.sib.at[k, m], self.nc + m, k)
            add_into(self.tx.at[k, m], self.src.at[flip(f, 2 * m), flip(z, k)], self.sib.at[k, m])
            self.push(self.tx.at[k, m], self.rx.at[k, m], m, k, (flip(f, 2 * m), z))

    def home(self, k, out=None):
        f, z = self.f, self.z
        self.arrive(self.sib.at[k, 0], self.nc, k)
        for m in range(1, self.nc):
            self.arrive(self.rx.at[k, m], m, k)
        terms = [self.src.at[f, flip(z, k)], self.sib.at[k, 0]]
        terms += [self.rx.at[k, m] for m in range(1, self.nc)]
        if k == 0:
            add_into(out, *terms)
            return
        add_into(self.ty.at[k], *terms)
        self.push(self.ty.at[k], self.land.at[k], 0, k, (f, flip(z, k)))

    def landed(self, k):
        self.arrive(self.land.at[k], 0, k)

    def finish(self):
        for copy in self.sent:
            copy.wait_send()


def add_into(out, *terms):
    rows = out.shape[0]
    step = 16 if rows % 16 == 0 else rows

    def body(i, carry):
        at = pl.ds(pl.multiple_of(i * step, step), step)
        total = terms[0][at, :].astype(F32)
        for term in terms[1:]:
            total = total + term[at, :].astype(F32)
        out[at, :] = total.astype(out.dtype)
        return carry

    lax.fori_loop(0, rows // step, body, 0)


def call(kernel, ident, **kw):
    return pl.pallas_call(
        kernel,
        compiler_params=pltpu.CompilerParams(
            collective_id=ident, has_side_effects=True, vmem_limit_bytes=56 * 2**20
        ),
        **kw,
    )


def run_gathers(gathers, nz):
    for k in range(nz):
        for g in gathers:
            if k > 0:
                g.along(k)
        for g in gathers:
            if g.tree and k > 0:
                g.over(relay_of(k - 1), k - 1)
    for g in gathers:
        if g.tree:
            g.over(relay_of(nz - 1), nz - 1)
    for k in range(nz):
        for g in gathers:
            for m in range(1, g.nc):
                if g.tree and m == relay_of(k):
                    continue
                g.over(m, k)


def first_kernel(nf, nz, attn, gy, pair, attn_all, gy_all, pair_all, s1, s2, s3):
    greet(nf, nz, True)
    weights = Gather(nf, nz, lambda zz: attn, attn_all, s1)
    rows = Gather(nf, nz, lambda zz: gy.at[zz], gy_all, s2)
    swap = Swap(nf, pair, pair_all, s3)
    weights.begin()
    rows.begin()
    swap.start()
    run_gathers([weights, rows], nz)
    weights.finish()
    rows.finish()
    swap.finish()


def rows_kernel(nf, nz, b, b_all, s1):
    greet(nf, nz, False)
    rows = Gather(nf, nz, lambda zz: b.at[zz], b_all, s1)
    rows.begin()
    run_gathers([rows], nz)
    rows.finish()


def back_kernel(nf, nz, terms, out, sib, tx, rx, ty, land, sems):
    greet(nf, nz, False)
    s = Scatter(nf, nz, terms, sib, tx, rx, ty, land, sems)
    z = s.z
    for k in range(nz - 1, -1, -1):
        s.pairs(k)
    for k in range(nz - 1, -1, -1):
        s.chips(k)
    for k in range(nz - 1, -1, -1):
        s.home(k, out.at[z])
    for k in range(1, nz):
        s.landed(k)
        out[flip(z, k)] = land[k]
    s.finish()


def last_kernel(nf, nz, terms, pair, out, pair_all, sib, tx, rx, ty, land, sems, s2):
    greet(nf, nz, True)
    s = Scatter(nf, nz, terms, sib, tx, rx, ty, land, sems)
    swap = Swap(nf, pair, pair_all, s2)
    for k in range(nz - 1, -1, -1):
        s.pairs(k)
    swap.start()
    for k in range(nz - 1, -1, -1):
        s.chips(k)
    for k in range(nz - 1, -1, -1):
        s.home(k, out)
    for k in range(1, nz):
        s.landed(k)
        add_into(out, out, land.at[k])
    s.finish()
    swap.finish()


def rms_norm(values, gain_vector):
    return (
        values * lax.rsqrt(jnp.mean(values * values, axis=-1, keepdims=True) + 1e-05) * gain_vector
    )


def attend(qkv_rows):
    frame_count = qkv_rows.shape[0]
    positions = qkv_rows.shape[1]
    split_rows = qkv_rows.reshape(frame_count, positions, 3, H, HD)
    queries = split_rows[:, :, 0]
    keys_all = split_rows[:, :, 1]
    values_all = split_rows[:, :, 2]
    scores = jnp.einsum("fqhe,fkhe->fhqk", queries, keys_all, preferred_element_type=F32) * (
        1.0 / math.sqrt(HD)
    )
    causal = jnp.arange(positions)[:, None] >= jnp.arange(positions)[None, :]
    scores = jnp.where(causal, scores, -1e30)
    weights = jax.nn.softmax(scores, axis=-1)
    mixed = jnp.einsum("fhqk,fkhe->fqhe", weights, values_all, preferred_element_type=F32)
    return mixed.reshape(frame_count, positions, H * HD)


def local(
    frame_rows,
    frame_mask,
    gain_attention,
    gain_feed,
    qkv_master,
    out_master,
    gate_master,
    up_master,
    down_master,
    out_cotangent,
):
    nf = lax.axis_size("frames")
    nz = lax.axis_size("pos")
    lp, dslice, ff = gate_master.shape
    ffs = down_master.shape[1]
    fr, npos, d = frame_rows.shape

    keep_rows = frame_mask.astype(F32)[:, None, None]
    inputs = frame_rows.astype(F32)

    def turned(w):
        return w.astype(BF).reshape(lp, dslice, nf, ffs).transpose(2, 0, 3, 1)

    def untwist(w):
        return w.transpose(1, 2, 0, 3).reshape(lp, ffs, d)

    def to_pos(rows):
        return rows.transpose(1, 0, 2).reshape(nz, lp * fr, d)

    def gathered(every):
        every = every.reshape(nf, nz, lp, fr, d)
        return every.transpose(2, 0, 1, 3, 4).reshape(lp, nf * nz * fr, d)

    rows_shape = jax.ShapeDtypeStruct((nf, nz, lp * fr, d), BF)
    back_shape = jax.ShapeDtypeStruct((nz, lp * fr, d), BF)
    gather_sems = pltpu.SemaphoreType.DMA(Gather.sem_shape(nf, nz))
    swap_sems = pltpu.SemaphoreType.DMA(Swap.sem_shape(nf))

    def scattered(rows, ident):
        moved = rows.reshape(lp, nf, nz, fr, d).transpose(1, 2, 0, 3, 4)
        moved = moved.reshape(nf, nz, lp * fr, d)
        back = call(
            functools.partial(back_kernel, nf, nz),
            ident,
            out_shape=back_shape,
            in_specs=[VM],
            out_specs=VM,
            scratch_shapes=Scatter.scratch(nf, nz, lp * fr, d),
        )(moved)
        return back.reshape(npos, fr, d).transpose(1, 0, 2)

    both = jnp.concatenate((qkv_master.astype(BF), out_master.astype(BF)), axis=1)
    pair = jnp.stack((turned(gate_master), turned(up_master)), axis=1)
    upstream = keep_rows * out_cotangent.astype(F32)
    own_rows = both.shape[0]
    w_all, gy_all, pair = call(
        functools.partial(first_kernel, nf, nz),
        0,
        out_shape=(
            jax.ShapeDtypeStruct((nf, nz) + both.shape, BF),
            rows_shape,
            jax.ShapeDtypeStruct(pair.shape, BF),
        ),
        in_specs=[ANY] * 3,
        out_specs=(ANY,) * 3,
        scratch_shapes=[gather_sems, gather_sems, swap_sems],
    )(both, to_pos(upstream.astype(BF)), pair)
    w_all = w_all.reshape(d, both.shape[1])
    w_qkv = w_all[:, : 3 * d]
    w_out = w_all[:, 3 * d :]
    gate_t = untwist(pair[:, 0])
    up_t = untwist(pair[:, 1])
    down = down_master.astype(BF)
    gy = gathered(gy_all)

    normed_one, norm_one_pull = jax.vjp(rms_norm, inputs, gain_attention)
    normed_low = normed_one.astype(BF)
    qkv_rows = jnp.einsum("fpd,de->fpe", normed_low, w_qkv, preferred_element_type=F32)
    mixed, attend_pull = jax.vjp(attend, qkv_rows)
    mixed_low = mixed.astype(BF)
    branch = jnp.einsum("fpd,de->fpe", mixed_low, w_out, preferred_element_type=F32)
    middle = inputs + branch
    normed_two, norm_two_pull = jax.vjp(rms_norm, middle, gain_feed)
    b_all = call(
        functools.partial(rows_kernel, nf, nz),
        1,
        out_shape=rows_shape,
        in_specs=[ANY],
        out_specs=ANY,
        scratch_shapes=[gather_sems],
    )(to_pos(normed_two.astype(BF)))
    b = gathered(b_all)

    gate_rows = jnp.einsum("prd,phd->phr", b, gate_t, preferred_element_type=F32)
    up_rows = jnp.einsum("prd,phd->phr", b, up_t, preferred_element_type=F32)
    hidden_grad = jnp.einsum("prd,phd->phr", gy, down, preferred_element_type=F32)
    sigma = jax.nn.sigmoid(gate_rows)
    silu_gate = gate_rows * sigma
    hidden = (silu_gate * up_rows).astype(BF)
    gate_back = (hidden_grad * up_rows * sigma * (1.0 + gate_rows * (1.0 - sigma))).astype(BF)
    up_back = (hidden_grad * silu_gate).astype(BF)
    db = jnp.einsum("phr,phd->prd", gate_back, gate_t, preferred_element_type=F32) + jnp.einsum(
        "phr,phd->prd", up_back, up_t, preferred_element_type=F32
    )
    back_rows = scattered(db.astype(BF), 2).astype(F32)
    feed = jnp.einsum("phr,phd->prd", hidden, down, preferred_element_type=F32)
    returned = scattered(feed.astype(BF), 3).astype(F32)
    block_out = (keep_rows * (middle + returned)).astype(BF)
    gate_grad = jnp.einsum("phr,prd->phd", gate_back, b, preferred_element_type=F32).astype(BF)
    up_grad = jnp.einsum("phr,prd->phd", up_back, b, preferred_element_type=F32).astype(BF)
    down_grad = jnp.einsum("phr,prd->phd", hidden, gy, preferred_element_type=F32)

    grads = jnp.stack((gate_grad, up_grad), axis=0).reshape(2, lp, ffs, nf, dslice)
    grads = grads.transpose(3, 0, 1, 2, 4)

    pulled_two = norm_two_pull(back_rows)
    middle_grad = upstream + pulled_two[0]
    branch_grad = middle_grad.astype(BF)
    out_weight_grad = jnp.einsum("fpd,fpe->de", mixed_low, branch_grad, preferred_element_type=F32)
    mixed_grad = jnp.einsum("fpe,de->fpd", branch_grad, w_out, preferred_element_type=F32)
    qkv_back = attend_pull(mixed_grad)[0].astype(BF)
    qkv_weight_grad = jnp.einsum("fpd,fpe->de", normed_low, qkv_back, preferred_element_type=F32)
    normed_grad = jnp.einsum("fpe,de->fpd", qkv_back, w_qkv, preferred_element_type=F32)
    pulled_one = norm_one_pull(normed_grad)
    rows_grad = middle_grad + pulled_one[0]

    gains = jnp.stack((pulled_one[1], pulled_two[1]), axis=1)
    gains_hi = gains.astype(BF)
    gains_lo = (gains - gains_hi.astype(F32)).astype(BF)
    tail = jnp.concatenate((gains_hi, gains_lo, jnp.zeros((d, 124), BF)), axis=1)
    total = jnp.concatenate(
        (qkv_weight_grad.astype(BF), out_weight_grad.astype(BF), tail), axis=1
    )
    total = total.reshape(nf, nz, own_rows, total.shape[1])
    total, grads = call(
        functools.partial(last_kernel, nf, nz),
        4,
        out_shape=(
            jax.ShapeDtypeStruct(total.shape[2:], F32),
            jax.ShapeDtypeStruct(grads.shape, BF),
        ),
        in_specs=[VM, ANY],
        out_specs=(VM, ANY),
        scratch_shapes=Scatter.scratch(nf, nz, *total.shape[2:]) + [swap_sems],
    )(total, grads)
    grads = grads.transpose(1, 2, 4, 0, 3).reshape(2, lp, dslice, ff).astype(F32)
    gain_grads = total[:, 4 * d : 4 * d + 2] + total[:, 4 * d + 2 : 4 * d + 4]
    return (
        block_out,
        rows_grad,
        gain_grads[:, 0],
        gain_grads[:, 1],
        total[:, : 3 * d],
        total[:, 3 * d : 4 * d],
        grads[0],
        grads[1],
        down_grad,
    )
def solution(mesh):
    in_specs = (
        P(("frames", "pos"), None, None),
        P(("frames", "pos")),
        P(),
        P(),
        P(("frames", "pos"), None),
        P(("frames", "pos"), None),
        P("pos", "frames", None),
        P("pos", "frames", None),
        P("pos", "frames", None),
        P(("frames", "pos"), None, None),
    )
    out_specs = (
        P(("frames", "pos"), None, None),
        P(("frames", "pos"), None, None),
        P(("frames", "pos")),
        P(("frames", "pos")),
        P(("frames", "pos"), None),
        P(("frames", "pos"), None),
        P("pos", "frames", None),
        P("pos", "frames", None),
        P("pos", "frames", None),
    )
    return jax.shard_map(local, mesh=mesh, in_specs=in_specs, out_specs=out_specs, check_vma=False)
```

```python
import functools
import math

import jax
import jax.numpy as jnp
from jax import lax
from jax.experimental import pallas as pl
from jax.experimental.pallas import tpu as pltpu
from jax.sharding import PartitionSpec as P

H = 16
HD = 64
BF = jnp.bfloat16
F32 = jnp.float32
MESH = pl.DeviceIdType.MESH
ANY = pl.BlockSpec(memory_space=pl.ANY)
VM = pl.BlockSpec(memory_space=pltpu.VMEM)


def place():
    return lax.axis_index("frames"), lax.axis_index("pos")


def flip(index, mask):
    bit = 1
    while bit <= mask:
        if mask & bit:
            index = index + bit * (1 - 2 * ((index // bit) % 2))
        bit *= 2
    return index


def greet(nf, nz, every_frame):
    f, z = place()
    hops = [1] + [2 * m for m in range(1, nf // 2)]
    if every_frame:
        hops = list(range(1, nf))
    others = [(flip(f, h), z) for h in hops] + [(f, flip(z, k)) for k in range(1, nz)]
    barrier = pltpu.get_barrier_semaphore()
    for other in others:
        pl.semaphore_signal(barrier, inc=1, device_id=other, device_id_type=MESH)
    pl.semaphore_wait(barrier, len(others))


def remote(src, dst, send, recv, to):
    copy = pltpu.make_async_remote_copy(
        src_ref=src, dst_ref=dst, send_sem=send, recv_sem=recv, device_id=to, device_id_type=MESH
    )
    copy.start()
    return copy


def relay_of(k):
    return 1 if k % 2 == 0 else 2


class Gather:
    def __init__(self, nf, nz, src_for, out_at, sems):
        self.nf, self.nz, self.nc = nf, nz, nf // 2
        self.f, self.z = place()
        self.src_for, self.out_at, self.sems = src_for, out_at, sems
        self.sent = []
        self.tree = self.nc == 4

    @staticmethod
    def sem_shape(nf, nz):
        return (2, 1 + 2 * (nf // 2), nz)

    def push(self, src, dst, hop, k, to):
        self.sent.append(remote(src, dst, self.sems.at[0, hop, k], self.sems.at[1, hop, k], to))

    def arrive(self, dst, hop, k):
        pltpu.make_async_remote_copy(
            src_ref=dst,
            dst_ref=dst,
            send_sem=self.sems.at[0, hop, k],
            recv_sem=self.sems.at[1, hop, k],
            device_id=(flip(self.f, 1), self.z),
            device_id_type=MESH,
        ).wait_recv()

    def begin(self):
        f, z = self.f, self.z
        for k in range(1, self.nz):
            self.push(self.src_for(flip(z, k)), self.out_at(f, z), 0, k, (f, flip(z, k)))
        self.own = pltpu.make_async_copy(self.src_for(z), self.out_at(f, z), self.sems.at[0, 0, 0])
        self.own.start()
        self.spread(self.src_for(z), 0)

    def spread(self, src, k):
        f, z = self.f, self.z
        block = self.out_at(f, flip(z, k))
        for m in range(1, self.nc):
            if self.tree and m == 3:
                continue
            self.push(src, block, m, k, (flip(f, 2 * m), z))
        self.push(src, block, self.nc, k, (flip(f, 1), z))

    def along(self, k):
        block = self.out_at(self.f, flip(self.z, k))
        self.arrive(block, 0, k)
        self.spread(block, k)

    def over(self, m, k):
        f, z = self.f, self.z
        block = self.out_at(flip(f, 2 * m), flip(z, k))
        self.arrive(block, m, k)
        if self.tree and m == relay_of(k):
            self.push(block, block, 3, k, (flip(f, 2 * (3 - m)), z))
        self.push(block, block, self.nc + m, k, (flip(f, 1), z))

    def order(self, k):
        first = relay_of(k) if self.tree else 1
        return [first] + [m for m in range(1, self.nc) if m != first]

    def finish(self):
        f, z = self.f, self.z
        for k in range(self.nz):
            for m in range(self.nc):
                self.arrive(self.out_at(flip(f, 2 * m + 1), flip(z, k)), self.nc + m, k)
        self.own.wait()
        for copy in self.sent:
            copy.wait_send()


class Swap:
    def __init__(self, nf, src_at, out_at, sems):
        self.nf, self.src_at, self.out_at, self.sems = nf, src_at, out_at, sems
        self.f, self.z = place()
        self.sent = []

    @staticmethod
    def sem_shape(nf):
        return (2, nf)

    def start(self):
        f, z = self.f, self.z
        self.own = pltpu.make_async_copy(self.src_at(f), self.out_at(f), self.sems.at[0, 0])
        self.own.start()
        for m in range(self.nf - 1, 0, -1):
            self.sent.append(
                remote(
                    self.src_at(flip(f, m)),
                    self.out_at(f),
                    self.sems.at[0, m],
                    self.sems.at[1, m],
                    (flip(f, m), z),
                )
            )

    def finish(self):
        self.own.wait()
        for copy in self.sent:
            copy.wait()


class Scatter:
    def __init__(self, nf, nz, src_at, own_at, sib, rx, land, sems):
        self.nf, self.nz, self.nc = nf, nz, nf // 2
        self.f, self.z = place()
        self.src_at, self.own_at, self.sib, self.rx = src_at, own_at, sib, rx
        self.land, self.sems = land, sems
        self.sent = []
        self.tree = self.nc == 4

    @staticmethod
    def scratch(nf, nz, rows, columns):
        nc = nf // 2
        block = (rows, columns)
        return [
            pltpu.VMEM((nz, nc) + block, BF),
            pltpu.VMEM((nz, nc - 1) + block, BF),
            pltpu.VMEM((nz - 1,) + block, BF),
            pltpu.SemaphoreType.DMA((2, 1 + 2 * nc, nz)),
        ]

    def push(self, src, dst, hop, k, to):
        copy = remote(src, dst, self.sems.at[0, hop, k], self.sems.at[1, hop, k], to)
        self.sent.append(copy)

    def arrive(self, dst, hop, k):
        pltpu.make_async_remote_copy(
            src_ref=dst,
            dst_ref=dst,
            send_sem=self.sems.at[0, hop, k],
            recv_sem=self.sems.at[1, hop, k],
            device_id=(flip(self.f, 1), self.z),
            device_id_type=MESH,
        ).wait_recv()

    def first(self, k):
        if self.tree:
            return [3, relay_of(k)]
        return list(range(self.nc - 1, 0, -1))

    def pairs(self, k):
        f, z = self.f, self.z
        order = self.first(k)
        for m in order + [m for m in range(self.nc - 1, -1, -1) if m not in order]:
            self.push(
                self.src_at(flip(f, 2 * m + 1), flip(z, k)),
                self.sib.at[k, m],
                self.nc + m,
                k,
                (flip(f, 1), z),
            )

    def chips(self, k):
        f, z = self.f, self.z
        for m in self.first(k):
            self.arrive(self.sib.at[k, m], self.nc + m, k)
            add_into(self.sib.at[k, m], self.own_at(k, m), self.sib.at[k, m])
            hop, to = m, m
            if self.tree:
                hop, to = (2 if m == 3 else 1), relay_of(k)
            self.push(self.sib.at[k, m], self.rx.at[k, hop - 1], hop, k, (flip(f, 2 * to), z))

    def across(self, k):
        if not self.tree:
            return
        f, z = self.f, self.z
        m = 3 - relay_of(k)
        self.arrive(self.sib.at[k, m], self.nc + m, k)
        self.arrive(self.rx.at[k, 1], 2, k)
        add_into(self.sib.at[k, m], self.own_at(k, m), self.sib.at[k, m], self.rx.at[k, 1])
        self.push(self.sib.at[k, m], self.rx.at[k, 2], 3, k, (flip(f, 2 * m), z))

    def home(self, k, out):
        f, z = self.f, self.z
        self.arrive(self.sib.at[k, 0], self.nc, k)
        terms = [self.own_at(k, 0), self.sib.at[k, 0]]
        for m in range(1, self.nc):
            if self.tree and m == 2:
                continue
            self.arrive(self.rx.at[k, m - 1], m, k)
            terms.append(self.rx.at[k, m - 1])
        if k == 0:
            add_into(out, *terms)
            return
        add_into(self.sib.at[k, 0], *terms)
        self.push(self.sib.at[k, 0], self.land.at[k - 1], 0, k, (f, flip(z, k)))

    def landed(self, k):
        self.arrive(self.land.at[k - 1], 0, k)

    def finish(self):
        for copy in self.sent:
            copy.wait_send()


def add_into(out, *terms):
    rows = out.shape[0]
    step = 16 if rows % 16 == 0 else rows

    def body(i, carry):
        at = pl.ds(pl.multiple_of(i * step, step), step)
        total = terms[0][at, :].astype(F32)
        for term in terms[1:]:
            total = total + term[at, :].astype(F32)
        out[at, :] = total.astype(out.dtype)
        return carry

    lax.fori_loop(0, rows // step, body, 0)


def call(kernel, ident, **kw):
    return pl.pallas_call(
        kernel,
        compiler_params=pltpu.CompilerParams(
            collective_id=ident, has_side_effects=True, vmem_limit_bytes=56 * 2**20
        ),
        **kw,
    )


def run_gathers(gathers, nz):
    for k in range(nz):
        for g in gathers:
            if k > 0:
                g.along(k)
        for g in gathers:
            if g.tree and k > 0:
                g.over(relay_of(k - 1), k - 1)
    for g in gathers:
        if g.tree:
            g.over(relay_of(nz - 1), nz - 1)
    for k in range(nz):
        for g in gathers:
            for m in range(1, g.nc):
                if g.tree and m == relay_of(k):
                    continue
                g.over(m, k)


def first_kernel(nf, nz, attn, gy, pair, attn_all, gy_all, pair_all, s1, s2, s3):
    greet(nf, nz, True)
    weights = Gather(nf, nz, lambda zz: attn, lambda ff, zz: attn_all.at[ff, zz], s1)
    rows = Gather(nf, nz, lambda zz: gy.at[zz], lambda ff, zz: gy_all.at[ff, zz], s2)
    swap = Swap(nf, lambda ff: pair.at[ff], lambda ff: pair_all.at[ff], s3)
    weights.begin()
    rows.begin()
    swap.start()
    run_gathers([weights, rows], nz)
    weights.finish()
    rows.finish()
    swap.finish()


def rows_kernel(nf, nz, b, b_all, s1):
    greet(nf, nz, False)
    rows = Gather(nf, nz, lambda zz: b.at[zz], lambda ff, zz: b_all.at[ff, zz], s1)
    rows.begin()
    run_gathers([rows], nz)
    rows.finish()


def in_place(terms):
    f, z = place()
    return lambda ff, zz: terms.at[ff, zz], lambda k, m: terms.at[flip(f, 2 * m), flip(z, k)]


def back_kernel(nf, nz, terms, out, sib, rx, land, sems):
    greet(nf, nz, False)
    s = Scatter(nf, nz, *in_place(terms), sib, rx, land, sems)
    z = s.z
    backward = range(nz - 1, -1, -1)
    for step in (s.pairs, s.chips, s.across, lambda k: s.home(k, out.at[z])):
        for k in backward:
            step(k)
    for k in range(1, nz):
        s.landed(k)
        out[flip(z, k)] = land[k - 1]
    s.finish()


def last_kernel(nf, nz, terms, pair, out, pair_all, sib, rx, land, sems, s2):
    greet(nf, nz, True)
    s = Scatter(nf, nz, *in_place(terms), sib, rx, land, sems)
    swap = Swap(nf, lambda ff: pair.at[ff], lambda ff: pair_all.at[ff], s2)
    backward = range(nz - 1, -1, -1)
    for k in backward:
        s.pairs(k)
    swap.start()
    for step in (s.chips, s.across, lambda k: s.home(k, out)):
        for k in backward:
            step(k)
    for k in range(1, nz):
        s.landed(k)
        add_into(out, out, land.at[k - 1])
    s.finish()
    swap.finish()


def contract(a, b, at_a, at_b):
    return lax.dot_general(a, b, (((at_a,), (at_b,)), ((), ())), preferred_element_type=F32)


def nt(a, b):
    return contract(a, b, 1, 1)


def nn(a, b):
    return contract(a, b, 1, 0)


def tn(a, b):
    return contract(a, b, 0, 0)


def by_position(rows, npos, fr, back=False):
    i = lax.broadcasted_iota(jnp.int32, (rows, rows), 0)
    j = lax.broadcasted_iota(jnp.int32, (rows, rows), 1)
    if back:
        i, j = j, i
    return ((i % fr) * npos + i // fr == j).astype(F32).astype(BF)


def causal(rows, npos):
    i = lax.broadcasted_iota(jnp.int32, (rows, rows), 0)
    j = lax.broadcasted_iota(jnp.int32, (rows, rows), 1)
    return jnp.logical_and(i // npos == j // npos, j <= i)


def soft(q, k, mask):
    s = jnp.where(mask, nt(q, k) * (1.0 / math.sqrt(HD)), -1e30)
    e = jnp.exp(s - jnp.max(s, axis=1, keepdims=True))
    return e / jnp.sum(e, axis=1, keepdims=True)

GROUP=128

def attention_fwd(npos, fr, x, gain1, gain2, w, a_out, qkv, ob, x1_out, b_out):
    rows, d = x.shape
    xf = x[...].astype(F32)
    rinv1 = lax.rsqrt(jnp.mean(xf * xf, axis=1, keepdims=True) + 1e-05)
    a_out[...] = (xf * rinv1 * gain1[...]).astype(BF)
    step = 512
    def project(i, c):
        at = pl.ds(pl.multiple_of(i * step, step), step)
        qkv[:, at] = nn(a_out[...], w[:, at]).astype(BF)
        return c
    lax.fori_loop(0, 3 * d // step, project, 0)
    mask = causal(GROUP, npos)
    low = lax.broadcasted_iota(jnp.int32, (GROUP, 2 * HD), 1) < HD
    def heads(i, c):
        for g in range(rows // GROUP):
            at = pl.ds(g * GROUP, GROUP)
            q, k, v = (qkv[at, pl.ds(pl.multiple_of(i * 2 * HD + t * d, 2 * HD), 2 * HD)] for t in range(3))
            zero = jnp.zeros_like(q)
            p0 = soft(jnp.where(low, q, zero), k, mask).astype(BF)
            p1 = soft(jnp.where(low, zero, q), k, mask).astype(BF)
            ob[at, pl.ds(pl.multiple_of(i * 2 * HD, 2 * HD), 2 * HD)] = jnp.where(low, nn(p0, v), nn(p1, v)).astype(BF)
        return c
    lax.fori_loop(0, d // (2 * HD), heads, 0)
    def out(i, c):
        at = pl.ds(pl.multiple_of(i * step, step), step)
        x1_out[:, at] = x[:, at].astype(F32) + nn(ob[...], w[:, pl.ds(pl.multiple_of(3 * d + i * step, step), step)])
        return c
    lax.fori_loop(0, d // step, out, 0)
    x1 = x1_out[...]
    rinv2 = lax.rsqrt(jnp.mean(x1 * x1, axis=1, keepdims=True) + 1e-05)
    b = (x1 * rinv2 * gain2[...]).astype(BF)
    b_out[...] = nn(by_position(rows, npos, fr), b).astype(BF)


def attention_bwd_in(npos, fr, db_pos, gy, keep, x1_ref, ob, w, gain2, dx1_s, dxb, do_s, terms):
    rows, d = x1_ref.shape
    db = nn(by_position(rows, npos, fr, True), db_pos[...])
    x1 = x1_ref[...]
    rinv2 = lax.rsqrt(jnp.mean(x1 * x1, axis=1, keepdims=True) + 1e-05)
    n2 = db * gain2[...]
    inner = jnp.mean(n2 * x1, axis=1, keepdims=True)
    dx1 = keep[...] * gy[...].astype(F32) + rinv2 * n2 - x1 * (rinv2 * rinv2 * rinv2 * inner)
    dx1_s[...] = dx1
    dxb[...] = dx1.astype(BF)
    step = 512

    def weights(i, c):
        at = pl.ds(pl.multiple_of(i * step, step), step)
        to = pl.ds(pl.multiple_of(3 * d + i * step, step), step)
        terms[:, to] = tn(ob[...], dxb[:, at]).astype(BF)
        return c

    lax.fori_loop(0, d // step, weights, 0)
    do_s[...] = nt(dxb[...], w[:, 3 * d : 4 * d]).astype(BF)
    return jnp.sum(db * x1 * rinv2, axis=0, keepdims=True)


def attention_bwd_heads(npos, qkv, do_s, dqkv):
    rows, d = do_s.shape
    mask = causal(GROUP, npos)
    low = lax.broadcasted_iota(jnp.int32, (GROUP, 2 * HD), 1) < HD
    scale = 1.0 / math.sqrt(HD)

    def heads(i, c):
        for g in range(rows // GROUP):
            at = pl.ds(g * GROUP, GROUP)
            lanes = [pl.ds(pl.multiple_of(i * 2 * HD + t * d, 2 * HD), 2 * HD) for t in range(3)]
            q, k, v = (qkv[at, l] for l in lanes)
            do = do_s[at, lanes[0]]
            zero = jnp.zeros_like(q)
            parts = []
            for h in range(2):
                keep = low if h == 0 else jnp.logical_not(low)
                p = soft(jnp.where(keep, q, zero), k, mask)
                dp = nt(jnp.where(keep, do, zero), v)
                ds = (p * (dp - jnp.sum(p * dp, axis=1, keepdims=True)) * scale).astype(BF)
                parts.append((nn(ds, k), tn(ds, q), tn(p.astype(BF), do)))
            for t in range(3):
                dqkv[at, lanes[t]] = jnp.where(low, parts[0][t], parts[1][t]).astype(BF)
        return c

    lax.fori_loop(0, d // (2 * HD), heads, 0)


def attention_bwd_weights(a, dqkv, terms):
    step = 512

    def weights(i, c):
        at = pl.ds(pl.multiple_of(i * step, step), step)
        terms[:, at] = tn(a[...], dqkv[:, at]).astype(BF)
        return c

    lax.fori_loop(0, dqkv.shape[1] // step, weights, 0)


def attention_bwd_rows(x, dqkv, w, gain1, dx1, rows_out):
    d = x.shape[1]
    da = nt(dqkv[...], w[:, 0 : 3 * d])
    xf = x[...].astype(F32)
    rinv1 = lax.rsqrt(jnp.mean(xf * xf, axis=1, keepdims=True) + 1e-05)
    n1 = da * gain1[...]
    inner = jnp.mean(n1 * xf, axis=1, keepdims=True)
    rows_out[...] = dx1[...] + rinv1 * n1 - xf * (rinv1 * rinv1 * rinv1 * inner)
    return jnp.sum(da * xf * rinv1, axis=0, keepdims=True)


def gains_into(gain1_grad, gain2_grad, terms):
    d = gain1_grad.shape[1]
    high1 = gain1_grad.astype(BF).astype(F32)
    high2 = gain2_grad.astype(BF).astype(F32)
    at = lax.broadcasted_iota(jnp.int32, (128, d), 0)
    tail = jnp.where(at == 0, high1, 0.0)
    tail = jnp.where(at == 1, high2, tail)
    tail = jnp.where(at == 2, gain1_grad - high1, tail)
    tail = jnp.where(at == 3, gain2_grad - high2, tail)
    terms[:, 4 * d : 4 * d + 128] = tail.T.astype(BF)


def by_row(ref, rows, nz):
    return lambda ff, zz: ref.at[pl.ds(pl.multiple_of((ff * nz + zz) * rows, rows), rows)]


def pack(master, stage, sems, send, mat):
    nf, _, lp, ffs, _ = send.shape

    def fetch(p):
        return pltpu.make_async_copy(master.at[p], stage.at[p % 2], sems.at[p % 2])

    fetch(0).start()

    def body(p, carry):
        @pl.when(p + 1 < lp)
        def _():
            fetch(p + 1).start()

        fetch(p).wait()
        turned = stage[p % 2].T.astype(BF)
        for j in range(nf):
            send[j, mat, p] = turned[j * ffs : (j + 1) * ffs]
        return carry

    lax.fori_loop(0, lp, body, 0)


def forward_kernel(
    nf, nz, npos, fr,
    x, gy, keep, gain1, gain2, qkv_w, out_w, gate_w, up_w,
    w_out, gy_all, b_all, pair_all, a, qkv, ob, x1,
    own_w, w, gy_pos, b_pos, send, stage, sems_w, sems_gy, sems_b, sems_gate, sems_up, sems_in, sem_w,
):
    d = x.shape[1]
    each = own_w.shape[0]
    lp = npos // nz
    greet(nf, nz, True)
    own_w[:, : 3 * d] = qkv_w[...].astype(BF)
    own_w[:, 3 * d :] = out_w[...].astype(BF)
    weights = Gather(nf, nz, lambda zz: own_w, by_row(w, each, nz), sems_w)
    weights.begin()
    turn = by_position(npos * fr, npos, fr)
    kept = (gy[...].astype(F32) * keep[...]).astype(BF)
    gy_pos[...] = nn(turn, kept).astype(BF).reshape(gy_pos.shape)
    grads = Gather(nf, nz, lambda zz: gy_pos.at[zz], lambda ff, zz: gy_all.at[ff, zz], sems_gy)
    pack(gate_w, stage, sems_in, send, 0)
    for k in range(1, nz):
        weights.along(k)
    for k in range(nz):
        weights.over(relay_of(k), k)
    grads.begin()
    pack(up_w, stage, sems_in, send, 1)
    for k in range(nz):
        for m in weights.order(k)[1:]:
            weights.over(m, k)
    for k in range(1, nz):
        grads.along(k)
    gate = Swap(nf, lambda ff: send.at[ff, 0], lambda ff: pair_all.at[ff, 0], sems_gate)
    up = Swap(nf, lambda ff: send.at[ff, 1], lambda ff: pair_all.at[ff, 1], sems_up)
    gate.start()
    for k in range(nz):
        grads.over(relay_of(k), k)
    weights.finish()
    save = pltpu.make_async_copy(w, w_out, sem_w)
    save.start()
    attention_fwd(npos, fr, x, gain1, gain2, w, a, qkv, ob, x1, b_pos)
    rows = Gather(nf, nz, lambda zz: b_pos.at[pl.ds(pl.multiple_of(zz * lp * fr, lp * fr), lp * fr)], lambda ff, zz: b_all.at[ff, zz], sems_b)
    rows.begin()
    for k in range(nz):
        for m in grads.order(k)[1:]:
            grads.over(m, k)
    for k in range(1, nz):
        rows.along(k)
    for k in range(nz):
        rows.over(relay_of(k), k)
    up.start()
    for k in range(nz):
        for m in rows.order(k)[1:]:
            rows.over(m, k)
    save.wait()
    rows.finish()
    grads.finish()
    gate.finish()
    up.finish()


def feed_kernel(gy, b, pair, down, db, z, grads, down_grad, wg, wu):
    nf = pair.shape[0]
    width = pair.shape[4]
    rows, d = gy.shape[0] * gy.shape[1] * gy.shape[2], gy.shape[3]
    for s in range(nf):
        wg[:, s * width : (s + 1) * width] = pair[s, 0, 0]
        wu[:, s * width : (s + 1) * width] = pair[s, 1, 0]
    b_rows = b[...].reshape(rows, d)
    gy_rows = gy[...].reshape(rows, d)
    wd = down[0].astype(BF)
    gate = nt(wg[...], b_rows)
    up = nt(wu[...], b_rows)
    dhid = nt(wd, gy_rows)
    s = jax.nn.sigmoid(gate)
    silu = gate * s
    hid = (silu * up).astype(BF)
    dgate = (dhid * up * s * (1.0 + gate * (1.0 - s))).astype(BF)
    dup = (dhid * silu).astype(BF)
    for at, term in enumerate((dgate, dup)):
        grad = nn(term, b_rows).astype(BF)
        for j in range(nf):
            grads[j, at, 0] = grad[:, j * width : (j + 1) * width]
    down_grad[0] = nn(hid, gy_rows)
    db[...] = (tn(dgate, wg[...]) + tn(dup, wu[...])).astype(BF).reshape(db.shape)
    z[...] = tn(hid, wd).astype(BF).reshape(z.shape)


def backward_kernel(
    nf, nz, npos, fr,
    db_terms, z_terms, grads, w_in, x, gy, keep, gain1, gain2, x1, a, qkv, ob,
    block_out, rows_grad, total, pair_all,
    db_own, db_sib, db_rx, db_land, db_sems,
    z_own, z_sib, z_rx, z_land, z_sems,
    t_sib, t_rx, t_land, t_sems,
    sems_gate, sems_up, sems_own, sem_w,
    w, terms, db_rows, z_rows, dx1, dxb, do, dqkv,
):
    d = x.shape[1]
    each = total.shape[0]
    lrows = db_own.shape[2]
    nc = nf // 2
    f, z = place()
    greet(nf, nz, True)
    backward = range(nz - 1, -1, -1)

    def own_copies(src, own, at):
        return [
            pltpu.make_async_copy(
                src.at[flip(f, 2 * m), flip(z, k)], own.at[k, m], sems_own.at[at, k, m]
            )
            for k in backward
            for m in range(nc)
        ]

    def scatter(src, own, sib, rx, land, sems):
        return Scatter(
            nf, nz, lambda ff, zz: src.at[ff, zz], lambda k, m: own.at[k, m], sib, rx, land, sems
        )

    s_db = scatter(db_terms, db_own, db_sib, db_rx, db_land, db_sems)
    s_z = scatter(z_terms, z_own, z_sib, z_rx, z_land, z_sems)
    for k in backward:
        s_db.pairs(k)
    load_db = own_copies(db_terms, db_own, 0)
    load_z = own_copies(z_terms, z_own, 1)
    for copy in load_db:
        copy.start()
    load_w = pltpu.make_async_copy(w_in, w, sem_w)
    load_w.start()
    for copy in load_db:
        copy.wait()
    for k in backward:
        s_db.chips(k)
    for k in backward:
        s_z.pairs(k)
    for copy in load_z:
        copy.start()
    for k in backward:
        s_db.across(k)

    def at_pos(zz):
        return pl.ds(pl.multiple_of(zz * lrows, lrows), lrows)

    for k in backward:
        s_db.home(k, db_rows.at[at_pos(z)])
    gate = Swap(nf, lambda ff: grads.at[ff, 0], lambda ff: pair_all.at[ff, 0], sems_gate)
    up = Swap(nf, lambda ff: grads.at[ff, 1], lambda ff: pair_all.at[ff, 1], sems_up)
    for copy in load_z:
        copy.wait()
    for k in backward:
        s_z.chips(k)
    gate.start()
    for k in range(1, nz):
        s_db.landed(k)
        db_rows[at_pos(flip(z, k)), :] = db_land[k - 1]
    load_w.wait()
    gain2_grad = attention_bwd_in(npos, fr, db_rows, gy, keep, x1, ob, w, gain2, dx1, dxb, do, terms)
    for k in backward:
        s_z.across(k)
    up.start()
    attention_bwd_heads(npos, qkv, do, dqkv)
    for k in backward:
        s_z.home(k, z_rows.at[at_pos(z)])
    attention_bwd_weights(a, dqkv, terms)
    gain1_grad = attention_bwd_rows(x, dqkv, w, gain1, dx1, rows_grad)
    gains_into(gain1_grad, gain2_grad, terms)
    src_at = by_row(terms, each, nz)
    s_t = Scatter(
        nf, nz, src_at, lambda k, m: src_at(flip(f, 2 * m), flip(z, k)), t_sib, t_rx, t_land, t_sems
    )
    for step in (s_t.pairs, s_t.chips):
        for k in backward:
            step(k)
    for k in range(1, nz):
        s_z.landed(k)
        z_rows[at_pos(flip(z, k)), :] = z_land[k - 1]
    back = nn(by_position(npos * fr, npos, fr, True), z_rows[...])
    block_out[...] = (keep[...] * (x1[...] + back)).astype(BF)
    for step in (s_t.across, lambda k: s_t.home(k, total)):
        for k in backward:
            step(k)
    for k in range(1, nz):
        s_t.landed(k)
        add_into(total, total, t_land.at[k - 1])
    for task in (s_db, s_z, s_t, gate, up):
        task.finish()


def unpack_kernel(pair, gate, up):
    nf, _, _, ffs, width = pair.shape
    for at, out in enumerate((gate, up)):
        out[0] = pair[:, at, 0].astype(F32).reshape(nf * ffs, width).T


def rms_norm(values, gain_vector):
    return (
        values * lax.rsqrt(jnp.mean(values * values, axis=-1, keepdims=True) + 1e-05) * gain_vector
    )


def attend(qkv_rows):
    frame_count = qkv_rows.shape[0]
    positions = qkv_rows.shape[1]
    split_rows = qkv_rows.reshape(frame_count, positions, 3, H, HD)
    queries = split_rows[:, :, 0]
    keys_all = split_rows[:, :, 1]
    values_all = split_rows[:, :, 2]
    scores = jnp.einsum("fqhe,fkhe->fhqk", queries, keys_all, preferred_element_type=F32) * (
        1.0 / math.sqrt(HD)
    )
    causal = jnp.arange(positions)[:, None] >= jnp.arange(positions)[None, :]
    scores = jnp.where(causal, scores, -1e30)
    weights = jax.nn.softmax(scores, axis=-1)
    mixed = jnp.einsum("fhqk,fkhe->fqhe", weights, values_all, preferred_element_type=F32)
    return mixed.reshape(frame_count, positions, H * HD)


def local_general(
    frame_rows,
    frame_mask,
    gain_attention,
    gain_feed,
    qkv_master,
    out_master,
    gate_master,
    up_master,
    down_master,
    out_cotangent,
):
    nf = lax.axis_size("frames")
    nz = lax.axis_size("pos")
    lp, dslice, ff = gate_master.shape
    ffs = down_master.shape[1]
    fr, npos, d = frame_rows.shape

    keep_rows = frame_mask.astype(F32)[:, None, None]
    inputs = frame_rows.astype(F32)

    def turned(w):
        return w.astype(BF).reshape(lp, dslice, nf, ffs).transpose(2, 0, 3, 1)

    def untwist(w):
        return w.transpose(1, 2, 0, 3).reshape(lp, ffs, d)

    def to_pos(rows):
        return rows.transpose(1, 0, 2).reshape(nz, lp * fr, d)

    def gathered(every):
        every = every.reshape(nf, nz, lp, fr, d)
        return every.transpose(2, 0, 1, 3, 4).reshape(lp, nf * nz * fr, d)

    rows_shape = jax.ShapeDtypeStruct((nf, nz, lp * fr, d), BF)
    back_shape = jax.ShapeDtypeStruct((nz, lp * fr, d), BF)
    gather_sems = pltpu.SemaphoreType.DMA(Gather.sem_shape(nf, nz))
    swap_sems = pltpu.SemaphoreType.DMA(Swap.sem_shape(nf))

    def scattered(rows, ident):
        moved = rows.reshape(lp, nf, nz, fr, d).transpose(1, 2, 0, 3, 4)
        moved = moved.reshape(nf, nz, lp * fr, d)
        back = call(
            functools.partial(back_kernel, nf, nz),
            ident,
            out_shape=back_shape,
            in_specs=[VM],
            out_specs=VM,
            scratch_shapes=Scatter.scratch(nf, nz, lp * fr, d),
        )(moved)
        return back.reshape(npos, fr, d).transpose(1, 0, 2)

    both = jnp.concatenate((qkv_master.astype(BF), out_master.astype(BF)), axis=1)
    pair = jnp.stack((turned(gate_master), turned(up_master)), axis=1)
    upstream = keep_rows * out_cotangent.astype(F32)
    own_rows = both.shape[0]
    w_all, gy_all, pair = call(
        functools.partial(first_kernel, nf, nz),
        0,
        out_shape=(
            jax.ShapeDtypeStruct((nf, nz) + both.shape, BF),
            rows_shape,
            jax.ShapeDtypeStruct(pair.shape, BF),
        ),
        in_specs=[ANY] * 3,
        out_specs=(ANY,) * 3,
        scratch_shapes=[gather_sems, gather_sems, swap_sems],
    )(both, to_pos(upstream.astype(BF)), pair)
    w_all = w_all.reshape(d, both.shape[1])
    w_qkv = w_all[:, : 3 * d]
    w_out = w_all[:, 3 * d :]
    gate_t = untwist(pair[:, 0])
    up_t = untwist(pair[:, 1])
    down = down_master.astype(BF)
    gy = gathered(gy_all)

    normed_one, norm_one_pull = jax.vjp(rms_norm, inputs, gain_attention)
    normed_low = normed_one.astype(BF)
    qkv_rows = jnp.einsum("fpd,de->fpe", normed_low, w_qkv, preferred_element_type=F32)
    mixed, attend_pull = jax.vjp(attend, qkv_rows)
    mixed_low = mixed.astype(BF)
    branch = jnp.einsum("fpd,de->fpe", mixed_low, w_out, preferred_element_type=F32)
    middle = inputs + branch
    normed_two, norm_two_pull = jax.vjp(rms_norm, middle, gain_feed)
    b_all = call(
        functools.partial(rows_kernel, nf, nz),
        1,
        out_shape=rows_shape,
        in_specs=[ANY],
        out_specs=ANY,
        scratch_shapes=[gather_sems],
    )(to_pos(normed_two.astype(BF)))
    b = gathered(b_all)

    gate_rows = jnp.einsum("prd,phd->phr", b, gate_t, preferred_element_type=F32)
    up_rows = jnp.einsum("prd,phd->phr", b, up_t, preferred_element_type=F32)
    hidden_grad = jnp.einsum("prd,phd->phr", gy, down, preferred_element_type=F32)
    sigma = jax.nn.sigmoid(gate_rows)
    silu_gate = gate_rows * sigma
    hidden = (silu_gate * up_rows).astype(BF)
    gate_back = (hidden_grad * up_rows * sigma * (1.0 + gate_rows * (1.0 - sigma))).astype(BF)
    up_back = (hidden_grad * silu_gate).astype(BF)
    db = jnp.einsum("phr,phd->prd", gate_back, gate_t, preferred_element_type=F32) + jnp.einsum(
        "phr,phd->prd", up_back, up_t, preferred_element_type=F32
    )
    back_rows = scattered(db.astype(BF), 2).astype(F32)
    feed = jnp.einsum("phr,phd->prd", hidden, down, preferred_element_type=F32)
    returned = scattered(feed.astype(BF), 3).astype(F32)
    block_out = (keep_rows * (middle + returned)).astype(BF)
    gate_grad = jnp.einsum("phr,prd->phd", gate_back, b, preferred_element_type=F32).astype(BF)
    up_grad = jnp.einsum("phr,prd->phd", up_back, b, preferred_element_type=F32).astype(BF)
    down_grad = jnp.einsum("phr,prd->phd", hidden, gy, preferred_element_type=F32)

    grads = jnp.stack((gate_grad, up_grad), axis=0).reshape(2, lp, ffs, nf, dslice)
    grads = grads.transpose(3, 0, 1, 2, 4)

    pulled_two = norm_two_pull(back_rows)
    middle_grad = upstream + pulled_two[0]
    branch_grad = middle_grad.astype(BF)
    out_weight_grad = jnp.einsum("fpd,fpe->de", mixed_low, branch_grad, preferred_element_type=F32)
    mixed_grad = jnp.einsum("fpe,de->fpd", branch_grad, w_out, preferred_element_type=F32)
    qkv_back = attend_pull(mixed_grad)[0].astype(BF)
    qkv_weight_grad = jnp.einsum("fpd,fpe->de", normed_low, qkv_back, preferred_element_type=F32)
    normed_grad = jnp.einsum("fpe,de->fpd", qkv_back, w_qkv, preferred_element_type=F32)
    pulled_one = norm_one_pull(normed_grad)
    rows_grad = middle_grad + pulled_one[0]

    gains = jnp.stack((pulled_one[1], pulled_two[1]), axis=1)
    gains_hi = gains.astype(BF)
    gains_lo = (gains - gains_hi.astype(F32)).astype(BF)
    tail = jnp.concatenate((gains_hi, gains_lo, jnp.zeros((d, 124), BF)), axis=1)
    total = jnp.concatenate(
        (qkv_weight_grad.astype(BF), out_weight_grad.astype(BF), tail), axis=1
    )
    total = total.reshape(nf, nz, own_rows, total.shape[1])
    total, grads = call(
        functools.partial(last_kernel, nf, nz),
        4,
        out_shape=(
            jax.ShapeDtypeStruct(total.shape[2:], F32),
            jax.ShapeDtypeStruct(grads.shape, BF),
        ),
        in_specs=[VM, ANY],
        out_specs=(VM, ANY),
        scratch_shapes=Scatter.scratch(nf, nz, *total.shape[2:]) + [swap_sems],
    )(total, grads)
    grads = grads.transpose(1, 2, 4, 0, 3).reshape(2, lp, dslice, ff).astype(F32)
    gain_grads = total[:, 4 * d : 4 * d + 2] + total[:, 4 * d + 2 : 4 * d + 4]
    return (
        block_out,
        rows_grad,
        gain_grads[:, 0],
        gain_grads[:, 1],
        total[:, : 3 * d],
        total[:, 3 * d : 4 * d],
        grads[0],
        grads[1],
        down_grad,
    )
def local_fused(
    frame_rows,
    frame_mask,
    gain_attention,
    gain_feed,
    qkv_master,
    out_master,
    gate_master,
    up_master,
    down_master,
    out_cotangent,
):
    nf = lax.axis_size("frames")
    nz = lax.axis_size("pos")
    lp, dslice, ff = gate_master.shape
    ffs = down_master.shape[1]
    fr, npos, d = frame_rows.shape
    rows = fr * npos
    each = qkv_master.shape[0]

    def make(shape, kind=BF):
        return jax.ShapeDtypeStruct(shape, kind)

    x = frame_rows.reshape(rows, d)
    gy = out_cotangent.reshape(rows, d)
    keep = jnp.broadcast_to(frame_mask.astype(F32)[:, None], (fr, npos)).reshape(rows, 1)
    gain1 = gain_attention.reshape(1, d)
    gain2 = gain_feed.reshape(1, d)
    gather_sems = pltpu.SemaphoreType.DMA(Gather.sem_shape(nf, nz))
    swap_sems = pltpu.SemaphoreType.DMA(Swap.sem_shape(nf))
    rows_shape = make((nf, nz, lp * fr, d))
    pair_shape = make((nf, 2, lp, ffs, dslice))
    w_all, gy_all, b_all, pair_all, a, qkv, ob, x1 = call(
        functools.partial(forward_kernel, nf, nz, npos, fr),
        0,
        out_shape=(
            make((d, 4 * d)),
            rows_shape,
            rows_shape,
            pair_shape,
            make((rows, d)),
            make((rows, 3 * d)),
            make((rows, d)),
            make((rows, d), F32),
        ),
        in_specs=[VM] * 7 + [ANY] * 2,
        out_specs=(ANY,) * 4 + (VM,) * 4,
        scratch_shapes=[
            pltpu.VMEM((each, 4 * d), BF),
            pltpu.VMEM((d, 4 * d), BF),
            pltpu.VMEM((nz, lp * fr, d), BF),
            pltpu.VMEM((rows, d), BF),
            pltpu.VMEM(pair_shape.shape, BF),
            pltpu.VMEM((2, dslice, ff), F32),
            gather_sems,
            gather_sems,
            gather_sems,
            swap_sems,
            swap_sems,
            pltpu.SemaphoreType.DMA((2,)),
            pltpu.SemaphoreType.DMA,
        ],
    )(x, gy, keep, gain1, gain2, qkv_master, out_master, gate_master, up_master)
    rows_block = pl.BlockSpec((nf, nz, fr, d), lambda p: (0, 0, p, 0))
    pair_block = pl.BlockSpec((nf, 2, 1, ffs, dslice), lambda p: (0, 0, p, 0, 0))
    down_block = pl.BlockSpec((1, ffs, d), lambda p: (p, 0, 0))
    local_params = pltpu.CompilerParams(vmem_limit_bytes=56 * 2**20)
    db_terms, z_terms, grads, down_grad = pl.pallas_call(
        feed_kernel,
        grid=(lp,),
        out_shape=(rows_shape, rows_shape, pair_shape, make((lp, ffs, d), F32)),
        in_specs=[rows_block, rows_block, pair_block, down_block],
        out_specs=(rows_block, rows_block, pair_block, down_block),
        scratch_shapes=[pltpu.VMEM((ffs, d), BF)] * 2,
        compiler_params=local_params,
    )(gy_all, b_all, pair_all, down_master)
    small = (nf, nz, lp * fr, d)
    wide = 4 * d + 128
    own = pltpu.VMEM((nz, nf // 2, lp * fr, d), BF)
    block_out, rows_grad, total, back = call(
        functools.partial(backward_kernel, nf, nz, npos, fr),
        1,
        out_shape=(
            make((rows, d)),
            make((rows, d), F32),
            make((each, wide), F32),
            pair_shape,
        ),
        in_specs=[ANY] * 4 + [VM] * 9,
        out_specs=(VM,) * 3 + (ANY,),
        scratch_shapes=[
            own,
            *Scatter.scratch(*small),
            own,
            *Scatter.scratch(*small),
            *Scatter.scratch(nf, nz, each, wide),
            swap_sems,
            swap_sems,
            pltpu.SemaphoreType.DMA((2, nz, nf // 2)),
            pltpu.SemaphoreType.DMA,
            pltpu.VMEM((d, 4 * d), BF),
            pltpu.VMEM((d, wide), BF),
            pltpu.VMEM((rows, d), BF),
            pltpu.VMEM((rows, d), BF),
            pltpu.VMEM((rows, d), F32),
            pltpu.VMEM((rows, d), BF),
            pltpu.VMEM((rows, d), BF),
            pltpu.VMEM((rows, 3 * d), BF),
        ],
    )(db_terms, z_terms, grads, w_all, x, gy, keep, gain1, gain2, x1, a, qkv, ob)
    whole_block = pl.BlockSpec((1, dslice, ff), lambda p: (p, 0, 0))
    gate_grad, up_grad = pl.pallas_call(
        unpack_kernel,
        grid=(lp,),
        out_shape=(make((lp, dslice, ff), F32),) * 2,
        in_specs=[pair_block],
        out_specs=(whole_block, whole_block),
        compiler_params=local_params,
    )(back)
    gains = total[:, 4 * d : 4 * d + 2] + total[:, 4 * d + 2 : 4 * d + 4]
    return (
        block_out.reshape(fr, npos, d),
        rows_grad.reshape(fr, npos, d),
        gains[:, 0],
        gains[:, 1],
        total[:, : 3 * d],
        total[:, 3 * d : 4 * d],
        gate_grad,
        up_grad,
        down_grad,
    )


def local(*args):
    _, dslice, _ = args[6].shape
    if lax.axis_size("frames") == 8 and dslice % 128 == 0:
        return local_fused(*args)
    return local_general(*args)


def solution(mesh):
    in_specs = (
        P(("frames", "pos"), None, None),
        P(("frames", "pos")),
        P(),
        P(),
        P(("frames", "pos"), None),
        P(("frames", "pos"), None),
        P("pos", "frames", None),
        P("pos", "frames", None),
        P("pos", "frames", None),
        P(("frames", "pos"), None, None),
    )
    out_specs = (
        P(("frames", "pos"), None, None),
        P(("frames", "pos"), None, None),
        P(("frames", "pos")),
        P(("frames", "pos")),
        P(("frames", "pos"), None),
        P(("frames", "pos"), None),
        P("pos", "frames", None),
        P("pos", "frames", None),
        P("pos", "frames", None),
    )
    return jax.shard_map(local, mesh=mesh, in_specs=in_specs, out_specs=out_specs, check_vma=False)
```

```python
import functools
import math

import jax
import jax.numpy as jnp
from jax import lax
from jax.experimental import pallas as pl
from jax.experimental.pallas import tpu as pltpu
from jax.sharding import PartitionSpec as P

H = 16
HD = 64
BF = jnp.bfloat16
F32 = jnp.float32
MESH = pl.DeviceIdType.MESH
ANY = pl.BlockSpec(memory_space=pl.ANY)
VM = pl.BlockSpec(memory_space=pltpu.VMEM)


def place():
    return lax.axis_index("frames"), lax.axis_index("pos")


def flip(index, mask):
    bit = 1
    while bit <= mask:
        if mask & bit:
            index = index + bit * (1 - 2 * ((index // bit) % 2))
        bit *= 2
    return index


def greet(nf, nz, every_frame):
    f, z = place()
    hops = [1] + [2 * m for m in range(1, nf // 2)]
    if every_frame:
        hops = list(range(1, nf))
    others = [(flip(f, h), z) for h in hops] + [(f, flip(z, k)) for k in range(1, nz)]
    barrier = pltpu.get_barrier_semaphore()
    for other in others:
        pl.semaphore_signal(barrier, inc=1, device_id=other, device_id_type=MESH)
    pl.semaphore_wait(barrier, len(others))


def remote(src, dst, send, recv, to):
    copy = pltpu.make_async_remote_copy(
        src_ref=src, dst_ref=dst, send_sem=send, recv_sem=recv, device_id=to, device_id_type=MESH
    )
    copy.start()
    return copy


def relay_of(k):
    return 1 if k % 2 == 0 else 2


class Gather:
    def __init__(self, nf, nz, src_for, out_at, sems):
        self.nf, self.nz, self.nc = nf, nz, nf // 2
        self.f, self.z = place()
        self.src_for, self.out_at, self.sems = src_for, out_at, sems
        self.sent = []
        self.tree = self.nc == 4

    @staticmethod
    def sem_shape(nf, nz):
        return (2, 1 + 2 * (nf // 2), nz)

    def push(self, src, dst, hop, k, to):
        self.sent.append(remote(src, dst, self.sems.at[0, hop, k], self.sems.at[1, hop, k], to))

    def arrive(self, dst, hop, k):
        pltpu.make_async_remote_copy(
            src_ref=dst,
            dst_ref=dst,
            send_sem=self.sems.at[0, hop, k],
            recv_sem=self.sems.at[1, hop, k],
            device_id=(flip(self.f, 1), self.z),
            device_id_type=MESH,
        ).wait_recv()

    def begin(self):
        f, z = self.f, self.z
        for k in range(1, self.nz):
            self.push(self.src_for(flip(z, k)), self.out_at(f, z), 0, k, (f, flip(z, k)))
        self.own = pltpu.make_async_copy(self.src_for(z), self.out_at(f, z), self.sems.at[0, 0, 0])
        self.own.start()
        self.spread(self.src_for(z), 0)

    def spread(self, src, k):
        f, z = self.f, self.z
        block = self.out_at(f, flip(z, k))
        for m in range(1, self.nc):
            if self.tree and m == 3:
                continue
            self.push(src, block, m, k, (flip(f, 2 * m), z))
        self.push(src, block, self.nc, k, (flip(f, 1), z))

    def along(self, k):
        block = self.out_at(self.f, flip(self.z, k))
        self.arrive(block, 0, k)
        self.spread(block, k)

    def over(self, m, k):
        f, z = self.f, self.z
        block = self.out_at(flip(f, 2 * m), flip(z, k))
        self.arrive(block, m, k)
        if self.tree and m == relay_of(k):
            self.push(block, block, 3, k, (flip(f, 2 * (3 - m)), z))
        self.push(block, block, self.nc + m, k, (flip(f, 1), z))

    def order(self, k):
        first = relay_of(k) if self.tree else 1
        return [first] + [m for m in range(1, self.nc) if m != first]

    def finish(self):
        f, z = self.f, self.z
        for k in range(self.nz):
            for m in range(self.nc):
                self.arrive(self.out_at(flip(f, 2 * m + 1), flip(z, k)), self.nc + m, k)
        self.own.wait()
        for copy in self.sent:
            copy.wait_send()


class Swap:
    def __init__(self, nf, src_at, out_at, sems):
        self.nf, self.src_at, self.out_at, self.sems = nf, src_at, out_at, sems
        self.f, self.z = place()
        self.sent = []

    @staticmethod
    def sem_shape(nf):
        return (2, nf)

    def start(self):
        f, z = self.f, self.z
        self.own = pltpu.make_async_copy(self.src_at(f), self.out_at(f), self.sems.at[0, 0])
        self.own.start()
        for m in range(self.nf - 1, 0, -1):
            self.sent.append(
                remote(
                    self.src_at(flip(f, m)),
                    self.out_at(f),
                    self.sems.at[0, m],
                    self.sems.at[1, m],
                    (flip(f, m), z),
                )
            )

    def finish(self):
        self.own.wait()
        for copy in self.sent:
            copy.wait()


class Sums:
    def __init__(self, nf, nz, src_at, own_at, sib, rx, sems):
        self.nf, self.nz, self.nc = nf, nz, nf // 2
        self.f, self.z = place()
        self.src_at, self.own_at, self.sib, self.rx = src_at, own_at, sib, rx
        self.sems = sems
        self.sent = []
        self.tree = self.nc == 4

    @staticmethod
    def buffers(nf, parts, rows, columns):
        nc = nf // 2
        return [
            pltpu.VMEM((parts, nc, rows, columns), BF),
            pltpu.VMEM((parts, nc - 1, rows, columns), BF),
            pltpu.SemaphoreType.DMA((2, 2 * nc, parts)),
        ]

    def push(self, src, dst, sems, hop, k, to):
        self.sent.append(remote(src, dst, sems.at[0, hop, k], sems.at[1, hop, k], to))

    def arrive(self, dst, sems, hop, k):
        pltpu.make_async_remote_copy(
            src_ref=dst,
            dst_ref=dst,
            send_sem=sems.at[0, hop, k],
            recv_sem=sems.at[1, hop, k],
            device_id=(flip(self.f, 1), self.z),
            device_id_type=MESH,
        ).wait_recv()

    def first(self, k):
        if self.tree:
            return [3, relay_of(k)]
        return list(range(self.nc - 1, 0, -1))

    def pairs(self, k):
        f, z = self.f, self.z
        order = self.first(k)
        for m in order + [m for m in range(self.nc - 1, -1, -1) if m not in order]:
            src = self.src_at(flip(f, 2 * m + 1), k)
            self.push(src, self.sib.at[k, m], self.sems, self.nc + m, k, (flip(f, 1), z))

    def chips(self, k):
        f, z = self.f, self.z
        for m in self.first(k):
            sib = self.sib.at[k, m]
            self.arrive(sib, self.sems, self.nc + m, k)
            add_into(sib, self.own_at(k, m), sib)
            hop, to = m, m
            if self.tree:
                hop, to = (2 if m == 3 else 1), relay_of(k)
            self.push(sib, self.rx.at[k, hop - 1], self.sems, hop, k, (flip(f, 2 * to), z))

    def across(self, k):
        if not self.tree:
            return
        m = 3 - relay_of(k)
        sib = self.sib.at[k, m]
        self.arrive(sib, self.sems, self.nc + m, k)
        self.arrive(self.rx.at[k, 1], self.sems, 2, k)
        add_into(sib, self.own_at(k, m), sib, self.rx.at[k, 1])
        self.push(sib, self.rx.at[k, 2], self.sems, 3, k, (flip(self.f, 2 * m), self.z))

    def total(self, k, out):
        self.arrive(self.sib.at[k, 0], self.sems, self.nc, k)
        terms = [self.own_at(k, 0), self.sib.at[k, 0]]
        for m in range(1, self.nc):
            if self.tree and m == 2:
                continue
            self.arrive(self.rx.at[k, m - 1], self.sems, m, k)
            terms.append(self.rx.at[k, m - 1])
        add_into(out, *terms)

    def finish(self):
        for copy in self.sent:
            copy.wait_send()


class Scatter(Sums):
    def __init__(self, nf, nz, src_at, own_at, sib, rx, sems, land):
        super().__init__(nf, nz, src_at, own_at, sib, rx, sems)
        self.land = land

    @staticmethod
    def scratch(nf, nz, rows, columns):
        sib, rx, sems = Sums.buffers(nf, nz, rows, columns)
        return [sib, rx, pltpu.VMEM((nz - 1, rows, columns), BF), sems]

    def home(self, k, out):
        if k == 0:
            self.total(0, out)
            return
        sib = self.sib.at[k, 0]
        self.total(k, sib)
        self.push(sib, self.land.at[k - 1], self.sems, 0, k, (self.f, flip(self.z, k)))

    def landed(self, k):
        self.arrive(self.land.at[k - 1], self.sems, 0, k)


class RowScatter(Sums):
    def __init__(self, nf, nz, src_at, own_at, sib, rx, sems, home_sems, land, each):
        super().__init__(nf, nz, src_at, own_at, sib, rx, sems)
        self.home_sems, self.land, self.each = home_sems, land, each

    @staticmethod
    def scratch(nf, nz, lp, rows, columns):
        sib, rx, sems = Sums.buffers(nf, lp, rows, columns)
        return [sib, rx, sems, pltpu.SemaphoreType.DMA((2, nz, lp))]

    def rows_of(self, ref, at):
        return ref.at[pl.ds(pl.multiple_of(at * self.each, self.each), self.each)]

    def home(self, p):
        f, z, lp = self.f, self.z, self.sib.shape[0]
        whole = self.sib.at[p, 0]
        self.total(p, whole)
        land = self.rows_of(self.land, z * lp + p)
        for k in range(1, self.nz):
            src = self.rows_of(whole, flip(z, k))
            self.push(src, land, self.home_sems, k, p, (f, flip(z, k)))
        land[...] = self.rows_of(whole, z)[...]

    def landed(self, p):
        lp = self.sib.shape[0]
        for k in range(1, self.nz):
            land = self.rows_of(self.land, flip(self.z, k) * lp + p)
            self.arrive(land, self.home_sems, k, p)


def add_into(out, *terms):
    rows = out.shape[0]
    step = 16 if rows % 16 == 0 else rows

    def body(i, carry):
        at = pl.ds(pl.multiple_of(i * step, step), step)
        total = terms[0][at, :].astype(F32)
        for term in terms[1:]:
            total = total + term[at, :].astype(F32)
        out[at, :] = total.astype(out.dtype)
        return carry

    lax.fori_loop(0, rows // step, body, 0)


def call(kernel, ident, **kw):
    return pl.pallas_call(
        kernel,
        compiler_params=pltpu.CompilerParams(
            collective_id=ident, has_side_effects=True, vmem_limit_bytes=60 * 2**20
        ),
        **kw,
    )


def run_gathers(gathers, nz):
    for k in range(nz):
        for g in gathers:
            if k > 0:
                g.along(k)
        for g in gathers:
            if g.tree and k > 0:
                g.over(relay_of(k - 1), k - 1)
    for g in gathers:
        if g.tree:
            g.over(relay_of(nz - 1), nz - 1)
    for k in range(nz):
        for g in gathers:
            for m in range(1, g.nc):
                if g.tree and m == relay_of(k):
                    continue
                g.over(m, k)


def first_kernel(nf, nz, attn, gy, pair, attn_all, gy_all, pair_all, s1, s2, s3):
    greet(nf, nz, True)
    weights = Gather(nf, nz, lambda zz: attn, lambda ff, zz: attn_all.at[ff, zz], s1)
    rows = Gather(nf, nz, lambda zz: gy.at[zz], lambda ff, zz: gy_all.at[ff, zz], s2)
    swap = Swap(nf, lambda ff: pair.at[ff], lambda ff: pair_all.at[ff], s3)
    weights.begin()
    rows.begin()
    swap.start()
    run_gathers([weights, rows], nz)
    weights.finish()
    rows.finish()
    swap.finish()


def rows_kernel(nf, nz, b, b_all, s1):
    greet(nf, nz, False)
    rows = Gather(nf, nz, lambda zz: b.at[zz], lambda ff, zz: b_all.at[ff, zz], s1)
    rows.begin()
    run_gathers([rows], nz)
    rows.finish()


def in_place(terms):
    f, z = place()
    return (
        lambda ff, k: terms.at[ff, flip(z, k)],
        lambda k, m: terms.at[flip(f, 2 * m), flip(z, k)],
    )


def back_kernel(nf, nz, terms, out, sib, rx, land, sems):
    greet(nf, nz, False)
    s = Scatter(nf, nz, *in_place(terms), sib, rx, sems, land)
    z = s.z
    backward = range(nz - 1, -1, -1)
    for step in (s.pairs, s.chips, s.across, lambda k: s.home(k, out.at[z])):
        for k in backward:
            step(k)
    for k in range(1, nz):
        s.landed(k)
        out[flip(z, k)] = land[k - 1]
    s.finish()


def last_kernel(nf, nz, terms, pair, out, pair_all, sib, rx, land, sems, s2):
    greet(nf, nz, True)
    s = Scatter(nf, nz, *in_place(terms), sib, rx, sems, land)
    swap = Swap(nf, lambda ff: pair.at[ff], lambda ff: pair_all.at[ff], s2)
    backward = range(nz - 1, -1, -1)
    for k in backward:
        s.pairs(k)
    swap.start()
    for step in (s.chips, s.across, lambda k: s.home(k, out)):
        for k in backward:
            step(k)
    for k in range(1, nz):
        s.landed(k)
        add_into(out, out, land.at[k - 1])
    s.finish()
    swap.finish()


def contract(a, b, at_a, at_b):
    return lax.dot_general(a, b, (((at_a,), (at_b,)), ((), ())), preferred_element_type=F32)


def nt(a, b):
    return contract(a, b, 1, 1)


def nn(a, b):
    return contract(a, b, 1, 0)


def tn(a, b):
    return contract(a, b, 0, 0)


def by_position(rows, npos, fr, back=False):
    i = lax.broadcasted_iota(jnp.int32, (rows, rows), 0)
    j = lax.broadcasted_iota(jnp.int32, (rows, rows), 1)
    if back:
        i, j = j, i
    return ((i % fr) * npos + i // fr == j).astype(F32).astype(BF)


def causal(rows, npos):
    i = lax.broadcasted_iota(jnp.int32, (rows, rows), 0)
    j = lax.broadcasted_iota(jnp.int32, (rows, rows), 1)
    return jnp.logical_and(i // npos == j // npos, j <= i)


def soft(q, k, mask):
    s = jnp.where(mask, nt(q, k) * (1.0 / math.sqrt(HD)), -1e30)
    e = jnp.exp(s - jnp.max(s, axis=1, keepdims=True))
    return e / jnp.sum(e, axis=1, keepdims=True)

GROUP=128

def attention_fwd(npos, fr, x, gain1, gain2, w, a_out, qkv, ob, x1_out, b_out):
    rows, d = x.shape
    xf = x[...].astype(F32)
    rinv1 = lax.rsqrt(jnp.mean(xf * xf, axis=1, keepdims=True) + 1e-05)
    a_out[...] = (xf * rinv1 * gain1[...]).astype(BF)
    step = 512
    def project(i, c):
        at = pl.ds(pl.multiple_of(i * step, step), step)
        for t in range(3):
            to = pl.ds(pl.multiple_of(t * d + i * step, step), step)
            qkv[:, to] = nn(a_out[...], w[t, :, at]).astype(BF)
        return c
    lax.fori_loop(0, d // step, project, 0)
    mask = causal(GROUP, npos)
    low = lax.broadcasted_iota(jnp.int32, (GROUP, 2 * HD), 1) < HD
    def heads(i, c):
        for g in range(rows // GROUP):
            at = pl.ds(g * GROUP, GROUP)
            q, k, v = (qkv[at, pl.ds(pl.multiple_of(i * 2 * HD + t * d, 2 * HD), 2 * HD)] for t in range(3))
            zero = jnp.zeros_like(q)
            p0 = soft(jnp.where(low, q, zero), k, mask).astype(BF)
            p1 = soft(jnp.where(low, zero, q), k, mask).astype(BF)
            ob[at, pl.ds(pl.multiple_of(i * 2 * HD, 2 * HD), 2 * HD)] = jnp.where(low, nn(p0, v), nn(p1, v)).astype(BF)
        return c
    lax.fori_loop(0, d // (2 * HD), heads, 0)
    def out(i, c):
        at = pl.ds(pl.multiple_of(i * step, step), step)
        x1_out[:, at] = x[:, at].astype(F32) + nn(ob[...], w[3, :, at])
        return c
    lax.fori_loop(0, d // step, out, 0)
    x1 = x1_out[...]
    rinv2 = lax.rsqrt(jnp.mean(x1 * x1, axis=1, keepdims=True) + 1e-05)
    b = (x1 * rinv2 * gain2[...]).astype(BF)
    b_out[...] = nn(by_position(rows, npos, fr), b).astype(BF)


def attention_bwd_in(npos, fr, db_pos, gy, keep, x1_ref, ob, w, gain2, dx1_s, dxb, do_s, terms):
    rows, d = x1_ref.shape
    db = nn(by_position(rows, npos, fr, True), db_pos[...])
    x1 = x1_ref[...]
    rinv2 = lax.rsqrt(jnp.mean(x1 * x1, axis=1, keepdims=True) + 1e-05)
    n2 = db * gain2[...]
    inner = jnp.mean(n2 * x1, axis=1, keepdims=True)
    dx1 = keep[...] * gy[...].astype(F32) + rinv2 * n2 - x1 * (rinv2 * rinv2 * rinv2 * inner)
    dx1_s[...] = dx1
    dxb[...] = dx1.astype(BF)
    step = 512

    def weights(i, c):
        at = pl.ds(pl.multiple_of(i * step, step), step)
        to = pl.ds(pl.multiple_of(3 * d + i * step, step), step)
        terms[:, to] = tn(ob[...], dxb[:, at]).astype(BF)
        return c

    lax.fori_loop(0, d // step, weights, 0)
    do_s[...] = nt(dxb[...], w[3]).astype(BF)
    return jnp.sum(db * x1 * rinv2, axis=0, keepdims=True)


def attention_bwd_heads(npos, qkv, do_s, dqkv):
    rows, d = do_s.shape
    mask = causal(GROUP, npos)
    low = lax.broadcasted_iota(jnp.int32, (GROUP, 2 * HD), 1) < HD
    scale = 1.0 / math.sqrt(HD)

    def heads(i, c):
        for g in range(rows // GROUP):
            at = pl.ds(g * GROUP, GROUP)
            lanes = [pl.ds(pl.multiple_of(i * 2 * HD + t * d, 2 * HD), 2 * HD) for t in range(3)]
            q, k, v = (qkv[at, l] for l in lanes)
            do = do_s[at, lanes[0]]
            zero = jnp.zeros_like(q)
            parts = []
            for h in range(2):
                keep = low if h == 0 else jnp.logical_not(low)
                p = soft(jnp.where(keep, q, zero), k, mask)
                dp = nt(jnp.where(keep, do, zero), v)
                ds = (p * (dp - jnp.sum(p * dp, axis=1, keepdims=True)) * scale).astype(BF)
                parts.append((nn(ds, k), tn(ds, q), tn(p.astype(BF), do)))
            for t in range(3):
                dqkv[at, lanes[t]] = jnp.where(low, parts[0][t], parts[1][t]).astype(BF)
        return c

    lax.fori_loop(0, d // (2 * HD), heads, 0)


def attention_bwd_weights(a, dqkv, terms):
    step = 512

    def weights(i, c):
        at = pl.ds(pl.multiple_of(i * step, step), step)
        terms[:, at] = tn(a[...], dqkv[:, at]).astype(BF)
        return c

    lax.fori_loop(0, dqkv.shape[1] // step, weights, 0)


def attention_bwd_rows(x, dqkv, w, gain1, dx1, rows_out):
    d = x.shape[1]
    da = sum(nt(dqkv[:, t * d : (t + 1) * d], w[t]) for t in range(3))
    xf = x[...].astype(F32)
    rinv1 = lax.rsqrt(jnp.mean(xf * xf, axis=1, keepdims=True) + 1e-05)
    n1 = da * gain1[...]
    inner = jnp.mean(n1 * xf, axis=1, keepdims=True)
    rows_out[...] = dx1[...] + rinv1 * n1 - xf * (rinv1 * rinv1 * rinv1 * inner)
    return jnp.sum(da * xf * rinv1, axis=0, keepdims=True)


def gains_into(gain1_grad, gain2_grad, terms):
    d = gain1_grad.shape[1]
    high1 = gain1_grad.astype(BF).astype(F32)
    high2 = gain2_grad.astype(BF).astype(F32)
    at = lax.broadcasted_iota(jnp.int32, (128, d), 0)
    tail = jnp.where(at == 0, high1, 0.0)
    tail = jnp.where(at == 1, high2, tail)
    tail = jnp.where(at == 2, gain1_grad - high1, tail)
    tail = jnp.where(at == 3, gain2_grad - high2, tail)
    terms[:, 4 * d : 4 * d + 128] = tail.T.astype(BF)


def by_row(ref, rows, nz):
    return lambda ff, zz: ref.at[pl.ds(pl.multiple_of((ff * nz + zz) * rows, rows), rows)]


def pack(masters, stage, sems, send, p):
    nf, _, _, ffs, _ = send.shape
    copies = [
        pltpu.make_async_copy(master.at[p], stage.at[i], sems.at[i])
        for i, master in enumerate(masters)
    ]
    for copy in copies:
        copy.start()
    for i, copy in enumerate(copies):
        copy.wait()
        turned = stage[i].T.astype(BF)
        for j in range(nf):
            send[j, i, p] = turned[j * ffs : (j + 1) * ffs]


def feed(p, fr, gy_all, b_all, pair, wd, rows_g, rows_b, hid_out, grads, db, z):
    nf, _, _, _, width = grads.shape
    count, d = rows_b.shape
    blocks = count // fr
    each = b_all.shape[0] // blocks
    for i in range(blocks):
        rows_g[i * fr : (i + 1) * fr] = gy_all[i * each + p * fr : i * each + (p + 1) * fr]
        rows_b[i * fr : (i + 1) * fr] = b_all[i * each + p * fr : i * each + (p + 1) * fr]
    b_rows = rows_b[...]
    gate = nt(pair[0, p], b_rows)
    up = nt(pair[1, p], b_rows)
    dhid = nt(wd, rows_g[...])
    s = jax.nn.sigmoid(gate)
    silu = gate * s
    hid = (silu * up).astype(BF)
    dgate = (dhid * up * s * (1.0 + gate * (1.0 - s))).astype(BF)
    dup = (dhid * silu).astype(BF)
    hid_out[p] = hid
    db[...] = (tn(dgate, pair[0, p]) + tn(dup, pair[1, p])).astype(BF)
    z[...] = tn(hid, wd).astype(BF)
    for at, term in enumerate((dgate, dup)):
        grad = nn(term, b_rows).astype(BF)
        for j in range(nf):
            grads[j, at, p] = grad[:, j * width : (j + 1) * width]


def ahead_kernel(
    nf, nz, npos, fr,
    x, gy, keep, gain1, gain2, qkv_w, out_w, gate_w, up_w, down_w,
    w_out, gy_out, grads_out, hid_out, a, qkv, ob, x1, db_rows, z_rows,
    own_w, w, gy_pos, b_pos, send, stage, down, gy_all, b_all, pair, rows_g, rows_b,
    db_sib, db_rx, z_sib, z_rx,
    sems_w, sems_gy, sems_b, sems_swap, sems_in, sems_out, sems_grads, sems_down,
    sems_db, sems_db_home, sems_z, sems_z_home,
):
    d = x.shape[1]
    each = own_w.shape[1]
    lp = npos // nz
    lrows = lp * fr
    width = send.shape[4]
    f, z = place()
    greet(nf, nz, True)
    for i in range(3):
        own_w[i] = qkv_w[:, i * d : (i + 1) * d].astype(BF)
    own_w[3] = out_w[...].astype(BF)

    def w_at(ff, zz):
        return w.at[:, pl.ds(pl.multiple_of((ff * nz + zz) * each, each), each)]

    def pos_rows(ref):
        return lambda zz: ref.at[pl.ds(pl.multiple_of(zz * lrows, lrows), lrows)]

    weights = Gather(nf, nz, lambda zz: own_w, w_at, sems_w)
    weights.begin()
    kept = (gy[...].astype(F32) * keep[...]).astype(BF)
    gy_pos[...] = nn(by_position(npos * fr, npos, fr), kept).astype(BF)
    grads = Gather(nf, nz, pos_rows(gy_pos), by_row(gy_all, lrows, nz), sems_gy)
    masters = (gate_w, up_w)

    def pair_at(p):
        def at(ff):
            return pair.at[:, p, :, pl.ds(pl.multiple_of(ff * width, width), width)]

        return at

    def send_at(p):
        return lambda ff: send.at[ff, :, p]

    swaps = [Swap(nf, send_at(p), pair_at(p), sems_swap.at[p]) for p in range(lp)]
    half = lp // 2
    for p in range(half):
        pack(masters, stage, sems_in, send, p)
    for k in range(1, nz):
        weights.along(k)
    for k in range(nz):
        weights.over(relay_of(k), k)
    grads.begin()
    for p in range(half, lp):
        pack(masters, stage, sems_in, send, p)
    for k in range(nz):
        for m in weights.order(k)[1:]:
            weights.over(m, k)
    for k in range(1, nz):
        grads.along(k)
    for p in range(half):
        swaps[p].start()
    for k in range(nz):
        grads.over(relay_of(k), k)
    weights.finish()
    save_w = pltpu.make_async_copy(w, w_out, sems_out.at[0])
    save_w.start()
    attention_fwd(npos, fr, x, gain1, gain2, w, a, qkv, ob, x1, b_pos)
    rows = Gather(nf, nz, pos_rows(b_pos), by_row(b_all, lrows, nz), sems_b)
    rows.begin()
    for k in range(nz):
        for m in grads.order(k)[1:]:
            grads.over(m, k)
    for k in range(1, nz):
        rows.along(k)
    for k in range(nz):
        rows.over(relay_of(k), k)
    for p in range(half, lp):
        swaps[p].start()
    for k in range(nz):
        for m in rows.order(k)[1:]:
            rows.over(m, k)
    grads.finish()
    save_gy = pltpu.make_async_copy(gy_all, gy_out, sems_out.at[1])
    save_gy.start()
    save_w.wait()
    rows.finish()

    count = rows_b.shape[0]
    share = count // nf

    def term_at(first, p):
        per = d // count
        return w.at[first + p // per, pl.ds((p % per) * count, count)]

    def part_at(first):
        def at(ff, p):
            return term_at(first, p).at[pl.ds(pl.multiple_of(ff * share, share), share)]

        return at

    def sums(first, sib, rx, sems, home_sems, land):
        at = part_at(first)
        return RowScatter(
            nf, nz, at, lambda p, m: at(flip(f, 2 * m), p), sib, rx, sems, home_sems, land, fr
        )

    s_db = sums(0, db_sib, db_rx, sems_db, sems_db_home, db_rows)
    s_z = sums(2, z_sib, z_rx, sems_z, sems_z_home, z_rows)

    def fetch(p):
        return pltpu.make_async_copy(down_w.at[p], down.at[p % 2], sems_down.at[p % 2])

    saves = []
    fetch(0).start()
    for p in range(lp):
        if p + 1 < lp:
            fetch(p + 1).start()
        fetch(p).wait()
        wd = down[p % 2].astype(BF)
        swaps[p].finish()
        feed(
            p, fr, gy_all, b_all, pair, wd, rows_g, rows_b, hid_out, send,
            term_at(0, p), term_at(2, p),
        )
        saves.append(
            pltpu.make_async_copy(send.at[:, :, p], grads_out.at[:, :, p], sems_grads.at[p])
        )
        saves[-1].start()
        s_db.pairs(p)
        if p >= 1:
            s_db.chips(p - 1)
        s_z.pairs(p)
        if p >= 2:
            s_db.across(p - 2)
        if p >= 3:
            s_db.home(p - 3)
            s_z.chips(p - 3)
    for step, last in ((s_db.chips, 1), (s_db.across, 2), (s_db.home, 3), (s_z.chips, 3)):
        for p in range(max(lp - last, 0), lp):
            step(p)
    for step in (s_z.across, s_z.home, s_db.landed, s_z.landed):
        for p in range(lp):
            step(p)
    save_gy.wait()
    for copy in saves:
        copy.wait()
    s_db.finish()
    s_z.finish()


def behind_kernel(
    nf, nz, npos, fr,
    grads, w_in, x, gy, keep, gain1, gain2, x1, a, qkv, ob, db_rows, z_rows,
    block_out, rows_grad, total, pair_all,
    t_sib, t_rx, t_land, t_sems, sems_swap, sem_w,
    w, terms, dx1, dxb, do, dqkv,
):
    each = total.shape[0]
    lp = npos // nz
    f, z = place()
    load_w = pltpu.make_async_copy(w_in, w, sem_w)
    load_w.start()
    greet(nf, nz, True)
    backward = range(nz - 1, -1, -1)

    def part(ref, p):
        return lambda ff: ref.at[ff, :, p]

    swaps = [Swap(nf, part(grads, p), part(pair_all, p), sems_swap.at[p]) for p in range(lp)]
    for swap in swaps:
        swap.start()
    load_w.wait()
    gain2_grad = attention_bwd_in(npos, fr, db_rows, gy, keep, x1, ob, w, gain2, dx1, dxb, do, terms)
    attention_bwd_heads(npos, qkv, do, dqkv)
    attention_bwd_weights(a, dqkv, terms)
    gain1_grad = attention_bwd_rows(x, dqkv, w, gain1, dx1, rows_grad)
    gains_into(gain1_grad, gain2_grad, terms)
    src_at = by_row(terms, each, nz)
    s_t = Scatter(
        nf,
        nz,
        lambda ff, k: src_at(ff, flip(z, k)),
        lambda k, m: src_at(flip(f, 2 * m), flip(z, k)),
        t_sib, t_rx, t_sems, t_land,
    )
    for step in (s_t.pairs, s_t.chips):
        for k in backward:
            step(k)
    back = nn(by_position(npos * fr, npos, fr, True), z_rows[...])
    block_out[...] = (keep[...] * (x1[...] + back)).astype(BF)
    for step in (s_t.across, lambda k: s_t.home(k, total)):
        for k in backward:
            step(k)
    for k in range(1, nz):
        s_t.landed(k)
        add_into(total, total, t_land.at[k - 1])
    s_t.finish()
    for swap in swaps:
        swap.finish()


def last_local_kernel(pair, hid, gy, total, gate, up, down, qkv_grad, out_grad, gains):
    nf, _, _, ffs, width = pair.shape
    d = gy.shape[3]

    @pl.when(pl.program_id(0) == 0)
    def _():
        qkv_grad[...] = total[:, : 3 * d]
        out_grad[...] = total[:, 3 * d : 4 * d]
        gains[...] = total[:, 4 * d :]

    for at, out in enumerate((gate, up)):
        out[0] = pair[:, at, 0].astype(F32).reshape(nf * ffs, width).T
    down[0] = nn(hid[0], gy[...].reshape(hid.shape[2], d))


def rms_norm(values, gain_vector):
    return (
        values * lax.rsqrt(jnp.mean(values * values, axis=-1, keepdims=True) + 1e-05) * gain_vector
    )


def attend(qkv_rows):
    frame_count = qkv_rows.shape[0]
    positions = qkv_rows.shape[1]
    split_rows = qkv_rows.reshape(frame_count, positions, 3, H, HD)
    queries = split_rows[:, :, 0]
    keys_all = split_rows[:, :, 1]
    values_all = split_rows[:, :, 2]
    scores = jnp.einsum("fqhe,fkhe->fhqk", queries, keys_all, preferred_element_type=F32) * (
        1.0 / math.sqrt(HD)
    )
    causal = jnp.arange(positions)[:, None] >= jnp.arange(positions)[None, :]
    scores = jnp.where(causal, scores, -1e30)
    weights = jax.nn.softmax(scores, axis=-1)
    mixed = jnp.einsum("fhqk,fkhe->fqhe", weights, values_all, preferred_element_type=F32)
    return mixed.reshape(frame_count, positions, H * HD)


def local_general(
    frame_rows,
    frame_mask,
    gain_attention,
    gain_feed,
    qkv_master,
    out_master,
    gate_master,
    up_master,
    down_master,
    out_cotangent,
):
    nf = lax.axis_size("frames")
    nz = lax.axis_size("pos")
    lp, dslice, ff = gate_master.shape
    ffs = down_master.shape[1]
    fr, npos, d = frame_rows.shape

    keep_rows = frame_mask.astype(F32)[:, None, None]
    inputs = frame_rows.astype(F32)

    def turned(w):
        return w.astype(BF).reshape(lp, dslice, nf, ffs).transpose(2, 0, 3, 1)

    def untwist(w):
        return w.transpose(1, 2, 0, 3).reshape(lp, ffs, d)

    def to_pos(rows):
        return rows.transpose(1, 0, 2).reshape(nz, lp * fr, d)

    def gathered(every):
        every = every.reshape(nf, nz, lp, fr, d)
        return every.transpose(2, 0, 1, 3, 4).reshape(lp, nf * nz * fr, d)

    rows_shape = jax.ShapeDtypeStruct((nf, nz, lp * fr, d), BF)
    back_shape = jax.ShapeDtypeStruct((nz, lp * fr, d), BF)
    gather_sems = pltpu.SemaphoreType.DMA(Gather.sem_shape(nf, nz))
    swap_sems = pltpu.SemaphoreType.DMA(Swap.sem_shape(nf))

    def scattered(rows, ident):
        moved = rows.reshape(lp, nf, nz, fr, d).transpose(1, 2, 0, 3, 4)
        moved = moved.reshape(nf, nz, lp * fr, d)
        back = call(
            functools.partial(back_kernel, nf, nz),
            ident,
            out_shape=back_shape,
            in_specs=[VM],
            out_specs=VM,
            scratch_shapes=Scatter.scratch(nf, nz, lp * fr, d),
        )(moved)
        return back.reshape(npos, fr, d).transpose(1, 0, 2)

    both = jnp.concatenate((qkv_master.astype(BF), out_master.astype(BF)), axis=1)
    pair = jnp.stack((turned(gate_master), turned(up_master)), axis=1)
    upstream = keep_rows * out_cotangent.astype(F32)
    own_rows = both.shape[0]
    w_all, gy_all, pair = call(
        functools.partial(first_kernel, nf, nz),
        0,
        out_shape=(
            jax.ShapeDtypeStruct((nf, nz) + both.shape, BF),
            rows_shape,
            jax.ShapeDtypeStruct(pair.shape, BF),
        ),
        in_specs=[ANY] * 3,
        out_specs=(ANY,) * 3,
        scratch_shapes=[gather_sems, gather_sems, swap_sems],
    )(both, to_pos(upstream.astype(BF)), pair)
    w_all = w_all.reshape(d, both.shape[1])
    w_qkv = w_all[:, : 3 * d]
    w_out = w_all[:, 3 * d :]
    gate_t = untwist(pair[:, 0])
    up_t = untwist(pair[:, 1])
    down = down_master.astype(BF)
    gy = gathered(gy_all)

    normed_one, norm_one_pull = jax.vjp(rms_norm, inputs, gain_attention)
    normed_low = normed_one.astype(BF)
    qkv_rows = jnp.einsum("fpd,de->fpe", normed_low, w_qkv, preferred_element_type=F32)
    mixed, attend_pull = jax.vjp(attend, qkv_rows)
    mixed_low = mixed.astype(BF)
    branch = jnp.einsum("fpd,de->fpe", mixed_low, w_out, preferred_element_type=F32)
    middle = inputs + branch
    normed_two, norm_two_pull = jax.vjp(rms_norm, middle, gain_feed)
    b_all = call(
        functools.partial(rows_kernel, nf, nz),
        1,
        out_shape=rows_shape,
        in_specs=[ANY],
        out_specs=ANY,
        scratch_shapes=[gather_sems],
    )(to_pos(normed_two.astype(BF)))
    b = gathered(b_all)

    gate_rows = jnp.einsum("prd,phd->phr", b, gate_t, preferred_element_type=F32)
    up_rows = jnp.einsum("prd,phd->phr", b, up_t, preferred_element_type=F32)
    hidden_grad = jnp.einsum("prd,phd->phr", gy, down, preferred_element_type=F32)
    sigma = jax.nn.sigmoid(gate_rows)
    silu_gate = gate_rows * sigma
    hidden = (silu_gate * up_rows).astype(BF)
    gate_back = (hidden_grad * up_rows * sigma * (1.0 + gate_rows * (1.0 - sigma))).astype(BF)
    up_back = (hidden_grad * silu_gate).astype(BF)
    db = jnp.einsum("phr,phd->prd", gate_back, gate_t, preferred_element_type=F32) + jnp.einsum(
        "phr,phd->prd", up_back, up_t, preferred_element_type=F32
    )
    back_rows = scattered(db.astype(BF), 2).astype(F32)
    feed = jnp.einsum("phr,phd->prd", hidden, down, preferred_element_type=F32)
    returned = scattered(feed.astype(BF), 3).astype(F32)
    block_out = (keep_rows * (middle + returned)).astype(BF)
    gate_grad = jnp.einsum("phr,prd->phd", gate_back, b, preferred_element_type=F32).astype(BF)
    up_grad = jnp.einsum("phr,prd->phd", up_back, b, preferred_element_type=F32).astype(BF)
    down_grad = jnp.einsum("phr,prd->phd", hidden, gy, preferred_element_type=F32)

    grads = jnp.stack((gate_grad, up_grad), axis=0).reshape(2, lp, ffs, nf, dslice)
    grads = grads.transpose(3, 0, 1, 2, 4)

    pulled_two = norm_two_pull(back_rows)
    middle_grad = upstream + pulled_two[0]
    branch_grad = middle_grad.astype(BF)
    out_weight_grad = jnp.einsum("fpd,fpe->de", mixed_low, branch_grad, preferred_element_type=F32)
    mixed_grad = jnp.einsum("fpe,de->fpd", branch_grad, w_out, preferred_element_type=F32)
    qkv_back = attend_pull(mixed_grad)[0].astype(BF)
    qkv_weight_grad = jnp.einsum("fpd,fpe->de", normed_low, qkv_back, preferred_element_type=F32)
    normed_grad = jnp.einsum("fpe,de->fpd", qkv_back, w_qkv, preferred_element_type=F32)
    pulled_one = norm_one_pull(normed_grad)
    rows_grad = middle_grad + pulled_one[0]

    gains = jnp.stack((pulled_one[1], pulled_two[1]), axis=1)
    gains_hi = gains.astype(BF)
    gains_lo = (gains - gains_hi.astype(F32)).astype(BF)
    tail = jnp.concatenate((gains_hi, gains_lo, jnp.zeros((d, 124), BF)), axis=1)
    total = jnp.concatenate(
        (qkv_weight_grad.astype(BF), out_weight_grad.astype(BF), tail), axis=1
    )
    total = total.reshape(nf, nz, own_rows, total.shape[1])
    total, grads = call(
        functools.partial(last_kernel, nf, nz),
        4,
        out_shape=(
            jax.ShapeDtypeStruct(total.shape[2:], F32),
            jax.ShapeDtypeStruct(grads.shape, BF),
        ),
        in_specs=[VM, ANY],
        out_specs=(VM, ANY),
        scratch_shapes=Scatter.scratch(nf, nz, *total.shape[2:]) + [swap_sems],
    )(total, grads)
    grads = grads.transpose(1, 2, 4, 0, 3).reshape(2, lp, dslice, ff).astype(F32)
    gain_grads = total[:, 4 * d : 4 * d + 2] + total[:, 4 * d + 2 : 4 * d + 4]
    return (
        block_out,
        rows_grad,
        gain_grads[:, 0],
        gain_grads[:, 1],
        total[:, : 3 * d],
        total[:, 3 * d : 4 * d],
        grads[0],
        grads[1],
        down_grad,
    )
def local_fused(
    frame_rows,
    frame_mask,
    gain_attention,
    gain_feed,
    qkv_master,
    out_master,
    gate_master,
    up_master,
    down_master,
    out_cotangent,
):
    nf = lax.axis_size("frames")
    nz = lax.axis_size("pos")
    lp, dslice, ff = gate_master.shape
    ffs = down_master.shape[1]
    fr, npos, d = frame_rows.shape
    rows = fr * npos
    each = qkv_master.shape[0]
    count = nf * nz * fr

    def make(shape, kind=BF):
        return jax.ShapeDtypeStruct(shape, kind)

    def vmem(shape, kind=BF):
        return pltpu.VMEM(shape, kind)

    def dma(*shape):
        return pltpu.SemaphoreType.DMA(shape)

    x = frame_rows.reshape(rows, d)
    gy = out_cotangent.reshape(rows, d)
    keep = jnp.broadcast_to(frame_mask.astype(F32)[:, None], (fr, npos)).reshape(rows, 1)
    gain1 = gain_attention.reshape(1, d)
    gain2 = gain_feed.reshape(1, d)
    gather_sems = dma(*Gather.sem_shape(nf, nz))
    swap_sems = dma(lp, *Swap.sem_shape(nf))
    pair_shape = (nf, 2, lp, ffs, dslice)
    row_scratch = RowScatter.scratch(nf, nz, lp, nz * fr, d)
    w_all, gy_all, grads, hid, a, qkv, ob, x1, db_rows, z_rows = call(
        functools.partial(ahead_kernel, nf, nz, npos, fr),
        0,
        out_shape=(
            make((4, d, d)),
            make((lp * count, d)),
            make(pair_shape),
            make((lp, ffs, count)),
            make((rows, d)),
            make((rows, 3 * d)),
            make((rows, d)),
            make((rows, d), F32),
            make((rows, d)),
            make((rows, d)),
        ),
        in_specs=[VM] * 7 + [ANY] * 3,
        out_specs=(ANY,) * 3 + (VM,) * 7,
        scratch_shapes=[
            vmem((4, each, d)),
            vmem((4, d, d)),
            vmem((rows, d)),
            vmem((rows, d)),
            vmem(pair_shape),
            vmem((2, dslice, ff), F32),
            vmem((2, ffs, d), F32),
            vmem((lp * count, d)),
            vmem((lp * count, d)),
            vmem((2, lp, ffs, d)),
            vmem((count, d)),
            vmem((count, d)),
            *row_scratch[:2],
            *row_scratch[:2],
            gather_sems,
            gather_sems,
            gather_sems,
            swap_sems,
            dma(2),
            dma(2),
            dma(lp),
            dma(2),
            *row_scratch[2:],
            *row_scratch[2:],
        ],
    )(x, gy, keep, gain1, gain2, qkv_master, out_master, gate_master, up_master, down_master)
    wide = 4 * d + 128
    block_out, rows_grad, total, back = call(
        functools.partial(behind_kernel, nf, nz, npos, fr),
        1,
        out_shape=(
            make((rows, d)),
            make((rows, d), F32),
            make((each, wide), F32),
            make(pair_shape),
        ),
        in_specs=[ANY] * 2 + [VM] * 11,
        out_specs=(VM,) * 3 + (ANY,),
        scratch_shapes=[
            *Scatter.scratch(nf, nz, each, wide),
            swap_sems,
            pltpu.SemaphoreType.DMA,
            vmem((4, d, d)),
            vmem((d, wide)),
            vmem((rows, d), F32),
            vmem((rows, d)),
            vmem((rows, d)),
            vmem((rows, 3 * d)),
        ],
    )(grads, w_all, x, gy, keep, gain1, gain2, x1, a, qkv, ob, db_rows, z_rows)
    whole_block = pl.BlockSpec((1, dslice, ff), lambda p: (p, 0, 0))

    def once(*shape):
        return pl.BlockSpec(shape, lambda p: (0, 0))

    gate_grad, up_grad, down_grad, qkv_grad, out_grad, gains = pl.pallas_call(
        last_local_kernel,
        grid=(lp,),
        out_shape=(
            make((lp, dslice, ff), F32),
            make((lp, dslice, ff), F32),
            make((lp, ffs, d), F32),
            make((each, 3 * d), F32),
            make((each, d), F32),
            make((each, 128), F32),
        ),
        in_specs=[
            pl.BlockSpec((nf, 2, 1, ffs, dslice), lambda p: (0, 0, p, 0, 0)),
            pl.BlockSpec((1, ffs, count), lambda p: (p, 0, 0)),
            pl.BlockSpec((nf, nz, fr, d), lambda p: (0, 0, p, 0)),
            once(each, wide),
        ],
        out_specs=(
            whole_block,
            whole_block,
            pl.BlockSpec((1, ffs, d), lambda p: (p, 0, 0)),
            once(each, 3 * d),
            once(each, d),
            once(each, 128),
        ),
        compiler_params=pltpu.CompilerParams(vmem_limit_bytes=48 * 2**20),
    )(back, hid, gy_all.reshape(nf, nz, lp * fr, d), total)
    gains = gains[:, :2] + gains[:, 2:4]
    return (
        block_out.reshape(fr, npos, d),
        rows_grad.reshape(fr, npos, d),
        gains[:, 0],
        gains[:, 1],
        qkv_grad,
        out_grad,
        gate_grad,
        up_grad,
        down_grad,
    )


def local(*args):
    _, dslice, _ = args[6].shape
    if lax.axis_size("frames") == 8 and dslice % 128 == 0:
        return local_fused(*args)
    return local_general(*args)


def solution(mesh):
    in_specs = (
        P(("frames", "pos"), None, None),
        P(("frames", "pos")),
        P(),
        P(),
        P(("frames", "pos"), None),
        P(("frames", "pos"), None),
        P("pos", "frames", None),
        P("pos", "frames", None),
        P("pos", "frames", None),
        P(("frames", "pos"), None, None),
    )
    out_specs = (
        P(("frames", "pos"), None, None),
        P(("frames", "pos"), None, None),
        P(("frames", "pos")),
        P(("frames", "pos")),
        P(("frames", "pos"), None),
        P(("frames", "pos"), None),
        P("pos", "frames", None),
        P("pos", "frames", None),
        P("pos", "frames", None),
    )
    return jax.shard_map(local, mesh=mesh, in_specs=in_specs, out_specs=out_specs, check_vma=False)
```

```python
import functools
import math

import jax
import jax.numpy as jnp
from jax import lax
from jax.experimental import pallas as pl
from jax.experimental.pallas import tpu as pltpu
from jax.sharding import PartitionSpec as P

H = 16
HD = 64
BF = jnp.bfloat16
F32 = jnp.float32
MESH = pl.DeviceIdType.MESH
ANY = pl.BlockSpec(memory_space=pl.ANY)
VM = pl.BlockSpec(memory_space=pltpu.VMEM)


def place():
    return lax.axis_index("frames"), lax.axis_index("pos")


def flip(index, mask):
    bit = 1
    while bit <= mask:
        if mask & bit:
            index = index + bit * (1 - 2 * ((index // bit) % 2))
        bit *= 2
    return index


def greet(nf, nz, every_frame):
    f, z = place()
    hops = [1] + [2 * m for m in range(1, nf // 2)]
    if every_frame:
        hops = list(range(1, nf))
    others = [(flip(f, h), z) for h in hops] + [(f, flip(z, k)) for k in range(1, nz)]
    barrier = pltpu.get_barrier_semaphore()
    for other in others:
        pl.semaphore_signal(barrier, inc=1, device_id=other, device_id_type=MESH)
    pl.semaphore_wait(barrier, len(others))


def remote(src, dst, send, recv, to):
    copy = pltpu.make_async_remote_copy(
        src_ref=src, dst_ref=dst, send_sem=send, recv_sem=recv, device_id=to, device_id_type=MESH
    )
    copy.start()
    return copy


def arrival(dst, send, recv):
    f, z = place()
    pltpu.make_async_remote_copy(
        src_ref=dst,
        dst_ref=dst,
        send_sem=send,
        recv_sem=recv,
        device_id=(flip(f, 1), z),
        device_id_type=MESH,
    ).wait_recv()


def relay_of(k):
    return 1 if k % 2 == 0 else 2


class Gather:
    def __init__(self, nf, nz, src_for, out_at, group_at, sems):
        self.nf, self.nz, self.nc = nf, nz, nf // 2
        self.f, self.z = place()
        self.src_for, self.out_at, self.group_at, self.sems = src_for, out_at, group_at, sems
        self.sent = []
        self.own = {}
        self.tree = self.nc == 4

    @staticmethod
    def sem_shape(nf, nz, parts=1):
        return (2, nz + nf, parts)

    def push(self, src, dst, hop, c, to):
        self.sent.append(remote(src, dst, self.sems.at[0, hop, c], self.sems.at[1, hop, c], to))

    def arrive(self, dst, hop, c):
        arrival(dst, self.sems.at[0, hop, c], self.sems.at[1, hop, c])

    def near(self, m, c):
        return self.group_at(flip(self.f, 2 * m), c)

    def begin(self, c=0):
        f, z = self.f, self.z
        for k in range(self.nz - 1, 0, -1):
            self.push(self.src_for(flip(z, k), c), self.out_at(f, z, c), k, c, (f, flip(z, k)))
        src, dst = self.src_for(z, c), self.out_at(f, z, c)
        self.own[c] = pltpu.make_async_copy(src, dst, self.sems.at[0, 0, c])
        self.own[c].start()

    def along(self, c=0):
        f, z = self.f, self.z
        self.own[c].wait()
        for k in range(1, self.nz):
            self.arrive(self.out_at(f, flip(z, k), c), k, c)
        group = self.near(0, c)
        for m in range(1, self.nc):
            if not (self.tree and m == 3):
                self.push(group, group, self.nz + m, c, (flip(f, 2 * m), z))
        self.push(group, group, self.nz + self.nc, c, (flip(f, 1), z))

    def over(self, m, c):
        f, z = self.f, self.z
        group = self.near(m, c)
        self.arrive(group, self.nz + m, c)
        if self.tree and m == relay_of(c):
            self.push(group, group, self.nz + 3, c, (flip(f, 2 * (3 - m)), z))
        self.push(group, group, self.nz + self.nc + m, c, (flip(f, 1), z))

    def relay(self, c=0):
        if self.tree:
            self.over(relay_of(c), c)

    def rest(self, c=0):
        for m in range(1, self.nc):
            if not (self.tree and m == relay_of(c)):
                self.over(m, c)

    def whole(self, c=0):
        for m in range(self.nc):
            group = self.group_at(flip(self.f, 2 * m + 1), c)
            self.arrive(group, self.nz + self.nc + m, c)

    def finish(self):
        for copy in self.sent:
            copy.wait_send()


class Swap:
    def __init__(self, nf, src_at, out_at, sems):
        self.nf, self.src_at, self.out_at, self.sems = nf, src_at, out_at, sems
        self.f, self.z = place()
        self.sent = []

    @staticmethod
    def sem_shape(nf):
        return (2, nf)

    def start(self):
        f, z = self.f, self.z
        self.own = pltpu.make_async_copy(self.src_at(f), self.out_at(f), self.sems.at[0, 0])
        self.own.start()
        for m in range(self.nf - 1, 0, -1):
            self.sent.append(
                remote(
                    self.src_at(flip(f, m)),
                    self.out_at(f),
                    self.sems.at[0, m],
                    self.sems.at[1, m],
                    (flip(f, m), z),
                )
            )

    def finish(self):
        self.own.wait()
        for copy in self.sent:
            copy.wait()


class Sums:
    def __init__(self, nf, nz, src_at, own_at, sib, rx, sems):
        self.nf, self.nz, self.nc = nf, nz, nf // 2
        self.f, self.z = place()
        self.src_at, self.own_at, self.sib, self.rx = src_at, own_at, sib, rx
        self.sems = sems
        self.sent = []
        self.tree = self.nc == 4

    @staticmethod
    def buffers(nf, parts, rows, columns):
        nc = nf // 2
        return [
            pltpu.VMEM((parts, nc, rows, columns), BF),
            pltpu.VMEM((parts, nc - 1, rows, columns), BF),
            pltpu.SemaphoreType.DMA((2, 2 * nc, parts)),
        ]

    def push(self, src, dst, sems, hop, k, to):
        self.sent.append(remote(src, dst, sems.at[0, hop, k], sems.at[1, hop, k], to))

    def arrive(self, dst, sems, hop, k):
        arrival(dst, sems.at[0, hop, k], sems.at[1, hop, k])

    def first(self, k):
        if self.tree:
            return [3, relay_of(k)]
        return list(range(self.nc - 1, 0, -1))

    def pairs(self, k):
        f, z = self.f, self.z
        order = self.first(k)
        for m in order + [m for m in range(self.nc - 1, -1, -1) if m not in order]:
            src = self.src_at(flip(f, 2 * m + 1), k)
            self.push(src, self.sib.at[k, m], self.sems, self.nc + m, k, (flip(f, 1), z))

    def chips(self, k):
        f, z = self.f, self.z
        for m in self.first(k):
            sib = self.sib.at[k, m]
            self.arrive(sib, self.sems, self.nc + m, k)
            add_into(sib, self.own_at(k, m), sib)
            hop, to = m, m
            if self.tree:
                hop, to = (2 if m == 3 else 1), relay_of(k)
            self.push(sib, self.rx.at[k, hop - 1], self.sems, hop, k, (flip(f, 2 * to), z))

    def across(self, k):
        if not self.tree:
            return
        m = 3 - relay_of(k)
        sib = self.sib.at[k, m]
        self.arrive(sib, self.sems, self.nc + m, k)
        self.arrive(self.rx.at[k, 1], self.sems, 2, k)
        add_into(sib, self.own_at(k, m), sib, self.rx.at[k, 1])
        self.push(sib, self.rx.at[k, 2], self.sems, 3, k, (flip(self.f, 2 * m), self.z))

    def total(self, k, out):
        self.arrive(self.sib.at[k, 0], self.sems, self.nc, k)
        terms = [self.own_at(k, 0), self.sib.at[k, 0]]
        for m in range(1, self.nc):
            if self.tree and m == 2:
                continue
            self.arrive(self.rx.at[k, m - 1], self.sems, m, k)
            terms.append(self.rx.at[k, m - 1])
        add_into(out, *terms)

    def finish(self):
        for copy in self.sent:
            copy.wait_send()


class HomeSums(Sums):
    def __init__(self, nf, nz, src_at, own_at, sib, rx, sems, home_sems, land, each):
        super().__init__(nf, nz, src_at, own_at, sib, rx, sems)
        self.home_sems, self.land, self.each = home_sems, land, each

    @staticmethod
    def scratch(nf, nz, parts, rows, columns):
        sib, rx, sems = Sums.buffers(nf, parts, rows, columns)
        return [sib, rx, sems, pltpu.SemaphoreType.DMA((2, nz, parts))]

    def rows_of(self, ref, at):
        return ref.at[pl.ds(pl.multiple_of(at * self.each, self.each), self.each)]

    def home(self, p):
        whole = self.sib.at[p, 0]
        self.total(p, whole)
        for k in range(self.nz - 1, 0, -1):
            src = self.rows_of(whole, flip(self.z, k))
            self.push(src, self.sent_to(k, p), self.home_sems, k, p, (self.f, flip(self.z, k)))


class RowSums(HomeSums):
    def at(self, zz, p):
        return self.rows_of(self.land, zz * self.sib.shape[0] + p)

    def sent_to(self, k, p):
        return self.at(self.z, p)

    def landed(self, p):
        self.at(self.z, p)[...] = self.rows_of(self.sib.at[p, 0], self.z)[...]
        for k in range(1, self.nz):
            self.arrive(self.at(flip(self.z, k), p), self.home_sems, k, p)


class BlockSums(HomeSums):
    def sent_to(self, k, p):
        return self.land.at[p, k - 1]

    def landed(self, p, out):
        terms = [self.rows_of(self.sib.at[p, 0], self.z)]
        for k in range(1, self.nz):
            self.arrive(self.land.at[p, k - 1], self.home_sems, k, p)
            terms.append(self.land.at[p, k - 1])
        add_into(out, *terms)


def add_into(out, *terms):
    rows = out.shape[0]
    step = 16 if rows % 16 == 0 else rows

    def body(i, carry):
        at = pl.ds(pl.multiple_of(i * step, step), step)
        total = terms[0][at, :].astype(F32)
        for term in terms[1:]:
            total = total + term[at, :].astype(F32)
        out[at, :] = total.astype(out.dtype)
        return carry

    lax.fori_loop(0, rows // step, body, 0)


def call(kernel, ident, **kw):
    return pl.pallas_call(
        kernel,
        compiler_params=pltpu.CompilerParams(
            collective_id=ident, has_side_effects=True, vmem_limit_bytes=60 * 2**20
        ),
        **kw,
    )


def by_block(nf, nz, src_for, out, sems):
    return Gather(
        nf, nz, src_for, lambda ff, zz, c: out.at[ff, zz], lambda ff, c: out.at[ff], sems
    )


def first_kernel(nf, nz, attn, gy, pair, attn_all, gy_all, pair_all, s1, s2, s3):
    greet(nf, nz, True)
    weights = by_block(nf, nz, lambda zz, c: attn, attn_all, s1)
    rows = by_block(nf, nz, lambda zz, c: gy.at[zz], gy_all, s2)
    swap = Swap(nf, lambda ff: pair.at[ff], lambda ff: pair_all.at[ff], s3)
    gathers = (weights, rows)
    for g in gathers:
        g.begin()
    for step in ("along", "relay", "rest", "whole", "finish"):
        for g in gathers:
            getattr(g, step)()
        if step == "relay":
            swap.start()
    swap.finish()


def rows_kernel(nf, nz, b, b_all, s1):
    greet(nf, nz, False)
    rows = by_block(nf, nz, lambda zz, c: b.at[zz], b_all, s1)
    for step in (rows.begin, rows.along, rows.relay, rows.rest, rows.whole, rows.finish):
        step()


def chip_terms(terms):
    f, _ = place()
    return lambda ff, p: terms.at[p, ff], lambda p, m: terms.at[p, flip(f, 2 * m)]


def back_kernel(nf, nz, each, terms, out, sib, rx, sems, home_sems):
    greet(nf, nz, False)
    s = RowSums(nf, nz, *chip_terms(terms), sib, rx, sems, home_sems, out, each)
    for step in (s.pairs, s.chips, s.across, s.home, s.landed):
        for p in range(terms.shape[0]):
            step(p)
    s.finish()


def last_kernel(nf, nz, terms, pair, out, pair_all, sib, rx, sems, home_sems, land, s2):
    greet(nf, nz, True)
    s = BlockSums(nf, nz, *chip_terms(terms), sib, rx, sems, home_sems, land, out.shape[0])
    swap = Swap(nf, lambda ff: pair.at[ff], lambda ff: pair_all.at[ff], s2)
    s.pairs(0)
    swap.start()
    for step in (s.chips, s.across, s.home):
        step(0)
    s.landed(0, out)
    s.finish()
    swap.finish()


def contract(a, b, at_a, at_b):
    return lax.dot_general(a, b, (((at_a,), (at_b,)), ((), ())), preferred_element_type=F32)


def nt(a, b):
    return contract(a, b, 1, 1)


def nn(a, b):
    return contract(a, b, 1, 0)


def tn(a, b):
    return contract(a, b, 0, 0)


def by_position(rows, npos, fr, back=False):
    i = lax.broadcasted_iota(jnp.int32, (rows, rows), 0)
    j = lax.broadcasted_iota(jnp.int32, (rows, rows), 1)
    if back:
        i, j = j, i
    return ((i % fr) * npos + i // fr == j).astype(F32).astype(BF)


def causal(rows, npos):
    i = lax.broadcasted_iota(jnp.int32, (rows, rows), 0)
    j = lax.broadcasted_iota(jnp.int32, (rows, rows), 1)
    return jnp.logical_and(i // npos == j // npos, j <= i)


def soft(q, k, mask):
    s = jnp.where(mask, nt(q, k) * (1.0 / math.sqrt(HD)), -1e30)
    e = jnp.exp(s - jnp.max(s, axis=1, keepdims=True))
    return e / jnp.sum(e, axis=1, keepdims=True)

GROUP=128

def attention_fwd(npos, fr, x, gain1, gain2, w, a_out, qkv, ob, x1_out, b_out):
    rows, d = x.shape
    xf = x[...].astype(F32)
    rinv1 = lax.rsqrt(jnp.mean(xf * xf, axis=1, keepdims=True) + 1e-05)
    a_out[...] = (xf * rinv1 * gain1[...]).astype(BF)
    step = 512
    def project(i, c):
        at = pl.ds(pl.multiple_of(i * step, step), step)
        for t in range(3):
            to = pl.ds(pl.multiple_of(t * d + i * step, step), step)
            qkv[:, to] = nn(a_out[...], w[t, :, at]).astype(BF)
        return c
    lax.fori_loop(0, d // step, project, 0)
    mask = causal(GROUP, npos)
    low = lax.broadcasted_iota(jnp.int32, (GROUP, 2 * HD), 1) < HD
    def heads(i, c):
        for g in range(rows // GROUP):
            at = pl.ds(g * GROUP, GROUP)
            q, k, v = (qkv[at, pl.ds(pl.multiple_of(i * 2 * HD + t * d, 2 * HD), 2 * HD)] for t in range(3))
            zero = jnp.zeros_like(q)
            p0 = soft(jnp.where(low, q, zero), k, mask).astype(BF)
            p1 = soft(jnp.where(low, zero, q), k, mask).astype(BF)
            ob[at, pl.ds(pl.multiple_of(i * 2 * HD, 2 * HD), 2 * HD)] = jnp.where(low, nn(p0, v), nn(p1, v)).astype(BF)
        return c
    lax.fori_loop(0, d // (2 * HD), heads, 0)
    def out(i, c):
        at = pl.ds(pl.multiple_of(i * step, step), step)
        x1_out[:, at] = x[:, at].astype(F32) + nn(ob[...], w[3, :, at])
        return c
    lax.fori_loop(0, d // step, out, 0)
    x1 = x1_out[...]
    rinv2 = lax.rsqrt(jnp.mean(x1 * x1, axis=1, keepdims=True) + 1e-05)
    b = (x1 * rinv2 * gain2[...]).astype(BF)
    b_out[...] = nn(by_position(rows, npos, fr), b).astype(BF)


def weight_terms(left, right, first, out):
    columns = out.shape[1]
    step = 512

    def body(i, c):
        at = pl.ds(pl.multiple_of(i * step, step), step)
        of = pl.ds(pl.multiple_of(first + i * step, step), step)
        out[:, at] = tn(left[...], right[:, of]).astype(BF)
        return c

    lax.fori_loop(0, columns // step, body, 0)


def attention_bwd_in(npos, fr, db_pos, gy, keep, x1_ref, ob, gain2, dx1_s, dxb, terms):
    rows, d = x1_ref.shape
    db = nn(by_position(rows, npos, fr, True), db_pos[...])
    x1 = x1_ref[...]
    rinv2 = lax.rsqrt(jnp.mean(x1 * x1, axis=1, keepdims=True) + 1e-05)
    n2 = db * gain2[...]
    inner = jnp.mean(n2 * x1, axis=1, keepdims=True)
    dx1 = keep[...] * gy[...].astype(F32) + rinv2 * n2 - x1 * (rinv2 * rinv2 * rinv2 * inner)
    dx1_s[...] = dx1
    dxb[...] = dx1.astype(BF)
    weight_terms(ob, dxb, 0, terms.at[3])
    return jnp.sum(db * x1 * rinv2, axis=0, keepdims=True)


def attention_bwd_heads(npos, qkv, do_s, dqkv):
    rows, d = do_s.shape
    mask = causal(GROUP, npos)
    low = lax.broadcasted_iota(jnp.int32, (GROUP, 2 * HD), 1) < HD
    scale = 1.0 / math.sqrt(HD)

    def heads(i, c):
        for g in range(rows // GROUP):
            at = pl.ds(g * GROUP, GROUP)
            lanes = [pl.ds(pl.multiple_of(i * 2 * HD + t * d, 2 * HD), 2 * HD) for t in range(3)]
            q, k, v = (qkv[at, l] for l in lanes)
            do = do_s[at, lanes[0]]
            zero = jnp.zeros_like(q)
            parts = []
            for h in range(2):
                keep = low if h == 0 else jnp.logical_not(low)
                p = soft(jnp.where(keep, q, zero), k, mask)
                dp = nt(jnp.where(keep, do, zero), v)
                ds = (p * (dp - jnp.sum(p * dp, axis=1, keepdims=True)) * scale).astype(BF)
                parts.append((nn(ds, k), tn(ds, q), tn(p.astype(BF), do)))
            for t in range(3):
                dqkv[at, lanes[t]] = jnp.where(low, parts[0][t], parts[1][t]).astype(BF)
        return c

    lax.fori_loop(0, d // (2 * HD), heads, 0)


def attention_bwd_rows(x, dqkv, w, gain1, dx1, rows_out):
    d = x.shape[1]
    da = sum(nt(dqkv[:, t * d : (t + 1) * d], w[t]) for t in range(3))
    xf = x[...].astype(F32)
    rinv1 = lax.rsqrt(jnp.mean(xf * xf, axis=1, keepdims=True) + 1e-05)
    n1 = da * gain1[...]
    inner = jnp.mean(n1 * xf, axis=1, keepdims=True)
    rows_out[...] = dx1[...] + rinv1 * n1 - xf * (rinv1 * rinv1 * rinv1 * inner)
    return jnp.sum(da * xf * rinv1, axis=0, keepdims=True)


def gains_into(gain1_grad, gain2_grad, terms):
    d = gain1_grad.shape[1]
    high1 = gain1_grad.astype(BF).astype(F32)
    high2 = gain2_grad.astype(BF).astype(F32)
    at = lax.broadcasted_iota(jnp.int32, (128, d), 0)
    tail = jnp.where(at == 0, high1, 0.0)
    tail = jnp.where(at == 1, high2, tail)
    tail = jnp.where(at == 2, gain1_grad - high1, tail)
    tail = jnp.where(at == 3, gain2_grad - high2, tail)
    terms[...] = tail.T.astype(BF)


class Packer:
    def __init__(self, masters, stage, sems, send):
        self.masters, self.stage, self.sems, self.send = masters, stage, sems, send

    def fetch(self, i, p):
        return pltpu.make_async_copy(self.masters[i].at[p], self.stage.at[i], self.sems.at[i])

    def begin(self):
        for i in range(len(self.masters)):
            self.fetch(i, 0).start()

    def pack(self, p):
        nf, _, lp, ffs, _ = self.send.shape
        for i in range(len(self.masters)):
            self.fetch(i, p).wait()
            turned = self.stage[i].T.astype(BF)
            for j in range(nf):
                self.send[j, i, p] = turned[j * ffs : (j + 1) * ffs]
            if p + 1 < lp:
                self.fetch(i, p + 1).start()


def feed(p, gy_rows, b_rows, pair, wd, hid_out, grads, db, z):
    nf, _, _, _, width = grads.shape
    b = b_rows[p]
    gate = nt(pair[0, p], b)
    up = nt(pair[1, p], b)
    dhid = nt(wd, gy_rows[p])
    s = jax.nn.sigmoid(gate)
    silu = gate * s
    hid = (silu * up).astype(BF)
    dgate = (dhid * up * s * (1.0 + gate * (1.0 - s))).astype(BF)
    dup = (dhid * silu).astype(BF)
    hid_out[p] = hid
    db[...] = (tn(dgate, pair[0, p]) + tn(dup, pair[1, p])).astype(BF)
    z[...] = tn(hid, wd).astype(BF)
    for at, term in enumerate((dgate, dup)):
        grad = nn(term, b).astype(BF)
        for j in range(nf):
            grads[j, at, p] = grad[:, j * width : (j + 1) * width]


def ahead_kernel(
    nf, nz, npos, fr,
    x, gy, keep, gain1, gain2, qkv_w, out_w, gate_w, up_w, down_w,
    w_out, gy_out, grads_out, hid_out, a, qkv, ob, x1, db_rows, z_rows,
    own_w, w, gy_pos, b_pos, send, stage, down, gy_all, b_all, pair,
    db_sib, db_rx, z_sib, z_rx,
    sems_w, sems_gy, sems_b, sems_swap, sems_in, sems_out, sems_grads, sems_down,
    sems_db, sems_db_home, sems_z, sems_z_home,
):
    d = x.shape[1]
    each = own_w.shape[1]
    lp = npos // nz
    width = send.shape[4]
    f, z = place()
    packer = Packer((gate_w, up_w), stage, sems_in, send)
    packer.begin()
    greet(nf, nz, True)
    for i in range(3):
        own_w[i] = qkv_w[:, i * d : (i + 1) * d].astype(BF)
    own_w[3] = out_w[...].astype(BF)

    def span(at, size):
        return pl.ds(pl.multiple_of(at * size, size), size)

    weights = Gather(
        nf, nz,
        lambda zz, c: own_w.at[c],
        lambda ff, zz, c: w.at[c, span(ff * nz + zz, each)],
        lambda ff, c: w.at[c, span(ff, nz * each)],
        sems_w,
    )

    def rows_gather(mine, every, sems):
        return Gather(
            nf, nz,
            lambda zz, p: mine.at[span(zz * lp + p, fr)],
            lambda ff, zz, p: every.at[p, span(ff * nz + zz, fr)],
            lambda ff, p: every.at[p, span(ff, nz * fr)],
            sems,
        )

    for c in range(4):
        weights.begin(c)
    kept = (gy[...].astype(F32) * keep[...]).astype(BF)
    gy_pos[...] = nn(by_position(npos * fr, npos, fr), kept).astype(BF)
    grads = rows_gather(gy_pos, gy_all, sems_gy)
    rows = rows_gather(b_pos, b_all, sems_b)

    def pair_at(p):
        return lambda ff: pair.at[:, p, :, span(ff, width)]

    def send_at(p):
        return lambda ff: send.at[ff, :, p]

    swaps = [Swap(nf, send_at(p), pair_at(p), sems_swap.at[p]) for p in range(lp)]
    half = lp // 2
    for c in range(4):
        weights.along(c)
        if c >= 1:
            weights.relay(c - 1)
        if c >= 2:
            weights.rest(c - 2)
        if c < lp:
            packer.pack(c)
    for p in range(lp):
        grads.begin(p)
    for p in range(4, lp):
        packer.pack(p)
    weights.relay(3)
    weights.rest(2)
    for p in range(lp):
        grads.along(p)
    weights.rest(3)
    for p in range(half):
        swaps[p].start()
    for p in range(lp):
        grads.relay(p)
    for c in range(4):
        weights.whole(c)
    weights.finish()
    save_w = pltpu.make_async_copy(w, w_out, sems_out.at[0])
    save_w.start()
    attention_fwd(npos, fr, x, gain1, gain2, w, a, qkv, ob, x1, b_pos)
    for p in range(lp):
        rows.begin(p)
    for p in range(lp):
        grads.rest(p)
    for p in range(lp):
        rows.along(p)
        if p >= 1:
            rows.relay(p - 1)
    rows.relay(lp - 1)
    for p in range(half, lp):
        swaps[p].start()
    for p in range(lp):
        grads.whole(p)
    grads.finish()
    save_gy = pltpu.make_async_copy(gy_all, gy_out, sems_out.at[1])
    save_gy.start()

    count = b_all.shape[1]
    share = count // nf

    def term_at(first, p):
        per = d // count
        return w.at[first + p // per, pl.ds((p % per) * count, count)]

    def sums(first, sib, rx, sems, home_sems, land):
        def at(ff, p):
            return term_at(first, p).at[span(ff, share)]

        return RowSums(
            nf, nz, at, lambda p, m: at(flip(f, 2 * m), p), sib, rx, sems, home_sems, land, fr
        )

    s_db = sums(0, db_sib, db_rx, sems_db, sems_db_home, db_rows)
    s_z = sums(2, z_sib, z_rx, sems_z, sems_z_home, z_rows)

    def fetch(p):
        return pltpu.make_async_copy(down_w.at[p], down.at[p % 2], sems_down.at[p % 2])

    saves = []
    fetch(0).start()
    rows.rest(0)
    save_w.wait()
    for p in range(lp):
        if p + 1 < lp:
            fetch(p + 1).start()
            rows.rest(p + 1)
        fetch(p).wait()
        wd = down[p % 2].astype(BF)
        rows.whole(p)
        swaps[p].finish()
        feed(p, gy_all, b_all, pair, wd, hid_out, send, term_at(0, p), term_at(2, p))
        saves.append(
            pltpu.make_async_copy(send.at[:, :, p], grads_out.at[:, :, p], sems_grads.at[p])
        )
        saves[-1].start()
        s_db.pairs(p)
        if p >= 1:
            s_db.chips(p - 1)
        s_z.pairs(p)
        if p >= 2:
            s_db.across(p - 2)
        if p >= 3:
            s_db.home(p - 3)
            s_z.chips(p - 3)
    for step, last in ((s_db.chips, 1), (s_db.across, 2), (s_db.home, 3), (s_z.chips, 3)):
        for p in range(max(lp - last, 0), lp):
            step(p)
    for step in (s_z.across, s_z.home, s_db.landed, s_z.landed):
        for p in range(lp):
            step(p)
    rows.finish()
    save_gy.wait()
    for copy in saves:
        copy.wait()
    s_db.finish()
    s_z.finish()


def behind_kernel(
    nf, nz, npos, fr,
    grads, w_in, x, gy, keep, gain1, gain2, x1, a, qkv, ob, db_rows, z_rows,
    block_out, rows_grad, total, gains, pair_all,
    t_sib, t_rx, t_sems, t_home, g_sib, g_rx, g_sems, g_home, t_land, g_land, sems_swap, sem_w,
    w, terms, tail, dx1, dxb, do, dqkv,
):
    d = x.shape[1]
    each = gains.shape[0]
    lp = npos // nz
    f, z = place()
    load_w = pltpu.make_async_copy(w_in, w, sem_w)
    load_w.start()
    greet(nf, nz, True)

    def part(ref, p):
        return lambda ff: ref.at[ff, :, p]

    swaps = [Swap(nf, part(grads, p), part(pair_all, p), sems_swap.at[p]) for p in range(lp)]
    for swap in swaps:
        swap.start()

    def span(ff):
        return pl.ds(pl.multiple_of(ff * nz * each, nz * each), nz * each)

    s_t = BlockSums(
        nf, nz,
        lambda ff, c: terms.at[c, span(ff)],
        lambda c, m: terms.at[c, span(flip(f, 2 * m))],
        t_sib, t_rx, t_sems, t_home, t_land, each,
    )
    s_g = BlockSums(
        nf, nz,
        lambda ff, c: tail.at[span(ff)],
        lambda c, m: tail.at[span(flip(f, 2 * m))],
        g_sib, g_rx, g_sems, g_home, g_land, each,
    )
    gain2_grad = attention_bwd_in(npos, fr, db_rows, gy, keep, x1, ob, gain2, dx1, dxb, terms)
    s_t.pairs(3)
    load_w.wait()
    do[...] = nt(dxb[...], w[3]).astype(BF)
    s_t.chips(3)
    attention_bwd_heads(npos, qkv, do, dqkv)
    s_t.across(3)
    weight_terms(a, dqkv, 0, terms.at[0])
    s_t.pairs(0)
    weight_terms(a, dqkv, d, terms.at[1])
    s_t.pairs(1)
    s_t.chips(0)
    weight_terms(a, dqkv, 2 * d, terms.at[2])
    s_t.pairs(2)
    s_t.chips(1)
    gain1_grad = attention_bwd_rows(x, dqkv, w, gain1, dx1, rows_grad)
    gains_into(gain1_grad, gain2_grad, tail)
    s_g.pairs(0)
    s_t.chips(2)
    s_g.chips(0)
    s_t.home(3)
    back = nn(by_position(npos * fr, npos, fr, True), z_rows[...])
    block_out[...] = (keep[...] * (x1[...] + back)).astype(BF)
    s_t.across(0)
    s_t.across(1)
    s_g.across(0)
    s_t.home(0)
    s_t.across(2)
    s_g.home(0)
    s_t.home(1)
    s_t.home(2)
    for c in (3, 0, 1, 2):
        s_t.landed(c, total.at[:, pl.ds(c * d, d)])
    s_g.landed(0, gains)
    s_t.finish()
    s_g.finish()
    for swap in swaps:
        swap.finish()


def last_local_kernel(pair, hid, gy, total, gate, up, down, qkv_grad, out_grad):
    nf, _, _, ffs, width = pair.shape
    d = gy.shape[2]

    @pl.when(pl.program_id(0) == 0)
    def _():
        qkv_grad[...] = total[:, : 3 * d]
        out_grad[...] = total[:, 3 * d :]

    for at, out in enumerate((gate, up)):
        out[0] = pair[:, at, 0].astype(F32).reshape(nf * ffs, width).T
    down[0] = nn(hid[0], gy[0])


def rms_norm(values, gain_vector):
    return (
        values * lax.rsqrt(jnp.mean(values * values, axis=-1, keepdims=True) + 1e-05) * gain_vector
    )


def attend(qkv_rows):
    frame_count = qkv_rows.shape[0]
    positions = qkv_rows.shape[1]
    split_rows = qkv_rows.reshape(frame_count, positions, 3, H, HD)
    queries = split_rows[:, :, 0]
    keys_all = split_rows[:, :, 1]
    values_all = split_rows[:, :, 2]
    scores = jnp.einsum("fqhe,fkhe->fhqk", queries, keys_all, preferred_element_type=F32) * (
        1.0 / math.sqrt(HD)
    )
    causal = jnp.arange(positions)[:, None] >= jnp.arange(positions)[None, :]
    scores = jnp.where(causal, scores, -1e30)
    weights = jax.nn.softmax(scores, axis=-1)
    mixed = jnp.einsum("fhqk,fkhe->fqhe", weights, values_all, preferred_element_type=F32)
    return mixed.reshape(frame_count, positions, H * HD)


def local_general(
    frame_rows,
    frame_mask,
    gain_attention,
    gain_feed,
    qkv_master,
    out_master,
    gate_master,
    up_master,
    down_master,
    out_cotangent,
):
    nf = lax.axis_size("frames")
    nz = lax.axis_size("pos")
    lp, dslice, ff = gate_master.shape
    ffs = down_master.shape[1]
    fr, npos, d = frame_rows.shape

    keep_rows = frame_mask.astype(F32)[:, None, None]
    inputs = frame_rows.astype(F32)

    def turned(w):
        return w.astype(BF).reshape(lp, dslice, nf, ffs).transpose(2, 0, 3, 1)

    def untwist(w):
        return w.transpose(1, 2, 0, 3).reshape(lp, ffs, d)

    def to_pos(rows):
        return rows.transpose(1, 0, 2).reshape(nz, lp * fr, d)

    def gathered(every):
        every = every.reshape(nf, nz, lp, fr, d)
        return every.transpose(2, 0, 1, 3, 4).reshape(lp, nf * nz * fr, d)

    rows_shape = jax.ShapeDtypeStruct((nf, nz, lp * fr, d), BF)
    back_shape = jax.ShapeDtypeStruct((npos * fr, d), BF)
    gather_sems = pltpu.SemaphoreType.DMA(Gather.sem_shape(nf, nz))
    swap_sems = pltpu.SemaphoreType.DMA(Swap.sem_shape(nf))

    def scattered(rows, ident):
        back = call(
            functools.partial(back_kernel, nf, nz, fr),
            ident,
            out_shape=back_shape,
            in_specs=[VM],
            out_specs=VM,
            scratch_shapes=HomeSums.scratch(nf, nz, lp, nz * fr, d),
        )(rows.reshape(lp, nf, nz * fr, d))
        return back.reshape(npos, fr, d).transpose(1, 0, 2)

    both = jnp.concatenate((qkv_master.astype(BF), out_master.astype(BF)), axis=1)
    pair = jnp.stack((turned(gate_master), turned(up_master)), axis=1)
    upstream = keep_rows * out_cotangent.astype(F32)
    own_rows = both.shape[0]
    w_all, gy_all, pair = call(
        functools.partial(first_kernel, nf, nz),
        0,
        out_shape=(
            jax.ShapeDtypeStruct((nf, nz) + both.shape, BF),
            rows_shape,
            jax.ShapeDtypeStruct(pair.shape, BF),
        ),
        in_specs=[ANY] * 3,
        out_specs=(ANY,) * 3,
        scratch_shapes=[gather_sems, gather_sems, swap_sems],
    )(both, to_pos(upstream.astype(BF)), pair)
    w_all = w_all.reshape(d, both.shape[1])
    w_qkv = w_all[:, : 3 * d]
    w_out = w_all[:, 3 * d :]
    gate_t = untwist(pair[:, 0])
    up_t = untwist(pair[:, 1])
    down = down_master.astype(BF)
    gy = gathered(gy_all)

    normed_one, norm_one_pull = jax.vjp(rms_norm, inputs, gain_attention)
    normed_low = normed_one.astype(BF)
    qkv_rows = jnp.einsum("fpd,de->fpe", normed_low, w_qkv, preferred_element_type=F32)
    mixed, attend_pull = jax.vjp(attend, qkv_rows)
    mixed_low = mixed.astype(BF)
    branch = jnp.einsum("fpd,de->fpe", mixed_low, w_out, preferred_element_type=F32)
    middle = inputs + branch
    normed_two, norm_two_pull = jax.vjp(rms_norm, middle, gain_feed)
    b_all = call(
        functools.partial(rows_kernel, nf, nz),
        1,
        out_shape=rows_shape,
        in_specs=[ANY],
        out_specs=ANY,
        scratch_shapes=[gather_sems],
    )(to_pos(normed_two.astype(BF)))
    b = gathered(b_all)

    gate_rows = jnp.einsum("prd,phd->phr", b, gate_t, preferred_element_type=F32)
    up_rows = jnp.einsum("prd,phd->phr", b, up_t, preferred_element_type=F32)
    hidden_grad = jnp.einsum("prd,phd->phr", gy, down, preferred_element_type=F32)
    sigma = jax.nn.sigmoid(gate_rows)
    silu_gate = gate_rows * sigma
    hidden = (silu_gate * up_rows).astype(BF)
    gate_back = (hidden_grad * up_rows * sigma * (1.0 + gate_rows * (1.0 - sigma))).astype(BF)
    up_back = (hidden_grad * silu_gate).astype(BF)
    db = jnp.einsum("phr,phd->prd", gate_back, gate_t, preferred_element_type=F32) + jnp.einsum(
        "phr,phd->prd", up_back, up_t, preferred_element_type=F32
    )
    back_rows = scattered(db.astype(BF), 2).astype(F32)
    feed = jnp.einsum("phr,phd->prd", hidden, down, preferred_element_type=F32)
    returned = scattered(feed.astype(BF), 3).astype(F32)
    block_out = (keep_rows * (middle + returned)).astype(BF)
    gate_grad = jnp.einsum("phr,prd->phd", gate_back, b, preferred_element_type=F32).astype(BF)
    up_grad = jnp.einsum("phr,prd->phd", up_back, b, preferred_element_type=F32).astype(BF)
    down_grad = jnp.einsum("phr,prd->phd", hidden, gy, preferred_element_type=F32)

    grads = jnp.stack((gate_grad, up_grad), axis=0).reshape(2, lp, ffs, nf, dslice)
    grads = grads.transpose(3, 0, 1, 2, 4)

    pulled_two = norm_two_pull(back_rows)
    middle_grad = upstream + pulled_two[0]
    branch_grad = middle_grad.astype(BF)
    out_weight_grad = jnp.einsum("fpd,fpe->de", mixed_low, branch_grad, preferred_element_type=F32)
    mixed_grad = jnp.einsum("fpe,de->fpd", branch_grad, w_out, preferred_element_type=F32)
    qkv_back = attend_pull(mixed_grad)[0].astype(BF)
    qkv_weight_grad = jnp.einsum("fpd,fpe->de", normed_low, qkv_back, preferred_element_type=F32)
    normed_grad = jnp.einsum("fpe,de->fpd", qkv_back, w_qkv, preferred_element_type=F32)
    pulled_one = norm_one_pull(normed_grad)
    rows_grad = middle_grad + pulled_one[0]

    gains = jnp.stack((pulled_one[1], pulled_two[1]), axis=1)
    gains_hi = gains.astype(BF)
    gains_lo = (gains - gains_hi.astype(F32)).astype(BF)
    unit = max(128, 2048 // own_rows)
    spare = -(4 * d + 4) % unit
    tail = jnp.concatenate((gains_hi, gains_lo, jnp.zeros((d, spare), BF)), axis=1)
    total = jnp.concatenate(
        (qkv_weight_grad.astype(BF), out_weight_grad.astype(BF), tail), axis=1
    )
    block = own_rows * total.shape[1] // 128
    total, grads = call(
        functools.partial(last_kernel, nf, nz),
        4,
        out_shape=(
            jax.ShapeDtypeStruct((block, 128), F32),
            jax.ShapeDtypeStruct(grads.shape, BF),
        ),
        in_specs=[VM, ANY],
        out_specs=(VM, ANY),
        scratch_shapes=HomeSums.scratch(nf, nz, 1, nz * block, 128)
        + [pltpu.VMEM((1, nz - 1, block, 128), BF), swap_sems],
    )(total.reshape(1, nf, nz * block, 128), grads)
    grads = grads.transpose(1, 2, 4, 0, 3).reshape(2, lp, dslice, ff).astype(F32)
    total = total.reshape(own_rows, 4 * d + 4 + spare)
    gain_grads = total[:, 4 * d : 4 * d + 2] + total[:, 4 * d + 2 : 4 * d + 4]
    return (
        block_out,
        rows_grad,
        gain_grads[:, 0],
        gain_grads[:, 1],
        total[:, : 3 * d],
        total[:, 3 * d : 4 * d],
        grads[0],
        grads[1],
        down_grad,
    )
def local_fused(
    frame_rows,
    frame_mask,
    gain_attention,
    gain_feed,
    qkv_master,
    out_master,
    gate_master,
    up_master,
    down_master,
    out_cotangent,
):
    nf = lax.axis_size("frames")
    nz = lax.axis_size("pos")
    lp, dslice, ff = gate_master.shape
    ffs = down_master.shape[1]
    fr, npos, d = frame_rows.shape
    rows = fr * npos
    each = qkv_master.shape[0]
    count = nf * nz * fr

    def make(shape, kind=BF):
        return jax.ShapeDtypeStruct(shape, kind)

    def vmem(shape, kind=BF):
        return pltpu.VMEM(shape, kind)

    def dma(*shape):
        return pltpu.SemaphoreType.DMA(shape)

    x = frame_rows.reshape(rows, d)
    gy = out_cotangent.reshape(rows, d)
    keep = jnp.broadcast_to(frame_mask.astype(F32)[:, None], (fr, npos)).reshape(rows, 1)
    gain1 = gain_attention.reshape(1, d)
    gain2 = gain_feed.reshape(1, d)
    gather_sems = dma(*Gather.sem_shape(nf, nz, 4))
    rows_sems = dma(*Gather.sem_shape(nf, nz, lp))
    swap_sems = dma(lp, *Swap.sem_shape(nf))
    pair_shape = (nf, 2, lp, ffs, dslice)
    row_scratch = HomeSums.scratch(nf, nz, lp, nz * fr, d)
    w_all, gy_all, grads, hid, a, qkv, ob, x1, db_rows, z_rows = call(
        functools.partial(ahead_kernel, nf, nz, npos, fr),
        0,
        out_shape=(
            make((4, d, d)),
            make((lp, count, d)),
            make(pair_shape),
            make((lp, ffs, count)),
            make((rows, d)),
            make((rows, 3 * d)),
            make((rows, d)),
            make((rows, d), F32),
            make((rows, d)),
            make((rows, d)),
        ),
        in_specs=[VM] * 7 + [ANY] * 3,
        out_specs=(ANY,) * 3 + (VM,) * 7,
        scratch_shapes=[
            vmem((4, each, d)),
            vmem((4, d, d)),
            vmem((rows, d)),
            vmem((rows, d)),
            vmem(pair_shape),
            vmem((2, dslice, ff), F32),
            vmem((2, ffs, d), F32),
            vmem((lp, count, d)),
            vmem((lp, count, d)),
            vmem((2, lp, ffs, d)),
            *row_scratch[:2],
            *row_scratch[:2],
            gather_sems,
            rows_sems,
            rows_sems,
            swap_sems,
            dma(2),
            dma(2),
            dma(lp),
            dma(2),
            *row_scratch[2:],
            *row_scratch[2:],
        ],
    )(x, gy, keep, gain1, gain2, qkv_master, out_master, gate_master, up_master, down_master)
    block_out, rows_grad, total, gains, back = call(
        functools.partial(behind_kernel, nf, nz, npos, fr),
        1,
        out_shape=(
            make((rows, d)),
            make((rows, d), F32),
            make((each, 4 * d), F32),
            make((each, 128), F32),
            make(pair_shape),
        ),
        in_specs=[ANY] * 2 + [VM] * 11,
        out_specs=(VM,) * 4 + (ANY,),
        scratch_shapes=[
            *HomeSums.scratch(nf, nz, 4, nz * each, d),
            *HomeSums.scratch(nf, nz, 1, nz * each, 128),
            vmem((4, nz - 1, each, d)),
            vmem((1, nz - 1, each, 128)),
            swap_sems,
            pltpu.SemaphoreType.DMA,
            vmem((4, d, d)),
            vmem((4, d, d)),
            vmem((d, 128)),
            vmem((rows, d), F32),
            vmem((rows, d)),
            vmem((rows, d)),
            vmem((rows, 3 * d)),
        ],
    )(grads, w_all, x, gy, keep, gain1, gain2, x1, a, qkv, ob, db_rows, z_rows)
    whole_block = pl.BlockSpec((1, dslice, ff), lambda p: (p, 0, 0))

    def once(*shape):
        return pl.BlockSpec(shape, lambda p: (0, 0))

    gate_grad, up_grad, down_grad, qkv_grad, out_grad = pl.pallas_call(
        last_local_kernel,
        grid=(lp,),
        out_shape=(
            make((lp, dslice, ff), F32),
            make((lp, dslice, ff), F32),
            make((lp, ffs, d), F32),
            make((each, 3 * d), F32),
            make((each, d), F32),
        ),
        in_specs=[
            pl.BlockSpec((nf, 2, 1, ffs, dslice), lambda p: (0, 0, p, 0, 0)),
            pl.BlockSpec((1, ffs, count), lambda p: (p, 0, 0)),
            pl.BlockSpec((1, count, d), lambda p: (p, 0, 0)),
            once(each, 4 * d),
        ],
        out_specs=(
            whole_block,
            whole_block,
            pl.BlockSpec((1, ffs, d), lambda p: (p, 0, 0)),
            once(each, 3 * d),
            once(each, d),
        ),
        compiler_params=pltpu.CompilerParams(vmem_limit_bytes=60 * 2**20),
    )(back, hid, gy_all, total)
    gains = gains[:, :2] + gains[:, 2:4]
    return (
        block_out.reshape(fr, npos, d),
        rows_grad.reshape(fr, npos, d),
        gains[:, 0],
        gains[:, 1],
        qkv_grad,
        out_grad,
        gate_grad,
        up_grad,
        down_grad,
    )


def local(*args):
    _, dslice, _ = args[6].shape
    if lax.axis_size("frames") == 8 and dslice % 128 == 0:
        return local_fused(*args)
    return local_general(*args)


def solution(mesh):
    in_specs = (
        P(("frames", "pos"), None, None),
        P(("frames", "pos")),
        P(),
        P(),
        P(("frames", "pos"), None),
        P(("frames", "pos"), None),
        P("pos", "frames", None),
        P("pos", "frames", None),
        P("pos", "frames", None),
        P(("frames", "pos"), None, None),
    )
    out_specs = (
        P(("frames", "pos"), None, None),
        P(("frames", "pos"), None, None),
        P(("frames", "pos")),
        P(("frames", "pos")),
        P(("frames", "pos"), None),
        P(("frames", "pos"), None),
        P("pos", "frames", None),
        P("pos", "frames", None),
        P("pos", "frames", None),
    )
    return jax.shard_map(local, mesh=mesh, in_specs=in_specs, out_specs=out_specs, check_vma=False)
```

```python
import functools
import math

import jax
import jax.numpy as jnp
from jax import lax
from jax.experimental import pallas as pl
from jax.experimental.pallas import tpu as pltpu
from jax.sharding import PartitionSpec as P

H = 16
HD = 64
BF = jnp.bfloat16
F32 = jnp.float32
MESH = pl.DeviceIdType.MESH
FILL = (10, 6)
PUMP = (14, 4, 3, 3)
LATE = (2, 3)
EARLY = tuple(c for c in range(4) if c not in LATE)
LATE_W = (2, 3)
EARLY_W = tuple(c for c in range(4) if c not in LATE_W)
ANY = pl.BlockSpec(memory_space=pl.ANY)
VM = pl.BlockSpec(memory_space=pltpu.VMEM)


def place():
    return lax.axis_index("frames"), lax.axis_index("pos")


def flip(index, mask):
    bit = 1
    while bit <= mask:
        if mask & bit:
            index = index + bit * (1 - 2 * ((index // bit) % 2))
        bit *= 2
    return index


def greet(nf, nz, every_frame):
    f, z = place()
    hops = [1] + [2 * m for m in range(1, nf // 2)]
    if every_frame:
        hops = list(range(1, nf))
    others = [(flip(f, h), z) for h in hops] + [(f, flip(z, k)) for k in range(1, nz)]
    barrier = pltpu.get_barrier_semaphore()
    for other in others:
        pl.semaphore_signal(barrier, inc=1, device_id=other, device_id_type=MESH)
    pl.semaphore_wait(barrier, len(others))


def remote(src, dst, send, recv, to):
    copy = pltpu.make_async_remote_copy(
        src_ref=src, dst_ref=dst, send_sem=send, recv_sem=recv, device_id=to, device_id_type=MESH
    )
    copy.start()
    return copy


def arrival(dst, send, recv):
    f, z = place()
    pltpu.make_async_remote_copy(
        src_ref=dst,
        dst_ref=dst,
        send_sem=send,
        recv_sem=recv,
        device_id=(flip(f, 1), z),
        device_id_type=MESH,
    ).wait_recv()


def relay_of(k):
    return 1 if k % 2 == 0 else 2


class Gather:
    def __init__(self, nf, nz, src_for, out_at, group_at, sems):
        self.nf, self.nz, self.nc = nf, nz, nf // 2
        self.f, self.z = place()
        self.src_for, self.out_at, self.group_at, self.sems = src_for, out_at, group_at, sems
        self.sent = []
        self.own = {}
        self.tree = self.nc == 4

    @staticmethod
    def sem_shape(nf, nz, parts=1):
        return (2, nz + nf, parts)

    def push(self, src, dst, hop, c, to):
        self.sent.append(remote(src, dst, self.sems.at[0, hop, c], self.sems.at[1, hop, c], to))

    def arrive(self, dst, hop, c):
        arrival(dst, self.sems.at[0, hop, c], self.sems.at[1, hop, c])

    def near(self, m, c):
        return self.group_at(flip(self.f, 2 * m), c)

    def begin(self, c=0):
        f, z = self.f, self.z
        for k in range(self.nz - 1, 0, -1):
            self.push(self.src_for(flip(z, k), c), self.out_at(f, z, c), k, c, (f, flip(z, k)))
        src, dst = self.src_for(z, c), self.out_at(f, z, c)
        self.own[c] = pltpu.make_async_copy(src, dst, self.sems.at[0, 0, c])
        self.own[c].start()

    def along(self, c=0):
        f, z = self.f, self.z
        self.own[c].wait()
        for k in range(1, self.nz):
            self.arrive(self.out_at(f, flip(z, k), c), k, c)
        group = self.near(0, c)
        for m in range(1, self.nc):
            if not (self.tree and m == 3):
                self.push(group, group, self.nz + m, c, (flip(f, 2 * m), z))
        self.push(group, group, self.nz + self.nc, c, (flip(f, 1), z))

    def over(self, m, c):
        f, z = self.f, self.z
        group = self.near(m, c)
        self.arrive(group, self.nz + m, c)
        if self.tree and m == relay_of(c):
            self.push(group, group, self.nz + 3, c, (flip(f, 2 * (3 - m)), z))
        self.push(group, group, self.nz + self.nc + m, c, (flip(f, 1), z))

    def relay(self, c=0):
        if self.tree:
            self.over(relay_of(c), c)

    def rest(self, c=0):
        for m in range(1, self.nc):
            if not (self.tree and m == relay_of(c)):
                self.over(m, c)

    def whole(self, c=0):
        for m in range(self.nc):
            group = self.group_at(flip(self.f, 2 * m + 1), c)
            self.arrive(group, self.nz + self.nc + m, c)

    def finish(self):
        for copy in self.sent:
            copy.wait_send()


class LateGather(Gather):
    def __init__(self, nf, nz, src_for, out_at, group_at, sems, late_sems):
        super().__init__(nf, nz, src_for, out_at, group_at, sems)
        self.late_sems = late_sems

    @staticmethod
    def late_shape(nf, nz, parts):
        return (2, nz * (nf // 2), parts)

    def block(self, m, k, c):
        return self.out_at(flip(self.f, 2 * m), flip(self.z, k), c)

    def begin(self, c=0):
        f, z = self.f, self.z
        src, dst = self.src_for(z, c), self.out_at(f, z, c)
        for m in range(1, self.nc):
            if not (self.tree and m == 3):
                self.push(src, dst, self.nz + m, c, (flip(f, 2 * m), z))
        self.own[c] = pltpu.make_async_copy(src, dst, self.sems.at[0, 0, c])
        self.own[c].start()

    def relay(self, c=0):
        if self.tree:
            m = relay_of(c)
            block = self.block(m, 0, c)
            self.arrive(block, self.nz + m, c)
            to = (flip(self.f, 2 * (3 - m)), self.z)
            self.push(block, block, self.nz + 3, c, to)

    def along(self, c=0):
        self.own[c].wait()
        for m in range(1, self.nc):
            if not (self.tree and m == relay_of(c)):
                self.arrive(self.block(m, 0, c), self.nz + m, c)
        for k in range(self.nz - 1, 0, -1):
            for m in range(self.nc):
                block, hop = self.block(m, 0, c), k * self.nc + m
                send, recv = self.late_sems.at[0, hop, c], self.late_sems.at[1, hop, c]
                self.sent.append(remote(block, block, send, recv, (self.f, flip(self.z, k))))

    def rest(self, c=0):
        for m in range(self.nc):
            for k in range(1, self.nz):
                hop = k * self.nc + m
                send, recv = self.late_sems.at[0, hop, c], self.late_sems.at[1, hop, c]
                arrival(self.block(m, k, c), send, recv)
            group = self.near(m, c)
            self.push(group, group, self.nz + self.nc + m, c, (flip(self.f, 1), self.z))


class Swap:
    def __init__(self, nf, src_at, out_at, sems):
        self.nf, self.src_at, self.out_at, self.sems = nf, src_at, out_at, sems
        self.f, self.z = place()
        self.sent = []
        self.own = None

    @staticmethod
    def sem_shape(nf):
        return (2, nf)

    def start(self, masks=None):
        f, z = self.f, self.z
        if self.own is None:
            self.own = pltpu.make_async_copy(self.src_at(f), self.out_at(f), self.sems.at[0, 0])
            self.own.start()
        for m in masks or range(self.nf - 1, 0, -1):
            self.sent.append(
                remote(
                    self.src_at(flip(f, m)),
                    self.out_at(f),
                    self.sems.at[0, m],
                    self.sems.at[1, m],
                    (flip(f, m), z),
                )
            )

    def finish(self):
        self.own.wait()
        for copy in self.sent:
            copy.wait()


class Sums:
    def __init__(self, nf, nz, src_at, own_at, sib, rx, sems):
        self.nf, self.nz, self.nc = nf, nz, nf // 2
        self.f, self.z = place()
        self.src_at, self.own_at, self.sib, self.rx = src_at, own_at, sib, rx
        self.sems = sems
        self.sent = []
        self.tree = self.nc == 4

    @staticmethod
    def buffers(nf, parts, rows, columns):
        nc = nf // 2
        return [
            pltpu.VMEM((parts, nc, rows, columns), BF),
            pltpu.VMEM((parts, nc - 1, rows, columns), BF),
            pltpu.SemaphoreType.DMA((2, 2 * nc, parts)),
        ]

    def push(self, src, dst, sems, hop, k, to):
        self.sent.append(remote(src, dst, sems.at[0, hop, k], sems.at[1, hop, k], to))

    def arrive(self, dst, sems, hop, k):
        arrival(dst, sems.at[0, hop, k], sems.at[1, hop, k])

    def first(self, k):
        if self.tree:
            return [3, relay_of(k)]
        return list(range(self.nc - 1, 0, -1))

    def pairs(self, k):
        f, z = self.f, self.z
        order = self.first(k)
        for m in order + [m for m in range(self.nc - 1, -1, -1) if m not in order]:
            src = self.src_at(flip(f, 2 * m + 1), k)
            self.push(src, self.sib.at[k, m], self.sems, self.nc + m, k, (flip(f, 1), z))

    def chips(self, k):
        f, z = self.f, self.z
        for m in self.first(k):
            sib = self.sib.at[k, m]
            self.arrive(sib, self.sems, self.nc + m, k)
            add_into(sib, self.own_at(k, m), sib)
            hop, to = m, m
            if self.tree:
                hop, to = (2 if m == 3 else 1), relay_of(k)
            self.push(sib, self.rx.at[k, hop - 1], self.sems, hop, k, (flip(f, 2 * to), z))

    def across(self, k):
        if not self.tree:
            return
        m = 3 - relay_of(k)
        sib = self.sib.at[k, m]
        self.arrive(sib, self.sems, self.nc + m, k)
        self.arrive(self.rx.at[k, 1], self.sems, 2, k)
        add_into(sib, self.own_at(k, m), sib, self.rx.at[k, 1])
        self.push(sib, self.rx.at[k, 2], self.sems, 3, k, (flip(self.f, 2 * m), self.z))

    def total(self, k, out):
        self.arrive(self.sib.at[k, 0], self.sems, self.nc, k)
        terms = [self.own_at(k, 0), self.sib.at[k, 0]]
        for m in range(1, self.nc):
            if self.tree and m == 2:
                continue
            self.arrive(self.rx.at[k, m - 1], self.sems, m, k)
            terms.append(self.rx.at[k, m - 1])
        add_into(out, *terms)

    def finish(self):
        for copy in self.sent:
            copy.wait_send()


class HomeSums(Sums):
    def __init__(self, nf, nz, src_at, own_at, sib, rx, sems, home_sems, land, each):
        super().__init__(nf, nz, src_at, own_at, sib, rx, sems)
        self.home_sems, self.land, self.each = home_sems, land, each

    @staticmethod
    def scratch(nf, nz, parts, rows, columns):
        sib, rx, sems = Sums.buffers(nf, parts, rows, columns)
        return [sib, rx, sems, pltpu.SemaphoreType.DMA((2, nz, parts))]

    def rows_of(self, ref, at):
        return ref.at[pl.ds(pl.multiple_of(at * self.each, self.each), self.each)]

    def home(self, p):
        whole = self.sib.at[p, 0]
        self.total(p, whole)
        for k in range(self.nz - 1, 0, -1):
            src = self.rows_of(whole, flip(self.z, k))
            self.push(src, self.sent_to(k, p), self.home_sems, k, p, (self.f, flip(self.z, k)))


class RowSums(HomeSums):
    def at(self, zz, p):
        return self.rows_of(self.land, zz * self.sib.shape[0] + p)

    def sent_to(self, k, p):
        return self.at(self.z, p)

    def landed(self, p):
        self.at(self.z, p)[...] = self.rows_of(self.sib.at[p, 0], self.z)[...]
        for k in range(1, self.nz):
            self.arrive(self.at(flip(self.z, k), p), self.home_sems, k, p)


class BlockSums(HomeSums):
    def sent_to(self, k, p):
        return self.land.at[p, k - 1]

    def landed(self, p, out):
        terms = [self.rows_of(self.sib.at[p, 0], self.z)]
        for k in range(1, self.nz):
            self.arrive(self.land.at[p, k - 1], self.home_sems, k, p)
            terms.append(self.land.at[p, k - 1])
        add_into(out, *terms)


class PosSums(Sums):
    def __init__(self, nf, nz, src_at, own_at, sib, rx, sems, late_sems, zl, each):
        super().__init__(nf, nz, src_at, own_at, sib, rx, sems)
        self.late_sems, self.zl, self.each = late_sems, zl, each

    @staticmethod
    def scratch(nf, nz, parts, each, columns):
        nc = nf // 2
        return [
            pltpu.VMEM((parts, nc, nz * each, columns), BF),
            pltpu.VMEM((parts, nc - 1, each, columns), BF),
            pltpu.SemaphoreType.DMA((2, 2 * nc, parts)),
            pltpu.SemaphoreType.DMA((2, nz * nc, parts)),
            pltpu.VMEM((parts, nc, nz - 1, each, columns), BF),
        ]

    def rows_of(self, ref, at):
        return ref.at[pl.ds(pl.multiple_of(at * self.each, self.each), self.each)]

    def order(self, c):
        first = self.first(c)
        return first + [m for m in range(self.nc - 1, -1, -1) if m not in first]

    def along(self, c):
        for m in self.order(c):
            sib = self.sib.at[c, m]
            self.arrive(sib, self.sems, self.nc + m, c)
            add_into(sib, self.own_at(c, m), sib)
            for k in range(self.nz - 1, 0, -1):
                src = self.rows_of(sib, flip(self.z, k))
                to = (self.f, flip(self.z, k))
                self.push(src, self.zl.at[c, m, k - 1], self.late_sems, k * self.nc + m, c, to)

    def mine(self, m, c):
        terms = [self.rows_of(self.sib.at[c, m], self.z)]
        for k in range(1, self.nz):
            land = self.zl.at[c, m, k - 1]
            self.arrive(land, self.late_sems, k * self.nc + m, c)
            terms.append(land)
        return terms

    def chips(self, c):
        for m in self.first(c):
            terms = self.mine(m, c)
            add_into(terms[0], *terms)
            hop, to = m, m
            if self.tree:
                hop, to = (2 if m == 3 else 1), relay_of(c)
            chip = (flip(self.f, 2 * to), self.z)
            self.push(terms[0], self.rx.at[c, hop - 1], self.sems, hop, c, chip)

    def across(self, c):
        if not self.tree:
            return
        m = 3 - relay_of(c)
        terms = self.mine(m, c)
        self.arrive(self.rx.at[c, 1], self.sems, 2, c)
        add_into(terms[0], *terms, self.rx.at[c, 1])
        self.push(terms[0], self.rx.at[c, 2], self.sems, 3, c, (flip(self.f, 2 * m), self.z))

    def landed(self, c, out):
        terms = self.mine(0, c)
        for m in range(1, self.nc):
            if self.tree and m == 2:
                continue
            self.arrive(self.rx.at[c, m - 1], self.sems, m, c)
            terms.append(self.rx.at[c, m - 1])
        add_into(out, *terms)


def add_into(out, *terms):
    rows = out.shape[0]
    step = 16 if rows % 16 == 0 else rows

    def body(i, carry):
        at = pl.ds(pl.multiple_of(i * step, step), step)
        total = terms[0][at, :].astype(F32)
        for term in terms[1:]:
            total = total + term[at, :].astype(F32)
        out[at, :] = total.astype(out.dtype)
        return carry

    lax.fori_loop(0, rows // step, body, 0)


def call(kernel, ident, **kw):
    return pl.pallas_call(
        kernel,
        compiler_params=pltpu.CompilerParams(
            collective_id=ident, has_side_effects=True, vmem_limit_bytes=60 * 2**20
        ),
        **kw,
    )


def by_block(nf, nz, src_for, out, sems):
    return Gather(
        nf, nz, src_for, lambda ff, zz, c: out.at[ff, zz], lambda ff, c: out.at[ff], sems
    )


def first_kernel(nf, nz, attn, gy, pair, attn_all, gy_all, pair_all, s1, s2, s3):
    greet(nf, nz, True)
    weights = by_block(nf, nz, lambda zz, c: attn, attn_all, s1)
    rows = by_block(nf, nz, lambda zz, c: gy.at[zz], gy_all, s2)
    swap = Swap(nf, lambda ff: pair.at[ff], lambda ff: pair_all.at[ff], s3)
    gathers = (weights, rows)
    for g in gathers:
        g.begin()
    for step in ("along", "relay", "rest", "whole", "finish"):
        for g in gathers:
            getattr(g, step)()
        if step == "relay":
            swap.start()
    swap.finish()


def rows_kernel(nf, nz, b, b_all, s1):
    greet(nf, nz, False)
    rows = by_block(nf, nz, lambda zz, c: b.at[zz], b_all, s1)
    for step in (rows.begin, rows.along, rows.relay, rows.rest, rows.whole, rows.finish):
        step()


def chip_terms(terms):
    f, _ = place()
    return lambda ff, p: terms.at[p, ff], lambda p, m: terms.at[p, flip(f, 2 * m)]


def back_kernel(nf, nz, each, terms, out, sib, rx, sems, home_sems):
    greet(nf, nz, False)
    s = RowSums(nf, nz, *chip_terms(terms), sib, rx, sems, home_sems, out, each)
    for step in (s.pairs, s.chips, s.across, s.home, s.landed):
        for p in range(terms.shape[0]):
            step(p)
    s.finish()


def last_kernel(nf, nz, terms, pair, out, pair_all, sib, rx, sems, home_sems, land, s2):
    greet(nf, nz, True)
    s = BlockSums(nf, nz, *chip_terms(terms), sib, rx, sems, home_sems, land, out.shape[0])
    swap = Swap(nf, lambda ff: pair.at[ff], lambda ff: pair_all.at[ff], s2)
    s.pairs(0)
    swap.start()
    for step in (s.chips, s.across, s.home):
        step(0)
    s.landed(0, out)
    s.finish()
    swap.finish()


def contract(a, b, at_a, at_b):
    return lax.dot_general(a, b, (((at_a,), (at_b,)), ((), ())), preferred_element_type=F32)


def nt(a, b):
    return contract(a, b, 1, 1)


def nn(a, b):
    return contract(a, b, 1, 0)


def tn(a, b):
    return contract(a, b, 0, 0)


def by_position(rows, npos, fr, back=False):
    i = lax.broadcasted_iota(jnp.int32, (rows, rows), 0)
    j = lax.broadcasted_iota(jnp.int32, (rows, rows), 1)
    if back:
        i, j = j, i
    return ((i % fr) * npos + i // fr == j).astype(F32).astype(BF)


def causal(rows, npos):
    i = lax.broadcasted_iota(jnp.int32, (rows, rows), 0)
    j = lax.broadcasted_iota(jnp.int32, (rows, rows), 1)
    return jnp.logical_and(i // npos == j // npos, j <= i)


def soft(q, k, mask):
    s = jnp.where(mask, nt(q, k) * (1.0 / math.sqrt(HD)), -1e30)
    e = jnp.exp(s - jnp.max(s, axis=1, keepdims=True))
    return e / jnp.sum(e, axis=1, keepdims=True)

GROUP=128

def attention_start(x, gain1, a_out):
    xf = x[...].astype(F32)
    rinv1 = lax.rsqrt(jnp.mean(xf * xf, axis=1, keepdims=True) + 1e-05)
    a_out[...] = (xf * rinv1 * gain1[...]).astype(BF)


def columns_of(left, right, first, out):
    step = 512

    def body(i, c):
        at = pl.ds(pl.multiple_of(i * step, step), step)
        to = pl.ds(pl.multiple_of(first + i * step, step), step)
        out[:, to] = nn(left[...], right[:, at]).astype(out.dtype)
        return c

    lax.fori_loop(0, right.shape[1] // step, body, 0)


def attention_heads(npos, qkv, ob):
    rows, d = ob.shape
    mask = causal(GROUP, npos)
    low = lax.broadcasted_iota(jnp.int32, (GROUP, 2 * HD), 1) < HD
    def heads(i, c):
        for g in range(rows // GROUP):
            at = pl.ds(g * GROUP, GROUP)
            q, k, v = (qkv[at, pl.ds(pl.multiple_of(i * 2 * HD + t * d, 2 * HD), 2 * HD)] for t in range(3))
            zero = jnp.zeros_like(q)
            p0 = soft(jnp.where(low, q, zero), k, mask).astype(BF)
            p1 = soft(jnp.where(low, zero, q), k, mask).astype(BF)
            ob[at, pl.ds(pl.multiple_of(i * 2 * HD, 2 * HD), 2 * HD)] = jnp.where(low, nn(p0, v), nn(p1, v)).astype(BF)
        return c
    lax.fori_loop(0, d // (2 * HD), heads, 0)


def attention_end(npos, fr, x, gain2, w_out, ob, x1_out, b_out):
    rows, _ = x.shape
    columns_of(ob, w_out, 0, x1_out)
    x1 = x1_out[...] + x[...].astype(F32)
    x1_out[...] = x1
    rinv2 = lax.rsqrt(jnp.mean(x1 * x1, axis=1, keepdims=True) + 1e-05)
    b = (x1 * rinv2 * gain2[...]).astype(BF)
    b_out[...] = nn(by_position(rows, npos, fr), b).astype(BF)


def weight_terms(left, right, first, out):
    columns = out.shape[1]
    step = 512

    def body(i, c):
        at = pl.ds(pl.multiple_of(i * step, step), step)
        of = pl.ds(pl.multiple_of(first + i * step, step), step)
        out[:, at] = tn(left[...], right[:, of]).astype(BF)
        return c

    lax.fori_loop(0, columns // step, body, 0)


def attention_bwd_in(npos, fr, db_pos, gy, keep, x1_ref, ob, gain2, dx1_s, dxb, terms):
    rows, d = x1_ref.shape
    db = nn(by_position(rows, npos, fr, True), db_pos[...])
    x1 = x1_ref[...]
    rinv2 = lax.rsqrt(jnp.mean(x1 * x1, axis=1, keepdims=True) + 1e-05)
    n2 = db * gain2[...]
    inner = jnp.mean(n2 * x1, axis=1, keepdims=True)
    dx1 = keep[...] * gy[...].astype(F32) + rinv2 * n2 - x1 * (rinv2 * rinv2 * rinv2 * inner)
    dx1_s[...] = dx1
    dxb[...] = dx1.astype(BF)
    weight_terms(ob, dxb, 0, terms.at[3])
    return jnp.sum(db * x1 * rinv2, axis=0, keepdims=True)


def attention_bwd_heads(npos, qkv, do_s, dqkv):
    rows, d = do_s.shape
    mask = causal(GROUP, npos)
    low = lax.broadcasted_iota(jnp.int32, (GROUP, 2 * HD), 1) < HD
    scale = 1.0 / math.sqrt(HD)

    def heads(i, c):
        for g in range(rows // GROUP):
            at = pl.ds(g * GROUP, GROUP)
            lanes = [pl.ds(pl.multiple_of(i * 2 * HD + t * d, 2 * HD), 2 * HD) for t in range(3)]
            q, k, v = (qkv[at, l] for l in lanes)
            do = do_s[at, lanes[0]]
            zero = jnp.zeros_like(q)
            parts = []
            for h in range(2):
                keep = low if h == 0 else jnp.logical_not(low)
                p = soft(jnp.where(keep, q, zero), k, mask)
                dp = nt(jnp.where(keep, do, zero), v)
                ds = (p * (dp - jnp.sum(p * dp, axis=1, keepdims=True)) * scale).astype(BF)
                parts.append((nn(ds, k), tn(ds, q), tn(p.astype(BF), do)))
            for t in range(3):
                dqkv[at, lanes[t]] = jnp.where(low, parts[0][t], parts[1][t]).astype(BF)
        return c

    lax.fori_loop(0, d // (2 * HD), heads, 0)


def attention_bwd_rows(x, dqkv, w, gain1, dx1, rows_out):
    d = x.shape[1]
    da = sum(nt(dqkv[:, t * d : (t + 1) * d], w[t]) for t in range(3))
    xf = x[...].astype(F32)
    rinv1 = lax.rsqrt(jnp.mean(xf * xf, axis=1, keepdims=True) + 1e-05)
    n1 = da * gain1[...]
    inner = jnp.mean(n1 * xf, axis=1, keepdims=True)
    rows_out[...] = dx1[...] + rinv1 * n1 - xf * (rinv1 * rinv1 * rinv1 * inner)
    return jnp.sum(da * xf * rinv1, axis=0, keepdims=True)


def gains_into(gain1_grad, gain2_grad, terms):
    d = gain1_grad.shape[1]
    high1 = gain1_grad.astype(BF).astype(F32)
    high2 = gain2_grad.astype(BF).astype(F32)
    at = lax.broadcasted_iota(jnp.int32, (128, d), 0)
    tail = jnp.where(at == 0, high1, 0.0)
    tail = jnp.where(at == 1, high2, tail)
    tail = jnp.where(at == 2, gain1_grad - high1, tail)
    tail = jnp.where(at == 3, gain2_grad - high2, tail)
    terms[...] = tail.T.astype(BF)


class Packer:
    def __init__(self, masters, stage, sems, send):
        self.masters, self.stage, self.sems, self.send = masters, stage, sems, send

    def fetch(self, i, p):
        return pltpu.make_async_copy(self.masters[i].at[p], self.stage.at[i], self.sems.at[i])

    def begin(self):
        for i in range(len(self.masters)):
            self.fetch(i, 0).start()

    def pack(self, p):
        nf, _, lp, ffs, _ = self.send.shape
        for i in range(len(self.masters)):
            self.fetch(i, p).wait()
            turned = self.stage[i].T.astype(BF)
            for j in range(nf):
                self.send[j, i, p] = turned[j * ffs : (j + 1) * ffs]
            if p + 1 < lp:
                self.fetch(i, p + 1).start()


def feed(p, gy_rows, b_rows, pair, wd, hid_out, grads, db, z):
    nf, _, _, _, width = grads.shape
    b = b_rows[p]
    gate = nt(pair[0, p], b)
    up = nt(pair[1, p], b)
    dhid = nt(wd, gy_rows[p])
    s = jax.nn.sigmoid(gate)
    silu = gate * s
    hid = (silu * up).astype(BF)
    dgate = (dhid * up * s * (1.0 + gate * (1.0 - s))).astype(BF)
    dup = (dhid * silu).astype(BF)
    hid_out[p] = hid
    db[...] = (tn(dgate, pair[0, p]) + tn(dup, pair[1, p])).astype(BF)
    z[...] = tn(hid, wd).astype(BF)
    for at, term in enumerate((dgate, dup)):
        grad = nn(term, b).astype(BF)
        for j in range(nf):
            grads[j, at, p] = grad[:, j * width : (j + 1) * width]


def ahead_kernel(
    nf, nz, npos, fr,
    x, gy, keep, gain1, gain2, qkv_w, out_w, gate_w, up_w, down_w,
    w_out, gy_out, grads_out, hid_out, a, qkv, ob, x1, db_rows, z_rows,
    own_w, w, gy_pos, b_pos, send, stage, down, gy_all, b_all, pair,
    db_sib, db_rx, z_sib, z_rx,
    sems_w, sems_late, sems_gy, sems_b, sems_swap, sems_in, sems_out, sems_grads, sems_down,
    sems_db, sems_db_home, sems_z, sems_z_home,
):
    d = x.shape[1]
    each = own_w.shape[1]
    lp = npos // nz
    width = send.shape[4]
    f, z = place()
    packer = Packer((gate_w, up_w), stage, sems_in, send)
    packer.begin()
    greet(nf, nz, True)
    for i in range(3):
        own_w[i] = qkv_w[:, i * d : (i + 1) * d].astype(BF)
    own_w[3] = out_w[...].astype(BF)

    def span(at, size):
        return pl.ds(pl.multiple_of(at * size, size), size)

    places = (
        lambda zz, c: own_w.at[c],
        lambda ff, zz, c: w.at[c, span(ff * nz + zz, each)],
        lambda ff, c: w.at[c, span(ff, nz * each)],
    )
    early = Gather(nf, nz, *places, sems_w)
    late = LateGather(nf, nz, *places, sems_w, sems_late)

    def rows_gather(mine, every, sems):
        return Gather(
            nf, nz,
            lambda zz, p: mine.at[span(zz * lp + p, fr)],
            lambda ff, zz, p: every.at[p, span(ff * nz + zz, fr)],
            lambda ff, p: every.at[p, span(ff, nz * fr)],
            sems,
        )

    for c in LATE_W:
        late.begin(c)
    for c in EARLY_W:
        early.begin(c)
    for c in LATE_W:
        late.relay(c)
    kept = (gy[...].astype(F32) * keep[...]).astype(BF)
    gy_pos[...] = nn(by_position(npos * fr, npos, fr), kept).astype(BF)
    grads = rows_gather(gy_pos, gy_all, sems_gy)
    rows = rows_gather(b_pos, b_all, sems_b)

    def pair_at(p):
        return lambda ff: pair.at[:, p, :, span(ff, width)]

    def send_at(p):
        return lambda ff: send.at[ff, :, p]

    swaps = [Swap(nf, send_at(p), pair_at(p), sems_swap.at[p]) for p in range(lp)]
    pieces = [(p, m) for p in range(lp) for m in range(nf - 1, 0, -1)]

    def pump(count):
        for p, m in pieces[:count]:
            swaps[p].start([m])
        del pieces[:count]

    for p in range(lp):
        grads.begin(p)
    packer.pack(0)
    for i, c in enumerate(EARLY_W):
        early.along(c)
        if i == 0:
            for at in LATE_W:
                late.along(at)
        else:
            early.relay(EARLY_W[i - 1])
        if i + 1 < lp:
            packer.pack(i + 1)
    early.relay(EARLY_W[-1])
    for c in EARLY_W:
        early.rest(c)
    for p in range(lp):
        grads.along(p)
    for p in range(len(EARLY_W) + 1, lp):
        packer.pack(p)
    attention_start(x, gain1, a)
    for c in range(3):
        if c in LATE_W:
            for p in range(lp if c == LATE_W[0] else 0):
                grads.relay(p)
            pump(FILL[0] if c == LATE_W[0] else 0)
            late.rest(c)
        (late if c in LATE_W else early).whole(c)
        columns_of(a, w.at[c], c * d, qkv)
    if LATE_W == (3,):
        for p in range(lp):
            grads.relay(p)
        pump(FILL[0])
    attention_heads(npos, qkv, ob)
    pump(FILL[1])
    late.rest(3)
    late.whole(3)
    attention_end(npos, fr, x, gain2, w.at[3], ob, x1, b_pos)
    for p in range(lp):
        rows.begin(p)
    early.finish()
    late.finish()
    save_w = pltpu.make_async_copy(w, w_out, sems_out.at[0])
    save_w.start()
    for p in range(lp):
        rows.along(p)
        if p >= 1:
            rows.relay(p - 1)
    rows.relay(lp - 1)
    pump(len(pieces))
    for p in range(lp):
        grads.rest(p)
    for p in range(lp):
        grads.whole(p)
    grads.finish()
    save_gy = pltpu.make_async_copy(gy_all, gy_out, sems_out.at[1])
    save_gy.start()

    count = b_all.shape[1]
    share = count // nf

    def term_at(first, p):
        per = d // count
        return w.at[first + p // per, pl.ds((p % per) * count, count)]

    def sums(first, sib, rx, sems, home_sems, land):
        def at(ff, p):
            return term_at(first, p).at[span(ff, share)]

        return RowSums(
            nf, nz, at, lambda p, m: at(flip(f, 2 * m), p), sib, rx, sems, home_sems, land, fr
        )

    s_db = sums(0, db_sib, db_rx, sems_db, sems_db_home, db_rows)
    s_z = sums(2, z_sib, z_rx, sems_z, sems_z_home, z_rows)

    def fetch(p):
        return pltpu.make_async_copy(down_w.at[p], down.at[p % 2], sems_down.at[p % 2])

    def steps(name, p):
        if p >= 0:
            for each_sum in (s_db, s_z):
                getattr(each_sum, name)(p)

    saves = []
    fetch(0).start()
    rows.rest(0)
    save_w.wait()
    for p in range(lp):
        if p + 1 < lp:
            fetch(p + 1).start()
            rows.rest(p + 1)
        fetch(p).wait()
        wd = down[p % 2].astype(BF)
        rows.whole(p)
        swaps[p].finish()
        feed(p, gy_all, b_all, pair, wd, hid_out, send, term_at(0, p), term_at(2, p))
        saves.append(
            pltpu.make_async_copy(send.at[:, :, p], grads_out.at[:, :, p], sems_grads.at[p])
        )
        saves[-1].start()
        steps("pairs", p)
        steps("chips", p - 1)
        steps("across", p - 2)
        steps("home", p - 3)
    for name, last in (("chips", 1), ("across", 2), ("home", 3), ("landed", lp)):
        for p in range(max(lp - last, 0), lp):
            steps(name, p)
    rows.finish()
    save_gy.wait()
    for copy in saves:
        copy.wait()
    s_db.finish()
    s_z.finish()


def behind_kernel(
    nf, nz, npos, fr,
    grads, w_in, x, gy, keep, gain1, gain2, x1, a, qkv, ob, db_rows, z_rows,
    block_out, rows_grad, total, gains, pair_all,
    t_sib, t_rx, t_sems, t_home, g_sib, g_rx, g_sems, g_home, t_land, g_land,
    l_sib, l_rx, l_sems, l_late, l_zl, sems_swap, sem_w,
    w, terms, tail, dx1, dxb, do, dqkv,
):
    d = x.shape[1]
    each = gains.shape[0]
    lp = npos // nz
    f, z = place()
    load_w = pltpu.make_async_copy(w_in, w, sem_w)
    load_w.start()
    greet(nf, nz, True)

    def part(ref, p):
        return lambda ff: ref.at[ff, :, p]

    swaps = [Swap(nf, part(grads, p), part(pair_all, p), sems_swap.at[p]) for p in range(lp)]
    pieces = [(p, m) for p in range(lp) for m in range(nf - 1, 0, -1)]

    def pump(count):
        for p, m in pieces[:count]:
            swaps[p].start([m])
        del pieces[:count]

    pump(PUMP[0])

    def span(ff):
        return pl.ds(pl.multiple_of(ff * nz * each, nz * each), nz * each)

    def terms_of(table):
        return (
            lambda ff, c: terms.at[table[c], span(ff)],
            lambda c, m: terms.at[table[c], span(flip(f, 2 * m))],
        )

    s_t = BlockSums(nf, nz, *terms_of(EARLY), t_sib, t_rx, t_sems, t_home, t_land, each)
    s_l = PosSums(nf, nz, *terms_of(LATE), l_sib, l_rx, l_sems, l_late, l_zl, each)
    s_g = BlockSums(
        nf, nz,
        lambda ff, c: tail.at[span(ff)],
        lambda c, m: tail.at[span(flip(f, 2 * m))],
        g_sib, g_rx, g_sems, g_home, g_land, each,
    )

    def both(step, c):
        sums, at = (s_l, LATE.index(c)) if c in LATE else (s_t, EARLY.index(c))
        if hasattr(sums, step):
            getattr(sums, step)(at)

    gain2_grad = attention_bwd_in(npos, fr, db_rows, gy, keep, x1, ob, gain2, dx1, dxb, terms)
    both("pairs", 3)
    load_w.wait()
    do[...] = nt(dxb[...], w[3]).astype(BF)
    both("along" if 3 in LATE else "chips", 3)
    attention_bwd_heads(npos, qkv, do, dqkv)
    if 3 not in LATE:
        both("across", 3)
    weight_terms(a, dqkv, 2 * d, terms.at[2])
    both("pairs", 2)
    pump(PUMP[1])
    weight_terms(a, dqkv, 0, terms.at[0])
    both("pairs", 0)
    both("along" if 2 in LATE else "chips", 2)
    weight_terms(a, dqkv, d, terms.at[1])
    both("pairs", 1)
    both("chips", 0)
    gain1_grad = attention_bwd_rows(x, dqkv, w, gain1, dx1, rows_grad)
    gains_into(gain1_grad, gain2_grad, tail)
    s_g.pairs(0)
    both("chips", 1)
    s_g.chips(0)
    pump(PUMP[2])
    order = [c for c in (2, 0, 1) if c in EARLY]
    for c in order:
        both("across", c)
    s_g.across(0)
    for c in LATE:
        both("chips", c)
    pump(PUMP[3])
    for c in ([3] if 3 in EARLY else []) + order:
        both("home", c)
    s_g.home(0)
    for c in LATE:
        both("across", c)
    pump(len(pieces))
    back = nn(by_position(npos * fr, npos, fr, True), z_rows[...])
    block_out[...] = (keep[...] * (x1[...] + back)).astype(BF)
    for sums, table in ((s_t, EARLY), (s_l, LATE)):
        for at, c in enumerate(table):
            sums.landed(at, total.at[:, pl.ds(c * d, d)])
    s_g.landed(0, gains)
    for sums in (s_t, s_l, s_g):
        sums.finish()
    for swap in swaps:
        swap.finish()


def last_local_kernel(pair, hid, gy, total, gate, up, down, qkv_grad, out_grad):
    nf, _, _, ffs, width = pair.shape
    d = gy.shape[2]

    @pl.when(pl.program_id(0) == 0)
    def _():
        qkv_grad[...] = total[:, : 3 * d]
        out_grad[...] = total[:, 3 * d :]

    for at, out in enumerate((gate, up)):
        out[0] = pair[:, at, 0].astype(F32).reshape(nf * ffs, width).T
    down[0] = nn(hid[0], gy[0])


def rms_norm(values, gain_vector):
    return (
        values * lax.rsqrt(jnp.mean(values * values, axis=-1, keepdims=True) + 1e-05) * gain_vector
    )


def attend(qkv_rows):
    frame_count = qkv_rows.shape[0]
    positions = qkv_rows.shape[1]
    split_rows = qkv_rows.reshape(frame_count, positions, 3, H, HD)
    queries = split_rows[:, :, 0]
    keys_all = split_rows[:, :, 1]
    values_all = split_rows[:, :, 2]
    scores = jnp.einsum("fqhe,fkhe->fhqk", queries, keys_all, preferred_element_type=F32) * (
        1.0 / math.sqrt(HD)
    )
    causal = jnp.arange(positions)[:, None] >= jnp.arange(positions)[None, :]
    scores = jnp.where(causal, scores, -1e30)
    weights = jax.nn.softmax(scores, axis=-1)
    mixed = jnp.einsum("fhqk,fkhe->fqhe", weights, values_all, preferred_element_type=F32)
    return mixed.reshape(frame_count, positions, H * HD)


def local_general(
    frame_rows,
    frame_mask,
    gain_attention,
    gain_feed,
    qkv_master,
    out_master,
    gate_master,
    up_master,
    down_master,
    out_cotangent,
):
    nf = lax.axis_size("frames")
    nz = lax.axis_size("pos")
    lp, dslice, ff = gate_master.shape
    ffs = down_master.shape[1]
    fr, npos, d = frame_rows.shape

    keep_rows = frame_mask.astype(F32)[:, None, None]
    inputs = frame_rows.astype(F32)

    def turned(w):
        return w.astype(BF).reshape(lp, dslice, nf, ffs).transpose(2, 0, 3, 1)

    def untwist(w):
        return w.transpose(1, 2, 0, 3).reshape(lp, ffs, d)

    def to_pos(rows):
        return rows.transpose(1, 0, 2).reshape(nz, lp * fr, d)

    def gathered(every):
        every = every.reshape(nf, nz, lp, fr, d)
        return every.transpose(2, 0, 1, 3, 4).reshape(lp, nf * nz * fr, d)

    rows_shape = jax.ShapeDtypeStruct((nf, nz, lp * fr, d), BF)
    back_shape = jax.ShapeDtypeStruct((npos * fr, d), BF)
    gather_sems = pltpu.SemaphoreType.DMA(Gather.sem_shape(nf, nz))
    swap_sems = pltpu.SemaphoreType.DMA(Swap.sem_shape(nf))

    def scattered(rows, ident):
        back = call(
            functools.partial(back_kernel, nf, nz, fr),
            ident,
            out_shape=back_shape,
            in_specs=[VM],
            out_specs=VM,
            scratch_shapes=HomeSums.scratch(nf, nz, lp, nz * fr, d),
        )(rows.reshape(lp, nf, nz * fr, d))
        return back.reshape(npos, fr, d).transpose(1, 0, 2)

    both = jnp.concatenate((qkv_master.astype(BF), out_master.astype(BF)), axis=1)
    pair = jnp.stack((turned(gate_master), turned(up_master)), axis=1)
    upstream = keep_rows * out_cotangent.astype(F32)
    own_rows = both.shape[0]
    w_all, gy_all, pair = call(
        functools.partial(first_kernel, nf, nz),
        0,
        out_shape=(
            jax.ShapeDtypeStruct((nf, nz) + both.shape, BF),
            rows_shape,
            jax.ShapeDtypeStruct(pair.shape, BF),
        ),
        in_specs=[ANY] * 3,
        out_specs=(ANY,) * 3,
        scratch_shapes=[gather_sems, gather_sems, swap_sems],
    )(both, to_pos(upstream.astype(BF)), pair)
    w_all = w_all.reshape(d, both.shape[1])
    w_qkv = w_all[:, : 3 * d]
    w_out = w_all[:, 3 * d :]
    gate_t = untwist(pair[:, 0])
    up_t = untwist(pair[:, 1])
    down = down_master.astype(BF)
    gy = gathered(gy_all)

    normed_one, norm_one_pull = jax.vjp(rms_norm, inputs, gain_attention)
    normed_low = normed_one.astype(BF)
    qkv_rows = jnp.einsum("fpd,de->fpe", normed_low, w_qkv, preferred_element_type=F32)
    mixed, attend_pull = jax.vjp(attend, qkv_rows)
    mixed_low = mixed.astype(BF)
    branch = jnp.einsum("fpd,de->fpe", mixed_low, w_out, preferred_element_type=F32)
    middle = inputs + branch
    normed_two, norm_two_pull = jax.vjp(rms_norm, middle, gain_feed)
    b_all = call(
        functools.partial(rows_kernel, nf, nz),
        1,
        out_shape=rows_shape,
        in_specs=[ANY],
        out_specs=ANY,
        scratch_shapes=[gather_sems],
    )(to_pos(normed_two.astype(BF)))
    b = gathered(b_all)

    gate_rows = jnp.einsum("prd,phd->phr", b, gate_t, preferred_element_type=F32)
    up_rows = jnp.einsum("prd,phd->phr", b, up_t, preferred_element_type=F32)
    hidden_grad = jnp.einsum("prd,phd->phr", gy, down, preferred_element_type=F32)
    sigma = jax.nn.sigmoid(gate_rows)
    silu_gate = gate_rows * sigma
    hidden = (silu_gate * up_rows).astype(BF)
    gate_back = (hidden_grad * up_rows * sigma * (1.0 + gate_rows * (1.0 - sigma))).astype(BF)
    up_back = (hidden_grad * silu_gate).astype(BF)
    db = jnp.einsum("phr,phd->prd", gate_back, gate_t, preferred_element_type=F32) + jnp.einsum(
        "phr,phd->prd", up_back, up_t, preferred_element_type=F32
    )
    back_rows = scattered(db.astype(BF), 2).astype(F32)
    feed = jnp.einsum("phr,phd->prd", hidden, down, preferred_element_type=F32)
    returned = scattered(feed.astype(BF), 3).astype(F32)
    block_out = (keep_rows * (middle + returned)).astype(BF)
    gate_grad = jnp.einsum("phr,prd->phd", gate_back, b, preferred_element_type=F32).astype(BF)
    up_grad = jnp.einsum("phr,prd->phd", up_back, b, preferred_element_type=F32).astype(BF)
    down_grad = jnp.einsum("phr,prd->phd", hidden, gy, preferred_element_type=F32)

    grads = jnp.stack((gate_grad, up_grad), axis=0).reshape(2, lp, ffs, nf, dslice)
    grads = grads.transpose(3, 0, 1, 2, 4)

    pulled_two = norm_two_pull(back_rows)
    middle_grad = upstream + pulled_two[0]
    branch_grad = middle_grad.astype(BF)
    out_weight_grad = jnp.einsum("fpd,fpe->de", mixed_low, branch_grad, preferred_element_type=F32)
    mixed_grad = jnp.einsum("fpe,de->fpd", branch_grad, w_out, preferred_element_type=F32)
    qkv_back = attend_pull(mixed_grad)[0].astype(BF)
    qkv_weight_grad = jnp.einsum("fpd,fpe->de", normed_low, qkv_back, preferred_element_type=F32)
    normed_grad = jnp.einsum("fpe,de->fpd", qkv_back, w_qkv, preferred_element_type=F32)
    pulled_one = norm_one_pull(normed_grad)
    rows_grad = middle_grad + pulled_one[0]

    gains = jnp.stack((pulled_one[1], pulled_two[1]), axis=1)
    gains_hi = gains.astype(BF)
    gains_lo = (gains - gains_hi.astype(F32)).astype(BF)
    unit = max(128, 2048 // own_rows)
    spare = -(4 * d + 4) % unit
    tail = jnp.concatenate((gains_hi, gains_lo, jnp.zeros((d, spare), BF)), axis=1)
    total = jnp.concatenate(
        (qkv_weight_grad.astype(BF), out_weight_grad.astype(BF), tail), axis=1
    )
    block = own_rows * total.shape[1] // 128
    total, grads = call(
        functools.partial(last_kernel, nf, nz),
        4,
        out_shape=(
            jax.ShapeDtypeStruct((block, 128), F32),
            jax.ShapeDtypeStruct(grads.shape, BF),
        ),
        in_specs=[VM, ANY],
        out_specs=(VM, ANY),
        scratch_shapes=HomeSums.scratch(nf, nz, 1, nz * block, 128)
        + [pltpu.VMEM((1, nz - 1, block, 128), BF), swap_sems],
    )(total.reshape(1, nf, nz * block, 128), grads)
    grads = grads.transpose(1, 2, 4, 0, 3).reshape(2, lp, dslice, ff).astype(F32)
    total = total.reshape(own_rows, 4 * d + 4 + spare)
    gain_grads = total[:, 4 * d : 4 * d + 2] + total[:, 4 * d + 2 : 4 * d + 4]
    return (
        block_out,
        rows_grad,
        gain_grads[:, 0],
        gain_grads[:, 1],
        total[:, : 3 * d],
        total[:, 3 * d : 4 * d],
        grads[0],
        grads[1],
        down_grad,
    )
def local_fused(
    frame_rows,
    frame_mask,
    gain_attention,
    gain_feed,
    qkv_master,
    out_master,
    gate_master,
    up_master,
    down_master,
    out_cotangent,
):
    nf = lax.axis_size("frames")
    nz = lax.axis_size("pos")
    lp, dslice, ff = gate_master.shape
    ffs = down_master.shape[1]
    fr, npos, d = frame_rows.shape
    rows = fr * npos
    each = qkv_master.shape[0]
    count = nf * nz * fr

    def make(shape, kind=BF):
        return jax.ShapeDtypeStruct(shape, kind)

    def vmem(shape, kind=BF):
        return pltpu.VMEM(shape, kind)

    def dma(*shape):
        return pltpu.SemaphoreType.DMA(shape)

    x = frame_rows.reshape(rows, d)
    gy = out_cotangent.reshape(rows, d)
    keep = jnp.broadcast_to(frame_mask.astype(F32)[:, None], (fr, npos)).reshape(rows, 1)
    gain1 = gain_attention.reshape(1, d)
    gain2 = gain_feed.reshape(1, d)
    gather_sems = dma(*Gather.sem_shape(nf, nz, 4))
    rows_sems = dma(*Gather.sem_shape(nf, nz, lp))
    swap_sems = dma(lp, *Swap.sem_shape(nf))
    pair_shape = (nf, 2, lp, ffs, dslice)
    row_scratch = HomeSums.scratch(nf, nz, lp, nz * fr, d)
    w_all, gy_all, grads, hid, a, qkv, ob, x1, db_rows, z_rows = call(
        functools.partial(ahead_kernel, nf, nz, npos, fr),
        0,
        out_shape=(
            make((4, d, d)),
            make((lp, count, d)),
            make(pair_shape),
            make((lp, ffs, count)),
            make((rows, d)),
            make((rows, 3 * d)),
            make((rows, d)),
            make((rows, d), F32),
            make((rows, d)),
            make((rows, d)),
        ),
        in_specs=[VM] * 7 + [ANY] * 3,
        out_specs=(ANY,) * 3 + (VM,) * 7,
        scratch_shapes=[
            vmem((4, each, d)),
            vmem((4, d, d)),
            vmem((rows, d)),
            vmem((rows, d)),
            vmem(pair_shape),
            vmem((2, dslice, ff), F32),
            vmem((2, ffs, d), F32),
            vmem((lp, count, d)),
            vmem((lp, count, d)),
            vmem((2, lp, ffs, d)),
            *row_scratch[:2],
            *row_scratch[:2],
            gather_sems,
            dma(*LateGather.late_shape(nf, nz, 4)),
            rows_sems,
            rows_sems,
            swap_sems,
            dma(2),
            dma(2),
            dma(lp),
            dma(2),
            *row_scratch[2:],
            *row_scratch[2:],
        ],
    )(x, gy, keep, gain1, gain2, qkv_master, out_master, gate_master, up_master, down_master)
    block_out, rows_grad, total, gains, back = call(
        functools.partial(behind_kernel, nf, nz, npos, fr),
        1,
        out_shape=(
            make((rows, d)),
            make((rows, d), F32),
            make((each, 4 * d), F32),
            make((each, 128), F32),
            make(pair_shape),
        ),
        in_specs=[ANY] * 2 + [VM] * 11,
        out_specs=(VM,) * 4 + (ANY,),
        scratch_shapes=[
            *HomeSums.scratch(nf, nz, len(EARLY), nz * each, d),
            *HomeSums.scratch(nf, nz, 1, nz * each, 128),
            vmem((len(EARLY), nz - 1, each, d)),
            vmem((1, nz - 1, each, 128)),
            *PosSums.scratch(nf, nz, len(LATE), each, d),
            swap_sems,
            pltpu.SemaphoreType.DMA,
            vmem((4, d, d)),
            vmem((4, d, d)),
            vmem((d, 128)),
            vmem((rows, d), F32),
            vmem((rows, d)),
            vmem((rows, d)),
            vmem((rows, 3 * d)),
        ],
    )(grads, w_all, x, gy, keep, gain1, gain2, x1, a, qkv, ob, db_rows, z_rows)
    whole_block = pl.BlockSpec((1, dslice, ff), lambda p: (p, 0, 0))

    def once(*shape):
        return pl.BlockSpec(shape, lambda p: (0, 0))

    gate_grad, up_grad, down_grad, qkv_grad, out_grad = pl.pallas_call(
        last_local_kernel,
        grid=(lp,),
        out_shape=(
            make((lp, dslice, ff), F32),
            make((lp, dslice, ff), F32),
            make((lp, ffs, d), F32),
            make((each, 3 * d), F32),
            make((each, d), F32),
        ),
        in_specs=[
            pl.BlockSpec((nf, 2, 1, ffs, dslice), lambda p: (0, 0, p, 0, 0)),
            pl.BlockSpec((1, ffs, count), lambda p: (p, 0, 0)),
            pl.BlockSpec((1, count, d), lambda p: (p, 0, 0)),
            once(each, 4 * d),
        ],
        out_specs=(
            whole_block,
            whole_block,
            pl.BlockSpec((1, ffs, d), lambda p: (p, 0, 0)),
            once(each, 3 * d),
            once(each, d),
        ),
        compiler_params=pltpu.CompilerParams(vmem_limit_bytes=60 * 2**20),
    )(back, hid, gy_all, total)
    gains = gains[:, :2] + gains[:, 2:4]
    return (
        block_out.reshape(fr, npos, d),
        rows_grad.reshape(fr, npos, d),
        gains[:, 0],
        gains[:, 1],
        qkv_grad,
        out_grad,
        gate_grad,
        up_grad,
        down_grad,
    )


def local(*args):
    _, dslice, _ = args[6].shape
    if lax.axis_size("frames") == 8 and dslice % 128 == 0:
        return local_fused(*args)
    return local_general(*args)


def solution(mesh):
    in_specs = (
        P(("frames", "pos"), None, None),
        P(("frames", "pos")),
        P(),
        P(),
        P(("frames", "pos"), None),
        P(("frames", "pos"), None),
        P("pos", "frames", None),
        P("pos", "frames", None),
        P("pos", "frames", None),
        P(("frames", "pos"), None, None),
    )
    out_specs = (
        P(("frames", "pos"), None, None),
        P(("frames", "pos"), None, None),
        P(("frames", "pos")),
        P(("frames", "pos")),
        P(("frames", "pos"), None),
        P(("frames", "pos"), None),
        P("pos", "frames", None),
        P("pos", "frames", None),
        P("pos", "frames", None),
    )
    return jax.shard_map(local, mesh=mesh, in_specs=in_specs, out_specs=out_specs, check_vma=False)
```

```python
import functools
import math

import jax
import jax.numpy as jnp
from jax import lax
from jax.experimental import pallas as pl
from jax.experimental.pallas import tpu as pltpu
from jax.sharding import PartitionSpec as P

H = 16
HD = 64
BF = jnp.bfloat16
F32 = jnp.float32
MESH = pl.DeviceIdType.MESH
MASKS = (1, 2, 4, 3, 5, 6, 7)
FILL = (7, 9, 4)
PUMP = (7, 0, 12, 4, 2, 2)
LATE = (2, 3)
EARLY = tuple(c for c in range(4) if c not in LATE)
LATE_W = (2, 3)
EARLY_W = tuple(c for c in range(4) if c not in LATE_W)
ANY = pl.BlockSpec(memory_space=pl.ANY)
VM = pl.BlockSpec(memory_space=pltpu.VMEM)


def place():
    return lax.axis_index("frames"), lax.axis_index("pos")


def flip(index, mask):
    bit = 1
    while bit <= mask:
        if mask & bit:
            index = index + bit * (1 - 2 * ((index // bit) % 2))
        bit *= 2
    return index


def greet(nf, nz, every_frame):
    f, z = place()
    hops = [1] + [2 * m for m in range(1, nf // 2)]
    if every_frame:
        hops = list(range(1, nf))
    others = [(flip(f, h), z) for h in hops] + [(f, flip(z, k)) for k in range(1, nz)]
    barrier = pltpu.get_barrier_semaphore()
    for other in others:
        pl.semaphore_signal(barrier, inc=1, device_id=other, device_id_type=MESH)
    pl.semaphore_wait(barrier, len(others))


def remote(src, dst, send, recv, to):
    copy = pltpu.make_async_remote_copy(
        src_ref=src, dst_ref=dst, send_sem=send, recv_sem=recv, device_id=to, device_id_type=MESH
    )
    copy.start()
    return copy


def arrival(dst, send, recv):
    f, z = place()
    pltpu.make_async_remote_copy(
        src_ref=dst,
        dst_ref=dst,
        send_sem=send,
        recv_sem=recv,
        device_id=(flip(f, 1), z),
        device_id_type=MESH,
    ).wait_recv()


def relay_of(k):
    return 1 if k % 2 == 0 else 2


class Gather:
    def __init__(self, nf, nz, src_for, out_at, group_at, sems):
        self.nf, self.nz, self.nc = nf, nz, nf // 2
        self.f, self.z = place()
        self.src_for, self.out_at, self.group_at, self.sems = src_for, out_at, group_at, sems
        self.sent = []
        self.own = {}
        self.tree = self.nc == 4

    @staticmethod
    def sem_shape(nf, nz, parts=1):
        return (2, nz + nf, parts)

    def push(self, src, dst, hop, c, to):
        copy = remote(src, dst, self.sems.at[0, hop, c], self.sems.at[1, hop, c], to)
        self.sent.append((c, copy))

    def arrive(self, dst, hop, c):
        arrival(dst, self.sems.at[0, hop, c], self.sems.at[1, hop, c])

    def near(self, m, c):
        return self.group_at(flip(self.f, 2 * m), c)

    def begin(self, c=0):
        f, z = self.f, self.z
        for k in range(self.nz - 1, 0, -1):
            self.push(self.src_for(flip(z, k), c), self.out_at(f, z, c), k, c, (f, flip(z, k)))
        src, dst = self.src_for(z, c), self.out_at(f, z, c)
        self.own[c] = pltpu.make_async_copy(src, dst, self.sems.at[0, 0, c])
        self.own[c].start()

    def along(self, c=0):
        f, z = self.f, self.z
        self.own[c].wait()
        for k in range(1, self.nz):
            self.arrive(self.out_at(f, flip(z, k), c), k, c)
        group = self.near(0, c)
        for m in range(1, self.nc):
            if not (self.tree and m == 3):
                self.push(group, group, self.nz + m, c, (flip(f, 2 * m), z))
        self.push(group, group, self.nz + self.nc, c, (flip(f, 1), z))

    def over(self, m, c):
        f, z = self.f, self.z
        group = self.near(m, c)
        self.arrive(group, self.nz + m, c)
        if self.tree and m == relay_of(c):
            self.push(group, group, self.nz + 3, c, (flip(f, 2 * (3 - m)), z))
        self.push(group, group, self.nz + self.nc + m, c, (flip(f, 1), z))

    def relay(self, c=0):
        if self.tree:
            self.over(relay_of(c), c)

    def rest(self, c=0):
        for m in range(1, self.nc):
            if not (self.tree and m == relay_of(c)):
                self.over(m, c)

    def whole(self, c=0):
        for m in range(self.nc):
            group = self.group_at(flip(self.f, 2 * m + 1), c)
            self.arrive(group, self.nz + self.nc + m, c)

    def finish(self, part=None):
        for c, copy in self.sent:
            if part is None or c == part:
                copy.wait_send()
        self.sent = [(c, copy) for c, copy in self.sent if part is not None and c != part]


class LateGather(Gather):
    def __init__(self, nf, nz, src_for, out_at, group_at, sems, late_sems):
        super().__init__(nf, nz, src_for, out_at, group_at, sems)
        self.late_sems = late_sems

    @staticmethod
    def late_shape(nf, nz, parts):
        return (2, nz * (nf // 2), parts)

    def block(self, m, k, c):
        return self.out_at(flip(self.f, 2 * m), flip(self.z, k), c)

    def begin(self, c=0):
        f, z = self.f, self.z
        src, dst = self.src_for(z, c), self.out_at(f, z, c)
        for m in range(1, self.nc):
            if not (self.tree and m == 3):
                self.push(src, dst, self.nz + m, c, (flip(f, 2 * m), z))
        self.own[c] = pltpu.make_async_copy(src, dst, self.sems.at[0, 0, c])
        self.own[c].start()

    def relay(self, c=0):
        if self.tree:
            m = relay_of(c)
            block = self.block(m, 0, c)
            self.arrive(block, self.nz + m, c)
            to = (flip(self.f, 2 * (3 - m)), self.z)
            self.push(block, block, self.nz + 3, c, to)

    def along(self, c=0):
        self.own[c].wait()
        for m in range(1, self.nc):
            if not (self.tree and m == relay_of(c)):
                self.arrive(self.block(m, 0, c), self.nz + m, c)
        for k in range(self.nz - 1, 0, -1):
            for m in range(self.nc):
                block, hop = self.block(m, 0, c), k * self.nc + m
                send, recv = self.late_sems.at[0, hop, c], self.late_sems.at[1, hop, c]
                copy = remote(block, block, send, recv, (self.f, flip(self.z, k)))
                self.sent.append((c, copy))

    def rest(self, c=0):
        for m in range(self.nc):
            for k in range(1, self.nz):
                hop = k * self.nc + m
                send, recv = self.late_sems.at[0, hop, c], self.late_sems.at[1, hop, c]
                arrival(self.block(m, k, c), send, recv)
            group = self.near(m, c)
            self.push(group, group, self.nz + self.nc + m, c, (flip(self.f, 1), self.z))


class Swap:
    def __init__(self, nf, src_at, out_at, sems):
        self.nf, self.src_at, self.out_at, self.sems = nf, src_at, out_at, sems
        self.f, self.z = place()
        self.sent = []
        self.own = None

    @staticmethod
    def sem_shape(nf):
        return (2, nf)

    def start(self, masks=None):
        f, z = self.f, self.z
        if self.own is None:
            self.own = pltpu.make_async_copy(self.src_at(f), self.out_at(f), self.sems.at[0, 0])
            self.own.start()
        for m in masks or range(self.nf - 1, 0, -1):
            self.sent.append(
                remote(
                    self.src_at(flip(f, m)),
                    self.out_at(f),
                    self.sems.at[0, m],
                    self.sems.at[1, m],
                    (flip(f, m), z),
                )
            )

    def finish(self):
        self.own.wait()
        for copy in self.sent:
            copy.wait()


class Sums:
    def __init__(self, nf, nz, src_at, own_at, sib, rx, sems):
        self.nf, self.nz, self.nc = nf, nz, nf // 2
        self.f, self.z = place()
        self.src_at, self.own_at, self.sib, self.rx = src_at, own_at, sib, rx
        self.sems = sems
        self.sent = []
        self.tree = self.nc == 4

    @staticmethod
    def buffers(nf, parts, rows, columns):
        nc = nf // 2
        return [
            pltpu.VMEM((parts, nc, rows, columns), BF),
            pltpu.VMEM((parts, nc - 1, rows, columns), BF),
            pltpu.SemaphoreType.DMA((2, 2 * nc, parts)),
        ]

    def push(self, src, dst, sems, hop, k, to):
        self.sent.append(remote(src, dst, sems.at[0, hop, k], sems.at[1, hop, k], to))

    def arrive(self, dst, sems, hop, k):
        arrival(dst, sems.at[0, hop, k], sems.at[1, hop, k])

    def first(self, k):
        if self.tree:
            return [3, relay_of(k)]
        return list(range(self.nc - 1, 0, -1))

    def pairs(self, k):
        f, z = self.f, self.z
        order = self.first(k)
        for m in order + [m for m in range(self.nc - 1, -1, -1) if m not in order]:
            src = self.src_at(flip(f, 2 * m + 1), k)
            self.push(src, self.sib.at[k, m], self.sems, self.nc + m, k, (flip(f, 1), z))

    def chips(self, k):
        f, z = self.f, self.z
        for m in self.first(k):
            sib = self.sib.at[k, m]
            self.arrive(sib, self.sems, self.nc + m, k)
            add_into(sib, self.own_at(k, m), sib)
            hop, to = m, m
            if self.tree:
                hop, to = (2 if m == 3 else 1), relay_of(k)
            self.push(sib, self.rx.at[k, hop - 1], self.sems, hop, k, (flip(f, 2 * to), z))

    def across(self, k):
        if not self.tree:
            return
        m = 3 - relay_of(k)
        sib = self.sib.at[k, m]
        self.arrive(sib, self.sems, self.nc + m, k)
        self.arrive(self.rx.at[k, 1], self.sems, 2, k)
        add_into(sib, self.own_at(k, m), sib, self.rx.at[k, 1])
        self.push(sib, self.rx.at[k, 2], self.sems, 3, k, (flip(self.f, 2 * m), self.z))

    def total(self, k, out):
        self.arrive(self.sib.at[k, 0], self.sems, self.nc, k)
        terms = [self.own_at(k, 0), self.sib.at[k, 0]]
        for m in range(1, self.nc):
            if self.tree and m == 2:
                continue
            self.arrive(self.rx.at[k, m - 1], self.sems, m, k)
            terms.append(self.rx.at[k, m - 1])
        add_into(out, *terms)

    def finish(self):
        for copy in self.sent:
            copy.wait_send()


class HomeSums(Sums):
    def __init__(self, nf, nz, src_at, own_at, sib, rx, sems, home_sems, land, each):
        super().__init__(nf, nz, src_at, own_at, sib, rx, sems)
        self.home_sems, self.land, self.each = home_sems, land, each

    @staticmethod
    def scratch(nf, nz, parts, rows, columns):
        sib, rx, sems = Sums.buffers(nf, parts, rows, columns)
        return [sib, rx, sems, pltpu.SemaphoreType.DMA((2, nz, parts))]

    def rows_of(self, ref, at):
        return ref.at[pl.ds(pl.multiple_of(at * self.each, self.each), self.each)]

    def home(self, p):
        whole = self.sib.at[p, 0]
        self.total(p, whole)
        for k in range(self.nz - 1, 0, -1):
            src = self.rows_of(whole, flip(self.z, k))
            self.push(src, self.sent_to(k, p), self.home_sems, k, p, (self.f, flip(self.z, k)))


class RowSums(HomeSums):
    def at(self, zz, p):
        return self.rows_of(self.land, zz * self.sib.shape[0] + p)

    def sent_to(self, k, p):
        return self.at(self.z, p)

    def landed(self, p):
        self.at(self.z, p)[...] = self.rows_of(self.sib.at[p, 0], self.z)[...]
        for k in range(1, self.nz):
            self.arrive(self.at(flip(self.z, k), p), self.home_sems, k, p)


class BlockSums(HomeSums):
    def sent_to(self, k, p):
        return self.land.at[p, k - 1]

    def landed(self, p, out):
        terms = [self.rows_of(self.sib.at[p, 0], self.z)]
        for k in range(1, self.nz):
            self.arrive(self.land.at[p, k - 1], self.home_sems, k, p)
            terms.append(self.land.at[p, k - 1])
        add_into(out, *terms)


class PosSums(Sums):
    def __init__(self, nf, nz, src_at, own_at, sib, rx, sems, late_sems, zl, each):
        super().__init__(nf, nz, src_at, own_at, sib, rx, sems)
        self.late_sems, self.zl, self.each = late_sems, zl, each

    @staticmethod
    def scratch(nf, nz, parts, each, columns):
        nc = nf // 2
        return [
            pltpu.VMEM((parts, nc, nz * each, columns), BF),
            pltpu.VMEM((parts, nc - 1, each, columns), BF),
            pltpu.SemaphoreType.DMA((2, 2 * nc, parts)),
            pltpu.SemaphoreType.DMA((2, nz * nc, parts)),
            pltpu.VMEM((parts, nc, nz - 1, each, columns), BF),
        ]

    def rows_of(self, ref, at):
        return ref.at[pl.ds(pl.multiple_of(at * self.each, self.each), self.each)]

    def order(self, c):
        first = self.first(c)
        return first + [m for m in range(self.nc - 1, -1, -1) if m not in first]

    def along(self, c):
        for m in self.order(c):
            sib = self.sib.at[c, m]
            self.arrive(sib, self.sems, self.nc + m, c)
            add_into(sib, self.own_at(c, m), sib)
            for k in range(self.nz - 1, 0, -1):
                src = self.rows_of(sib, flip(self.z, k))
                to = (self.f, flip(self.z, k))
                self.push(src, self.zl.at[c, m, k - 1], self.late_sems, k * self.nc + m, c, to)

    def mine(self, m, c):
        terms = [self.rows_of(self.sib.at[c, m], self.z)]
        for k in range(1, self.nz):
            land = self.zl.at[c, m, k - 1]
            self.arrive(land, self.late_sems, k * self.nc + m, c)
            terms.append(land)
        return terms

    def chips(self, c):
        for m in self.first(c):
            terms = self.mine(m, c)
            add_into(terms[0], *terms)
            hop, to = m, m
            if self.tree:
                hop, to = (2 if m == 3 else 1), relay_of(c)
            chip = (flip(self.f, 2 * to), self.z)
            self.push(terms[0], self.rx.at[c, hop - 1], self.sems, hop, c, chip)

    def across(self, c):
        if not self.tree:
            return
        m = 3 - relay_of(c)
        terms = self.mine(m, c)
        self.arrive(self.rx.at[c, 1], self.sems, 2, c)
        add_into(terms[0], *terms, self.rx.at[c, 1])
        self.push(terms[0], self.rx.at[c, 2], self.sems, 3, c, (flip(self.f, 2 * m), self.z))

    def landed(self, c, out):
        terms = self.mine(0, c)
        for m in range(1, self.nc):
            if self.tree and m == 2:
                continue
            self.arrive(self.rx.at[c, m - 1], self.sems, m, c)
            terms.append(self.rx.at[c, m - 1])
        add_into(out, *terms)


def add_into(out, *terms):
    rows = out.shape[0]
    step = 16 if rows % 16 == 0 else rows

    def body(i, carry):
        at = pl.ds(pl.multiple_of(i * step, step), step)
        total = terms[0][at, :].astype(F32)
        for term in terms[1:]:
            total = total + term[at, :].astype(F32)
        out[at, :] = total.astype(out.dtype)
        return carry

    lax.fori_loop(0, rows // step, body, 0)


def call(kernel, ident, **kw):
    return pl.pallas_call(
        kernel,
        compiler_params=pltpu.CompilerParams(
            collective_id=ident, has_side_effects=True, vmem_limit_bytes=63 * 2**20
        ),
        **kw,
    )


def by_block(nf, nz, src_for, out, sems):
    return Gather(
        nf, nz, src_for, lambda ff, zz, c: out.at[ff, zz], lambda ff, c: out.at[ff], sems
    )


def first_kernel(nf, nz, attn, gy, pair, attn_all, gy_all, pair_all, s1, s2, s3):
    greet(nf, nz, True)
    weights = by_block(nf, nz, lambda zz, c: attn, attn_all, s1)
    rows = by_block(nf, nz, lambda zz, c: gy.at[zz], gy_all, s2)
    swap = Swap(nf, lambda ff: pair.at[ff], lambda ff: pair_all.at[ff], s3)
    gathers = (weights, rows)
    for g in gathers:
        g.begin()
    for step in ("along", "relay", "rest", "whole", "finish"):
        for g in gathers:
            getattr(g, step)()
        if step == "relay":
            swap.start()
    swap.finish()


def rows_kernel(nf, nz, b, b_all, s1):
    greet(nf, nz, False)
    rows = by_block(nf, nz, lambda zz, c: b.at[zz], b_all, s1)
    for step in (rows.begin, rows.along, rows.relay, rows.rest, rows.whole, rows.finish):
        step()


def chip_terms(terms):
    f, _ = place()
    return lambda ff, p: terms.at[p, ff], lambda p, m: terms.at[p, flip(f, 2 * m)]


def back_kernel(nf, nz, each, terms, out, sib, rx, sems, home_sems):
    greet(nf, nz, False)
    s = RowSums(nf, nz, *chip_terms(terms), sib, rx, sems, home_sems, out, each)
    for step in (s.pairs, s.chips, s.across, s.home, s.landed):
        for p in range(terms.shape[0]):
            step(p)
    s.finish()


def last_kernel(nf, nz, terms, pair, out, pair_all, sib, rx, sems, home_sems, land, s2):
    greet(nf, nz, True)
    s = BlockSums(nf, nz, *chip_terms(terms), sib, rx, sems, home_sems, land, out.shape[0])
    swap = Swap(nf, lambda ff: pair.at[ff], lambda ff: pair_all.at[ff], s2)
    s.pairs(0)
    swap.start()
    for step in (s.chips, s.across, s.home):
        step(0)
    s.landed(0, out)
    s.finish()
    swap.finish()


def contract(a, b, at_a, at_b):
    return lax.dot_general(a, b, (((at_a,), (at_b,)), ((), ())), preferred_element_type=F32)


def nt(a, b):
    return contract(a, b, 1, 1)


def nn(a, b):
    return contract(a, b, 1, 0)


def tn(a, b):
    return contract(a, b, 0, 0)


def by_position(rows, npos, fr, back=False):
    i = lax.broadcasted_iota(jnp.int32, (rows, rows), 0)
    j = lax.broadcasted_iota(jnp.int32, (rows, rows), 1)
    if back:
        i, j = j, i
    return ((i % fr) * npos + i // fr == j).astype(F32).astype(BF)


def causal(rows, npos):
    i = lax.broadcasted_iota(jnp.int32, (rows, rows), 0)
    j = lax.broadcasted_iota(jnp.int32, (rows, rows), 1)
    return jnp.logical_and(i // npos == j // npos, j <= i)


def soft(q, k, mask):
    s = jnp.where(mask, nt(q, k) * (1.0 / math.sqrt(HD)), -1e30)
    e = jnp.exp(s - jnp.max(s, axis=1, keepdims=True))
    return e / jnp.sum(e, axis=1, keepdims=True)

GROUP=128

def attention_start(x, gain1, a_out):
    xf = x[...].astype(F32)
    rinv1 = lax.rsqrt(jnp.mean(xf * xf, axis=1, keepdims=True) + 1e-05)
    a_out[...] = (xf * rinv1 * gain1[...]).astype(BF)


def columns_of(left, right, first, out):
    step = 512

    def body(i, c):
        at = pl.ds(pl.multiple_of(i * step, step), step)
        to = pl.ds(pl.multiple_of(first + i * step, step), step)
        out[:, to] = nn(left[...], right[:, at]).astype(out.dtype)
        return c

    lax.fori_loop(0, right.shape[1] // step, body, 0)


def attention_heads(npos, qkv, ob):
    rows, d = ob.shape
    mask = causal(GROUP, npos)
    low = lax.broadcasted_iota(jnp.int32, (GROUP, 2 * HD), 1) < HD
    def heads(i, c):
        for g in range(rows // GROUP):
            at = pl.ds(g * GROUP, GROUP)
            q, k, v = (qkv[at, pl.ds(pl.multiple_of(i * 2 * HD + t * d, 2 * HD), 2 * HD)] for t in range(3))
            zero = jnp.zeros_like(q)
            p0 = soft(jnp.where(low, q, zero), k, mask).astype(BF)
            p1 = soft(jnp.where(low, zero, q), k, mask).astype(BF)
            ob[at, pl.ds(pl.multiple_of(i * 2 * HD, 2 * HD), 2 * HD)] = jnp.where(low, nn(p0, v), nn(p1, v)).astype(BF)
        return c
    lax.fori_loop(0, d // (2 * HD), heads, 0)


def attention_end(npos, fr, x, gain2, w_out, ob, x1_out, b_out):
    rows, _ = x.shape
    columns_of(ob, w_out, 0, x1_out)
    x1 = x1_out[...] + x[...].astype(F32)
    x1_out[...] = x1
    rinv2 = lax.rsqrt(jnp.mean(x1 * x1, axis=1, keepdims=True) + 1e-05)
    b = (x1 * rinv2 * gain2[...]).astype(BF)
    b_out[...] = nn(by_position(rows, npos, fr), b).astype(BF)


def weight_terms(left, right, first, out):
    columns = out.shape[1]
    step = 512

    def body(i, c):
        at = pl.ds(pl.multiple_of(i * step, step), step)
        of = pl.ds(pl.multiple_of(first + i * step, step), step)
        out[:, at] = tn(left[...], right[:, of]).astype(BF)
        return c

    lax.fori_loop(0, columns // step, body, 0)


def attention_bwd_in(npos, fr, db_pos, gy, keep, x1_ref, ob, gain2, dx1_s, dxb, terms):
    rows, d = x1_ref.shape
    db = nn(by_position(rows, npos, fr, True), db_pos[...])
    x1 = x1_ref[...]
    rinv2 = lax.rsqrt(jnp.mean(x1 * x1, axis=1, keepdims=True) + 1e-05)
    n2 = db * gain2[...]
    inner = jnp.mean(n2 * x1, axis=1, keepdims=True)
    dx1 = keep[...] * gy[...].astype(F32) + rinv2 * n2 - x1 * (rinv2 * rinv2 * rinv2 * inner)
    dx1_s[...] = dx1
    dxb[...] = dx1.astype(BF)
    weight_terms(ob, dxb, 0, terms.at[3])
    return jnp.sum(db * x1 * rinv2, axis=0, keepdims=True)


def attention_bwd_heads(npos, qkv, do_s, dqkv):
    rows, d = do_s.shape
    mask = causal(GROUP, npos)
    low = lax.broadcasted_iota(jnp.int32, (GROUP, 2 * HD), 1) < HD
    scale = 1.0 / math.sqrt(HD)

    def heads(i, c):
        for g in range(rows // GROUP):
            at = pl.ds(g * GROUP, GROUP)
            lanes = [pl.ds(pl.multiple_of(i * 2 * HD + t * d, 2 * HD), 2 * HD) for t in range(3)]
            q, k, v = (qkv[at, l] for l in lanes)
            do = do_s[at, lanes[0]]
            zero = jnp.zeros_like(q)
            parts = []
            for h in range(2):
                keep = low if h == 0 else jnp.logical_not(low)
                p = soft(jnp.where(keep, q, zero), k, mask)
                dp = nt(jnp.where(keep, do, zero), v)
                ds = (p * (dp - jnp.sum(p * dp, axis=1, keepdims=True)) * scale).astype(BF)
                parts.append((nn(ds, k), tn(ds, q), tn(p.astype(BF), do)))
            for t in range(3):
                dqkv[at, lanes[t]] = jnp.where(low, parts[0][t], parts[1][t]).astype(BF)
        return c

    lax.fori_loop(0, d // (2 * HD), heads, 0)


def attention_bwd_rows(x, dqkv, w, gain1, dx1, rows_out):
    d = x.shape[1]
    da = sum(nt(dqkv[:, t * d : (t + 1) * d], w[t]) for t in range(3))
    xf = x[...].astype(F32)
    rinv1 = lax.rsqrt(jnp.mean(xf * xf, axis=1, keepdims=True) + 1e-05)
    n1 = da * gain1[...]
    inner = jnp.mean(n1 * xf, axis=1, keepdims=True)
    rows_out[...] = dx1[...] + rinv1 * n1 - xf * (rinv1 * rinv1 * rinv1 * inner)
    return jnp.sum(da * xf * rinv1, axis=0, keepdims=True)


def gains_into(gain1_grad, gain2_grad, terms):
    d = gain1_grad.shape[1]
    high1 = gain1_grad.astype(BF).astype(F32)
    high2 = gain2_grad.astype(BF).astype(F32)
    at = lax.broadcasted_iota(jnp.int32, (128, d), 0)
    tail = jnp.where(at == 0, high1, 0.0)
    tail = jnp.where(at == 1, high2, tail)
    tail = jnp.where(at == 2, gain1_grad - high1, tail)
    tail = jnp.where(at == 3, gain2_grad - high2, tail)
    terms[...] = tail.T.astype(BF)


class Packer:
    def __init__(self, masters, stage, sems, send):
        self.masters, self.stage, self.sems, self.send = masters, stage, sems, send

    def fetch(self, i, p):
        return pltpu.make_async_copy(self.masters[i].at[p], self.stage.at[i], self.sems.at[i])

    def begin(self):
        for i in range(len(self.masters)):
            self.fetch(i, 0).start()

    def pack(self, p):
        nf, _, lp, ffs, _ = self.send.shape
        for i in range(len(self.masters)):
            self.fetch(i, p).wait()
            turned = self.stage[i].T.astype(BF)
            for j in range(nf):
                self.send[j, i, p] = turned[j * ffs : (j + 1) * ffs]
            if p + 1 < lp:
                self.fetch(i, p + 1).start()


def feed(p, gy_rows, b_rows, pair, wd, hid_out, grads, db, z):
    nf, _, _, _, width = grads.shape
    b = b_rows[...]
    gate = nt(pair[0, p], b)
    up = nt(pair[1, p], b)
    dhid = nt(wd[...], gy_rows[...])
    s = jax.nn.sigmoid(gate)
    silu = gate * s
    hid = (silu * up).astype(BF)
    dgate = (dhid * up * s * (1.0 + gate * (1.0 - s))).astype(BF)
    dup = (dhid * silu).astype(BF)
    hid_out[...] = hid
    z[...] = tn(hid, wd[...]).astype(BF)
    for at, term in enumerate((dgate, dup)):
        grad = nn(term, b_rows[...]).astype(BF)
        for j in range(nf):
            grads[j, at, p] = grad[:, j * width : (j + 1) * width]
    db[...] = (tn(dgate, pair[0, p]) + tn(dup, pair[1, p])).astype(BF)


def layer_kernel(
    nf, nz, npos, fr,
    x, gy, keep, gain1, gain2, qkv_w, out_w, gate_w, up_w, down_w,
    block_out, rows_grad, total, gains, gy_out, hid_out, back,
    own_w, w, gy_pos, b_pos, send, stage, down, wd, hid, big, pair,
    a, qkv, ob, x1, db_rows, z_rows, tail,
    db_sib, db_rx, z_sib, z_rx,
    t_sib, t_rx, t_sems, t_home, g_sib, g_rx, g_sems, g_home, t_land, g_land,
    l_sib, l_rx, l_sems, l_late, l_zl,
    sems_w, sems_late, sems_gy, sems_b, sems_swap, sems_back, sems_in, sems_out, sems_hid, sem_down,
    sems_db, sems_db_home, sems_z, sems_z_home,
):
    d = x.shape[1]
    each = own_w.shape[1]
    lp = npos // nz
    width = send.shape[4]
    count = nf * nz * fr
    f, z = place()
    packer = Packer((gate_w, up_w), stage, sems_in, send)
    packer.begin()

    def fetch(p):
        return pltpu.make_async_copy(down_w.at[p], down, sem_down)

    fetch(0).start()
    greet(nf, nz, True)
    for i in range(3):
        own_w[i] = qkv_w[:, i * d : (i + 1) * d].astype(BF)
    own_w[3] = out_w[...].astype(BF)

    def span(at, size):
        return pl.ds(pl.multiple_of(at * size, size), size)

    per = d // count

    def rows_at(first, p):
        return big.at[first + p // per, pl.ds((p % per) * count, count)]

    places = (
        lambda zz, c: own_w.at[c],
        lambda ff, zz, c: w.at[c, span(ff * nz + zz, each)],
        lambda ff, c: w.at[c, span(ff, nz * each)],
    )
    early = Gather(nf, nz, *places, sems_w)
    late = LateGather(nf, nz, *places, sems_w, sems_late)

    def rows_gather(mine, every, sems):
        return Gather(
            nf, nz,
            lambda zz, p: mine.at[span(zz * lp + p, fr)],
            lambda ff, zz, p: every(p).at[span(ff * nz + zz, fr)],
            lambda ff, p: every(p).at[span(ff, nz * fr)],
            sems,
        )

    for c in LATE_W:
        late.begin(c)
    for c in EARLY_W:
        early.begin(c)
    kept = (gy[...].astype(F32) * keep[...]).astype(BF)
    gy_pos[...] = nn(by_position(npos * fr, npos, fr), kept).astype(BF)
    grads = rows_gather(gy_pos, lambda p: rows_at(0, p), sems_gy)
    rows = rows_gather(b_pos, lambda p: rows_at(2, p), sems_b)

    def pair_at(p):
        return lambda ff: pair.at[:, p, :, span(ff, width)]

    def send_at(p):
        return lambda ff: send.at[ff, :, p]

    swaps = [Swap(nf, send_at(p), pair_at(p), sems_swap.at[p]) for p in range(lp)]
    pieces = [(p, m) for p in range(lp) for m in MASKS]

    def pump(count):
        for p, m in pieces[:count]:
            swaps[p].start([m])
        del pieces[:count]

    for p in range(lp):
        grads.begin(p)
    packer.pack(0)
    pump(FILL[0])
    for c in LATE_W:
        late.relay(c)
    for i, c in enumerate(EARLY_W):
        early.along(c)
        if i == 0:
            for at in LATE_W:
                late.along(at)
        else:
            early.relay(EARLY_W[i - 1])
        if i + 1 < lp:
            packer.pack(i + 1)
    early.relay(EARLY_W[-1])
    for c in EARLY_W:
        early.rest(c)
    for p in range(lp):
        grads.along(p)
    for p in range(len(EARLY_W) + 1, lp):
        packer.pack(p)
    attention_start(x, gain1, a)
    for c in range(3):
        if c in LATE_W:
            for p in range(lp if c == LATE_W[0] else 0):
                grads.relay(p)
            pump(FILL[1] if c == LATE_W[0] else 0)
            late.rest(c)
        (late if c in LATE_W else early).whole(c)
        columns_of(a, w.at[c], c * d, qkv)
    attention_heads(npos, qkv, ob)
    pump(FILL[2])
    late.rest(3)
    late.whole(3)
    attention_end(npos, fr, x, gain2, w.at[3], ob, x1, b_pos)
    for p in range(lp):
        rows.begin(p)
    early.finish()
    late.finish()
    for p in range(lp):
        grads.rest(p)
    for p in range(lp):
        rows.along(p)
        if p >= 1:
            rows.relay(p - 1)
    rows.relay(lp - 1)
    pump(len(pieces))
    for p in range(lp):
        grads.whole(p)
    grads.finish()
    save_gy = pltpu.make_async_copy(big.at[: 2], gy_out, sems_out.at[0])
    save_gy.start()
    share = count // nf

    def sums(first, sib, rx, sems, home_sems, land):
        def at(ff, p):
            return rows_at(first, p).at[span(ff, share)]

        return RowSums(
            nf, nz, at, lambda p, m: at(flip(f, 2 * m), p), sib, rx, sems, home_sems, land, fr
        )

    s_db = sums(2, db_sib, db_rx, sems_db, sems_db_home, db_rows)
    s_z = sums(0, z_sib, z_rx, sems_z, sems_z_home, z_rows)

    def back_at(p):
        return lambda ff: back.at[ff, :, p]

    backs = [Swap(nf, send_at(p), back_at(p), sems_back.at[p]) for p in range(lp)]
    grad_pieces = [(p, m) for p in range(lp) for m in MASKS]

    def pump_back(size):
        for p, m in grad_pieces[:size]:
            backs[p].start([m])
        del grad_pieces[:size]

    def save_hid(p):
        return pltpu.make_async_copy(hid.at[p % 2], hid_out.at[p], sems_hid.at[p % 2])

    rows.rest(0)
    save_gy.wait()
    for p in range(lp):
        if p + 1 < lp:
            rows.rest(p + 1)
        fetch(p).wait()
        wd[...] = down[...].astype(BF)
        if p + 1 < lp:
            fetch(p + 1).start()
        rows.whole(p)
        rows.finish(p)
        swaps[p].finish()
        if p >= 2:
            save_hid(p - 2).wait()
        gy_rows, b_rows = rows_at(0, p), rows_at(2, p)
        feed(p, gy_rows, b_rows, pair, wd, hid.at[p % 2], send, b_rows, gy_rows)
        save_hid(p).start()
        s_db.pairs(p)
        if p >= 1:
            s_db.chips(p - 1)
        if p >= 2:
            s_db.across(p - 2)
        if p >= 3:
            s_db.home(p - 3)
        s_z.pairs(p)
    for name, last in (("chips", 1), ("across", 2)):
        for p in range(max(lp - last, 0), lp):
            getattr(s_db, name)(p)
        if name == "chips":
            s_z.chips(0)
            s_z.chips(1)
    pump_back(PUMP[0])
    for p in range(max(lp - 3, 0), lp):
        s_db.home(p)
    for p in range(2, lp):
        s_z.chips(p)
    for p in range(2):
        s_z.across(p)
    pump_back(PUMP[1])
    for p in range(lp):
        s_db.landed(p)
    s_db.finish()

    def terms_of(table):
        return (
            lambda ff, c: big.at[table[c], span(ff, nz * each)],
            lambda c, m: big.at[table[c], span(flip(f, 2 * m), nz * each)],
        )

    s_t = BlockSums(nf, nz, *terms_of(EARLY), t_sib, t_rx, t_sems, t_home, t_land, each)
    s_l = PosSums(nf, nz, *terms_of(LATE), l_sib, l_rx, l_sems, l_late, l_zl, each)
    s_g = BlockSums(
        nf, nz,
        lambda ff, c: tail.at[span(ff, nz * each)],
        lambda c, m: tail.at[span(flip(f, 2 * m), nz * each)],
        g_sib, g_rx, g_sems, g_home, g_land, each,
    )

    def both(step, c):
        group, at = (s_l, LATE.index(c)) if c in LATE else (s_t, EARLY.index(c))
        getattr(group, step)(at)

    dx1, dxb, do, dqkv = rows_grad, b_pos, gy_pos, qkv
    gain2_grad = attention_bwd_in(npos, fr, db_rows, gy, keep, x1, ob, gain2, dx1, dxb, big)
    both("pairs", 3)
    do[...] = nt(dxb[...], w[3]).astype(BF)
    both("along", 3)
    for p in range(2, lp):
        s_z.across(p)
    pump_back(PUMP[2])
    attention_bwd_heads(npos, qkv, do, dqkv)
    weight_terms(a, dqkv, 2 * d, big.at[2])
    both("pairs", 2)
    for p in range(lp):
        s_z.home(p)
    s_z.finish()
    pump_back(PUMP[3])
    weight_terms(a, dqkv, 0, big.at[0])
    both("pairs", 0)
    both("along", 2)
    weight_terms(a, dqkv, d, big.at[1])
    both("pairs", 1)
    both("chips", 0)
    gain1_grad = attention_bwd_rows(x, dqkv, w, gain1, dx1, rows_grad)
    gains_into(gain1_grad, gain2_grad, tail)
    s_g.pairs(0)
    both("chips", 1)
    s_g.chips(0)
    pump_back(PUMP[4])
    both("across", 0)
    both("across", 1)
    s_g.across(0)
    for c in LATE:
        both("chips", c)
    pump_back(PUMP[5])
    both("home", 0)
    both("home", 1)
    s_g.home(0)
    for c in LATE:
        both("across", c)
    pump_back(len(grad_pieces))
    for p in range(lp):
        s_z.landed(p)
    turned = nn(by_position(npos * fr, npos, fr, True), z_rows[...])
    block_out[...] = (keep[...] * (x1[...] + turned)).astype(BF)
    for group, table in ((s_t, EARLY), (s_l, LATE)):
        for at, c in enumerate(table):
            group.landed(at, total.at[:, pl.ds(c * d, d)])
    s_g.landed(0, gains)
    for p in range(max(lp - 2, 0), lp):
        save_hid(p).wait()
    for group in (s_t, s_l, s_g):
        group.finish()
    for swap in backs:
        swap.finish()


def last_local_kernel(pair, hid, gy, total, gate, up, down, qkv_grad, out_grad):
    nf, _, _, ffs, width = pair.shape
    d = gy.shape[2]

    @pl.when(pl.program_id(0) == 0)
    def _():
        qkv_grad[...] = total[:, : 3 * d]
        out_grad[...] = total[:, 3 * d :]

    for at, out in enumerate((gate, up)):
        out[0] = pair[:, at, 0].astype(F32).reshape(nf * ffs, width).T
    down[0] = nn(hid[0], gy[0])


def rms_norm(values, gain_vector):
    return (
        values * lax.rsqrt(jnp.mean(values * values, axis=-1, keepdims=True) + 1e-05) * gain_vector
    )


def attend(qkv_rows):
    frame_count = qkv_rows.shape[0]
    positions = qkv_rows.shape[1]
    split_rows = qkv_rows.reshape(frame_count, positions, 3, H, HD)
    queries = split_rows[:, :, 0]
    keys_all = split_rows[:, :, 1]
    values_all = split_rows[:, :, 2]
    scores = jnp.einsum("fqhe,fkhe->fhqk", queries, keys_all, preferred_element_type=F32) * (
        1.0 / math.sqrt(HD)
    )
    causal = jnp.arange(positions)[:, None] >= jnp.arange(positions)[None, :]
    scores = jnp.where(causal, scores, -1e30)
    weights = jax.nn.softmax(scores, axis=-1)
    mixed = jnp.einsum("fhqk,fkhe->fqhe", weights, values_all, preferred_element_type=F32)
    return mixed.reshape(frame_count, positions, H * HD)


def local_general(
    frame_rows,
    frame_mask,
    gain_attention,
    gain_feed,
    qkv_master,
    out_master,
    gate_master,
    up_master,
    down_master,
    out_cotangent,
):
    nf = lax.axis_size("frames")
    nz = lax.axis_size("pos")
    lp, dslice, ff = gate_master.shape
    ffs = down_master.shape[1]
    fr, npos, d = frame_rows.shape

    keep_rows = frame_mask.astype(F32)[:, None, None]
    inputs = frame_rows.astype(F32)

    def turned(w):
        return w.astype(BF).reshape(lp, dslice, nf, ffs).transpose(2, 0, 3, 1)

    def untwist(w):
        return w.transpose(1, 2, 0, 3).reshape(lp, ffs, d)

    def to_pos(rows):
        return rows.transpose(1, 0, 2).reshape(nz, lp * fr, d)

    def gathered(every):
        every = every.reshape(nf, nz, lp, fr, d)
        return every.transpose(2, 0, 1, 3, 4).reshape(lp, nf * nz * fr, d)

    rows_shape = jax.ShapeDtypeStruct((nf, nz, lp * fr, d), BF)
    back_shape = jax.ShapeDtypeStruct((npos * fr, d), BF)
    gather_sems = pltpu.SemaphoreType.DMA(Gather.sem_shape(nf, nz))
    swap_sems = pltpu.SemaphoreType.DMA(Swap.sem_shape(nf))

    def scattered(rows, ident):
        back = call(
            functools.partial(back_kernel, nf, nz, fr),
            ident,
            out_shape=back_shape,
            in_specs=[VM],
            out_specs=VM,
            scratch_shapes=HomeSums.scratch(nf, nz, lp, nz * fr, d),
        )(rows.reshape(lp, nf, nz * fr, d))
        return back.reshape(npos, fr, d).transpose(1, 0, 2)

    both = jnp.concatenate((qkv_master.astype(BF), out_master.astype(BF)), axis=1)
    pair = jnp.stack((turned(gate_master), turned(up_master)), axis=1)
    upstream = keep_rows * out_cotangent.astype(F32)
    own_rows = both.shape[0]
    w_all, gy_all, pair = call(
        functools.partial(first_kernel, nf, nz),
        0,
        out_shape=(
            jax.ShapeDtypeStruct((nf, nz) + both.shape, BF),
            rows_shape,
            jax.ShapeDtypeStruct(pair.shape, BF),
        ),
        in_specs=[ANY] * 3,
        out_specs=(ANY,) * 3,
        scratch_shapes=[gather_sems, gather_sems, swap_sems],
    )(both, to_pos(upstream.astype(BF)), pair)
    w_all = w_all.reshape(d, both.shape[1])
    w_qkv = w_all[:, : 3 * d]
    w_out = w_all[:, 3 * d :]
    gate_t = untwist(pair[:, 0])
    up_t = untwist(pair[:, 1])
    down = down_master.astype(BF)
    gy = gathered(gy_all)

    normed_one, norm_one_pull = jax.vjp(rms_norm, inputs, gain_attention)
    normed_low = normed_one.astype(BF)
    qkv_rows = jnp.einsum("fpd,de->fpe", normed_low, w_qkv, preferred_element_type=F32)
    mixed, attend_pull = jax.vjp(attend, qkv_rows)
    mixed_low = mixed.astype(BF)
    branch = jnp.einsum("fpd,de->fpe", mixed_low, w_out, preferred_element_type=F32)
    middle = inputs + branch
    normed_two, norm_two_pull = jax.vjp(rms_norm, middle, gain_feed)
    b_all = call(
        functools.partial(rows_kernel, nf, nz),
        1,
        out_shape=rows_shape,
        in_specs=[ANY],
        out_specs=ANY,
        scratch_shapes=[gather_sems],
    )(to_pos(normed_two.astype(BF)))
    b = gathered(b_all)

    gate_rows = jnp.einsum("prd,phd->phr", b, gate_t, preferred_element_type=F32)
    up_rows = jnp.einsum("prd,phd->phr", b, up_t, preferred_element_type=F32)
    hidden_grad = jnp.einsum("prd,phd->phr", gy, down, preferred_element_type=F32)
    sigma = jax.nn.sigmoid(gate_rows)
    silu_gate = gate_rows * sigma
    hidden = (silu_gate * up_rows).astype(BF)
    gate_back = (hidden_grad * up_rows * sigma * (1.0 + gate_rows * (1.0 - sigma))).astype(BF)
    up_back = (hidden_grad * silu_gate).astype(BF)
    db = jnp.einsum("phr,phd->prd", gate_back, gate_t, preferred_element_type=F32) + jnp.einsum(
        "phr,phd->prd", up_back, up_t, preferred_element_type=F32
    )
    back_rows = scattered(db.astype(BF), 2).astype(F32)
    feed = jnp.einsum("phr,phd->prd", hidden, down, preferred_element_type=F32)
    returned = scattered(feed.astype(BF), 3).astype(F32)
    block_out = (keep_rows * (middle + returned)).astype(BF)
    gate_grad = jnp.einsum("phr,prd->phd", gate_back, b, preferred_element_type=F32).astype(BF)
    up_grad = jnp.einsum("phr,prd->phd", up_back, b, preferred_element_type=F32).astype(BF)
    down_grad = jnp.einsum("phr,prd->phd", hidden, gy, preferred_element_type=F32)

    grads = jnp.stack((gate_grad, up_grad), axis=0).reshape(2, lp, ffs, nf, dslice)
    grads = grads.transpose(3, 0, 1, 2, 4)

    pulled_two = norm_two_pull(back_rows)
    middle_grad = upstream + pulled_two[0]
    branch_grad = middle_grad.astype(BF)
    out_weight_grad = jnp.einsum("fpd,fpe->de", mixed_low, branch_grad, preferred_element_type=F32)
    mixed_grad = jnp.einsum("fpe,de->fpd", branch_grad, w_out, preferred_element_type=F32)
    qkv_back = attend_pull(mixed_grad)[0].astype(BF)
    qkv_weight_grad = jnp.einsum("fpd,fpe->de", normed_low, qkv_back, preferred_element_type=F32)
    normed_grad = jnp.einsum("fpe,de->fpd", qkv_back, w_qkv, preferred_element_type=F32)
    pulled_one = norm_one_pull(normed_grad)
    rows_grad = middle_grad + pulled_one[0]

    gains = jnp.stack((pulled_one[1], pulled_two[1]), axis=1)
    gains_hi = gains.astype(BF)
    gains_lo = (gains - gains_hi.astype(F32)).astype(BF)
    unit = max(128, 2048 // own_rows)
    spare = -(4 * d + 4) % unit
    tail = jnp.concatenate((gains_hi, gains_lo, jnp.zeros((d, spare), BF)), axis=1)
    total = jnp.concatenate(
        (qkv_weight_grad.astype(BF), out_weight_grad.astype(BF), tail), axis=1
    )
    block = own_rows * total.shape[1] // 128
    total, grads = call(
        functools.partial(last_kernel, nf, nz),
        4,
        out_shape=(
            jax.ShapeDtypeStruct((block, 128), F32),
            jax.ShapeDtypeStruct(grads.shape, BF),
        ),
        in_specs=[VM, ANY],
        out_specs=(VM, ANY),
        scratch_shapes=HomeSums.scratch(nf, nz, 1, nz * block, 128)
        + [pltpu.VMEM((1, nz - 1, block, 128), BF), swap_sems],
    )(total.reshape(1, nf, nz * block, 128), grads)
    grads = grads.transpose(1, 2, 4, 0, 3).reshape(2, lp, dslice, ff).astype(F32)
    total = total.reshape(own_rows, 4 * d + 4 + spare)
    gain_grads = total[:, 4 * d : 4 * d + 2] + total[:, 4 * d + 2 : 4 * d + 4]
    return (
        block_out,
        rows_grad,
        gain_grads[:, 0],
        gain_grads[:, 1],
        total[:, : 3 * d],
        total[:, 3 * d : 4 * d],
        grads[0],
        grads[1],
        down_grad,
    )
def local_fused(
    frame_rows,
    frame_mask,
    gain_attention,
    gain_feed,
    qkv_master,
    out_master,
    gate_master,
    up_master,
    down_master,
    out_cotangent,
):
    nf = lax.axis_size("frames")
    nz = lax.axis_size("pos")
    lp, dslice, ff = gate_master.shape
    ffs = down_master.shape[1]
    fr, npos, d = frame_rows.shape
    rows = fr * npos
    each = qkv_master.shape[0]
    count = nf * nz * fr

    def make(shape, kind=BF):
        return jax.ShapeDtypeStruct(shape, kind)

    def vmem(shape, kind=BF):
        return pltpu.VMEM(shape, kind)

    def dma(*shape):
        return pltpu.SemaphoreType.DMA(shape)

    x = frame_rows.reshape(rows, d)
    gy = out_cotangent.reshape(rows, d)
    keep = jnp.broadcast_to(frame_mask.astype(F32)[:, None], (fr, npos)).reshape(rows, 1)
    gain1 = gain_attention.reshape(1, d)
    gain2 = gain_feed.reshape(1, d)
    gather_sems = dma(*Gather.sem_shape(nf, nz, 4))
    rows_sems = dma(*Gather.sem_shape(nf, nz, lp))
    swap_sems = dma(lp, *Swap.sem_shape(nf))
    pair_shape = (nf, 2, lp, ffs, dslice)
    row_scratch = HomeSums.scratch(nf, nz, lp, nz * fr, d)
    block_out, rows_grad, total, gains, gy_all, hid, back = call(
        functools.partial(layer_kernel, nf, nz, npos, fr),
        0,
        out_shape=(
            make((rows, d)),
            make((rows, d), F32),
            make((each, 4 * d), F32),
            make((each, 128), F32),
            make((2, d, d)),
            make((lp, ffs, count)),
            make(pair_shape),
        ),
        in_specs=[VM] * 7 + [ANY] * 3,
        out_specs=(VM,) * 4 + (ANY,) * 3,
        scratch_shapes=[
            vmem((4, each, d)),
            vmem((4, d, d)),
            vmem((rows, d)),
            vmem((rows, d)),
            vmem(pair_shape),
            vmem((2, dslice, ff), F32),
            vmem((ffs, d), F32),
            vmem((ffs, d)),
            vmem((2, ffs, count)),
            vmem((4, d, d)),
            vmem((2, lp, ffs, d)),
            vmem((rows, d)),
            vmem((rows, 3 * d)),
            vmem((rows, d)),
            vmem((rows, d), F32),
            vmem((rows, d)),
            vmem((rows, d)),
            vmem((d, 128)),
            *row_scratch[:2],
            *row_scratch[:2],
            *HomeSums.scratch(nf, nz, len(EARLY), nz * each, d),
            *HomeSums.scratch(nf, nz, 1, nz * each, 128),
            vmem((len(EARLY), nz - 1, each, d)),
            vmem((1, nz - 1, each, 128)),
            *PosSums.scratch(nf, nz, len(LATE), each, d),
            gather_sems,
            dma(*LateGather.late_shape(nf, nz, 4)),
            rows_sems,
            rows_sems,
            swap_sems,
            swap_sems,
            dma(2),
            dma(1),
            dma(2),
            pltpu.SemaphoreType.DMA,
            *row_scratch[2:],
            *row_scratch[2:],
        ],
    )(x, gy, keep, gain1, gain2, qkv_master, out_master, gate_master, up_master, down_master)
    gy_all = gy_all.reshape(lp, count, d)
    whole_block = pl.BlockSpec((1, dslice, ff), lambda p: (p, 0, 0))

    def once(*shape):
        return pl.BlockSpec(shape, lambda p: (0, 0))

    gate_grad, up_grad, down_grad, qkv_grad, out_grad = pl.pallas_call(
        last_local_kernel,
        grid=(lp,),
        out_shape=(
            make((lp, dslice, ff), F32),
            make((lp, dslice, ff), F32),
            make((lp, ffs, d), F32),
            make((each, 3 * d), F32),
            make((each, d), F32),
        ),
        in_specs=[
            pl.BlockSpec((nf, 2, 1, ffs, dslice), lambda p: (0, 0, p, 0, 0)),
            pl.BlockSpec((1, ffs, count), lambda p: (p, 0, 0)),
            pl.BlockSpec((1, count, d), lambda p: (p, 0, 0)),
            once(each, 4 * d),
        ],
        out_specs=(
            whole_block,
            whole_block,
            pl.BlockSpec((1, ffs, d), lambda p: (p, 0, 0)),
            once(each, 3 * d),
            once(each, d),
        ),
        compiler_params=pltpu.CompilerParams(vmem_limit_bytes=60 * 2**20),
    )(back, hid, gy_all, total)
    gains = gains[:, :2] + gains[:, 2:4]
    return (
        block_out.reshape(fr, npos, d),
        rows_grad.reshape(fr, npos, d),
        gains[:, 0],
        gains[:, 1],
        qkv_grad,
        out_grad,
        gate_grad,
        up_grad,
        down_grad,
    )


def local(*args):
    _, dslice, _ = args[6].shape
    sizes = lax.axis_size("frames"), lax.axis_size("pos")
    if sizes == (8, 4) and dslice % 128 == 0:
        return local_fused(*args)
    return local_general(*args)


def solution(mesh):
    in_specs = (
        P(("frames", "pos"), None, None),
        P(("frames", "pos")),
        P(),
        P(),
        P(("frames", "pos"), None),
        P(("frames", "pos"), None),
        P("pos", "frames", None),
        P("pos", "frames", None),
        P("pos", "frames", None),
        P(("frames", "pos"), None, None),
    )
    out_specs = (
        P(("frames", "pos"), None, None),
        P(("frames", "pos"), None, None),
        P(("frames", "pos")),
        P(("frames", "pos")),
        P(("frames", "pos"), None),
        P(("frames", "pos"), None),
        P("pos", "frames", None),
        P("pos", "frames", None),
        P("pos", "frames", None),
    )
    return jax.shard_map(local, mesh=mesh, in_specs=in_specs, out_specs=out_specs, check_vma=False)
```

```python
import functools
import math

import jax
import jax.numpy as jnp
from jax import lax
from jax.experimental import pallas as pl
from jax.experimental.pallas import tpu as pltpu
from jax.sharding import PartitionSpec as P

H = 16
HD = 64
BF = jnp.bfloat16
F32 = jnp.float32
MESH = pl.DeviceIdType.MESH
MASKS = (1, 2, 4, 3, 5, 6, 7)
FILL = (7, 9, 4)
PUMP = (7, 0, 12, 4, 2, 2)
LATE = (2, 3)
EARLY = tuple(c for c in range(4) if c not in LATE)
LATE_W = (2, 3)
EARLY_W = tuple(c for c in range(4) if c not in LATE_W)
ANY = pl.BlockSpec(memory_space=pl.ANY)
VM = pl.BlockSpec(memory_space=pltpu.VMEM)


def place():
    return lax.axis_index("frames"), lax.axis_index("pos")


def flip(index, mask):
    bit = 1
    while bit <= mask:
        if mask & bit:
            index = index + bit * (1 - 2 * ((index // bit) % 2))
        bit *= 2
    return index


def greet(nf, nz, every_frame):
    f, z = place()
    hops = [1] + [2 * m for m in range(1, nf // 2)]
    if every_frame:
        hops = list(range(1, nf))
    others = [(flip(f, h), z) for h in hops] + [(f, flip(z, k)) for k in range(1, nz)]
    barrier = pltpu.get_barrier_semaphore()
    for other in others:
        pl.semaphore_signal(barrier, inc=1, device_id=other, device_id_type=MESH)
    pl.semaphore_wait(barrier, len(others))


def remote(src, dst, send, recv, to):
    copy = pltpu.make_async_remote_copy(
        src_ref=src, dst_ref=dst, send_sem=send, recv_sem=recv, device_id=to, device_id_type=MESH
    )
    copy.start()
    return copy


def arrival(dst, send, recv):
    f, z = place()
    pltpu.make_async_remote_copy(
        src_ref=dst,
        dst_ref=dst,
        send_sem=send,
        recv_sem=recv,
        device_id=(flip(f, 1), z),
        device_id_type=MESH,
    ).wait_recv()


def relay_of(k):
    return 1 if k % 2 == 0 else 2


class Gather:
    def __init__(self, nf, nz, src_for, out_at, group_at, sems):
        self.nf, self.nz, self.nc = nf, nz, nf // 2
        self.f, self.z = place()
        self.src_for, self.out_at, self.group_at, self.sems = src_for, out_at, group_at, sems
        self.sent = []
        self.own = {}
        self.tree = self.nc == 4

    @staticmethod
    def sem_shape(nf, nz, parts=1):
        return (2, nz + nf, parts)

    def push(self, src, dst, hop, c, to):
        copy = remote(src, dst, self.sems.at[0, hop, c], self.sems.at[1, hop, c], to)
        self.sent.append((c, copy))

    def arrive(self, dst, hop, c):
        arrival(dst, self.sems.at[0, hop, c], self.sems.at[1, hop, c])

    def near(self, m, c):
        return self.group_at(flip(self.f, 2 * m), c)

    def begin(self, c=0):
        f, z = self.f, self.z
        for k in range(self.nz - 1, 0, -1):
            self.push(self.src_for(flip(z, k), c), self.out_at(f, z, c), k, c, (f, flip(z, k)))
        src, dst = self.src_for(z, c), self.out_at(f, z, c)
        self.own[c] = pltpu.make_async_copy(src, dst, self.sems.at[0, 0, c])
        self.own[c].start()

    def along(self, c=0):
        f, z = self.f, self.z
        self.own[c].wait()
        for k in range(1, self.nz):
            self.arrive(self.out_at(f, flip(z, k), c), k, c)
        group = self.near(0, c)
        for m in range(1, self.nc):
            if not (self.tree and m == 3):
                self.push(group, group, self.nz + m, c, (flip(f, 2 * m), z))
        self.push(group, group, self.nz + self.nc, c, (flip(f, 1), z))

    def over(self, m, c):
        f, z = self.f, self.z
        group = self.near(m, c)
        self.arrive(group, self.nz + m, c)
        if self.tree and m == relay_of(c):
            self.push(group, group, self.nz + 3, c, (flip(f, 2 * (3 - m)), z))
        self.push(group, group, self.nz + self.nc + m, c, (flip(f, 1), z))

    def relay(self, c=0):
        if self.tree:
            self.over(relay_of(c), c)

    def rest(self, c=0):
        for m in range(1, self.nc):
            if not (self.tree and m == relay_of(c)):
                self.over(m, c)

    def whole(self, c=0):
        for m in range(self.nc):
            group = self.group_at(flip(self.f, 2 * m + 1), c)
            self.arrive(group, self.nz + self.nc + m, c)

    def finish(self, part=None):
        for c, copy in self.sent:
            if part is None or c == part:
                copy.wait_send()
        self.sent = [(c, copy) for c, copy in self.sent if part is not None and c != part]


class LateGather(Gather):
    def __init__(self, nf, nz, src_for, out_at, group_at, sems, late_sems):
        super().__init__(nf, nz, src_for, out_at, group_at, sems)
        self.late_sems = late_sems

    @staticmethod
    def late_shape(nf, nz, parts):
        return (2, nz * (nf // 2), parts)

    def block(self, m, k, c):
        return self.out_at(flip(self.f, 2 * m), flip(self.z, k), c)

    def begin(self, c=0):
        f, z = self.f, self.z
        src, dst = self.src_for(z, c), self.out_at(f, z, c)
        for m in range(1, self.nc):
            if not (self.tree and m == 3):
                self.push(src, dst, self.nz + m, c, (flip(f, 2 * m), z))
        self.own[c] = pltpu.make_async_copy(src, dst, self.sems.at[0, 0, c])
        self.own[c].start()

    def relay(self, c=0):
        if self.tree:
            m = relay_of(c)
            block = self.block(m, 0, c)
            self.arrive(block, self.nz + m, c)
            to = (flip(self.f, 2 * (3 - m)), self.z)
            self.push(block, block, self.nz + 3, c, to)

    def along(self, c=0):
        self.own[c].wait()
        for m in range(1, self.nc):
            if not (self.tree and m == relay_of(c)):
                self.arrive(self.block(m, 0, c), self.nz + m, c)
        for k in range(self.nz - 1, 0, -1):
            for m in range(self.nc):
                block, hop = self.block(m, 0, c), k * self.nc + m
                send, recv = self.late_sems.at[0, hop, c], self.late_sems.at[1, hop, c]
                copy = remote(block, block, send, recv, (self.f, flip(self.z, k)))
                self.sent.append((c, copy))

    def rest(self, c=0):
        for m in range(self.nc):
            for k in range(1, self.nz):
                hop = k * self.nc + m
                send, recv = self.late_sems.at[0, hop, c], self.late_sems.at[1, hop, c]
                arrival(self.block(m, k, c), send, recv)
            group = self.near(m, c)
            self.push(group, group, self.nz + self.nc + m, c, (flip(self.f, 1), self.z))


class Swap:
    def __init__(self, nf, src_at, out_at, sems):
        self.nf, self.src_at, self.out_at, self.sems = nf, src_at, out_at, sems
        self.f, self.z = place()
        self.sent = []
        self.own = None

    @staticmethod
    def sem_shape(nf):
        return (2, nf)

    def start(self, masks=None):
        f, z = self.f, self.z
        if self.own is None:
            self.own = pltpu.make_async_copy(self.src_at(f), self.out_at(f), self.sems.at[0, 0])
            self.own.start()
        for m in masks or range(self.nf - 1, 0, -1):
            self.sent.append(
                remote(
                    self.src_at(flip(f, m)),
                    self.out_at(f),
                    self.sems.at[0, m],
                    self.sems.at[1, m],
                    (flip(f, m), z),
                )
            )

    def finish(self):
        self.own.wait()
        for copy in self.sent:
            copy.wait()


class Sums:
    def __init__(self, nf, nz, src_at, own_at, sib, rx, sems):
        self.nf, self.nz, self.nc = nf, nz, nf // 2
        self.f, self.z = place()
        self.src_at, self.own_at, self.sib, self.rx = src_at, own_at, sib, rx
        self.sems = sems
        self.sent = []
        self.tree = self.nc == 4

    @staticmethod
    def buffers(nf, parts, rows, columns):
        nc = nf // 2
        return [
            pltpu.VMEM((parts, nc, rows, columns), BF),
            pltpu.VMEM((parts, nc - 1, rows, columns), BF),
            pltpu.SemaphoreType.DMA((2, 2 * nc, parts)),
        ]

    def push(self, src, dst, sems, hop, k, to):
        self.sent.append(remote(src, dst, sems.at[0, hop, k], sems.at[1, hop, k], to))

    def arrive(self, dst, sems, hop, k):
        arrival(dst, sems.at[0, hop, k], sems.at[1, hop, k])

    def first(self, k):
        if self.tree:
            return [3, relay_of(k)]
        return list(range(self.nc - 1, 0, -1))

    def pairs(self, k):
        f, z = self.f, self.z
        order = self.first(k)
        for m in order + [m for m in range(self.nc - 1, -1, -1) if m not in order]:
            src = self.src_at(flip(f, 2 * m + 1), k)
            self.push(src, self.sib.at[k, m], self.sems, self.nc + m, k, (flip(f, 1), z))

    def chips(self, k):
        f, z = self.f, self.z
        for m in self.first(k):
            sib = self.sib.at[k, m]
            self.arrive(sib, self.sems, self.nc + m, k)
            add_into(sib, self.own_at(k, m), sib)
            hop, to = m, m
            if self.tree:
                hop, to = (2 if m == 3 else 1), relay_of(k)
            self.push(sib, self.rx.at[k, hop - 1], self.sems, hop, k, (flip(f, 2 * to), z))

    def across(self, k):
        if not self.tree:
            return
        m = 3 - relay_of(k)
        sib = self.sib.at[k, m]
        self.arrive(sib, self.sems, self.nc + m, k)
        self.arrive(self.rx.at[k, 1], self.sems, 2, k)
        add_into(sib, self.own_at(k, m), sib, self.rx.at[k, 1])
        self.push(sib, self.rx.at[k, 2], self.sems, 3, k, (flip(self.f, 2 * m), self.z))

    def total(self, k, out):
        self.arrive(self.sib.at[k, 0], self.sems, self.nc, k)
        terms = [self.own_at(k, 0), self.sib.at[k, 0]]
        for m in range(1, self.nc):
            if self.tree and m == 2:
                continue
            self.arrive(self.rx.at[k, m - 1], self.sems, m, k)
            terms.append(self.rx.at[k, m - 1])
        add_into(out, *terms)

    def finish(self):
        for copy in self.sent:
            copy.wait_send()


class HomeSums(Sums):
    def __init__(self, nf, nz, src_at, own_at, sib, rx, sems, home_sems, land, each):
        super().__init__(nf, nz, src_at, own_at, sib, rx, sems)
        self.home_sems, self.land, self.each = home_sems, land, each

    @staticmethod
    def scratch(nf, nz, parts, rows, columns):
        sib, rx, sems = Sums.buffers(nf, parts, rows, columns)
        return [sib, rx, sems, pltpu.SemaphoreType.DMA((2, nz, parts))]

    def rows_of(self, ref, at):
        return ref.at[pl.ds(pl.multiple_of(at * self.each, self.each), self.each)]

    def home(self, p):
        whole = self.sib.at[p, 0]
        self.total(p, whole)
        for k in range(self.nz - 1, 0, -1):
            src = self.rows_of(whole, flip(self.z, k))
            self.push(src, self.sent_to(k, p), self.home_sems, k, p, (self.f, flip(self.z, k)))


class RowSums(HomeSums):
    def at(self, zz, p):
        return self.rows_of(self.land, zz * self.sib.shape[0] + p)

    def sent_to(self, k, p):
        return self.at(self.z, p)

    def landed(self, p):
        self.at(self.z, p)[...] = self.rows_of(self.sib.at[p, 0], self.z)[...]
        for k in range(1, self.nz):
            self.arrive(self.at(flip(self.z, k), p), self.home_sems, k, p)


class BlockSums(HomeSums):
    def sent_to(self, k, p):
        return self.land.at[p, k - 1]

    def landed(self, p, out):
        terms = [self.rows_of(self.sib.at[p, 0], self.z)]
        for k in range(1, self.nz):
            self.arrive(self.land.at[p, k - 1], self.home_sems, k, p)
            terms.append(self.land.at[p, k - 1])
        add_into(out, *terms)


class PosSums(Sums):
    def __init__(self, nf, nz, src_at, own_at, sib, rx, sems, late_sems, zl, each):
        super().__init__(nf, nz, src_at, own_at, sib, rx, sems)
        self.late_sems, self.zl, self.each = late_sems, zl, each

    @staticmethod
    def scratch(nf, nz, parts, each, columns):
        nc = nf // 2
        return [
            pltpu.VMEM((parts, nc, nz * each, columns), BF),
            pltpu.VMEM((parts, nc - 1, each, columns), BF),
            pltpu.SemaphoreType.DMA((2, 2 * nc, parts)),
            pltpu.SemaphoreType.DMA((2, nz * nc, parts)),
            pltpu.VMEM((parts, nc, nz - 1, each, columns), BF),
        ]

    def rows_of(self, ref, at):
        return ref.at[pl.ds(pl.multiple_of(at * self.each, self.each), self.each)]

    def order(self, c):
        first = self.first(c)
        return first + [m for m in range(self.nc - 1, -1, -1) if m not in first]

    def along(self, c):
        for m in self.order(c):
            sib = self.sib.at[c, m]
            self.arrive(sib, self.sems, self.nc + m, c)
            add_into(sib, self.own_at(c, m), sib)
            for k in range(self.nz - 1, 0, -1):
                src = self.rows_of(sib, flip(self.z, k))
                to = (self.f, flip(self.z, k))
                self.push(src, self.zl.at[c, m, k - 1], self.late_sems, k * self.nc + m, c, to)

    def mine(self, m, c):
        terms = [self.rows_of(self.sib.at[c, m], self.z)]
        for k in range(1, self.nz):
            land = self.zl.at[c, m, k - 1]
            self.arrive(land, self.late_sems, k * self.nc + m, c)
            terms.append(land)
        return terms

    def chips(self, c):
        for m in self.first(c):
            terms = self.mine(m, c)
            add_into(terms[0], *terms)
            hop, to = m, m
            if self.tree:
                hop, to = (2 if m == 3 else 1), relay_of(c)
            chip = (flip(self.f, 2 * to), self.z)
            self.push(terms[0], self.rx.at[c, hop - 1], self.sems, hop, c, chip)

    def across(self, c):
        if not self.tree:
            return
        m = 3 - relay_of(c)
        terms = self.mine(m, c)
        self.arrive(self.rx.at[c, 1], self.sems, 2, c)
        add_into(terms[0], *terms, self.rx.at[c, 1])
        self.push(terms[0], self.rx.at[c, 2], self.sems, 3, c, (flip(self.f, 2 * m), self.z))

    def landed(self, c, out):
        terms = self.mine(0, c)
        for m in range(1, self.nc):
            if self.tree and m == 2:
                continue
            self.arrive(self.rx.at[c, m - 1], self.sems, m, c)
            terms.append(self.rx.at[c, m - 1])
        add_into(out, *terms)


def add_into(out, *terms):
    rows = out.shape[0]
    step = 16 if rows % 16 == 0 else rows

    def body(i, carry):
        at = pl.ds(pl.multiple_of(i * step, step), step)
        total = terms[0][at, :].astype(F32)
        for term in terms[1:]:
            total = total + term[at, :].astype(F32)
        out[at, :] = total.astype(out.dtype)
        return carry

    lax.fori_loop(0, rows // step, body, 0)


def call(kernel, ident, **kw):
    return pl.pallas_call(
        kernel,
        compiler_params=pltpu.CompilerParams(
            collective_id=ident, has_side_effects=True, vmem_limit_bytes=63 * 2**20
        ),
        **kw,
    )


def by_block(nf, nz, src_for, out, sems):
    return Gather(
        nf, nz, src_for, lambda ff, zz, c: out.at[ff, zz], lambda ff, c: out.at[ff], sems
    )


def first_kernel(nf, nz, attn, gy, pair, attn_all, gy_all, pair_all, s1, s2, s3):
    greet(nf, nz, True)
    weights = by_block(nf, nz, lambda zz, c: attn, attn_all, s1)
    rows = by_block(nf, nz, lambda zz, c: gy.at[zz], gy_all, s2)
    swap = Swap(nf, lambda ff: pair.at[ff], lambda ff: pair_all.at[ff], s3)
    gathers = (weights, rows)
    for g in gathers:
        g.begin()
    for step in ("along", "relay", "rest", "whole", "finish"):
        for g in gathers:
            getattr(g, step)()
        if step == "relay":
            swap.start()
    swap.finish()


def rows_kernel(nf, nz, b, b_all, s1):
    greet(nf, nz, False)
    rows = by_block(nf, nz, lambda zz, c: b.at[zz], b_all, s1)
    for step in (rows.begin, rows.along, rows.relay, rows.rest, rows.whole, rows.finish):
        step()


def chip_terms(terms):
    f, _ = place()
    return lambda ff, p: terms.at[p, ff], lambda p, m: terms.at[p, flip(f, 2 * m)]


def back_kernel(nf, nz, each, terms, out, sib, rx, sems, home_sems):
    greet(nf, nz, False)
    s = RowSums(nf, nz, *chip_terms(terms), sib, rx, sems, home_sems, out, each)
    for step in (s.pairs, s.chips, s.across, s.home, s.landed):
        for p in range(terms.shape[0]):
            step(p)
    s.finish()


def last_kernel(nf, nz, terms, pair, out, pair_all, sib, rx, sems, home_sems, land, s2):
    greet(nf, nz, True)
    s = BlockSums(nf, nz, *chip_terms(terms), sib, rx, sems, home_sems, land, out.shape[0])
    swap = Swap(nf, lambda ff: pair.at[ff], lambda ff: pair_all.at[ff], s2)
    s.pairs(0)
    swap.start()
    for step in (s.chips, s.across, s.home):
        step(0)
    s.landed(0, out)
    s.finish()
    swap.finish()


def contract(a, b, at_a, at_b):
    return lax.dot_general(a, b, (((at_a,), (at_b,)), ((), ())), preferred_element_type=F32)


def nt(a, b):
    return contract(a, b, 1, 1)


def nn(a, b):
    return contract(a, b, 1, 0)


def tn(a, b):
    return contract(a, b, 0, 0)


def by_position(rows, npos, fr, back=False):
    i = lax.broadcasted_iota(jnp.int32, (rows, rows), 0)
    j = lax.broadcasted_iota(jnp.int32, (rows, rows), 1)
    if back:
        i, j = j, i
    return ((i % fr) * npos + i // fr == j).astype(F32).astype(BF)


def causal(rows, npos):
    i = lax.broadcasted_iota(jnp.int32, (rows, rows), 0)
    j = lax.broadcasted_iota(jnp.int32, (rows, rows), 1)
    return jnp.logical_and(i // npos == j // npos, j <= i)


def soft(q, k, mask):
    s = jnp.where(mask, nt(q, k) * (1.0 / math.sqrt(HD)), -1e30)
    e = jnp.exp(s - jnp.max(s, axis=1, keepdims=True))
    return e / jnp.sum(e, axis=1, keepdims=True)

GROUP=128

def attention_start(x, gain1, a_out):
    xf = x[...].astype(F32)
    rinv1 = lax.rsqrt(jnp.mean(xf * xf, axis=1, keepdims=True) + 1e-05)
    a_out[...] = (xf * rinv1 * gain1[...]).astype(BF)


def columns_of(left, right, first, out):
    step = 512

    def body(i, c):
        at = pl.ds(pl.multiple_of(i * step, step), step)
        to = pl.ds(pl.multiple_of(first + i * step, step), step)
        out[:, to] = nn(left[...], right[:, at]).astype(out.dtype)
        return c

    lax.fori_loop(0, right.shape[1] // step, body, 0)


def attention_heads(npos, qkv, ob):
    rows, d = ob.shape
    mask = causal(GROUP, npos)
    low = lax.broadcasted_iota(jnp.int32, (GROUP, 2 * HD), 1) < HD
    def heads(i, c):
        for g in range(rows // GROUP):
            at = pl.ds(g * GROUP, GROUP)
            q, k, v = (qkv[at, pl.ds(pl.multiple_of(i * 2 * HD + t * d, 2 * HD), 2 * HD)] for t in range(3))
            zero = jnp.zeros_like(q)
            p0 = soft(jnp.where(low, q, zero), k, mask).astype(BF)
            p1 = soft(jnp.where(low, zero, q), k, mask).astype(BF)
            ob[at, pl.ds(pl.multiple_of(i * 2 * HD, 2 * HD), 2 * HD)] = jnp.where(low, nn(p0, v), nn(p1, v)).astype(BF)
        return c
    lax.fori_loop(0, d // (2 * HD), heads, 0)


def attention_end(npos, fr, x, gain2, w_out, ob, x1_out, b_out):
    rows, _ = x.shape
    columns_of(ob, w_out, 0, x1_out)
    x1 = x1_out[...] + x[...].astype(F32)
    x1_out[...] = x1
    rinv2 = lax.rsqrt(jnp.mean(x1 * x1, axis=1, keepdims=True) + 1e-05)
    b = (x1 * rinv2 * gain2[...]).astype(BF)
    b_out[...] = nn(by_position(rows, npos, fr), b).astype(BF)


def weight_terms(left, right, first, out):
    columns = out.shape[1]
    step = 512

    def body(i, c):
        at = pl.ds(pl.multiple_of(i * step, step), step)
        of = pl.ds(pl.multiple_of(first + i * step, step), step)
        out[:, at] = tn(left[...], right[:, of]).astype(BF)
        return c

    lax.fori_loop(0, columns // step, body, 0)


def attention_bwd_in(npos, fr, db_pos, gy, keep, x1_ref, ob, gain2, dx1_s, dxb, terms):
    rows, d = x1_ref.shape
    db = nn(by_position(rows, npos, fr, True), db_pos[...])
    x1 = x1_ref[...]
    rinv2 = lax.rsqrt(jnp.mean(x1 * x1, axis=1, keepdims=True) + 1e-05)
    n2 = db * gain2[...]
    inner = jnp.mean(n2 * x1, axis=1, keepdims=True)
    dx1 = keep[...] * gy[...].astype(F32) + rinv2 * n2 - x1 * (rinv2 * rinv2 * rinv2 * inner)
    dx1_s[...] = dx1
    dxb[...] = dx1.astype(BF)
    weight_terms(ob, dxb, 0, terms.at[3])
    return jnp.sum(db * x1 * rinv2, axis=0, keepdims=True)


def attention_bwd_heads(npos, qkv, do_s, dqkv):
    rows, d = do_s.shape
    mask = causal(GROUP, npos)
    low = lax.broadcasted_iota(jnp.int32, (GROUP, 2 * HD), 1) < HD
    scale = 1.0 / math.sqrt(HD)

    def heads(i, c):
        for g in range(rows // GROUP):
            at = pl.ds(g * GROUP, GROUP)
            lanes = [pl.ds(pl.multiple_of(i * 2 * HD + t * d, 2 * HD), 2 * HD) for t in range(3)]
            q, k, v = (qkv[at, l] for l in lanes)
            do = do_s[at, lanes[0]]
            zero = jnp.zeros_like(q)
            parts = []
            for h in range(2):
                keep = low if h == 0 else jnp.logical_not(low)
                p = soft(jnp.where(keep, q, zero), k, mask)
                dp = nt(jnp.where(keep, do, zero), v)
                ds = (p * (dp - jnp.sum(p * dp, axis=1, keepdims=True)) * scale).astype(BF)
                parts.append((nn(ds, k), tn(ds, q), tn(p.astype(BF), do)))
            for t in range(3):
                dqkv[at, lanes[t]] = jnp.where(low, parts[0][t], parts[1][t]).astype(BF)
        return c

    lax.fori_loop(0, d // (2 * HD), heads, 0)


def attention_bwd_rows(x, dqkv, w, gain1, dx1, rows_out):
    d = x.shape[1]
    da = sum(nt(dqkv[:, t * d : (t + 1) * d], w[t]) for t in range(3))
    xf = x[...].astype(F32)
    rinv1 = lax.rsqrt(jnp.mean(xf * xf, axis=1, keepdims=True) + 1e-05)
    n1 = da * gain1[...]
    inner = jnp.mean(n1 * xf, axis=1, keepdims=True)
    rows_out[...] = dx1[...] + rinv1 * n1 - xf * (rinv1 * rinv1 * rinv1 * inner)
    return jnp.sum(da * xf * rinv1, axis=0, keepdims=True)


def gains_into(gain1_grad, gain2_grad, terms):
    d = gain1_grad.shape[1]
    high1 = gain1_grad.astype(BF).astype(F32)
    high2 = gain2_grad.astype(BF).astype(F32)
    at = lax.broadcasted_iota(jnp.int32, (128, d), 0)
    tail = jnp.where(at == 0, high1, 0.0)
    tail = jnp.where(at == 1, high2, tail)
    tail = jnp.where(at == 2, gain1_grad - high1, tail)
    tail = jnp.where(at == 3, gain2_grad - high2, tail)
    terms[...] = tail.T.astype(BF)


class Packer:
    def __init__(self, masters, stage, sems, send):
        self.masters, self.stage, self.sems, self.send = masters, stage, sems, send

    def fetch(self, i, p):
        return pltpu.make_async_copy(self.masters[i].at[p], self.stage.at[i], self.sems.at[i])

    def begin(self):
        for i in range(len(self.masters)):
            self.fetch(i, 0).start()

    def pack(self, p):
        nf, _, lp, ffs, _ = self.send.shape
        for i in range(len(self.masters)):
            self.fetch(i, p).wait()
            turned = self.stage[i].T.astype(BF)
            for j in range(nf):
                self.send[j, i, p] = turned[j * ffs : (j + 1) * ffs]
            if p + 1 < lp:
                self.fetch(i, p + 1).start()


def feed(p, gy_rows, b_rows, pair, wd, hid_out, grads, db, z):
    nf, _, _, _, width = grads.shape
    b = b_rows[...]
    gate = nt(pair[0, p], b)
    up = nt(pair[1, p], b)
    dhid = nt(wd[...], gy_rows[...])
    s = jax.nn.sigmoid(gate)
    silu = gate * s
    hid = (silu * up).astype(BF)
    dgate = (dhid * up * s * (1.0 + gate * (1.0 - s))).astype(BF)
    dup = (dhid * silu).astype(BF)
    hid_out[...] = hid
    z[...] = tn(hid, wd[...]).astype(BF)
    for at, term in enumerate((dgate, dup)):
        grad = nn(term, b_rows[...]).astype(BF)
        for j in range(nf):
            grads[j, at, p] = grad[:, j * width : (j + 1) * width]
    db[...] = (tn(dgate, pair[0, p]) + tn(dup, pair[1, p])).astype(BF)


def layer_kernel(
    nf, nz, npos, fr,
    x, gy, mask, gain1, gain2, qkv_w, out_w, gate_w, up_w, down_w,
    block_out, rows_grad, total, gains, gy_out, hid_out, back,
    keep, own_w, w, gy_pos, b_pos, send, stage, down, wd, hid, big, pair,
    a, qkv, ob, x1, db_rows, z_rows, tail,
    db_sib, db_rx, z_sib, z_rx,
    t_sib, t_rx, t_sems, t_home, g_sib, g_rx, g_sems, g_home, t_land, g_land,
    l_sib, l_rx, l_sems, l_late, l_zl,
    sems_w, sems_late, sems_gy, sems_b, sems_swap, sems_back, sems_in, sems_out, sems_hid, sem_down,
    sems_db, sems_db_home, sems_z, sems_z_home,
):
    d = x.shape[1]
    each = own_w.shape[1]
    lp = npos // nz
    width = send.shape[4]
    count = nf * nz * fr
    f, z = place()
    packer = Packer((gate_w, up_w), stage, sems_in, send)
    packer.begin()

    def fetch(p):
        return pltpu.make_async_copy(down_w.at[p], down, sem_down)

    fetch(0).start()
    greet(nf, nz, True)
    for i in range(3):
        own_w[i] = qkv_w[:, i * d : (i + 1) * d].astype(BF)
    own_w[3] = out_w[...].astype(BF)

    def span(at, size):
        return pl.ds(pl.multiple_of(at * size, size), size)

    per = d // count

    def rows_at(first, p):
        return big.at[first + p // per, pl.ds((p % per) * count, count)]

    places = (
        lambda zz, c: own_w.at[c],
        lambda ff, zz, c: w.at[c, span(ff * nz + zz, each)],
        lambda ff, c: w.at[c, span(ff, nz * each)],
    )
    early = Gather(nf, nz, *places, sems_w)
    late = LateGather(nf, nz, *places, sems_w, sems_late)

    def rows_gather(mine, every, sems):
        return Gather(
            nf, nz,
            lambda zz, p: mine.at[span(zz * lp + p, fr)],
            lambda ff, zz, p: every(p).at[span(ff * nz + zz, fr)],
            lambda ff, p: every(p).at[span(ff, nz * fr)],
            sems,
        )

    for c in LATE_W:
        late.begin(c)
    for c in EARLY_W:
        early.begin(c)
    frame = lax.broadcasted_iota(jnp.int32, (npos * fr, fr), 0) // npos
    chosen = frame == lax.broadcasted_iota(jnp.int32, (npos * fr, fr), 1)
    alive = jnp.where(chosen, mask[...].astype(F32), 0.0)
    keep[...] = jnp.sum(alive, axis=1, keepdims=True)
    kept = (gy[...].astype(F32) * keep[...]).astype(BF)
    gy_pos[...] = nn(by_position(npos * fr, npos, fr), kept).astype(BF)
    grads = rows_gather(gy_pos, lambda p: rows_at(0, p), sems_gy)
    rows = rows_gather(b_pos, lambda p: rows_at(2, p), sems_b)

    def pair_at(p):
        return lambda ff: pair.at[:, p, :, span(ff, width)]

    def send_at(p):
        return lambda ff: send.at[ff, :, p]

    swaps = [Swap(nf, send_at(p), pair_at(p), sems_swap.at[p]) for p in range(lp)]
    pieces = [(p, m) for p in range(lp) for m in MASKS]

    def pump(count):
        for p, m in pieces[:count]:
            swaps[p].start([m])
        del pieces[:count]

    for p in range(lp):
        grads.begin(p)
    packer.pack(0)
    pump(FILL[0])
    for c in LATE_W:
        late.relay(c)
    for i, c in enumerate(EARLY_W):
        early.along(c)
        if i == 0:
            for at in LATE_W:
                late.along(at)
        else:
            early.relay(EARLY_W[i - 1])
        if i + 1 < lp:
            packer.pack(i + 1)
    early.relay(EARLY_W[-1])
    for c in EARLY_W:
        early.rest(c)
    for p in range(lp):
        grads.along(p)
    for p in range(len(EARLY_W) + 1, lp):
        packer.pack(p)
    attention_start(x, gain1, a)
    for c in range(3):
        if c in LATE_W:
            for p in range(lp if c == LATE_W[0] else 0):
                grads.relay(p)
            pump(FILL[1] if c == LATE_W[0] else 0)
            late.rest(c)
        (late if c in LATE_W else early).whole(c)
        columns_of(a, w.at[c], c * d, qkv)
    attention_heads(npos, qkv, ob)
    pump(FILL[2])
    late.rest(3)
    late.whole(3)
    attention_end(npos, fr, x, gain2, w.at[3], ob, x1, b_pos)
    for p in range(lp):
        rows.begin(p)
    early.finish()
    late.finish()
    for p in range(lp):
        grads.rest(p)
    for p in range(lp):
        rows.along(p)
        if p >= 1:
            rows.relay(p - 1)
    rows.relay(lp - 1)
    pump(len(pieces))
    for p in range(lp):
        grads.whole(p)
    grads.finish()
    save_gy = pltpu.make_async_copy(big.at[: 2], gy_out, sems_out.at[0])
    save_gy.start()
    share = count // nf

    def sums(first, sib, rx, sems, home_sems, land):
        def at(ff, p):
            return rows_at(first, p).at[span(ff, share)]

        return RowSums(
            nf, nz, at, lambda p, m: at(flip(f, 2 * m), p), sib, rx, sems, home_sems, land, fr
        )

    s_db = sums(2, db_sib, db_rx, sems_db, sems_db_home, db_rows)
    s_z = sums(0, z_sib, z_rx, sems_z, sems_z_home, z_rows)

    def back_at(p):
        return lambda ff: back.at[ff, :, p]

    backs = [Swap(nf, send_at(p), back_at(p), sems_back.at[p]) for p in range(lp)]
    grad_pieces = [(p, m) for p in range(lp) for m in MASKS]

    def pump_back(size):
        for p, m in grad_pieces[:size]:
            backs[p].start([m])
        del grad_pieces[:size]

    def save_hid(p):
        return pltpu.make_async_copy(hid.at[p % 2], hid_out.at[p], sems_hid.at[p % 2])

    rows.rest(0)
    save_gy.wait()
    for p in range(lp):
        if p + 1 < lp:
            rows.rest(p + 1)
        fetch(p).wait()
        wd[...] = down[...].astype(BF)
        if p + 1 < lp:
            fetch(p + 1).start()
        rows.whole(p)
        rows.finish(p)
        swaps[p].finish()
        if p >= 2:
            save_hid(p - 2).wait()
        gy_rows, b_rows = rows_at(0, p), rows_at(2, p)
        feed(p, gy_rows, b_rows, pair, wd, hid.at[p % 2], send, b_rows, gy_rows)
        save_hid(p).start()
        s_db.pairs(p)
        if p >= 1:
            s_db.chips(p - 1)
        if p >= 2:
            s_db.across(p - 2)
        if p >= 3:
            s_db.home(p - 3)
        s_z.pairs(p)
    for name, last in (("chips", 1), ("across", 2)):
        for p in range(max(lp - last, 0), lp):
            getattr(s_db, name)(p)
        if name == "chips":
            s_z.chips(0)
            s_z.chips(1)
    pump_back(PUMP[0])
    for p in range(max(lp - 3, 0), lp):
        s_db.home(p)
    for p in range(2, lp):
        s_z.chips(p)
    for p in range(2):
        s_z.across(p)
    pump_back(PUMP[1])
    for p in range(lp):
        s_db.landed(p)
    s_db.finish()

    def terms_of(table):
        return (
            lambda ff, c: big.at[table[c], span(ff, nz * each)],
            lambda c, m: big.at[table[c], span(flip(f, 2 * m), nz * each)],
        )

    s_t = BlockSums(nf, nz, *terms_of(EARLY), t_sib, t_rx, t_sems, t_home, t_land, each)
    s_l = PosSums(nf, nz, *terms_of(LATE), l_sib, l_rx, l_sems, l_late, l_zl, each)
    s_g = BlockSums(
        nf, nz,
        lambda ff, c: tail.at[span(ff, nz * each)],
        lambda c, m: tail.at[span(flip(f, 2 * m), nz * each)],
        g_sib, g_rx, g_sems, g_home, g_land, each,
    )

    def both(step, c):
        group, at = (s_l, LATE.index(c)) if c in LATE else (s_t, EARLY.index(c))
        getattr(group, step)(at)

    dx1, dxb, do, dqkv = rows_grad, b_pos, gy_pos, qkv
    gain2_grad = attention_bwd_in(npos, fr, db_rows, gy, keep, x1, ob, gain2, dx1, dxb, big)
    both("pairs", 3)
    do[...] = nt(dxb[...], w[3]).astype(BF)
    both("along", 3)
    for p in range(2, lp):
        s_z.across(p)
    pump_back(PUMP[2])
    attention_bwd_heads(npos, qkv, do, dqkv)
    weight_terms(a, dqkv, 2 * d, big.at[2])
    both("pairs", 2)
    for p in range(lp):
        s_z.home(p)
    s_z.finish()
    pump_back(PUMP[3])
    weight_terms(a, dqkv, 0, big.at[0])
    both("pairs", 0)
    both("along", 2)
    weight_terms(a, dqkv, d, big.at[1])
    both("pairs", 1)
    both("chips", 0)
    gain1_grad = attention_bwd_rows(x, dqkv, w, gain1, dx1, rows_grad)
    gains_into(gain1_grad, gain2_grad, tail)
    s_g.pairs(0)
    both("chips", 1)
    s_g.chips(0)
    pump_back(PUMP[4])
    both("across", 0)
    both("across", 1)
    s_g.across(0)
    for c in LATE:
        both("chips", c)
    pump_back(PUMP[5])
    both("home", 0)
    both("home", 1)
    s_g.home(0)
    for c in LATE:
        both("across", c)
    pump_back(len(grad_pieces))
    for p in range(lp):
        s_z.landed(p)
    turned = nn(by_position(npos * fr, npos, fr, True), z_rows[...])
    block_out[...] = (keep[...] * (x1[...] + turned)).astype(BF)
    for group, table in ((s_t, EARLY), (s_l, LATE)):
        for at, c in enumerate(table):
            group.landed(at, total.at[:, pl.ds(c * d, d)])
    s_g.landed(0, gains)
    for p in range(max(lp - 2, 0), lp):
        save_hid(p).wait()
    for group in (s_t, s_l, s_g):
        group.finish()
    for swap in backs:
        swap.finish()


def last_local_kernel(
    pair, hid, gy, total, gains, block_out, rows_grad,
    gate, up, down, qkv_grad, out_grad, gain1_grad, gain2_grad, y, dx,
):
    nf, _, _, ffs, width = pair.shape
    d = gy.shape[2]

    @pl.when(pl.program_id(0) == 0)
    def _():
        qkv_grad[...] = total[:, : 3 * d]
        out_grad[...] = total[:, 3 * d :]
        turned = gains[...].T
        gain1_grad[...] = turned[0] + turned[2]
        gain2_grad[...] = turned[1] + turned[3]

    y[...] = block_out[...]
    dx[...] = rows_grad[...]
    for at, out in enumerate((gate, up)):
        out[0] = pair[:, at, 0].astype(F32).reshape(nf * ffs, width).T
    down[0] = nn(hid[0], gy[0])


def rms_norm(values, gain_vector):
    return (
        values * lax.rsqrt(jnp.mean(values * values, axis=-1, keepdims=True) + 1e-05) * gain_vector
    )


def attend(qkv_rows):
    frame_count = qkv_rows.shape[0]
    positions = qkv_rows.shape[1]
    split_rows = qkv_rows.reshape(frame_count, positions, 3, H, HD)
    queries = split_rows[:, :, 0]
    keys_all = split_rows[:, :, 1]
    values_all = split_rows[:, :, 2]
    scores = jnp.einsum("fqhe,fkhe->fhqk", queries, keys_all, preferred_element_type=F32) * (
        1.0 / math.sqrt(HD)
    )
    causal = jnp.arange(positions)[:, None] >= jnp.arange(positions)[None, :]
    scores = jnp.where(causal, scores, -1e30)
    weights = jax.nn.softmax(scores, axis=-1)
    mixed = jnp.einsum("fhqk,fkhe->fqhe", weights, values_all, preferred_element_type=F32)
    return mixed.reshape(frame_count, positions, H * HD)


def local_general(
    frame_rows,
    frame_mask,
    gain_attention,
    gain_feed,
    qkv_master,
    out_master,
    gate_master,
    up_master,
    down_master,
    out_cotangent,
):
    nf = lax.axis_size("frames")
    nz = lax.axis_size("pos")
    lp, dslice, ff = gate_master.shape
    ffs = down_master.shape[1]
    fr, npos, d = frame_rows.shape

    keep_rows = frame_mask.astype(F32)[:, None, None]
    inputs = frame_rows.astype(F32)

    def turned(w):
        return w.astype(BF).reshape(lp, dslice, nf, ffs).transpose(2, 0, 3, 1)

    def untwist(w):
        return w.transpose(1, 2, 0, 3).reshape(lp, ffs, d)

    def to_pos(rows):
        return rows.transpose(1, 0, 2).reshape(nz, lp * fr, d)

    def gathered(every):
        every = every.reshape(nf, nz, lp, fr, d)
        return every.transpose(2, 0, 1, 3, 4).reshape(lp, nf * nz * fr, d)

    rows_shape = jax.ShapeDtypeStruct((nf, nz, lp * fr, d), BF)
    back_shape = jax.ShapeDtypeStruct((npos * fr, d), BF)
    gather_sems = pltpu.SemaphoreType.DMA(Gather.sem_shape(nf, nz))
    swap_sems = pltpu.SemaphoreType.DMA(Swap.sem_shape(nf))

    def scattered(rows, ident):
        back = call(
            functools.partial(back_kernel, nf, nz, fr),
            ident,
            out_shape=back_shape,
            in_specs=[VM],
            out_specs=VM,
            scratch_shapes=HomeSums.scratch(nf, nz, lp, nz * fr, d),
        )(rows.reshape(lp, nf, nz * fr, d))
        return back.reshape(npos, fr, d).transpose(1, 0, 2)

    both = jnp.concatenate((qkv_master.astype(BF), out_master.astype(BF)), axis=1)
    pair = jnp.stack((turned(gate_master), turned(up_master)), axis=1)
    upstream = keep_rows * out_cotangent.astype(F32)
    own_rows = both.shape[0]
    w_all, gy_all, pair = call(
        functools.partial(first_kernel, nf, nz),
        0,
        out_shape=(
            jax.ShapeDtypeStruct((nf, nz) + both.shape, BF),
            rows_shape,
            jax.ShapeDtypeStruct(pair.shape, BF),
        ),
        in_specs=[ANY] * 3,
        out_specs=(ANY,) * 3,
        scratch_shapes=[gather_sems, gather_sems, swap_sems],
    )(both, to_pos(upstream.astype(BF)), pair)
    w_all = w_all.reshape(d, both.shape[1])
    w_qkv = w_all[:, : 3 * d]
    w_out = w_all[:, 3 * d :]
    gate_t = untwist(pair[:, 0])
    up_t = untwist(pair[:, 1])
    down = down_master.astype(BF)
    gy = gathered(gy_all)

    normed_one, norm_one_pull = jax.vjp(rms_norm, inputs, gain_attention)
    normed_low = normed_one.astype(BF)
    qkv_rows = jnp.einsum("fpd,de->fpe", normed_low, w_qkv, preferred_element_type=F32)
    mixed, attend_pull = jax.vjp(attend, qkv_rows)
    mixed_low = mixed.astype(BF)
    branch = jnp.einsum("fpd,de->fpe", mixed_low, w_out, preferred_element_type=F32)
    middle = inputs + branch
    normed_two, norm_two_pull = jax.vjp(rms_norm, middle, gain_feed)
    b_all = call(
        functools.partial(rows_kernel, nf, nz),
        1,
        out_shape=rows_shape,
        in_specs=[ANY],
        out_specs=ANY,
        scratch_shapes=[gather_sems],
    )(to_pos(normed_two.astype(BF)))
    b = gathered(b_all)

    gate_rows = jnp.einsum("prd,phd->phr", b, gate_t, preferred_element_type=F32)
    up_rows = jnp.einsum("prd,phd->phr", b, up_t, preferred_element_type=F32)
    hidden_grad = jnp.einsum("prd,phd->phr", gy, down, preferred_element_type=F32)
    sigma = jax.nn.sigmoid(gate_rows)
    silu_gate = gate_rows * sigma
    hidden = (silu_gate * up_rows).astype(BF)
    gate_back = (hidden_grad * up_rows * sigma * (1.0 + gate_rows * (1.0 - sigma))).astype(BF)
    up_back = (hidden_grad * silu_gate).astype(BF)
    db = jnp.einsum("phr,phd->prd", gate_back, gate_t, preferred_element_type=F32) + jnp.einsum(
        "phr,phd->prd", up_back, up_t, preferred_element_type=F32
    )
    back_rows = scattered(db.astype(BF), 2).astype(F32)
    feed = jnp.einsum("phr,phd->prd", hidden, down, preferred_element_type=F32)
    returned = scattered(feed.astype(BF), 3).astype(F32)
    block_out = (keep_rows * (middle + returned)).astype(BF)
    gate_grad = jnp.einsum("phr,prd->phd", gate_back, b, preferred_element_type=F32).astype(BF)
    up_grad = jnp.einsum("phr,prd->phd", up_back, b, preferred_element_type=F32).astype(BF)
    down_grad = jnp.einsum("phr,prd->phd", hidden, gy, preferred_element_type=F32)

    grads = jnp.stack((gate_grad, up_grad), axis=0).reshape(2, lp, ffs, nf, dslice)
    grads = grads.transpose(3, 0, 1, 2, 4)

    pulled_two = norm_two_pull(back_rows)
    middle_grad = upstream + pulled_two[0]
    branch_grad = middle_grad.astype(BF)
    out_weight_grad = jnp.einsum("fpd,fpe->de", mixed_low, branch_grad, preferred_element_type=F32)
    mixed_grad = jnp.einsum("fpe,de->fpd", branch_grad, w_out, preferred_element_type=F32)
    qkv_back = attend_pull(mixed_grad)[0].astype(BF)
    qkv_weight_grad = jnp.einsum("fpd,fpe->de", normed_low, qkv_back, preferred_element_type=F32)
    normed_grad = jnp.einsum("fpe,de->fpd", qkv_back, w_qkv, preferred_element_type=F32)
    pulled_one = norm_one_pull(normed_grad)
    rows_grad = middle_grad + pulled_one[0]

    gains = jnp.stack((pulled_one[1], pulled_two[1]), axis=1)
    gains_hi = gains.astype(BF)
    gains_lo = (gains - gains_hi.astype(F32)).astype(BF)
    unit = max(128, 2048 // own_rows)
    spare = -(4 * d + 4) % unit
    tail = jnp.concatenate((gains_hi, gains_lo, jnp.zeros((d, spare), BF)), axis=1)
    total = jnp.concatenate(
        (qkv_weight_grad.astype(BF), out_weight_grad.astype(BF), tail), axis=1
    )
    block = own_rows * total.shape[1] // 128
    total, grads = call(
        functools.partial(last_kernel, nf, nz),
        4,
        out_shape=(
            jax.ShapeDtypeStruct((block, 128), F32),
            jax.ShapeDtypeStruct(grads.shape, BF),
        ),
        in_specs=[VM, ANY],
        out_specs=(VM, ANY),
        scratch_shapes=HomeSums.scratch(nf, nz, 1, nz * block, 128)
        + [pltpu.VMEM((1, nz - 1, block, 128), BF), swap_sems],
    )(total.reshape(1, nf, nz * block, 128), grads)
    grads = grads.transpose(1, 2, 4, 0, 3).reshape(2, lp, dslice, ff).astype(F32)
    total = total.reshape(own_rows, 4 * d + 4 + spare)
    gain_grads = total[:, 4 * d : 4 * d + 2] + total[:, 4 * d + 2 : 4 * d + 4]
    return (
        block_out,
        rows_grad,
        gain_grads[:, 0],
        gain_grads[:, 1],
        total[:, : 3 * d],
        total[:, 3 * d : 4 * d],
        grads[0],
        grads[1],
        down_grad,
    )
def local_fused(
    frame_rows,
    frame_mask,
    gain_attention,
    gain_feed,
    qkv_master,
    out_master,
    gate_master,
    up_master,
    down_master,
    out_cotangent,
):
    nf = lax.axis_size("frames")
    nz = lax.axis_size("pos")
    lp, dslice, ff = gate_master.shape
    ffs = down_master.shape[1]
    fr, npos, d = frame_rows.shape
    rows = fr * npos
    each = qkv_master.shape[0]
    count = nf * nz * fr

    def make(shape, kind=BF):
        return jax.ShapeDtypeStruct(shape, kind)

    def vmem(shape, kind=BF):
        return pltpu.VMEM(shape, kind)

    def dma(*shape):
        return pltpu.SemaphoreType.DMA(shape)

    x = frame_rows.reshape(rows, d)
    gy = out_cotangent.reshape(rows, d)
    mask = frame_mask.reshape(1, fr)
    gain1 = gain_attention.reshape(1, d)
    gain2 = gain_feed.reshape(1, d)
    gather_sems = dma(*Gather.sem_shape(nf, nz, 4))
    rows_sems = dma(*Gather.sem_shape(nf, nz, lp))
    swap_sems = dma(lp, *Swap.sem_shape(nf))
    pair_shape = (nf, 2, lp, ffs, dslice)
    row_scratch = HomeSums.scratch(nf, nz, lp, nz * fr, d)
    block_out, rows_grad, total, gains, gy_all, hid, back = call(
        functools.partial(layer_kernel, nf, nz, npos, fr),
        0,
        out_shape=(
            make((rows, d)),
            make((rows, d), F32),
            make((each, 4 * d), F32),
            make((each, 128), F32),
            make((2, d, d)),
            make((lp, ffs, count)),
            make(pair_shape),
        ),
        in_specs=[VM] * 7 + [ANY] * 3,
        out_specs=(VM,) * 4 + (ANY,) * 3,
        scratch_shapes=[
            vmem((rows, 1), F32),
            vmem((4, each, d)),
            vmem((4, d, d)),
            vmem((rows, d)),
            vmem((rows, d)),
            vmem(pair_shape),
            vmem((2, dslice, ff), F32),
            vmem((ffs, d), F32),
            vmem((ffs, d)),
            vmem((2, ffs, count)),
            vmem((4, d, d)),
            vmem((2, lp, ffs, d)),
            vmem((rows, d)),
            vmem((rows, 3 * d)),
            vmem((rows, d)),
            vmem((rows, d), F32),
            vmem((rows, d)),
            vmem((rows, d)),
            vmem((d, 128)),
            *row_scratch[:2],
            *row_scratch[:2],
            *HomeSums.scratch(nf, nz, len(EARLY), nz * each, d),
            *HomeSums.scratch(nf, nz, 1, nz * each, 128),
            vmem((len(EARLY), nz - 1, each, d)),
            vmem((1, nz - 1, each, 128)),
            *PosSums.scratch(nf, nz, len(LATE), each, d),
            gather_sems,
            dma(*LateGather.late_shape(nf, nz, 4)),
            rows_sems,
            rows_sems,
            swap_sems,
            swap_sems,
            dma(2),
            dma(1),
            dma(2),
            pltpu.SemaphoreType.DMA,
            *row_scratch[2:],
            *row_scratch[2:],
        ],
    )(x, gy, mask, gain1, gain2, qkv_master, out_master, gate_master, up_master, down_master)
    gy_all = gy_all.reshape(lp, count, d)
    whole_block = pl.BlockSpec((1, dslice, ff), lambda p: (p, 0, 0))

    def once(*shape):
        return pl.BlockSpec(shape, lambda p: (0, 0))

    part_block = pl.BlockSpec((rows // lp, d), lambda p: (p, 0))
    one = pl.BlockSpec((each,), lambda p: (0,))
    gate_grad, up_grad, down_grad, qkv_grad, out_grad, gain1_grad, gain2_grad, y, dx = pl.pallas_call(
        last_local_kernel,
        grid=(lp,),
        out_shape=(
            make((lp, dslice, ff), F32),
            make((lp, dslice, ff), F32),
            make((lp, ffs, d), F32),
            make((each, 3 * d), F32),
            make((each, d), F32),
            make((each,), F32),
            make((each,), F32),
            make((rows, d)),
            make((rows, d), F32),
        ),
        in_specs=[
            pl.BlockSpec((nf, 2, 1, ffs, dslice), lambda p: (0, 0, p, 0, 0)),
            pl.BlockSpec((1, ffs, count), lambda p: (p, 0, 0)),
            pl.BlockSpec((1, count, d), lambda p: (p, 0, 0)),
            once(each, 4 * d),
            once(each, 128),
            part_block,
            part_block,
        ],
        out_specs=(
            whole_block,
            whole_block,
            pl.BlockSpec((1, ffs, d), lambda p: (p, 0, 0)),
            once(each, 3 * d),
            once(each, d),
            one,
            one,
            part_block,
            part_block,
        ),
        compiler_params=pltpu.CompilerParams(vmem_limit_bytes=60 * 2**20),
    )(back, hid, gy_all, total, gains, block_out, rows_grad)
    return (
        y.reshape(fr, npos, d),
        dx.reshape(fr, npos, d),
        gain1_grad,
        gain2_grad,
        qkv_grad,
        out_grad,
        gate_grad,
        up_grad,
        down_grad,
    )


def local(*args):
    _, dslice, _ = args[6].shape
    sizes = lax.axis_size("frames"), lax.axis_size("pos")
    if sizes == (8, 4) and dslice % 128 == 0:
        return local_fused(*args)
    return local_general(*args)


def solution(mesh):
    in_specs = (
        P(("frames", "pos"), None, None),
        P(("frames", "pos")),
        P(),
        P(),
        P(("frames", "pos"), None),
        P(("frames", "pos"), None),
        P("pos", "frames", None),
        P("pos", "frames", None),
        P("pos", "frames", None),
        P(("frames", "pos"), None, None),
    )
    out_specs = (
        P(("frames", "pos"), None, None),
        P(("frames", "pos"), None, None),
        P(("frames", "pos")),
        P(("frames", "pos")),
        P(("frames", "pos"), None),
        P(("frames", "pos"), None),
        P("pos", "frames", None),
        P("pos", "frames", None),
        P("pos", "frames", None),
    )
    return jax.shard_map(local, mesh=mesh, in_specs=in_specs, out_specs=out_specs, check_vma=False)
```

```python
import functools
import math

import jax
import jax.numpy as jnp
from jax import lax
from jax.experimental import pallas as pl
from jax.experimental.pallas import tpu as pltpu
from jax.sharding import PartitionSpec as P

H = 16
HD = 64
BF = jnp.bfloat16
F32 = jnp.float32
MESH = pl.DeviceIdType.MESH
MASKS = (1, 2, 4, 3, 5, 6, 7)
FILL = (7, 9, 4)
PUMP = (8, 0, 12, 4, 2, 1)
LATE = (2, 3)
EARLY = tuple(c for c in range(4) if c not in LATE)
LATE_W = (2, 3)
EARLY_W = tuple(c for c in range(4) if c not in LATE_W)
ANY = pl.BlockSpec(memory_space=pl.ANY)
VM = pl.BlockSpec(memory_space=pltpu.VMEM)


def place():
    return lax.axis_index("frames"), lax.axis_index("pos")


def flip(index, mask):
    bit = 1
    while bit <= mask:
        if mask & bit:
            index = index + bit * (1 - 2 * ((index // bit) % 2))
        bit *= 2
    return index


def greet(nf, nz, every_frame):
    f, z = place()
    hops = [1] + [2 * m for m in range(1, nf // 2)]
    if every_frame:
        hops = list(range(1, nf))
    others = [(flip(f, h), z) for h in hops] + [(f, flip(z, k)) for k in range(1, nz)]
    barrier = pltpu.get_barrier_semaphore()
    for other in others:
        pl.semaphore_signal(barrier, inc=1, device_id=other, device_id_type=MESH)
    pl.semaphore_wait(barrier, len(others))


def remote(src, dst, send, recv, to):
    copy = pltpu.make_async_remote_copy(
        src_ref=src, dst_ref=dst, send_sem=send, recv_sem=recv, device_id=to, device_id_type=MESH
    )
    copy.start()
    return copy


def arrival(dst, send, recv):
    f, z = place()
    pltpu.make_async_remote_copy(
        src_ref=dst,
        dst_ref=dst,
        send_sem=send,
        recv_sem=recv,
        device_id=(flip(f, 1), z),
        device_id_type=MESH,
    ).wait_recv()


def relay_of(k):
    return 1 if k % 2 == 0 else 2


class Gather:
    def __init__(self, nf, nz, src_for, out_at, group_at, sems):
        self.nf, self.nz, self.nc = nf, nz, nf // 2
        self.f, self.z = place()
        self.src_for, self.out_at, self.group_at, self.sems = src_for, out_at, group_at, sems
        self.sent = []
        self.own = {}
        self.tree = self.nc == 4

    @staticmethod
    def sem_shape(nf, nz, parts=1):
        return (2, nz + nf, parts)

    def push(self, src, dst, hop, c, to):
        copy = remote(src, dst, self.sems.at[0, hop, c], self.sems.at[1, hop, c], to)
        self.sent.append((c, copy))

    def arrive(self, dst, hop, c):
        arrival(dst, self.sems.at[0, hop, c], self.sems.at[1, hop, c])

    def near(self, m, c):
        return self.group_at(flip(self.f, 2 * m), c)

    def begin(self, c=0):
        f, z = self.f, self.z
        for k in range(self.nz - 1, 0, -1):
            self.push(self.src_for(flip(z, k), c), self.out_at(f, z, c), k, c, (f, flip(z, k)))
        src, dst = self.src_for(z, c), self.out_at(f, z, c)
        self.own[c] = pltpu.make_async_copy(src, dst, self.sems.at[0, 0, c])
        self.own[c].start()

    def along(self, c=0):
        f, z = self.f, self.z
        self.own[c].wait()
        for k in range(1, self.nz):
            self.arrive(self.out_at(f, flip(z, k), c), k, c)
        group = self.near(0, c)
        for m in range(1, self.nc):
            if not (self.tree and m == 3):
                self.push(group, group, self.nz + m, c, (flip(f, 2 * m), z))
        self.push(group, group, self.nz + self.nc, c, (flip(f, 1), z))

    def over(self, m, c):
        f, z = self.f, self.z
        group = self.near(m, c)
        self.arrive(group, self.nz + m, c)
        if self.tree and m == relay_of(c):
            self.push(group, group, self.nz + 3, c, (flip(f, 2 * (3 - m)), z))
        self.push(group, group, self.nz + self.nc + m, c, (flip(f, 1), z))

    def relay(self, c=0):
        if self.tree:
            self.over(relay_of(c), c)

    def rest(self, c=0):
        for m in range(1, self.nc):
            if not (self.tree and m == relay_of(c)):
                self.over(m, c)

    def whole(self, c=0):
        for m in range(self.nc):
            group = self.group_at(flip(self.f, 2 * m + 1), c)
            self.arrive(group, self.nz + self.nc + m, c)

    def finish(self, part=None):
        for c, copy in self.sent:
            if part is None or c == part:
                copy.wait_send()
        self.sent = [(c, copy) for c, copy in self.sent if part is not None and c != part]


class LateGather(Gather):
    def __init__(self, nf, nz, src_for, out_at, group_at, sems, late_sems):
        super().__init__(nf, nz, src_for, out_at, group_at, sems)
        self.late_sems = late_sems

    @staticmethod
    def late_shape(nf, nz, parts):
        return (2, nz * (nf // 2), parts)

    def block(self, m, k, c):
        return self.out_at(flip(self.f, 2 * m), flip(self.z, k), c)

    def begin(self, c=0):
        f, z = self.f, self.z
        src, dst = self.src_for(z, c), self.out_at(f, z, c)
        for m in range(1, self.nc):
            if not (self.tree and m == 3):
                self.push(src, dst, self.nz + m, c, (flip(f, 2 * m), z))
        self.own[c] = pltpu.make_async_copy(src, dst, self.sems.at[0, 0, c])
        self.own[c].start()

    def relay(self, c=0):
        if self.tree:
            m = relay_of(c)
            block = self.block(m, 0, c)
            self.arrive(block, self.nz + m, c)
            to = (flip(self.f, 2 * (3 - m)), self.z)
            self.push(block, block, self.nz + 3, c, to)

    def along(self, c=0):
        self.own[c].wait()
        for m in range(1, self.nc):
            if not (self.tree and m == relay_of(c)):
                self.arrive(self.block(m, 0, c), self.nz + m, c)
        for k in range(self.nz - 1, 0, -1):
            for m in range(self.nc):
                block, hop = self.block(m, 0, c), k * self.nc + m
                send, recv = self.late_sems.at[0, hop, c], self.late_sems.at[1, hop, c]
                copy = remote(block, block, send, recv, (self.f, flip(self.z, k)))
                self.sent.append((c, copy))

    def rest(self, c=0):
        for m in range(self.nc):
            for k in range(1, self.nz):
                hop = k * self.nc + m
                send, recv = self.late_sems.at[0, hop, c], self.late_sems.at[1, hop, c]
                arrival(self.block(m, k, c), send, recv)
            group = self.near(m, c)
            self.push(group, group, self.nz + self.nc + m, c, (flip(self.f, 1), self.z))


class Swap:
    def __init__(self, nf, src_at, out_at, sems):
        self.nf, self.src_at, self.out_at, self.sems = nf, src_at, out_at, sems
        self.f, self.z = place()
        self.sent = []
        self.own = None

    @staticmethod
    def sem_shape(nf):
        return (2, nf)

    def start(self, masks=None):
        f, z = self.f, self.z
        if self.own is None:
            self.own = pltpu.make_async_copy(self.src_at(f), self.out_at(f), self.sems.at[0, 0])
            self.own.start()
        for m in masks or range(self.nf - 1, 0, -1):
            self.sent.append(
                remote(
                    self.src_at(flip(f, m)),
                    self.out_at(f),
                    self.sems.at[0, m],
                    self.sems.at[1, m],
                    (flip(f, m), z),
                )
            )

    def finish(self):
        self.own.wait()
        for copy in self.sent:
            copy.wait()


class Sums:
    def __init__(self, nf, nz, src_at, own_at, sib, rx, sems):
        self.nf, self.nz, self.nc = nf, nz, nf // 2
        self.f, self.z = place()
        self.src_at, self.own_at, self.sib, self.rx = src_at, own_at, sib, rx
        self.sems = sems
        self.sent = []
        self.tree = self.nc == 4

    @staticmethod
    def buffers(nf, parts, rows, columns):
        nc = nf // 2
        return [
            pltpu.VMEM((parts, nc, rows, columns), BF),
            pltpu.VMEM((parts, nc - 1, rows, columns), BF),
            pltpu.SemaphoreType.DMA((2, 2 * nc, parts)),
        ]

    def push(self, src, dst, sems, hop, k, to):
        self.sent.append(remote(src, dst, sems.at[0, hop, k], sems.at[1, hop, k], to))

    def arrive(self, dst, sems, hop, k):
        arrival(dst, sems.at[0, hop, k], sems.at[1, hop, k])

    def first(self, k):
        if self.tree:
            return [3, relay_of(k)]
        return list(range(self.nc - 1, 0, -1))

    def pairs(self, k):
        f, z = self.f, self.z
        order = self.first(k)
        for m in order + [m for m in range(self.nc - 1, -1, -1) if m not in order]:
            src = self.src_at(flip(f, 2 * m + 1), k)
            self.push(src, self.sib.at[k, m], self.sems, self.nc + m, k, (flip(f, 1), z))

    def chips(self, k):
        f, z = self.f, self.z
        for m in self.first(k):
            sib = self.sib.at[k, m]
            self.arrive(sib, self.sems, self.nc + m, k)
            add_into(sib, self.own_at(k, m), sib)
            hop, to = m, m
            if self.tree:
                hop, to = (2 if m == 3 else 1), relay_of(k)
            self.push(sib, self.rx.at[k, hop - 1], self.sems, hop, k, (flip(f, 2 * to), z))

    def across(self, k):
        if not self.tree:
            return
        m = 3 - relay_of(k)
        sib = self.sib.at[k, m]
        self.arrive(sib, self.sems, self.nc + m, k)
        self.arrive(self.rx.at[k, 1], self.sems, 2, k)
        add_into(sib, self.own_at(k, m), sib, self.rx.at[k, 1])
        self.push(sib, self.rx.at[k, 2], self.sems, 3, k, (flip(self.f, 2 * m), self.z))

    def total(self, k, out):
        self.arrive(self.sib.at[k, 0], self.sems, self.nc, k)
        terms = [self.own_at(k, 0), self.sib.at[k, 0]]
        for m in range(1, self.nc):
            if self.tree and m == 2:
                continue
            self.arrive(self.rx.at[k, m - 1], self.sems, m, k)
            terms.append(self.rx.at[k, m - 1])
        add_into(out, *terms)

    def finish(self):
        for copy in self.sent:
            copy.wait_send()


class HomeSums(Sums):
    def __init__(self, nf, nz, src_at, own_at, sib, rx, sems, home_sems, land, each):
        super().__init__(nf, nz, src_at, own_at, sib, rx, sems)
        self.home_sems, self.land, self.each = home_sems, land, each

    @staticmethod
    def scratch(nf, nz, parts, rows, columns):
        sib, rx, sems = Sums.buffers(nf, parts, rows, columns)
        return [sib, rx, sems, pltpu.SemaphoreType.DMA((2, nz, parts))]

    def rows_of(self, ref, at):
        return ref.at[pl.ds(pl.multiple_of(at * self.each, self.each), self.each)]

    def home(self, p):
        whole = self.sib.at[p, 0]
        self.total(p, whole)
        for k in range(self.nz - 1, 0, -1):
            src = self.rows_of(whole, flip(self.z, k))
            self.push(src, self.sent_to(k, p), self.home_sems, k, p, (self.f, flip(self.z, k)))


class RowSums(HomeSums):
    def at(self, zz, p):
        return self.rows_of(self.land, zz * self.sib.shape[0] + p)

    def sent_to(self, k, p):
        return self.at(self.z, p)

    def landed(self, p):
        self.at(self.z, p)[...] = self.rows_of(self.sib.at[p, 0], self.z)[...]
        for k in range(1, self.nz):
            self.arrive(self.at(flip(self.z, k), p), self.home_sems, k, p)


class BlockSums(HomeSums):
    def sent_to(self, k, p):
        return self.land.at[p, k - 1]

    def landed(self, p, out):
        terms = [self.rows_of(self.sib.at[p, 0], self.z)]
        for k in range(1, self.nz):
            self.arrive(self.land.at[p, k - 1], self.home_sems, k, p)
            terms.append(self.land.at[p, k - 1])
        add_into(out, *terms)


class PosSums(Sums):
    def __init__(self, nf, nz, src_at, own_at, sib, rx, sems, late_sems, zl, each):
        super().__init__(nf, nz, src_at, own_at, sib, rx, sems)
        self.late_sems, self.zl, self.each = late_sems, zl, each

    @staticmethod
    def scratch(nf, nz, parts, each, columns):
        nc = nf // 2
        return [
            pltpu.VMEM((parts, nc, nz * each, columns), BF),
            pltpu.VMEM((parts, nc - 1, each, columns), BF),
            pltpu.SemaphoreType.DMA((2, 2 * nc, parts)),
            pltpu.SemaphoreType.DMA((2, nz * nc, parts)),
            pltpu.VMEM((parts, nc, nz - 1, each, columns), BF),
        ]

    def rows_of(self, ref, at):
        return ref.at[pl.ds(pl.multiple_of(at * self.each, self.each), self.each)]

    def order(self, c):
        first = self.first(c)
        return first + [m for m in range(self.nc - 1, -1, -1) if m not in first]

    def along(self, c):
        for m in self.order(c):
            sib = self.sib.at[c, m]
            self.arrive(sib, self.sems, self.nc + m, c)
            add_into(sib, self.own_at(c, m), sib)
            for k in range(self.nz - 1, 0, -1):
                src = self.rows_of(sib, flip(self.z, k))
                to = (self.f, flip(self.z, k))
                self.push(src, self.zl.at[c, m, k - 1], self.late_sems, k * self.nc + m, c, to)

    def mine(self, m, c):
        terms = [self.rows_of(self.sib.at[c, m], self.z)]
        for k in range(1, self.nz):
            land = self.zl.at[c, m, k - 1]
            self.arrive(land, self.late_sems, k * self.nc + m, c)
            terms.append(land)
        return terms

    def chips(self, c):
        for m in self.first(c):
            terms = self.mine(m, c)
            add_into(terms[0], *terms)
            hop, to = m, m
            if self.tree:
                hop, to = (2 if m == 3 else 1), relay_of(c)
            chip = (flip(self.f, 2 * to), self.z)
            self.push(terms[0], self.rx.at[c, hop - 1], self.sems, hop, c, chip)

    def across(self, c):
        if not self.tree:
            return
        m = 3 - relay_of(c)
        terms = self.mine(m, c)
        self.arrive(self.rx.at[c, 1], self.sems, 2, c)
        add_into(terms[0], *terms, self.rx.at[c, 1])
        self.push(terms[0], self.rx.at[c, 2], self.sems, 3, c, (flip(self.f, 2 * m), self.z))

    def landed(self, c, out):
        terms = self.mine(0, c)
        for m in range(1, self.nc):
            if self.tree and m == 2:
                continue
            self.arrive(self.rx.at[c, m - 1], self.sems, m, c)
            terms.append(self.rx.at[c, m - 1])
        add_into(out, *terms)


def add_into(out, *terms):
    rows = out.shape[0]
    step = 16 if rows % 16 == 0 else rows

    def body(i, carry):
        at = pl.ds(pl.multiple_of(i * step, step), step)
        total = terms[0][at, :].astype(F32)
        for term in terms[1:]:
            total = total + term[at, :].astype(F32)
        out[at, :] = total.astype(out.dtype)
        return carry

    lax.fori_loop(0, rows // step, body, 0)


def call(kernel, ident, **kw):
    return pl.pallas_call(
        kernel,
        compiler_params=pltpu.CompilerParams(
            collective_id=ident, has_side_effects=True, vmem_limit_bytes=63 * 2**20
        ),
        **kw,
    )


def by_block(nf, nz, src_for, out, sems):
    return Gather(
        nf, nz, src_for, lambda ff, zz, c: out.at[ff, zz], lambda ff, c: out.at[ff], sems
    )


def first_kernel(nf, nz, attn, gy, pair, attn_all, gy_all, pair_all, s1, s2, s3):
    greet(nf, nz, True)
    weights = by_block(nf, nz, lambda zz, c: attn, attn_all, s1)
    rows = by_block(nf, nz, lambda zz, c: gy.at[zz], gy_all, s2)
    swap = Swap(nf, lambda ff: pair.at[ff], lambda ff: pair_all.at[ff], s3)
    gathers = (weights, rows)
    for g in gathers:
        g.begin()
    for step in ("along", "relay", "rest", "whole", "finish"):
        for g in gathers:
            getattr(g, step)()
        if step == "relay":
            swap.start()
    swap.finish()


def rows_kernel(nf, nz, b, b_all, s1):
    greet(nf, nz, False)
    rows = by_block(nf, nz, lambda zz, c: b.at[zz], b_all, s1)
    for step in (rows.begin, rows.along, rows.relay, rows.rest, rows.whole, rows.finish):
        step()


def chip_terms(terms):
    f, _ = place()
    return lambda ff, p: terms.at[p, ff], lambda p, m: terms.at[p, flip(f, 2 * m)]


def back_kernel(nf, nz, each, terms, out, sib, rx, sems, home_sems):
    greet(nf, nz, False)
    s = RowSums(nf, nz, *chip_terms(terms), sib, rx, sems, home_sems, out, each)
    for step in (s.pairs, s.chips, s.across, s.home, s.landed):
        for p in range(terms.shape[0]):
            step(p)
    s.finish()


def last_kernel(nf, nz, terms, pair, out, pair_all, sib, rx, sems, home_sems, land, s2):
    greet(nf, nz, True)
    s = BlockSums(nf, nz, *chip_terms(terms), sib, rx, sems, home_sems, land, out.shape[0])
    swap = Swap(nf, lambda ff: pair.at[ff], lambda ff: pair_all.at[ff], s2)
    s.pairs(0)
    swap.start()
    for step in (s.chips, s.across, s.home):
        step(0)
    s.landed(0, out)
    s.finish()
    swap.finish()


def contract(a, b, at_a, at_b):
    return lax.dot_general(a, b, (((at_a,), (at_b,)), ((), ())), preferred_element_type=F32)


def nt(a, b):
    return contract(a, b, 1, 1)


def nn(a, b):
    return contract(a, b, 1, 0)


def tn(a, b):
    return contract(a, b, 0, 0)


def by_position(rows, npos, fr, back=False):
    i = lax.broadcasted_iota(jnp.int32, (rows, rows), 0)
    j = lax.broadcasted_iota(jnp.int32, (rows, rows), 1)
    if back:
        i, j = j, i
    return ((i % fr) * npos + i // fr == j).astype(F32).astype(BF)


def causal(rows, npos):
    i = lax.broadcasted_iota(jnp.int32, (rows, rows), 0)
    j = lax.broadcasted_iota(jnp.int32, (rows, rows), 1)
    return jnp.logical_and(i // npos == j // npos, j <= i)


def soft(q, k, mask):
    s = jnp.where(mask, nt(q, k) * (1.0 / math.sqrt(HD)), -1e30)
    e = jnp.exp(s - jnp.max(s, axis=1, keepdims=True))
    return e / jnp.sum(e, axis=1, keepdims=True)

GROUP=128

def attention_start(x, gain1, a_out):
    xf = x[...].astype(F32)
    rinv1 = lax.rsqrt(jnp.mean(xf * xf, axis=1, keepdims=True) + 1e-05)
    a_out[...] = (xf * rinv1 * gain1[...]).astype(BF)


def columns_of(left, right, first, out):
    step = 512

    def body(i, c):
        at = pl.ds(pl.multiple_of(i * step, step), step)
        to = pl.ds(pl.multiple_of(first + i * step, step), step)
        out[:, to] = nn(left[...], right[:, at]).astype(out.dtype)
        return c

    lax.fori_loop(0, right.shape[1] // step, body, 0)


def attention_heads(npos, qkv, ob):
    rows, d = ob.shape
    mask = causal(GROUP, npos)
    low = lax.broadcasted_iota(jnp.int32, (GROUP, 2 * HD), 1) < HD
    def heads(i, c):
        for g in range(rows // GROUP):
            at = pl.ds(g * GROUP, GROUP)
            q, k, v = (qkv[at, pl.ds(pl.multiple_of(i * 2 * HD + t * d, 2 * HD), 2 * HD)] for t in range(3))
            zero = jnp.zeros_like(q)
            p0 = soft(jnp.where(low, q, zero), k, mask).astype(BF)
            p1 = soft(jnp.where(low, zero, q), k, mask).astype(BF)
            ob[at, pl.ds(pl.multiple_of(i * 2 * HD, 2 * HD), 2 * HD)] = jnp.where(low, nn(p0, v), nn(p1, v)).astype(BF)
        return c
    lax.fori_loop(0, d // (2 * HD), heads, 0)


def attention_end(npos, fr, x, gain2, w_out, ob, x1_out, b_out):
    rows, _ = x.shape
    columns_of(ob, w_out, 0, x1_out)
    x1 = x1_out[...] + x[...].astype(F32)
    x1_out[...] = x1
    rinv2 = lax.rsqrt(jnp.mean(x1 * x1, axis=1, keepdims=True) + 1e-05)
    b = (x1 * rinv2 * gain2[...]).astype(BF)
    b_out[...] = nn(by_position(rows, npos, fr), b).astype(BF)


def weight_terms(left, right, first, out):
    columns = out.shape[1]
    step = 512

    def body(i, c):
        at = pl.ds(pl.multiple_of(i * step, step), step)
        of = pl.ds(pl.multiple_of(first + i * step, step), step)
        out[:, at] = tn(left[...], right[:, of]).astype(BF)
        return c

    lax.fori_loop(0, columns // step, body, 0)


def attention_bwd_in(npos, fr, db_pos, gy, keep, x1_ref, ob, gain2, dx1_s, dxb, terms):
    rows, d = x1_ref.shape
    db = nn(by_position(rows, npos, fr, True), db_pos[...])
    x1 = x1_ref[...]
    rinv2 = lax.rsqrt(jnp.mean(x1 * x1, axis=1, keepdims=True) + 1e-05)
    n2 = db * gain2[...]
    inner = jnp.mean(n2 * x1, axis=1, keepdims=True)
    dx1 = keep[...] * gy[...].astype(F32) + rinv2 * n2 - x1 * (rinv2 * rinv2 * rinv2 * inner)
    dx1_s[...] = dx1
    dxb[...] = dx1.astype(BF)
    weight_terms(ob, dxb, 0, terms)
    return jnp.sum(db * x1 * rinv2, axis=0, keepdims=True)


def attention_bwd_heads(npos, qkv, do_s, dqkv):
    rows, d = do_s.shape
    mask = causal(GROUP, npos)
    low = lax.broadcasted_iota(jnp.int32, (GROUP, 2 * HD), 1) < HD
    scale = 1.0 / math.sqrt(HD)

    def heads(i, c):
        for g in range(rows // GROUP):
            at = pl.ds(g * GROUP, GROUP)
            lanes = [pl.ds(pl.multiple_of(i * 2 * HD + t * d, 2 * HD), 2 * HD) for t in range(3)]
            q, k, v = (qkv[at, l] for l in lanes)
            do = do_s[at, lanes[0]]
            zero = jnp.zeros_like(q)
            parts = []
            for h in range(2):
                keep = low if h == 0 else jnp.logical_not(low)
                p = soft(jnp.where(keep, q, zero), k, mask)
                dp = nt(jnp.where(keep, do, zero), v)
                ds = (p * (dp - jnp.sum(p * dp, axis=1, keepdims=True)) * scale).astype(BF)
                parts.append((nn(ds, k), tn(ds, q), tn(p.astype(BF), do)))
            for t in range(3):
                dqkv[at, lanes[t]] = jnp.where(low, parts[0][t], parts[1][t]).astype(BF)
        return c

    lax.fori_loop(0, d // (2 * HD), heads, 0)


def attention_bwd_rows(x, dqkv, w, gain1, dx1, rows_out):
    d = x.shape[1]
    da = sum(nt(dqkv[:, t * d : (t + 1) * d], w[t]) for t in range(3))
    xf = x[...].astype(F32)
    rinv1 = lax.rsqrt(jnp.mean(xf * xf, axis=1, keepdims=True) + 1e-05)
    n1 = da * gain1[...]
    inner = jnp.mean(n1 * xf, axis=1, keepdims=True)
    rows_out[...] = dx1[...] + rinv1 * n1 - xf * (rinv1 * rinv1 * rinv1 * inner)
    return jnp.sum(da * xf * rinv1, axis=0, keepdims=True)


def gains_into(gain1_grad, gain2_grad, terms):
    d = gain1_grad.shape[1]
    high1 = gain1_grad.astype(BF).astype(F32)
    high2 = gain2_grad.astype(BF).astype(F32)
    at = lax.broadcasted_iota(jnp.int32, (128, d), 0)
    tail = jnp.where(at == 0, high1, 0.0)
    tail = jnp.where(at == 1, high2, tail)
    tail = jnp.where(at == 2, gain1_grad - high1, tail)
    tail = jnp.where(at == 3, gain2_grad - high2, tail)
    terms[...] = tail.T.astype(BF)


class Packer:
    def __init__(self, masters, stage, sems, send):
        self.masters, self.stage, self.sems, self.send = masters, stage, sems, send

    def fetch(self, i, p):
        return pltpu.make_async_copy(self.masters[i].at[p], self.stage.at[i], self.sems.at[i])

    def begin(self):
        for i in range(len(self.masters)):
            self.fetch(i, 0).start()

    def pack(self, p):
        nf, _, lp, ffs, _ = self.send.shape
        for i in range(len(self.masters)):
            self.fetch(i, p).wait()
            turned = self.stage[i].T.astype(BF)
            for j in range(nf):
                self.send[j, i, p] = turned[j * ffs : (j + 1) * ffs]
            if p + 1 < lp:
                self.fetch(i, p + 1).start()


def feed(p, gy_rows, b_rows, pair, wd, hid_out, grads, db, send_db, z):
    nf, _, _, _, width = grads.shape
    b = b_rows[...]
    gate = nt(pair[0, p], b)
    up = nt(pair[1, p], b)
    dhid = nt(wd[...], gy_rows[...])
    s = jax.nn.sigmoid(gate)
    silu = gate * s
    dgate = (dhid * up * s * (1.0 + gate * (1.0 - s))).astype(BF)
    dup = (dhid * silu).astype(BF)
    hid = (silu * up).astype(BF)
    db[...] = (tn(dgate, pair[0, p]) + tn(dup, pair[1, p])).astype(BF)
    send_db()
    hid_out[...] = hid
    for at, term in enumerate((dgate, dup)):
        grad = nn(term, b_rows[...]).astype(BF)
        for j in range(nf):
            grads[j, at, p] = grad[:, j * width : (j + 1) * width]
    z[...] = tn(hid, wd[...]).astype(BF)


def layer_kernel(
    nf, nz, npos, fr,
    x, gy, mask, gain1, gain2, qkv_w, out_w, gate_w, up_w, down_w,
    block_out, rows_grad, total, gains, gy_out, hid_out, back,
    keep, own_w, w, gy_pos, b_pos, send, stage, down, wd, hid, big, pair,
    a, qkv, ob, x1, db_rows, z_rows, tail,
    db_sib, db_rx, z_sib, z_rx,
    t_sib, t_rx, t_sems, t_home, g_sib, g_rx, g_sems, g_home, t_land, g_land,
    l_sib, l_rx, l_sems, l_late, l_zl,
    sems_w, sems_late, sems_gy, sems_b, sems_swap, sems_back, sems_in, sems_out, sems_hid, sem_down,
    sems_db, sems_db_home, sems_z, sems_z_home,
):
    d = x.shape[1]
    each = own_w.shape[1]
    lp = npos // nz
    width = send.shape[4]
    count = nf * nz * fr
    f, z = place()
    packer = Packer((gate_w, up_w), stage, sems_in, send)
    packer.begin()

    def fetch(p):
        return pltpu.make_async_copy(down_w.at[p], down, sem_down)

    fetch(0).start()
    greet(nf, nz, True)
    for i in range(3):
        own_w[i] = qkv_w[:, i * d : (i + 1) * d].astype(BF)
    own_w[3] = out_w[...].astype(BF)

    def span(at, size):
        return pl.ds(pl.multiple_of(at * size, size), size)

    per = d // count

    def rows_at(first, p):
        return big.at[first + p // per, pl.ds((p % per) * count, count)]

    places = (
        lambda zz, c: own_w.at[c],
        lambda ff, zz, c: w.at[c, span(ff * nz + zz, each)],
        lambda ff, c: w.at[c, span(ff, nz * each)],
    )
    early = Gather(nf, nz, *places, sems_w)
    late = LateGather(nf, nz, *places, sems_w, sems_late)

    def rows_gather(mine, every, sems):
        return Gather(
            nf, nz,
            lambda zz, p: mine.at[span(zz * lp + p, fr)],
            lambda ff, zz, p: every(p).at[span(ff * nz + zz, fr)],
            lambda ff, p: every(p).at[span(ff, nz * fr)],
            sems,
        )

    for c in LATE_W:
        late.begin(c)
    for c in EARLY_W:
        early.begin(c)
    frame = lax.broadcasted_iota(jnp.int32, (npos * fr, fr), 0) // npos
    chosen = frame == lax.broadcasted_iota(jnp.int32, (npos * fr, fr), 1)
    alive = jnp.where(chosen, mask[...].astype(F32), 0.0)
    keep[...] = jnp.sum(alive, axis=1, keepdims=True)
    kept = (gy[...].astype(F32) * keep[...]).astype(BF)
    gy_pos[...] = nn(by_position(npos * fr, npos, fr), kept).astype(BF)
    grads = rows_gather(gy_pos, lambda p: rows_at(0, p), sems_gy)
    rows = rows_gather(b_pos, lambda p: rows_at(2, p), sems_b)

    def pair_at(p):
        return lambda ff: pair.at[:, p, :, span(ff, width)]

    def send_at(p):
        return lambda ff: send.at[ff, :, p]

    swaps = [Swap(nf, send_at(p), pair_at(p), sems_swap.at[p]) for p in range(lp)]
    pieces = [(p, m) for p in range(lp) for m in MASKS]

    def pump(count):
        for p, m in pieces[:count]:
            swaps[p].start([m])
        del pieces[:count]

    for p in range(lp):
        grads.begin(p)
    packer.pack(0)
    pump(FILL[0])
    for c in LATE_W:
        late.relay(c)
    for i, c in enumerate(EARLY_W):
        early.along(c)
        if i == 0:
            for at in LATE_W:
                late.along(at)
        else:
            early.relay(EARLY_W[i - 1])
        if i + 1 < lp:
            packer.pack(i + 1)
    early.relay(EARLY_W[-1])
    for c in EARLY_W:
        early.rest(c)
    for p in range(lp):
        grads.along(p)
    for p in range(len(EARLY_W) + 1, lp):
        packer.pack(p)
    attention_start(x, gain1, a)
    for c in range(3):
        if c in LATE_W:
            for p in range(lp if c == LATE_W[0] else 0):
                grads.relay(p)
            pump(FILL[1] if c == LATE_W[0] else 0)
            late.rest(c)
        (late if c in LATE_W else early).whole(c)
        columns_of(a, w.at[c], c * d, qkv)
    attention_heads(npos, qkv, ob)
    pump(FILL[2])
    late.rest(3)
    late.whole(3)
    attention_end(npos, fr, x, gain2, w.at[3], ob, x1, b_pos)
    for p in range(lp):
        rows.begin(p)
    early.finish()
    late.finish()
    for p in range(lp):
        grads.rest(p)
    for p in range(lp):
        rows.along(p)
        if p >= 1:
            rows.relay(p - 1)
    rows.relay(lp - 1)
    pump(len(pieces))
    for p in range(lp):
        grads.whole(p)
    grads.finish()
    save_gy = pltpu.make_async_copy(big.at[: 2], gy_out, sems_out.at[0])
    save_gy.start()
    share = count // nf

    def sums(first, sib, rx, sems, home_sems, land):
        def at(ff, p):
            return rows_at(first, p).at[span(ff, share)]

        return RowSums(
            nf, nz, at, lambda p, m: at(flip(f, 2 * m), p), sib, rx, sems, home_sems, land, fr
        )

    s_db = sums(0, db_sib, db_rx, sems_db, sems_db_home, db_rows)
    s_z = sums(2, z_sib, z_rx, sems_z, sems_z_home, z_rows)

    def back_at(p):
        return lambda ff: back.at[ff, :, p]

    backs = [Swap(nf, send_at(p), back_at(p), sems_back.at[p]) for p in range(lp)]
    grad_pieces = [(p, m) for p in range(lp) for m in MASKS]

    def pump_back(size):
        for p, m in grad_pieces[:size]:
            backs[p].start([m])
        del grad_pieces[:size]

    def save_hid(p):
        return pltpu.make_async_copy(hid.at[p % 2], hid_out.at[p], sems_hid.at[p % 2])

    rows.rest(0)
    save_gy.wait()
    for p in range(lp):
        if p + 1 < lp:
            rows.rest(p + 1)
        fetch(p).wait()
        wd[...] = down[...].astype(BF)
        if p + 1 < lp:
            fetch(p + 1).start()
        rows.whole(p)
        rows.finish(p)
        swaps[p].finish()
        if p >= 2:
            save_hid(p - 2).wait()
        gy_rows, b_rows = rows_at(0, p), rows_at(2, p)
        send_db = functools.partial(s_db.pairs, p)
        feed(p, gy_rows, b_rows, pair, wd, hid.at[p % 2], send, gy_rows, send_db, b_rows)
        save_hid(p).start()
        if p >= 1:
            s_db.chips(p - 1)
        if p >= 2:
            s_db.across(p - 2)
        if p >= 3:
            s_db.home(p - 3)
        s_z.pairs(p)
    for name, last in (("chips", 1), ("across", 2)):
        for p in range(max(lp - last, 0), lp):
            getattr(s_db, name)(p)
        if name == "chips":
            s_z.chips(0)
            s_z.chips(1)
    pump_back(PUMP[0])
    for p in range(max(lp - 3, 0), lp):
        s_db.home(p)
    for p in range(2, lp):
        s_z.chips(p)
    for p in range(2):
        s_z.across(p)
    pump_back(PUMP[1])
    for p in range(lp):
        s_db.landed(p)
    s_db.finish()

    def slot(c):
        return big.at[(c + 2) % 4]

    def terms_of(table):
        return (
            lambda ff, c: slot(table[c]).at[span(ff, nz * each)],
            lambda c, m: slot(table[c]).at[span(flip(f, 2 * m), nz * each)],
        )

    s_t = BlockSums(nf, nz, *terms_of(EARLY), t_sib, t_rx, t_sems, t_home, t_land, each)
    s_l = PosSums(nf, nz, *terms_of(LATE), l_sib, l_rx, l_sems, l_late, l_zl, each)
    s_g = BlockSums(
        nf, nz,
        lambda ff, c: tail.at[span(ff, nz * each)],
        lambda c, m: tail.at[span(flip(f, 2 * m), nz * each)],
        g_sib, g_rx, g_sems, g_home, g_land, each,
    )

    def both(step, c):
        group, at = (s_l, LATE.index(c)) if c in LATE else (s_t, EARLY.index(c))
        getattr(group, step)(at)

    dx1, dxb, do, dqkv = rows_grad, b_pos, gy_pos, qkv
    gain2_grad = attention_bwd_in(npos, fr, db_rows, gy, keep, x1, ob, gain2, dx1, dxb, slot(3))
    both("pairs", 3)
    do[...] = nt(dxb[...], w[3]).astype(BF)
    both("along", 3)
    for p in range(2, lp):
        s_z.across(p)
    pump_back(PUMP[2])
    attention_bwd_heads(npos, qkv, do, dqkv)
    weight_terms(a, dqkv, 2 * d, slot(2))
    both("pairs", 2)
    for p in range(lp):
        s_z.home(p)
    s_z.finish()
    pump_back(PUMP[3])
    weight_terms(a, dqkv, 0, slot(0))
    both("pairs", 0)
    both("along", 2)
    weight_terms(a, dqkv, d, slot(1))
    both("pairs", 1)
    both("chips", 0)
    gain1_grad = attention_bwd_rows(x, dqkv, w, gain1, dx1, rows_grad)
    gains_into(gain1_grad, gain2_grad, tail)
    s_g.pairs(0)
    both("chips", 1)
    s_g.chips(0)
    pump_back(PUMP[4])
    both("across", 0)
    both("across", 1)
    s_g.across(0)
    for c in LATE:
        both("chips", c)
    pump_back(PUMP[5])
    both("home", 0)
    both("home", 1)
    s_g.home(0)
    for c in LATE:
        both("across", c)
    pump_back(len(grad_pieces))
    for p in range(lp):
        s_z.landed(p)
    turned = nn(by_position(npos * fr, npos, fr, True), z_rows[...])
    block_out[...] = (keep[...] * (x1[...] + turned)).astype(BF)
    for group, table in ((s_t, EARLY), (s_l, LATE)):
        for at, c in enumerate(table):
            group.landed(at, total.at[:, pl.ds(c * d, d)])
    s_g.landed(0, gains)
    for p in range(max(lp - 2, 0), lp):
        save_hid(p).wait()
    for group in (s_t, s_l, s_g):
        group.finish()
    for swap in backs:
        swap.finish()


def last_local_kernel(
    pair, hid, gy, total, gains, block_out, rows_grad,
    gate, up, down, qkv_grad, out_grad, gain1_grad, gain2_grad, y, dx,
):
    nf, _, _, ffs, width = pair.shape
    d = gy.shape[2]

    @pl.when(pl.program_id(0) == 0)
    def _():
        qkv_grad[...] = total[:, : 3 * d]
        out_grad[...] = total[:, 3 * d :]
        turned = gains[...].T
        gain1_grad[...] = turned[0] + turned[2]
        gain2_grad[...] = turned[1] + turned[3]

    y[...] = block_out[...]
    dx[...] = rows_grad[...]
    for at, out in enumerate((gate, up)):
        out[0] = pair[:, at, 0].astype(F32).reshape(nf * ffs, width).T
    down[0] = nn(hid[0], gy[0])


def rms_norm(values, gain_vector):
    return (
        values * lax.rsqrt(jnp.mean(values * values, axis=-1, keepdims=True) + 1e-05) * gain_vector
    )


def attend(qkv_rows):
    frame_count = qkv_rows.shape[0]
    positions = qkv_rows.shape[1]
    split_rows = qkv_rows.reshape(frame_count, positions, 3, H, HD)
    queries = split_rows[:, :, 0]
    keys_all = split_rows[:, :, 1]
    values_all = split_rows[:, :, 2]
    scores = jnp.einsum("fqhe,fkhe->fhqk", queries, keys_all, preferred_element_type=F32) * (
        1.0 / math.sqrt(HD)
    )
    causal = jnp.arange(positions)[:, None] >= jnp.arange(positions)[None, :]
    scores = jnp.where(causal, scores, -1e30)
    weights = jax.nn.softmax(scores, axis=-1)
    mixed = jnp.einsum("fhqk,fkhe->fqhe", weights, values_all, preferred_element_type=F32)
    return mixed.reshape(frame_count, positions, H * HD)


def local_general(
    frame_rows,
    frame_mask,
    gain_attention,
    gain_feed,
    qkv_master,
    out_master,
    gate_master,
    up_master,
    down_master,
    out_cotangent,
):
    nf = lax.axis_size("frames")
    nz = lax.axis_size("pos")
    lp, dslice, ff = gate_master.shape
    ffs = down_master.shape[1]
    fr, npos, d = frame_rows.shape

    keep_rows = frame_mask.astype(F32)[:, None, None]
    inputs = frame_rows.astype(F32)

    def turned(w):
        return w.astype(BF).reshape(lp, dslice, nf, ffs).transpose(2, 0, 3, 1)

    def untwist(w):
        return w.transpose(1, 2, 0, 3).reshape(lp, ffs, d)

    def to_pos(rows):
        return rows.transpose(1, 0, 2).reshape(nz, lp * fr, d)

    def gathered(every):
        every = every.reshape(nf, nz, lp, fr, d)
        return every.transpose(2, 0, 1, 3, 4).reshape(lp, nf * nz * fr, d)

    rows_shape = jax.ShapeDtypeStruct((nf, nz, lp * fr, d), BF)
    back_shape = jax.ShapeDtypeStruct((npos * fr, d), BF)
    gather_sems = pltpu.SemaphoreType.DMA(Gather.sem_shape(nf, nz))
    swap_sems = pltpu.SemaphoreType.DMA(Swap.sem_shape(nf))

    def scattered(rows, ident):
        back = call(
            functools.partial(back_kernel, nf, nz, fr),
            ident,
            out_shape=back_shape,
            in_specs=[VM],
            out_specs=VM,
            scratch_shapes=HomeSums.scratch(nf, nz, lp, nz * fr, d),
        )(rows.reshape(lp, nf, nz * fr, d))
        return back.reshape(npos, fr, d).transpose(1, 0, 2)

    both = jnp.concatenate((qkv_master.astype(BF), out_master.astype(BF)), axis=1)
    pair = jnp.stack((turned(gate_master), turned(up_master)), axis=1)
    upstream = keep_rows * out_cotangent.astype(F32)
    own_rows = both.shape[0]
    w_all, gy_all, pair = call(
        functools.partial(first_kernel, nf, nz),
        0,
        out_shape=(
            jax.ShapeDtypeStruct((nf, nz) + both.shape, BF),
            rows_shape,
            jax.ShapeDtypeStruct(pair.shape, BF),
        ),
        in_specs=[ANY] * 3,
        out_specs=(ANY,) * 3,
        scratch_shapes=[gather_sems, gather_sems, swap_sems],
    )(both, to_pos(upstream.astype(BF)), pair)
    w_all = w_all.reshape(d, both.shape[1])
    w_qkv = w_all[:, : 3 * d]
    w_out = w_all[:, 3 * d :]
    gate_t = untwist(pair[:, 0])
    up_t = untwist(pair[:, 1])
    down = down_master.astype(BF)
    gy = gathered(gy_all)

    normed_one, norm_one_pull = jax.vjp(rms_norm, inputs, gain_attention)
    normed_low = normed_one.astype(BF)
    qkv_rows = jnp.einsum("fpd,de->fpe", normed_low, w_qkv, preferred_element_type=F32)
    mixed, attend_pull = jax.vjp(attend, qkv_rows)
    mixed_low = mixed.astype(BF)
    branch = jnp.einsum("fpd,de->fpe", mixed_low, w_out, preferred_element_type=F32)
    middle = inputs + branch
    normed_two, norm_two_pull = jax.vjp(rms_norm, middle, gain_feed)
    b_all = call(
        functools.partial(rows_kernel, nf, nz),
        1,
        out_shape=rows_shape,
        in_specs=[ANY],
        out_specs=ANY,
        scratch_shapes=[gather_sems],
    )(to_pos(normed_two.astype(BF)))
    b = gathered(b_all)

    gate_rows = jnp.einsum("prd,phd->phr", b, gate_t, preferred_element_type=F32)
    up_rows = jnp.einsum("prd,phd->phr", b, up_t, preferred_element_type=F32)
    hidden_grad = jnp.einsum("prd,phd->phr", gy, down, preferred_element_type=F32)
    sigma = jax.nn.sigmoid(gate_rows)
    silu_gate = gate_rows * sigma
    hidden = (silu_gate * up_rows).astype(BF)
    gate_back = (hidden_grad * up_rows * sigma * (1.0 + gate_rows * (1.0 - sigma))).astype(BF)
    up_back = (hidden_grad * silu_gate).astype(BF)
    db = jnp.einsum("phr,phd->prd", gate_back, gate_t, preferred_element_type=F32) + jnp.einsum(
        "phr,phd->prd", up_back, up_t, preferred_element_type=F32
    )
    back_rows = scattered(db.astype(BF), 2).astype(F32)
    feed = jnp.einsum("phr,phd->prd", hidden, down, preferred_element_type=F32)
    returned = scattered(feed.astype(BF), 3).astype(F32)
    block_out = (keep_rows * (middle + returned)).astype(BF)
    gate_grad = jnp.einsum("phr,prd->phd", gate_back, b, preferred_element_type=F32).astype(BF)
    up_grad = jnp.einsum("phr,prd->phd", up_back, b, preferred_element_type=F32).astype(BF)
    down_grad = jnp.einsum("phr,prd->phd", hidden, gy, preferred_element_type=F32)

    grads = jnp.stack((gate_grad, up_grad), axis=0).reshape(2, lp, ffs, nf, dslice)
    grads = grads.transpose(3, 0, 1, 2, 4)

    pulled_two = norm_two_pull(back_rows)
    middle_grad = upstream + pulled_two[0]
    branch_grad = middle_grad.astype(BF)
    out_weight_grad = jnp.einsum("fpd,fpe->de", mixed_low, branch_grad, preferred_element_type=F32)
    mixed_grad = jnp.einsum("fpe,de->fpd", branch_grad, w_out, preferred_element_type=F32)
    qkv_back = attend_pull(mixed_grad)[0].astype(BF)
    qkv_weight_grad = jnp.einsum("fpd,fpe->de", normed_low, qkv_back, preferred_element_type=F32)
    normed_grad = jnp.einsum("fpe,de->fpd", qkv_back, w_qkv, preferred_element_type=F32)
    pulled_one = norm_one_pull(normed_grad)
    rows_grad = middle_grad + pulled_one[0]

    gains = jnp.stack((pulled_one[1], pulled_two[1]), axis=1)
    gains_hi = gains.astype(BF)
    gains_lo = (gains - gains_hi.astype(F32)).astype(BF)
    unit = max(128, 2048 // own_rows)
    spare = -(4 * d + 4) % unit
    tail = jnp.concatenate((gains_hi, gains_lo, jnp.zeros((d, spare), BF)), axis=1)
    total = jnp.concatenate(
        (qkv_weight_grad.astype(BF), out_weight_grad.astype(BF), tail), axis=1
    )
    block = own_rows * total.shape[1] // 128
    total, grads = call(
        functools.partial(last_kernel, nf, nz),
        4,
        out_shape=(
            jax.ShapeDtypeStruct((block, 128), F32),
            jax.ShapeDtypeStruct(grads.shape, BF),
        ),
        in_specs=[VM, ANY],
        out_specs=(VM, ANY),
        scratch_shapes=HomeSums.scratch(nf, nz, 1, nz * block, 128)
        + [pltpu.VMEM((1, nz - 1, block, 128), BF), swap_sems],
    )(total.reshape(1, nf, nz * block, 128), grads)
    grads = grads.transpose(1, 2, 4, 0, 3).reshape(2, lp, dslice, ff).astype(F32)
    total = total.reshape(own_rows, 4 * d + 4 + spare)
    gain_grads = total[:, 4 * d : 4 * d + 2] + total[:, 4 * d + 2 : 4 * d + 4]
    return (
        block_out,
        rows_grad,
        gain_grads[:, 0],
        gain_grads[:, 1],
        total[:, : 3 * d],
        total[:, 3 * d : 4 * d],
        grads[0],
        grads[1],
        down_grad,
    )
def local_fused(
    frame_rows,
    frame_mask,
    gain_attention,
    gain_feed,
    qkv_master,
    out_master,
    gate_master,
    up_master,
    down_master,
    out_cotangent,
):
    nf = lax.axis_size("frames")
    nz = lax.axis_size("pos")
    lp, dslice, ff = gate_master.shape
    ffs = down_master.shape[1]
    fr, npos, d = frame_rows.shape
    rows = fr * npos
    each = qkv_master.shape[0]
    count = nf * nz * fr

    def make(shape, kind=BF):
        return jax.ShapeDtypeStruct(shape, kind)

    def vmem(shape, kind=BF):
        return pltpu.VMEM(shape, kind)

    def dma(*shape):
        return pltpu.SemaphoreType.DMA(shape)

    x = frame_rows.reshape(rows, d)
    gy = out_cotangent.reshape(rows, d)
    mask = frame_mask.reshape(1, fr)
    gain1 = gain_attention.reshape(1, d)
    gain2 = gain_feed.reshape(1, d)
    gather_sems = dma(*Gather.sem_shape(nf, nz, 4))
    rows_sems = dma(*Gather.sem_shape(nf, nz, lp))
    swap_sems = dma(lp, *Swap.sem_shape(nf))
    pair_shape = (nf, 2, lp, ffs, dslice)
    row_scratch = HomeSums.scratch(nf, nz, lp, nz * fr, d)
    block_out, rows_grad, total, gains, gy_all, hid, back = call(
        functools.partial(layer_kernel, nf, nz, npos, fr),
        0,
        out_shape=(
            make((rows, d)),
            make((rows, d), F32),
            make((each, 4 * d), F32),
            make((each, 128), F32),
            make((2, d, d)),
            make((lp, ffs, count)),
            make(pair_shape),
        ),
        in_specs=[VM] * 7 + [ANY] * 3,
        out_specs=(VM,) * 4 + (ANY,) * 3,
        scratch_shapes=[
            vmem((rows, 1), F32),
            vmem((4, each, d)),
            vmem((4, d, d)),
            vmem((rows, d)),
            vmem((rows, d)),
            vmem(pair_shape),
            vmem((2, dslice, ff), F32),
            vmem((ffs, d), F32),
            vmem((ffs, d)),
            vmem((2, ffs, count)),
            vmem((4, d, d)),
            vmem((2, lp, ffs, d)),
            vmem((rows, d)),
            vmem((rows, 3 * d)),
            vmem((rows, d)),
            vmem((rows, d), F32),
            vmem((rows, d)),
            vmem((rows, d)),
            vmem((d, 128)),
            *row_scratch[:2],
            *row_scratch[:2],
            *HomeSums.scratch(nf, nz, len(EARLY), nz * each, d),
            *HomeSums.scratch(nf, nz, 1, nz * each, 128),
            vmem((len(EARLY), nz - 1, each, d)),
            vmem((1, nz - 1, each, 128)),
            *PosSums.scratch(nf, nz, len(LATE), each, d),
            gather_sems,
            dma(*LateGather.late_shape(nf, nz, 4)),
            rows_sems,
            rows_sems,
            swap_sems,
            swap_sems,
            dma(2),
            dma(1),
            dma(2),
            pltpu.SemaphoreType.DMA,
            *row_scratch[2:],
            *row_scratch[2:],
        ],
    )(x, gy, mask, gain1, gain2, qkv_master, out_master, gate_master, up_master, down_master)
    gy_all = gy_all.reshape(lp, count, d)
    whole_block = pl.BlockSpec((1, dslice, ff), lambda p: (p, 0, 0))

    def once(*shape):
        return pl.BlockSpec(shape, lambda p: (0, 0))

    part_block = pl.BlockSpec((rows // lp, d), lambda p: (p, 0))
    one = pl.BlockSpec((each,), lambda p: (0,))
    gate_grad, up_grad, down_grad, qkv_grad, out_grad, gain1_grad, gain2_grad, y, dx = pl.pallas_call(
        last_local_kernel,
        grid=(lp,),
        out_shape=(
            make((lp, dslice, ff), F32),
            make((lp, dslice, ff), F32),
            make((lp, ffs, d), F32),
            make((each, 3 * d), F32),
            make((each, d), F32),
            make((each,), F32),
            make((each,), F32),
            make((rows, d)),
            make((rows, d), F32),
        ),
        in_specs=[
            pl.BlockSpec((nf, 2, 1, ffs, dslice), lambda p: (0, 0, p, 0, 0)),
            pl.BlockSpec((1, ffs, count), lambda p: (p, 0, 0)),
            pl.BlockSpec((1, count, d), lambda p: (p, 0, 0)),
            once(each, 4 * d),
            once(each, 128),
            part_block,
            part_block,
        ],
        out_specs=(
            whole_block,
            whole_block,
            pl.BlockSpec((1, ffs, d), lambda p: (p, 0, 0)),
            once(each, 3 * d),
            once(each, d),
            one,
            one,
            part_block,
            part_block,
        ),
        compiler_params=pltpu.CompilerParams(vmem_limit_bytes=60 * 2**20),
    )(back, hid, gy_all, total, gains, block_out, rows_grad)
    return (
        y.reshape(fr, npos, d),
        dx.reshape(fr, npos, d),
        gain1_grad,
        gain2_grad,
        qkv_grad,
        out_grad,
        gate_grad,
        up_grad,
        down_grad,
    )


def local(*args):
    _, dslice, _ = args[6].shape
    sizes = lax.axis_size("frames"), lax.axis_size("pos")
    if sizes == (8, 4) and dslice % 128 == 0:
        return local_fused(*args)
    return local_general(*args)


def solution(mesh):
    in_specs = (
        P(("frames", "pos"), None, None),
        P(("frames", "pos")),
        P(),
        P(),
        P(("frames", "pos"), None),
        P(("frames", "pos"), None),
        P("pos", "frames", None),
        P("pos", "frames", None),
        P("pos", "frames", None),
        P(("frames", "pos"), None, None),
    )
    out_specs = (
        P(("frames", "pos"), None, None),
        P(("frames", "pos"), None, None),
        P(("frames", "pos")),
        P(("frames", "pos")),
        P(("frames", "pos"), None),
        P(("frames", "pos"), None),
        P("pos", "frames", None),
        P("pos", "frames", None),
        P("pos", "frames", None),
    )
    return jax.shard_map(local, mesh=mesh, in_specs=in_specs, out_specs=out_specs, check_vma=False)
```

```python
import functools
import math

import jax
import jax.numpy as jnp
from jax import lax
from jax.experimental import pallas as pl
from jax.experimental.pallas import tpu as pltpu
from jax.sharding import PartitionSpec as P

H = 16
HD = 64
BF = jnp.bfloat16
F32 = jnp.float32
MESH = pl.DeviceIdType.MESH
MASKS = (1, 2, 4, 3, 5, 6, 7)
FILL = (7, 9, 4)
PUMP = (8, 0, 12, 4, 2, 1)
LATE = (2, 3)
EARLY = tuple(c for c in range(4) if c not in LATE)
LATE_W = (2, 3)
EARLY_W = tuple(c for c in range(4) if c not in LATE_W)
ANY = pl.BlockSpec(memory_space=pl.ANY)
VM = pl.BlockSpec(memory_space=pltpu.VMEM)


def place():
    return lax.axis_index("frames"), lax.axis_index("pos")


def flip(index, mask):
    bit = 1
    while bit <= mask:
        if mask & bit:
            index = index + bit * (1 - 2 * ((index // bit) % 2))
        bit *= 2
    return index


def greet(nf, nz, every_frame):
    f, z = place()
    hops = [1] + [2 * m for m in range(1, nf // 2)]
    if every_frame:
        hops = list(range(1, nf))
    others = [(flip(f, h), z) for h in hops] + [(f, flip(z, k)) for k in range(1, nz)]
    barrier = pltpu.get_barrier_semaphore()
    for other in others:
        pl.semaphore_signal(barrier, inc=1, device_id=other, device_id_type=MESH)
    pl.semaphore_wait(barrier, len(others))


def remote(src, dst, send, recv, to):
    copy = pltpu.make_async_remote_copy(
        src_ref=src, dst_ref=dst, send_sem=send, recv_sem=recv, device_id=to, device_id_type=MESH
    )
    copy.start()
    return copy


def arrival(dst, send, recv):
    f, z = place()
    pltpu.make_async_remote_copy(
        src_ref=dst,
        dst_ref=dst,
        send_sem=send,
        recv_sem=recv,
        device_id=(flip(f, 1), z),
        device_id_type=MESH,
    ).wait_recv()


def relay_of(k):
    return 1 if k % 2 == 0 else 2


class Gather:
    def __init__(self, nf, nz, src_for, out_at, group_at, sems):
        self.nf, self.nz, self.nc = nf, nz, nf // 2
        self.f, self.z = place()
        self.src_for, self.out_at, self.group_at, self.sems = src_for, out_at, group_at, sems
        self.sent = []
        self.own = {}
        self.tree = self.nc == 4

    @staticmethod
    def sem_shape(nf, nz, parts=1):
        return (2, nz + nf, parts)

    def push(self, src, dst, hop, c, to):
        copy = remote(src, dst, self.sems.at[0, hop, c], self.sems.at[1, hop, c], to)
        self.sent.append((c, copy))

    def arrive(self, dst, hop, c):
        arrival(dst, self.sems.at[0, hop, c], self.sems.at[1, hop, c])

    def near(self, m, c):
        return self.group_at(flip(self.f, 2 * m), c)

    def begin(self, c=0):
        f, z = self.f, self.z
        for k in range(self.nz - 1, 0, -1):
            self.push(self.src_for(flip(z, k), c), self.out_at(f, z, c), k, c, (f, flip(z, k)))
        src, dst = self.src_for(z, c), self.out_at(f, z, c)
        self.own[c] = pltpu.make_async_copy(src, dst, self.sems.at[0, 0, c])
        self.own[c].start()

    def along(self, c=0):
        f, z = self.f, self.z
        self.own[c].wait()
        for k in range(1, self.nz):
            self.arrive(self.out_at(f, flip(z, k), c), k, c)
        group = self.near(0, c)
        for m in range(1, self.nc):
            if not (self.tree and m == 3):
                self.push(group, group, self.nz + m, c, (flip(f, 2 * m), z))
        self.push(group, group, self.nz + self.nc, c, (flip(f, 1), z))

    def over(self, m, c):
        f, z = self.f, self.z
        group = self.near(m, c)
        self.arrive(group, self.nz + m, c)
        if self.tree and m == relay_of(c):
            self.push(group, group, self.nz + 3, c, (flip(f, 2 * (3 - m)), z))
        self.push(group, group, self.nz + self.nc + m, c, (flip(f, 1), z))

    def relay(self, c=0):
        if self.tree:
            self.over(relay_of(c), c)

    def rest(self, c=0):
        for m in range(1, self.nc):
            if not (self.tree and m == relay_of(c)):
                self.over(m, c)

    def whole(self, c=0):
        for m in range(self.nc):
            group = self.group_at(flip(self.f, 2 * m + 1), c)
            self.arrive(group, self.nz + self.nc + m, c)

    def finish(self, part=None):
        for c, copy in self.sent:
            if part is None or c == part:
                copy.wait_send()
        self.sent = [(c, copy) for c, copy in self.sent if part is not None and c != part]


class LateGather(Gather):
    def __init__(self, nf, nz, src_for, out_at, group_at, sems, late_sems):
        super().__init__(nf, nz, src_for, out_at, group_at, sems)
        self.late_sems = late_sems

    @staticmethod
    def late_shape(nf, nz, parts):
        return (2, nz * (nf // 2), parts)

    def block(self, m, k, c):
        return self.out_at(flip(self.f, 2 * m), flip(self.z, k), c)

    def begin(self, c=0):
        f, z = self.f, self.z
        src, dst = self.src_for(z, c), self.out_at(f, z, c)
        for m in range(1, self.nc):
            if not (self.tree and m == 3):
                self.push(src, dst, self.nz + m, c, (flip(f, 2 * m), z))
        self.own[c] = pltpu.make_async_copy(src, dst, self.sems.at[0, 0, c])
        self.own[c].start()

    def relay(self, c=0):
        if self.tree:
            m = relay_of(c)
            block = self.block(m, 0, c)
            self.arrive(block, self.nz + m, c)
            to = (flip(self.f, 2 * (3 - m)), self.z)
            self.push(block, block, self.nz + 3, c, to)

    def along(self, c=0):
        self.own[c].wait()
        for m in range(1, self.nc):
            if not (self.tree and m == relay_of(c)):
                self.arrive(self.block(m, 0, c), self.nz + m, c)
        for k in range(self.nz - 1, 0, -1):
            for m in range(self.nc):
                block, hop = self.block(m, 0, c), k * self.nc + m
                send, recv = self.late_sems.at[0, hop, c], self.late_sems.at[1, hop, c]
                copy = remote(block, block, send, recv, (self.f, flip(self.z, k)))
                self.sent.append((c, copy))

    def rest(self, c=0):
        for m in range(self.nc):
            for k in range(1, self.nz):
                hop = k * self.nc + m
                send, recv = self.late_sems.at[0, hop, c], self.late_sems.at[1, hop, c]
                arrival(self.block(m, k, c), send, recv)
            group = self.near(m, c)
            self.push(group, group, self.nz + self.nc + m, c, (flip(self.f, 1), self.z))


class Swap:
    def __init__(self, nf, src_at, out_at, sems):
        self.nf, self.src_at, self.out_at, self.sems = nf, src_at, out_at, sems
        self.f, self.z = place()
        self.sent = []
        self.own = None

    @staticmethod
    def sem_shape(nf):
        return (2, nf)

    def start(self, masks=None):
        f, z = self.f, self.z
        if self.own is None:
            self.own = pltpu.make_async_copy(self.src_at(f), self.out_at(f), self.sems.at[0, 0])
            self.own.start()
        for m in masks or range(self.nf - 1, 0, -1):
            self.sent.append(
                remote(
                    self.src_at(flip(f, m)),
                    self.out_at(f),
                    self.sems.at[0, m],
                    self.sems.at[1, m],
                    (flip(f, m), z),
                )
            )

    def finish(self):
        self.own.wait()
        for copy in self.sent:
            copy.wait()


class Sums:
    def __init__(self, nf, nz, src_at, own_at, sib, rx, sems):
        self.nf, self.nz, self.nc = nf, nz, nf // 2
        self.f, self.z = place()
        self.src_at, self.own_at, self.sib, self.rx = src_at, own_at, sib, rx
        self.sems = sems
        self.sent = []
        self.tree = self.nc == 4

    @staticmethod
    def buffers(nf, parts, rows, columns):
        nc = nf // 2
        return [
            pltpu.VMEM((parts, nc, rows, columns), BF),
            pltpu.VMEM((parts, nc - 1, rows, columns), BF),
            pltpu.SemaphoreType.DMA((2, 2 * nc, parts)),
        ]

    def push(self, src, dst, sems, hop, k, to):
        self.sent.append(remote(src, dst, sems.at[0, hop, k], sems.at[1, hop, k], to))

    def arrive(self, dst, sems, hop, k):
        arrival(dst, sems.at[0, hop, k], sems.at[1, hop, k])

    def first(self, k):
        if self.tree:
            return [3, relay_of(k)]
        return list(range(self.nc - 1, 0, -1))

    def pairs(self, k):
        f, z = self.f, self.z
        order = self.first(k)
        for m in order + [m for m in range(self.nc - 1, -1, -1) if m not in order]:
            src = self.src_at(flip(f, 2 * m + 1), k)
            self.push(src, self.sib.at[k, m], self.sems, self.nc + m, k, (flip(f, 1), z))

    def chips(self, k):
        f, z = self.f, self.z
        for m in self.first(k):
            sib = self.sib.at[k, m]
            self.arrive(sib, self.sems, self.nc + m, k)
            add_into(sib, self.own_at(k, m), sib)
            hop, to = m, m
            if self.tree:
                hop, to = (2 if m == 3 else 1), relay_of(k)
            self.push(sib, self.rx.at[k, hop - 1], self.sems, hop, k, (flip(f, 2 * to), z))

    def across(self, k):
        if not self.tree:
            return
        m = 3 - relay_of(k)
        sib = self.sib.at[k, m]
        self.arrive(sib, self.sems, self.nc + m, k)
        self.arrive(self.rx.at[k, 1], self.sems, 2, k)
        add_into(sib, self.own_at(k, m), sib, self.rx.at[k, 1])
        self.push(sib, self.rx.at[k, 2], self.sems, 3, k, (flip(self.f, 2 * m), self.z))

    def total(self, k, out):
        self.arrive(self.sib.at[k, 0], self.sems, self.nc, k)
        terms = [self.own_at(k, 0), self.sib.at[k, 0]]
        for m in range(1, self.nc):
            if self.tree and m == 2:
                continue
            self.arrive(self.rx.at[k, m - 1], self.sems, m, k)
            terms.append(self.rx.at[k, m - 1])
        add_into(out, *terms)

    def finish(self):
        for copy in self.sent:
            copy.wait_send()


class HomeSums(Sums):
    def __init__(self, nf, nz, src_at, own_at, sib, rx, sems, home_sems, land, each):
        super().__init__(nf, nz, src_at, own_at, sib, rx, sems)
        self.home_sems, self.land, self.each = home_sems, land, each

    @staticmethod
    def scratch(nf, nz, parts, rows, columns):
        sib, rx, sems = Sums.buffers(nf, parts, rows, columns)
        return [sib, rx, sems, pltpu.SemaphoreType.DMA((2, nz, parts))]

    def rows_of(self, ref, at):
        return ref.at[pl.ds(pl.multiple_of(at * self.each, self.each), self.each)]

    def home(self, p):
        whole = self.sib.at[p, 0]
        self.total(p, whole)
        for k in range(self.nz - 1, 0, -1):
            src = self.rows_of(whole, flip(self.z, k))
            self.push(src, self.sent_to(k, p), self.home_sems, k, p, (self.f, flip(self.z, k)))


class RowSums(HomeSums):
    def at(self, zz, p):
        return self.rows_of(self.land, zz * self.sib.shape[0] + p)

    def sent_to(self, k, p):
        return self.at(self.z, p)

    def landed(self, p):
        self.at(self.z, p)[...] = self.rows_of(self.sib.at[p, 0], self.z)[...]
        for k in range(1, self.nz):
            self.arrive(self.at(flip(self.z, k), p), self.home_sems, k, p)


class BlockSums(HomeSums):
    def sent_to(self, k, p):
        return self.land.at[p, k - 1]

    def landed(self, p, out):
        terms = [self.rows_of(self.sib.at[p, 0], self.z)]
        for k in range(1, self.nz):
            self.arrive(self.land.at[p, k - 1], self.home_sems, k, p)
            terms.append(self.land.at[p, k - 1])
        add_into(out, *terms)


class PosSums(Sums):
    def __init__(self, nf, nz, src_at, own_at, sib, rx, sems, late_sems, zl, each):
        super().__init__(nf, nz, src_at, own_at, sib, rx, sems)
        self.late_sems, self.zl, self.each = late_sems, zl, each

    @staticmethod
    def scratch(nf, nz, parts, each, columns):
        nc = nf // 2
        return [
            pltpu.VMEM((parts, nc, nz * each, columns), BF),
            pltpu.VMEM((parts, nc - 1, each, columns), BF),
            pltpu.SemaphoreType.DMA((2, 2 * nc, parts)),
            pltpu.SemaphoreType.DMA((2, nz * nc, parts)),
            pltpu.VMEM((parts, nc, nz - 1, each, columns), BF),
        ]

    def rows_of(self, ref, at):
        return ref.at[pl.ds(pl.multiple_of(at * self.each, self.each), self.each)]

    def order(self, c):
        first = self.first(c)
        return first + [m for m in range(self.nc - 1, -1, -1) if m not in first]

    def along(self, c):
        for m in self.order(c):
            sib = self.sib.at[c, m]
            self.arrive(sib, self.sems, self.nc + m, c)
            add_into(sib, self.own_at(c, m), sib)
            for k in range(self.nz - 1, 0, -1):
                src = self.rows_of(sib, flip(self.z, k))
                to = (self.f, flip(self.z, k))
                self.push(src, self.zl.at[c, m, k - 1], self.late_sems, k * self.nc + m, c, to)

    def mine(self, m, c):
        terms = [self.rows_of(self.sib.at[c, m], self.z)]
        for k in range(1, self.nz):
            land = self.zl.at[c, m, k - 1]
            self.arrive(land, self.late_sems, k * self.nc + m, c)
            terms.append(land)
        return terms

    def chips(self, c):
        for m in self.first(c):
            terms = self.mine(m, c)
            add_into(terms[0], *terms)
            hop, to = m, m
            if self.tree:
                hop, to = (2 if m == 3 else 1), relay_of(c)
            chip = (flip(self.f, 2 * to), self.z)
            self.push(terms[0], self.rx.at[c, hop - 1], self.sems, hop, c, chip)

    def across(self, c):
        if not self.tree:
            return
        m = 3 - relay_of(c)
        terms = self.mine(m, c)
        self.arrive(self.rx.at[c, 1], self.sems, 2, c)
        add_into(terms[0], *terms, self.rx.at[c, 1])
        self.push(terms[0], self.rx.at[c, 2], self.sems, 3, c, (flip(self.f, 2 * m), self.z))

    def landed(self, c, out):
        terms = self.mine(0, c)
        for m in range(1, self.nc):
            if self.tree and m == 2:
                continue
            self.arrive(self.rx.at[c, m - 1], self.sems, m, c)
            terms.append(self.rx.at[c, m - 1])
        add_into(out, *terms)


def add_into(out, *terms):
    rows = out.shape[0]
    step = 16 if rows % 16 == 0 else rows

    def body(i, carry):
        at = pl.ds(pl.multiple_of(i * step, step), step)
        total = terms[0][at, :].astype(F32)
        for term in terms[1:]:
            total = total + term[at, :].astype(F32)
        out[at, :] = total.astype(out.dtype)
        return carry

    lax.fori_loop(0, rows // step, body, 0)


def call(kernel, ident, **kw):
    return pl.pallas_call(
        kernel,
        compiler_params=pltpu.CompilerParams(
            collective_id=ident, has_side_effects=True, vmem_limit_bytes=63 * 2**20
        ),
        **kw,
    )


def by_block(nf, nz, src_for, out, sems):
    return Gather(
        nf, nz, src_for, lambda ff, zz, c: out.at[ff, zz], lambda ff, c: out.at[ff], sems
    )


def first_kernel(nf, nz, attn, gy, pair, attn_all, gy_all, pair_all, s1, s2, s3):
    greet(nf, nz, True)
    weights = by_block(nf, nz, lambda zz, c: attn, attn_all, s1)
    rows = by_block(nf, nz, lambda zz, c: gy.at[zz], gy_all, s2)
    swap = Swap(nf, lambda ff: pair.at[ff], lambda ff: pair_all.at[ff], s3)
    gathers = (weights, rows)
    for g in gathers:
        g.begin()
    for step in ("along", "relay", "rest", "whole", "finish"):
        for g in gathers:
            getattr(g, step)()
        if step == "relay":
            swap.start()
    swap.finish()


def rows_kernel(nf, nz, b, b_all, s1):
    greet(nf, nz, False)
    rows = by_block(nf, nz, lambda zz, c: b.at[zz], b_all, s1)
    for step in (rows.begin, rows.along, rows.relay, rows.rest, rows.whole, rows.finish):
        step()


def chip_terms(terms):
    f, _ = place()
    return lambda ff, p: terms.at[p, ff], lambda p, m: terms.at[p, flip(f, 2 * m)]


def back_kernel(nf, nz, each, terms, out, sib, rx, sems, home_sems):
    greet(nf, nz, False)
    s = RowSums(nf, nz, *chip_terms(terms), sib, rx, sems, home_sems, out, each)
    for step in (s.pairs, s.chips, s.across, s.home, s.landed):
        for p in range(terms.shape[0]):
            step(p)
    s.finish()


def last_kernel(nf, nz, terms, pair, out, pair_all, sib, rx, sems, home_sems, land, s2):
    greet(nf, nz, True)
    s = BlockSums(nf, nz, *chip_terms(terms), sib, rx, sems, home_sems, land, out.shape[0])
    swap = Swap(nf, lambda ff: pair.at[ff], lambda ff: pair_all.at[ff], s2)
    s.pairs(0)
    swap.start()
    for step in (s.chips, s.across, s.home):
        step(0)
    s.landed(0, out)
    s.finish()
    swap.finish()


def contract(a, b, at_a, at_b):
    return lax.dot_general(a, b, (((at_a,), (at_b,)), ((), ())), preferred_element_type=F32)


def nt(a, b):
    return contract(a, b, 1, 1)


def nn(a, b):
    return contract(a, b, 1, 0)


def tn(a, b):
    return contract(a, b, 0, 0)


def by_position(rows, npos, fr, back=False):
    i = lax.broadcasted_iota(jnp.int32, (rows, rows), 0)
    j = lax.broadcasted_iota(jnp.int32, (rows, rows), 1)
    if back:
        i, j = j, i
    return ((i % fr) * npos + i // fr == j).astype(F32).astype(BF)


def causal(rows, npos):
    i = lax.broadcasted_iota(jnp.int32, (rows, rows), 0)
    j = lax.broadcasted_iota(jnp.int32, (rows, rows), 1)
    return jnp.logical_and(i // npos == j // npos, j <= i)


def soft(q, k, mask):
    s = jnp.where(mask, nt(q, k) * (1.0 / math.sqrt(HD)), -1e30)
    e = jnp.exp(s - jnp.max(s, axis=1, keepdims=True))
    return e / jnp.sum(e, axis=1, keepdims=True)

GROUP=128

def attention_start(x, gain1, a_out):
    xf = x[...].astype(F32)
    rinv1 = lax.rsqrt(jnp.mean(xf * xf, axis=1, keepdims=True) + 1e-05)
    a_out[...] = (xf * rinv1 * gain1[...]).astype(BF)


def columns_of(left, right, first, out):
    step = 512

    def body(i, c):
        at = pl.ds(pl.multiple_of(i * step, step), step)
        to = pl.ds(pl.multiple_of(first + i * step, step), step)
        out[:, to] = nn(left[...], right[:, at]).astype(out.dtype)
        return c

    lax.fori_loop(0, right.shape[1] // step, body, 0)


def attention_heads(npos, qkv, ob):
    rows, d = ob.shape
    mask = causal(GROUP, npos)
    low = lax.broadcasted_iota(jnp.int32, (GROUP, 2 * HD), 1) < HD
    def heads(i, c):
        for g in range(rows // GROUP):
            at = pl.ds(g * GROUP, GROUP)
            q, k, v = (qkv[at, pl.ds(pl.multiple_of(i * 2 * HD + t * d, 2 * HD), 2 * HD)] for t in range(3))
            zero = jnp.zeros_like(q)
            p0 = soft(jnp.where(low, q, zero), k, mask).astype(BF)
            p1 = soft(jnp.where(low, zero, q), k, mask).astype(BF)
            ob[at, pl.ds(pl.multiple_of(i * 2 * HD, 2 * HD), 2 * HD)] = jnp.where(low, nn(p0, v), nn(p1, v)).astype(BF)
        return c
    lax.fori_loop(0, d // (2 * HD), heads, 0, unroll=2)


def attention_end(npos, fr, x, gain2, w_out, ob, x1_out, b_out):
    rows, _ = x.shape
    columns_of(ob, w_out, 0, x1_out)
    x1 = x1_out[...] + x[...].astype(F32)
    x1_out[...] = x1
    rinv2 = lax.rsqrt(jnp.mean(x1 * x1, axis=1, keepdims=True) + 1e-05)
    b = (x1 * rinv2 * gain2[...]).astype(BF)
    b_out[...] = nn(by_position(rows, npos, fr), b).astype(BF)


def weight_terms(left, right, first, out):
    columns = out.shape[1]
    step = 512

    def body(i, c):
        at = pl.ds(pl.multiple_of(i * step, step), step)
        of = pl.ds(pl.multiple_of(first + i * step, step), step)
        out[:, at] = tn(left[...], right[:, of]).astype(BF)
        return c

    lax.fori_loop(0, columns // step, body, 0)


def attention_bwd_in(npos, fr, db_pos, gy, keep, x1_ref, ob, gain2, dx1_s, dxb, terms):
    rows, d = x1_ref.shape
    db = nn(by_position(rows, npos, fr, True), db_pos[...])
    x1 = x1_ref[...]
    rinv2 = lax.rsqrt(jnp.mean(x1 * x1, axis=1, keepdims=True) + 1e-05)
    n2 = db * gain2[...]
    inner = jnp.mean(n2 * x1, axis=1, keepdims=True)
    dx1 = keep[...] * gy[...].astype(F32) + rinv2 * n2 - x1 * (rinv2 * rinv2 * rinv2 * inner)
    dx1_s[...] = dx1
    dxb[...] = dx1.astype(BF)
    weight_terms(ob, dxb, 0, terms)
    return jnp.sum(db * x1 * rinv2, axis=0, keepdims=True)


def attention_bwd_heads(npos, qkv, do_s, dqkv):
    rows, d = do_s.shape
    mask = causal(GROUP, npos)
    low = lax.broadcasted_iota(jnp.int32, (GROUP, 2 * HD), 1) < HD
    scale = 1.0 / math.sqrt(HD)

    def heads(i, c):
        for g in range(rows // GROUP):
            at = pl.ds(g * GROUP, GROUP)
            lanes = [pl.ds(pl.multiple_of(i * 2 * HD + t * d, 2 * HD), 2 * HD) for t in range(3)]
            q, k, v = (qkv[at, l] for l in lanes)
            do = do_s[at, lanes[0]]
            zero = jnp.zeros_like(q)
            parts = []
            for h in range(2):
                keep = low if h == 0 else jnp.logical_not(low)
                p = soft(jnp.where(keep, q, zero), k, mask)
                dp = nt(jnp.where(keep, do, zero), v)
                ds = (p * (dp - jnp.sum(p * dp, axis=1, keepdims=True)) * scale).astype(BF)
                parts.append((nn(ds, k), tn(ds, q), tn(p.astype(BF), do)))
            for t in range(3):
                dqkv[at, lanes[t]] = jnp.where(low, parts[0][t], parts[1][t]).astype(BF)
        return c

    lax.fori_loop(0, d // (2 * HD), heads, 0, unroll=2)


def attention_bwd_rows(x, dqkv, w, gain1, dx1, rows_out):
    d = x.shape[1]
    da = sum(nt(dqkv[:, t * d : (t + 1) * d], w[t]) for t in range(3))
    xf = x[...].astype(F32)
    rinv1 = lax.rsqrt(jnp.mean(xf * xf, axis=1, keepdims=True) + 1e-05)
    n1 = da * gain1[...]
    inner = jnp.mean(n1 * xf, axis=1, keepdims=True)
    rows_out[...] = dx1[...] + rinv1 * n1 - xf * (rinv1 * rinv1 * rinv1 * inner)
    return jnp.sum(da * xf * rinv1, axis=0, keepdims=True)


def gains_into(gain1_grad, gain2_grad, terms):
    d = gain1_grad.shape[1]
    high1 = gain1_grad.astype(BF).astype(F32)
    high2 = gain2_grad.astype(BF).astype(F32)
    at = lax.broadcasted_iota(jnp.int32, (128, d), 0)
    tail = jnp.where(at == 0, high1, 0.0)
    tail = jnp.where(at == 1, high2, tail)
    tail = jnp.where(at == 2, gain1_grad - high1, tail)
    tail = jnp.where(at == 3, gain2_grad - high2, tail)
    terms[...] = tail.T.astype(BF)


class Packer:
    def __init__(self, masters, stage, sems, send):
        self.masters, self.stage, self.sems, self.send = masters, stage, sems, send

    def fetch(self, i, p):
        return pltpu.make_async_copy(self.masters[i].at[p], self.stage.at[i], self.sems.at[i])

    def begin(self):
        for i in range(len(self.masters)):
            self.fetch(i, 0).start()

    def pack(self, p):
        nf, _, lp, ffs, _ = self.send.shape
        for i in range(len(self.masters)):
            self.fetch(i, p).wait()
            turned = self.stage[i].T.astype(BF)
            for j in range(nf):
                self.send[j, i, p] = turned[j * ffs : (j + 1) * ffs]
            if p + 1 < lp:
                self.fetch(i, p + 1).start()


def feed(p, gy_rows, b_rows, pair, wd, hid_out, grads, db, send_db, z):
    nf, _, _, _, width = grads.shape
    b = b_rows[...]
    gate = nt(pair[0, p], b)
    up = nt(pair[1, p], b)
    dhid = nt(wd[...], gy_rows[...])
    s = jax.nn.sigmoid(gate)
    silu = gate * s
    dgate = (dhid * up * s * (1.0 + gate * (1.0 - s))).astype(BF)
    dup = (dhid * silu).astype(BF)
    hid = (silu * up).astype(BF)
    db[...] = (tn(dgate, pair[0, p]) + tn(dup, pair[1, p])).astype(BF)
    send_db()
    hid_out[...] = hid
    for at, term in enumerate((dgate, dup)):
        grad = nn(term, b_rows[...]).astype(BF)
        for j in range(nf):
            grads[j, at, p] = grad[:, j * width : (j + 1) * width]
    z[...] = tn(hid, wd[...]).astype(BF)


def layer_kernel(
    nf, nz, npos, fr,
    x, gy, mask, gain1, gain2, qkv_w, out_w, gate_w, up_w, down_w,
    block_out, rows_grad, total, gains, gy_out, hid_out, back,
    keep, own_w, w, gy_pos, b_pos, send, stage, down, wd, hid, big, pair,
    a, qkv, ob, x1, db_rows, z_rows, tail,
    db_sib, db_rx, z_sib, z_rx,
    t_sib, t_rx, t_sems, t_home, g_sib, g_rx, g_sems, g_home, t_land, g_land,
    l_sib, l_rx, l_sems, l_late, l_zl,
    sems_w, sems_late, sems_gy, sems_b, sems_swap, sems_back, sems_in, sems_out, sems_hid, sem_down,
    sems_db, sems_db_home, sems_z, sems_z_home,
):
    d = x.shape[1]
    each = own_w.shape[1]
    lp = npos // nz
    width = send.shape[4]
    count = nf * nz * fr
    f, z = place()
    packer = Packer((gate_w, up_w), stage, sems_in, send)
    packer.begin()

    def fetch(p):
        return pltpu.make_async_copy(down_w.at[p], down, sem_down)

    fetch(0).start()
    greet(nf, nz, True)
    for i in range(3):
        own_w[i] = qkv_w[:, i * d : (i + 1) * d].astype(BF)
    own_w[3] = out_w[...].astype(BF)

    def span(at, size):
        return pl.ds(pl.multiple_of(at * size, size), size)

    per = d // count

    def rows_at(first, p):
        return big.at[first + p // per, pl.ds((p % per) * count, count)]

    places = (
        lambda zz, c: own_w.at[c],
        lambda ff, zz, c: w.at[c, span(ff * nz + zz, each)],
        lambda ff, c: w.at[c, span(ff, nz * each)],
    )
    early = Gather(nf, nz, *places, sems_w)
    late = LateGather(nf, nz, *places, sems_w, sems_late)

    def rows_gather(mine, every, sems):
        return Gather(
            nf, nz,
            lambda zz, p: mine.at[span(zz * lp + p, fr)],
            lambda ff, zz, p: every(p).at[span(ff * nz + zz, fr)],
            lambda ff, p: every(p).at[span(ff, nz * fr)],
            sems,
        )

    for c in LATE_W:
        late.begin(c)
    for c in EARLY_W:
        early.begin(c)
    frame = lax.broadcasted_iota(jnp.int32, (npos * fr, fr), 0) // npos
    chosen = frame == lax.broadcasted_iota(jnp.int32, (npos * fr, fr), 1)
    alive = jnp.where(chosen, mask[...].astype(F32), 0.0)
    keep[...] = jnp.sum(alive, axis=1, keepdims=True)
    kept = (gy[...].astype(F32) * keep[...]).astype(BF)
    gy_pos[...] = nn(by_position(npos * fr, npos, fr), kept).astype(BF)
    grads = rows_gather(gy_pos, lambda p: rows_at(0, p), sems_gy)
    rows = rows_gather(b_pos, lambda p: rows_at(2, p), sems_b)

    def pair_at(p):
        return lambda ff: pair.at[:, p, :, span(ff, width)]

    def send_at(p):
        return lambda ff: send.at[ff, :, p]

    swaps = [Swap(nf, send_at(p), pair_at(p), sems_swap.at[p]) for p in range(lp)]
    pieces = [(p, m) for p in range(lp) for m in MASKS]

    def pump(count):
        for p, m in pieces[:count]:
            swaps[p].start([m])
        del pieces[:count]

    for p in range(lp):
        grads.begin(p)
    packer.pack(0)
    pump(FILL[0])
    for c in LATE_W:
        late.relay(c)
    for i, c in enumerate(EARLY_W):
        early.along(c)
        if i == 0:
            for at in LATE_W:
                late.along(at)
        else:
            early.relay(EARLY_W[i - 1])
        if i + 1 < lp:
            packer.pack(i + 1)
    early.relay(EARLY_W[-1])
    for c in EARLY_W:
        early.rest(c)
    for p in range(lp):
        grads.along(p)
    for p in range(len(EARLY_W) + 1, lp):
        packer.pack(p)
    attention_start(x, gain1, a)
    for c in range(3):
        if c in LATE_W:
            for p in range(lp if c == LATE_W[0] else 0):
                grads.relay(p)
            pump(FILL[1] if c == LATE_W[0] else 0)
            late.rest(c)
        (late if c in LATE_W else early).whole(c)
        columns_of(a, w.at[c], c * d, qkv)
    attention_heads(npos, qkv, ob)
    pump(FILL[2])
    late.rest(3)
    late.whole(3)
    attention_end(npos, fr, x, gain2, w.at[3], ob, x1, b_pos)
    for p in range(lp):
        rows.begin(p)
    early.finish()
    late.finish()
    for p in range(lp):
        grads.rest(p)
    for p in range(lp):
        rows.along(p)
        if p >= 1:
            rows.relay(p - 1)
    rows.relay(lp - 1)
    pump(len(pieces))
    for p in range(lp):
        grads.whole(p)
    grads.finish()
    save_gy = pltpu.make_async_copy(big.at[: 2], gy_out, sems_out.at[0])
    save_gy.start()
    share = count // nf

    def sums(first, sib, rx, sems, home_sems, land):
        def at(ff, p):
            return rows_at(first, p).at[span(ff, share)]

        return RowSums(
            nf, nz, at, lambda p, m: at(flip(f, 2 * m), p), sib, rx, sems, home_sems, land, fr
        )

    s_db = sums(0, db_sib, db_rx, sems_db, sems_db_home, db_rows)
    s_z = sums(2, z_sib, z_rx, sems_z, sems_z_home, z_rows)

    def back_at(p):
        return lambda ff: back.at[ff, :, p]

    backs = [Swap(nf, send_at(p), back_at(p), sems_back.at[p]) for p in range(lp)]
    grad_pieces = [(p, m) for p in range(lp) for m in MASKS]

    def pump_back(size):
        for p, m in grad_pieces[:size]:
            backs[p].start([m])
        del grad_pieces[:size]

    def save_hid(p):
        return pltpu.make_async_copy(hid.at[p % 2], hid_out.at[p], sems_hid.at[p % 2])

    rows.rest(0)
    save_gy.wait()
    for p in range(lp):
        if p + 1 < lp:
            rows.rest(p + 1)
        fetch(p).wait()
        wd[...] = down[...].astype(BF)
        if p + 1 < lp:
            fetch(p + 1).start()
        rows.whole(p)
        rows.finish(p)
        swaps[p].finish()
        if p >= 2:
            save_hid(p - 2).wait()
        gy_rows, b_rows = rows_at(0, p), rows_at(2, p)
        send_db = functools.partial(s_db.pairs, p)
        feed(p, gy_rows, b_rows, pair, wd, hid.at[p % 2], send, gy_rows, send_db, b_rows)
        save_hid(p).start()
        if p >= 1:
            s_db.chips(p - 1)
        if p >= 2:
            s_db.across(p - 2)
        if p >= 3:
            s_db.home(p - 3)
        s_z.pairs(p)
    for name, last in (("chips", 1), ("across", 2)):
        for p in range(max(lp - last, 0), lp):
            getattr(s_db, name)(p)
        if name == "chips":
            s_z.chips(0)
            s_z.chips(1)
    pump_back(PUMP[0])
    for p in range(max(lp - 3, 0), lp):
        s_db.home(p)
    for p in range(2, lp):
        s_z.chips(p)
    for p in range(2):
        s_z.across(p)
    pump_back(PUMP[1])
    for p in range(lp):
        s_db.landed(p)
    s_db.finish()

    def slot(c):
        return big.at[(c + 2) % 4]

    def terms_of(table):
        return (
            lambda ff, c: slot(table[c]).at[span(ff, nz * each)],
            lambda c, m: slot(table[c]).at[span(flip(f, 2 * m), nz * each)],
        )

    s_t = BlockSums(nf, nz, *terms_of(EARLY), t_sib, t_rx, t_sems, t_home, t_land, each)
    s_l = PosSums(nf, nz, *terms_of(LATE), l_sib, l_rx, l_sems, l_late, l_zl, each)
    s_g = BlockSums(
        nf, nz,
        lambda ff, c: tail.at[span(ff, nz * each)],
        lambda c, m: tail.at[span(flip(f, 2 * m), nz * each)],
        g_sib, g_rx, g_sems, g_home, g_land, each,
    )

    def both(step, c):
        group, at = (s_l, LATE.index(c)) if c in LATE else (s_t, EARLY.index(c))
        getattr(group, step)(at)

    dx1, dxb, do, dqkv = rows_grad, b_pos, gy_pos, qkv
    gain2_grad = attention_bwd_in(npos, fr, db_rows, gy, keep, x1, ob, gain2, dx1, dxb, slot(3))
    both("pairs", 3)
    do[...] = nt(dxb[...], w[3]).astype(BF)
    both("along", 3)
    for p in range(2, lp):
        s_z.across(p)
    pump_back(PUMP[2])
    attention_bwd_heads(npos, qkv, do, dqkv)
    weight_terms(a, dqkv, 2 * d, slot(2))
    both("pairs", 2)
    for p in range(lp):
        s_z.home(p)
    s_z.finish()
    pump_back(PUMP[3])
    weight_terms(a, dqkv, 0, slot(0))
    both("pairs", 0)
    both("along", 2)
    weight_terms(a, dqkv, d, slot(1))
    both("pairs", 1)
    both("chips", 0)
    gain1_grad = attention_bwd_rows(x, dqkv, w, gain1, dx1, rows_grad)
    gains_into(gain1_grad, gain2_grad, tail)
    s_g.pairs(0)
    both("chips", 1)
    s_g.chips(0)
    pump_back(PUMP[4])
    both("across", 0)
    both("across", 1)
    s_g.across(0)
    for c in LATE:
        both("chips", c)
    pump_back(PUMP[5])
    both("home", 0)
    both("home", 1)
    s_g.home(0)
    for c in LATE:
        both("across", c)
    pump_back(len(grad_pieces))
    for p in range(lp):
        s_z.landed(p)
    turned = nn(by_position(npos * fr, npos, fr, True), z_rows[...])
    block_out[...] = (keep[...] * (x1[...] + turned)).astype(BF)
    for group, table in ((s_t, EARLY), (s_l, LATE)):
        for at, c in enumerate(table):
            group.landed(at, total.at[:, pl.ds(c * d, d)])
    s_g.landed(0, gains)
    for p in range(max(lp - 2, 0), lp):
        save_hid(p).wait()
    for group in (s_t, s_l, s_g):
        group.finish()
    for swap in backs:
        swap.finish()


def last_local_kernel(
    pair, hid, gy, total, gains, block_out, rows_grad,
    gate, up, down, qkv_grad, out_grad, gain1_grad, gain2_grad, y, dx,
):
    nf, _, _, ffs, width = pair.shape
    d = gy.shape[2]

    @pl.when(pl.program_id(0) == 0)
    def _():
        qkv_grad[...] = total[:, : 3 * d]
        out_grad[...] = total[:, 3 * d :]
        turned = gains[...].T
        gain1_grad[...] = turned[0] + turned[2]
        gain2_grad[...] = turned[1] + turned[3]

    y[...] = block_out[...]
    dx[...] = rows_grad[...]
    for at, out in enumerate((gate, up)):
        out[0] = pair[:, at, 0].astype(F32).reshape(nf * ffs, width).T
    down[0] = nn(hid[0], gy[0])


def rms_norm(values, gain_vector):
    return (
        values * lax.rsqrt(jnp.mean(values * values, axis=-1, keepdims=True) + 1e-05) * gain_vector
    )


def attend(qkv_rows):
    frame_count = qkv_rows.shape[0]
    positions = qkv_rows.shape[1]
    split_rows = qkv_rows.reshape(frame_count, positions, 3, H, HD)
    queries = split_rows[:, :, 0]
    keys_all = split_rows[:, :, 1]
    values_all = split_rows[:, :, 2]
    scores = jnp.einsum("fqhe,fkhe->fhqk", queries, keys_all, preferred_element_type=F32) * (
        1.0 / math.sqrt(HD)
    )
    causal = jnp.arange(positions)[:, None] >= jnp.arange(positions)[None, :]
    scores = jnp.where(causal, scores, -1e30)
    weights = jax.nn.softmax(scores, axis=-1)
    mixed = jnp.einsum("fhqk,fkhe->fqhe", weights, values_all, preferred_element_type=F32)
    return mixed.reshape(frame_count, positions, H * HD)


def local_general(
    frame_rows,
    frame_mask,
    gain_attention,
    gain_feed,
    qkv_master,
    out_master,
    gate_master,
    up_master,
    down_master,
    out_cotangent,
):
    nf = lax.axis_size("frames")
    nz = lax.axis_size("pos")
    lp, dslice, ff = gate_master.shape
    ffs = down_master.shape[1]
    fr, npos, d = frame_rows.shape

    keep_rows = frame_mask.astype(F32)[:, None, None]
    inputs = frame_rows.astype(F32)

    def turned(w):
        return w.astype(BF).reshape(lp, dslice, nf, ffs).transpose(2, 0, 3, 1)

    def untwist(w):
        return w.transpose(1, 2, 0, 3).reshape(lp, ffs, d)

    def to_pos(rows):
        return rows.transpose(1, 0, 2).reshape(nz, lp * fr, d)

    def gathered(every):
        every = every.reshape(nf, nz, lp, fr, d)
        return every.transpose(2, 0, 1, 3, 4).reshape(lp, nf * nz * fr, d)

    rows_shape = jax.ShapeDtypeStruct((nf, nz, lp * fr, d), BF)
    back_shape = jax.ShapeDtypeStruct((npos * fr, d), BF)
    gather_sems = pltpu.SemaphoreType.DMA(Gather.sem_shape(nf, nz))
    swap_sems = pltpu.SemaphoreType.DMA(Swap.sem_shape(nf))

    def scattered(rows, ident):
        back = call(
            functools.partial(back_kernel, nf, nz, fr),
            ident,
            out_shape=back_shape,
            in_specs=[VM],
            out_specs=VM,
            scratch_shapes=HomeSums.scratch(nf, nz, lp, nz * fr, d),
        )(rows.reshape(lp, nf, nz * fr, d))
        return back.reshape(npos, fr, d).transpose(1, 0, 2)

    both = jnp.concatenate((qkv_master.astype(BF), out_master.astype(BF)), axis=1)
    pair = jnp.stack((turned(gate_master), turned(up_master)), axis=1)
    upstream = keep_rows * out_cotangent.astype(F32)
    own_rows = both.shape[0]
    w_all, gy_all, pair = call(
        functools.partial(first_kernel, nf, nz),
        0,
        out_shape=(
            jax.ShapeDtypeStruct((nf, nz) + both.shape, BF),
            rows_shape,
            jax.ShapeDtypeStruct(pair.shape, BF),
        ),
        in_specs=[ANY] * 3,
        out_specs=(ANY,) * 3,
        scratch_shapes=[gather_sems, gather_sems, swap_sems],
    )(both, to_pos(upstream.astype(BF)), pair)
    w_all = w_all.reshape(d, both.shape[1])
    w_qkv = w_all[:, : 3 * d]
    w_out = w_all[:, 3 * d :]
    gate_t = untwist(pair[:, 0])
    up_t = untwist(pair[:, 1])
    down = down_master.astype(BF)
    gy = gathered(gy_all)

    normed_one, norm_one_pull = jax.vjp(rms_norm, inputs, gain_attention)
    normed_low = normed_one.astype(BF)
    qkv_rows = jnp.einsum("fpd,de->fpe", normed_low, w_qkv, preferred_element_type=F32)
    mixed, attend_pull = jax.vjp(attend, qkv_rows)
    mixed_low = mixed.astype(BF)
    branch = jnp.einsum("fpd,de->fpe", mixed_low, w_out, preferred_element_type=F32)
    middle = inputs + branch
    normed_two, norm_two_pull = jax.vjp(rms_norm, middle, gain_feed)
    b_all = call(
        functools.partial(rows_kernel, nf, nz),
        1,
        out_shape=rows_shape,
        in_specs=[ANY],
        out_specs=ANY,
        scratch_shapes=[gather_sems],
    )(to_pos(normed_two.astype(BF)))
    b = gathered(b_all)

    gate_rows = jnp.einsum("prd,phd->phr", b, gate_t, preferred_element_type=F32)
    up_rows = jnp.einsum("prd,phd->phr", b, up_t, preferred_element_type=F32)
    hidden_grad = jnp.einsum("prd,phd->phr", gy, down, preferred_element_type=F32)
    sigma = jax.nn.sigmoid(gate_rows)
    silu_gate = gate_rows * sigma
    hidden = (silu_gate * up_rows).astype(BF)
    gate_back = (hidden_grad * up_rows * sigma * (1.0 + gate_rows * (1.0 - sigma))).astype(BF)
    up_back = (hidden_grad * silu_gate).astype(BF)
    db = jnp.einsum("phr,phd->prd", gate_back, gate_t, preferred_element_type=F32) + jnp.einsum(
        "phr,phd->prd", up_back, up_t, preferred_element_type=F32
    )
    back_rows = scattered(db.astype(BF), 2).astype(F32)
    feed = jnp.einsum("phr,phd->prd", hidden, down, preferred_element_type=F32)
    returned = scattered(feed.astype(BF), 3).astype(F32)
    block_out = (keep_rows * (middle + returned)).astype(BF)
    gate_grad = jnp.einsum("phr,prd->phd", gate_back, b, preferred_element_type=F32).astype(BF)
    up_grad = jnp.einsum("phr,prd->phd", up_back, b, preferred_element_type=F32).astype(BF)
    down_grad = jnp.einsum("phr,prd->phd", hidden, gy, preferred_element_type=F32)

    grads = jnp.stack((gate_grad, up_grad), axis=0).reshape(2, lp, ffs, nf, dslice)
    grads = grads.transpose(3, 0, 1, 2, 4)

    pulled_two = norm_two_pull(back_rows)
    middle_grad = upstream + pulled_two[0]
    branch_grad = middle_grad.astype(BF)
    out_weight_grad = jnp.einsum("fpd,fpe->de", mixed_low, branch_grad, preferred_element_type=F32)
    mixed_grad = jnp.einsum("fpe,de->fpd", branch_grad, w_out, preferred_element_type=F32)
    qkv_back = attend_pull(mixed_grad)[0].astype(BF)
    qkv_weight_grad = jnp.einsum("fpd,fpe->de", normed_low, qkv_back, preferred_element_type=F32)
    normed_grad = jnp.einsum("fpe,de->fpd", qkv_back, w_qkv, preferred_element_type=F32)
    pulled_one = norm_one_pull(normed_grad)
    rows_grad = middle_grad + pulled_one[0]

    gains = jnp.stack((pulled_one[1], pulled_two[1]), axis=1)
    gains_hi = gains.astype(BF)
    gains_lo = (gains - gains_hi.astype(F32)).astype(BF)
    unit = max(128, 2048 // own_rows)
    spare = -(4 * d + 4) % unit
    tail = jnp.concatenate((gains_hi, gains_lo, jnp.zeros((d, spare), BF)), axis=1)
    total = jnp.concatenate(
        (qkv_weight_grad.astype(BF), out_weight_grad.astype(BF), tail), axis=1
    )
    block = own_rows * total.shape[1] // 128
    total, grads = call(
        functools.partial(last_kernel, nf, nz),
        4,
        out_shape=(
            jax.ShapeDtypeStruct((block, 128), F32),
            jax.ShapeDtypeStruct(grads.shape, BF),
        ),
        in_specs=[VM, ANY],
        out_specs=(VM, ANY),
        scratch_shapes=HomeSums.scratch(nf, nz, 1, nz * block, 128)
        + [pltpu.VMEM((1, nz - 1, block, 128), BF), swap_sems],
    )(total.reshape(1, nf, nz * block, 128), grads)
    grads = grads.transpose(1, 2, 4, 0, 3).reshape(2, lp, dslice, ff).astype(F32)
    total = total.reshape(own_rows, 4 * d + 4 + spare)
    gain_grads = total[:, 4 * d : 4 * d + 2] + total[:, 4 * d + 2 : 4 * d + 4]
    return (
        block_out,
        rows_grad,
        gain_grads[:, 0],
        gain_grads[:, 1],
        total[:, : 3 * d],
        total[:, 3 * d : 4 * d],
        grads[0],
        grads[1],
        down_grad,
    )
def local_fused(
    frame_rows,
    frame_mask,
    gain_attention,
    gain_feed,
    qkv_master,
    out_master,
    gate_master,
    up_master,
    down_master,
    out_cotangent,
):
    nf = lax.axis_size("frames")
    nz = lax.axis_size("pos")
    lp, dslice, ff = gate_master.shape
    ffs = down_master.shape[1]
    fr, npos, d = frame_rows.shape
    rows = fr * npos
    each = qkv_master.shape[0]
    count = nf * nz * fr

    def make(shape, kind=BF):
        return jax.ShapeDtypeStruct(shape, kind)

    def vmem(shape, kind=BF):
        return pltpu.VMEM(shape, kind)

    def dma(*shape):
        return pltpu.SemaphoreType.DMA(shape)

    x = frame_rows.reshape(rows, d)
    gy = out_cotangent.reshape(rows, d)
    mask = frame_mask.reshape(1, fr)
    gain1 = gain_attention.reshape(1, d)
    gain2 = gain_feed.reshape(1, d)
    gather_sems = dma(*Gather.sem_shape(nf, nz, 4))
    rows_sems = dma(*Gather.sem_shape(nf, nz, lp))
    swap_sems = dma(lp, *Swap.sem_shape(nf))
    pair_shape = (nf, 2, lp, ffs, dslice)
    row_scratch = HomeSums.scratch(nf, nz, lp, nz * fr, d)
    block_out, rows_grad, total, gains, gy_all, hid, back = call(
        functools.partial(layer_kernel, nf, nz, npos, fr),
        0,
        out_shape=(
            make((rows, d)),
            make((rows, d), F32),
            make((each, 4 * d), F32),
            make((each, 128), F32),
            make((2, d, d)),
            make((lp, ffs, count)),
            make(pair_shape),
        ),
        in_specs=[VM] * 7 + [ANY] * 3,
        out_specs=(VM,) * 4 + (ANY,) * 3,
        scratch_shapes=[
            vmem((rows, 1), F32),
            vmem((4, each, d)),
            vmem((4, d, d)),
            vmem((rows, d)),
            vmem((rows, d)),
            vmem(pair_shape),
            vmem((2, dslice, ff), F32),
            vmem((ffs, d), F32),
            vmem((ffs, d)),
            vmem((2, ffs, count)),
            vmem((4, d, d)),
            vmem((2, lp, ffs, d)),
            vmem((rows, d)),
            vmem((rows, 3 * d)),
            vmem((rows, d)),
            vmem((rows, d), F32),
            vmem((rows, d)),
            vmem((rows, d)),
            vmem((d, 128)),
            *row_scratch[:2],
            *row_scratch[:2],
            *HomeSums.scratch(nf, nz, len(EARLY), nz * each, d),
            *HomeSums.scratch(nf, nz, 1, nz * each, 128),
            vmem((len(EARLY), nz - 1, each, d)),
            vmem((1, nz - 1, each, 128)),
            *PosSums.scratch(nf, nz, len(LATE), each, d),
            gather_sems,
            dma(*LateGather.late_shape(nf, nz, 4)),
            rows_sems,
            rows_sems,
            swap_sems,
            swap_sems,
            dma(2),
            dma(1),
            dma(2),
            pltpu.SemaphoreType.DMA,
            *row_scratch[2:],
            *row_scratch[2:],
        ],
    )(x, gy, mask, gain1, gain2, qkv_master, out_master, gate_master, up_master, down_master)
    gy_all = gy_all.reshape(lp, count, d)
    whole_block = pl.BlockSpec((1, dslice, ff), lambda p: (p, 0, 0))

    def once(*shape):
        return pl.BlockSpec(shape, lambda p: (0, 0))

    part_block = pl.BlockSpec((rows // lp, d), lambda p: (p, 0))
    one = pl.BlockSpec((each,), lambda p: (0,))
    gate_grad, up_grad, down_grad, qkv_grad, out_grad, gain1_grad, gain2_grad, y, dx = pl.pallas_call(
        last_local_kernel,
        grid=(lp,),
        out_shape=(
            make((lp, dslice, ff), F32),
            make((lp, dslice, ff), F32),
            make((lp, ffs, d), F32),
            make((each, 3 * d), F32),
            make((each, d), F32),
            make((each,), F32),
            make((each,), F32),
            make((rows, d)),
            make((rows, d), F32),
        ),
        in_specs=[
            pl.BlockSpec((nf, 2, 1, ffs, dslice), lambda p: (0, 0, p, 0, 0)),
            pl.BlockSpec((1, ffs, count), lambda p: (p, 0, 0)),
            pl.BlockSpec((1, count, d), lambda p: (p, 0, 0)),
            once(each, 4 * d),
            once(each, 128),
            part_block,
            part_block,
        ],
        out_specs=(
            whole_block,
            whole_block,
            pl.BlockSpec((1, ffs, d), lambda p: (p, 0, 0)),
            once(each, 3 * d),
            once(each, d),
            one,
            one,
            part_block,
            part_block,
        ),
        compiler_params=pltpu.CompilerParams(vmem_limit_bytes=60 * 2**20),
    )(back, hid, gy_all, total, gains, block_out, rows_grad)
    return (
        y.reshape(fr, npos, d),
        dx.reshape(fr, npos, d),
        gain1_grad,
        gain2_grad,
        qkv_grad,
        out_grad,
        gate_grad,
        up_grad,
        down_grad,
    )


def local(*args):
    _, dslice, _ = args[6].shape
    sizes = lax.axis_size("frames"), lax.axis_size("pos")
    if sizes == (8, 4) and dslice % 128 == 0:
        return local_fused(*args)
    return local_general(*args)


def solution(mesh):
    in_specs = (
        P(("frames", "pos"), None, None),
        P(("frames", "pos")),
        P(),
        P(),
        P(("frames", "pos"), None),
        P(("frames", "pos"), None),
        P("pos", "frames", None),
        P("pos", "frames", None),
        P("pos", "frames", None),
        P(("frames", "pos"), None, None),
    )
    out_specs = (
        P(("frames", "pos"), None, None),
        P(("frames", "pos"), None, None),
        P(("frames", "pos")),
        P(("frames", "pos")),
        P(("frames", "pos"), None),
        P(("frames", "pos"), None),
        P("pos", "frames", None),
        P("pos", "frames", None),
        P("pos", "frames", None),
    )
    return jax.shard_map(local, mesh=mesh, in_specs=in_specs, out_specs=out_specs, check_vma=False)
```
